32 devices in a mesh: cfg: 2 (over x), space: 8 (over z, y), diag: 2 (over core).
Axes of the slice: x: 2, y: 2, z: 4, core: 2. Of those that a mesh axis runs over, the one named last changes fastest.
Arguments:
- eigvecs: bfloat16 [8, 2, 3, 128, 16, 256], P('cfg', None, None, None, ('space', 'diag')), parts along dimension 0, may hold values from -6 to 6
- gauge_links: float32 [8, 3, 2, 3, 3, 16, 256], P('cfg', None, None, None, None, ('space', 'diag')), parts along dimension 0, may hold values from -6 to 6
- momenta: int32 [4, 3], replicated, may hold values from -2 to 2
- spin_mix: float32 [16, 4, 4], replicated, may hold values from -4 to 4
- perambulators: bfloat16 [64, 4, 2, 128, 512], P(('cfg', 'space', 'diag')), parts along dimension 0, may hold values from -0.375 to 0.375
- contraction_list: int32 [32, 3], P(('space', 'diag')), may hold values from 0 to 63, as said below
Outputs:
- diagrams: bfloat16 [64, 4, 2, 128, 512], P(('cfg', 'space', 'diag')), parts along dimension 0
The draws below stay inside these ranges and needn't reach their ends.
There are 2 independent parts, one for each index of `cfg`. The reference program is written for one: setup_inputs(seed, part) draws one part's arguments, and reference() takes and returns one part's arrays. A program takes and returns all parts, laid end to end along the dimension named above; an argument that names none is the same for every part. Nothing has to cross between parts.
Inputs may be any that keep to these rules, and one draw needn't show every extreme that they name: `contraction_list`: row j is one diagram. Column 0 is an elemental item below 64, column 1 a spin structure below 16, column 2 a perambulator q with q // 2 == j // 2; each aligned group of 2 rows names each of its 2 perambulators exactly once.
All inputs are finite; a program needn't handle non-finite values.
Results may differ from the reference program's by a relative error of at most 0.0064.
Values may be sent and summed in bfloat16 or wider, within the bound.
A program may use at most 128 MiB of HBM per device.

```python
import math
import jax
import jax.numpy as jnp
from jax import lax

TW = 4
NEV = 128
NCOL = 3
NSPIN = 4
NMOM = 4
NDISP = 4
NGAMMA = 16
LX = 16
LY = 16
DIAG_DEV = 2
PERAM_DEV = 2
NZ = 16
NITEM = 64
NDIAG = 32
NPERAM = 32


def draw_contraction_list(key, part):
    key_elem = jax.random.fold_in(key, 11)
    key_spin = jax.random.fold_in(key, 12)
    key_slot = jax.random.fold_in(key, 13)
    owners = NDIAG // DIAG_DEV
    element = jax.random.randint(key_elem, (NDIAG,), 0, NITEM)
    element = element.at[0].set(NITEM - 1)
    structure = jax.random.randint(key_spin, (NDIAG,), 0, NGAMMA)
    pattern = jnp.arange(DIAG_DEV) % PERAM_DEV
    slots = jax.vmap(lambda sub_key: jax.random.permutation(sub_key, pattern))(jax.random.split(key_slot, owners))
    peram_index = (jnp.arange(owners)[:, None] * PERAM_DEV + slots).reshape(NDIAG)
    return jnp.stack([element, structure, peram_index], 1).astype(jnp.int32)


def plant(entries, own_key, smallest, largest):
    spot = [jax.random.randint(jax.random.fold_in(own_key, axis), (), 0, length) for axis, length in enumerate(entries.shape)]
    main_axis = entries.shape.index(max(entries.shape))
    beside = spot[:main_axis] + [(spot[main_axis] + 1) % entries.shape[main_axis]] + spot[main_axis + 1:]
    return entries.at[tuple(spot)].set(smallest).at[tuple(beside)].set(largest)


def shard_levels(rng, shape, cuts, least, top_value):
    loudness, own = 1.0, jax.random.fold_in(rng, 6)
    for dim, shards_of in cuts:
        steps = jnp.exp(jax.random.uniform(jax.random.fold_in(own, dim), (shards_of,), jnp.float32, least / len(cuts), top_value / len(cuts)))
        loudness = loudness * jnp.repeat(steps, shape[dim] // shards_of).reshape([-1 if axis == dim else 1 for axis in range(len(shape))])
    return loudness


def normal_values(own_key, dims, spread, most, cuts=(), dtype=jnp.bfloat16):
    drawn = jax.random.normal(own_key, dims, jnp.float32) * spread
    if len(cuts) > 0:
        drawn = shard_levels(own_key, dims, cuts, -0.22, 0.18) * drawn
    return jnp.clip(drawn, min=-most, max=most).astype(dtype)


def setup_inputs(seed: int = 0, part: int = 0) -> dict:
    arg_keys = jax.random.split(jax.random.key(seed), 7)
    part_keys = jax.random.split(jax.random.fold_in(arg_keys[6], part), 7)
    return {
        "eigvecs": normal_values(part_keys[0], (TW, 2, NCOL, NEV, NZ, LX * LY), 1.0, 6.0, ((4, 16),)),
        "gauge_links": normal_values(part_keys[1], (TW, 3, 2, NCOL, NCOL, NZ, LX * LY), 0.6, 6.0, ((5, 16),), jnp.float32),
        "momenta": plant(jax.random.randint(arg_keys[2], (NMOM, 3), -2, 3), jax.random.fold_in(arg_keys[2], 1), -2, 2).astype(jnp.int32),
        "spin_mix": normal_values(arg_keys[3], (NGAMMA, NSPIN, NSPIN), 0.5, 4.0, (), jnp.float32),
        "perambulators": normal_values(part_keys[4], (NPERAM, NSPIN, 2, NEV, NSPIN * NEV), (2 * NEV) ** -0.5, 0.375, ((0, 16),)),
        "contraction_list": draw_contraction_list(jax.random.fold_in(arg_keys[6], 71), part),
    }


highest = lax.Precision.HIGHEST

def widen(value):
    return lax.optimization_barrier(value).astype(jnp.float32)

def color_apply(matrix, vector):
    real_rows = []
    imag_rows = []
    for row in range(3):
        real_part = jnp.zeros(vector.shape[2:], jnp.float32)
        imag_part = jnp.zeros(vector.shape[2:], jnp.float32)
        for column in range(3):
            mreal = matrix[0, row, column][None]
            mimag = matrix[1, row, column][None]
            real_part = real_part + mreal * vector[0, column] - mimag * vector[1, column]
            imag_part = imag_part + mreal * vector[1, column] + mimag * vector[0, column]
        real_rows.append(real_part)
        imag_rows.append(imag_part)
    return jnp.stack([jnp.stack(real_rows), jnp.stack(imag_rows)])

def color_adjoint(matrix, vector):
    real_rows = []
    imag_rows = []
    for row in range(3):
        real_part = jnp.zeros(vector.shape[2:], jnp.float32)
        imag_part = jnp.zeros(vector.shape[2:], jnp.float32)
        for column in range(3):
            mreal = matrix[0, column, row][None]
            mimag = matrix[1, column, row][None]
            real_part = real_part + mreal * vector[0, column] + mimag * vector[1, column]
            imag_part = imag_part + mreal * vector[1, column] - mimag * vector[0, column]
        real_rows.append(real_part)
        imag_rows.append(imag_part)
    return jnp.stack([jnp.stack(real_rows), jnp.stack(imag_rows)])

def neighbour(field, direction, offset, width):
    xcoord = jnp.arange(field.shape[-1]) % width
    if direction == 0:
        if offset == 1:
            return jnp.where(xcoord == width - 1, jnp.roll(field, width - 1, -1), jnp.roll(field, -1, -1))
        return jnp.where(xcoord == 0, jnp.roll(field, 1 - width, -1), jnp.roll(field, 1, -1))
    if direction == 1:
        return jnp.roll(field, -offset * width, -1)
    return jnp.roll(field, -offset, -2)

def phase_table(momenta, zcoord, plane, total_z):
    flat = jnp.arange(plane)
    xcoord = (flat % LX).astype(jnp.float32)
    ycoord = (flat // LX).astype(jnp.float32)
    moment = momenta.astype(jnp.float32)
    zvalue = zcoord.astype(jnp.float32)
    angle = 2.0 * math.pi * (moment[:, 0, None, None] * xcoord[None, None, :] / LX + moment[:, 1, None, None] * ycoord[None, None, :] / LY + moment[:, 2, None, None] * zvalue[None, :, None] / total_z)
    return (jnp.cos(angle), jnp.sin(angle))

def phase_apply(cosine, sine, vector):
    cos_part = cosine[:, None, None]
    sin_part = sine[:, None, None]
    real_part = cos_part * vector[0] - sin_part * vector[1]
    imag_part = sin_part * vector[0] + cos_part * vector[1]
    return jnp.stack([real_part, imag_part], 1).astype(jnp.bfloat16)

def reference(eigvecs, gauge_links, momenta, spin_mix, perambulators, contraction_list):
    total_z = eigvecs.shape[4]
    plane = eigvecs.shape[5]
    scale = 1.0 / math.sqrt(3 * plane * total_z)
    cosine, sine = phase_table(momenta, jnp.arange(total_z), plane, total_z)
    item_list = []
    for slice_index in range(TW):
        vector = eigvecs[slice_index].astype(jnp.float32)
        links_now = gauge_links[slice_index]
        shifted_list = [eigvecs[slice_index]]
        for direction in range(3):
            adjoint = color_adjoint(links_now[direction], vector).astype(jnp.bfloat16)
            forward = color_apply(links_now[direction], neighbour(vector, direction, 1, LX))
            backward = neighbour(widen(adjoint), direction, -1, LX)
            shifted_list.append((0.5 * (forward - backward)).astype(jnp.bfloat16))
        phased = widen(phase_apply(cosine, sine, vector))
        per_disp = []
        for shifted in shifted_list:
            wide = widen(shifted)
            rhs = jnp.stack([wide, jnp.stack([wide[1], -wide[0]])])
            per_disp.append(jnp.einsum('mpckzs,opclzs->mokl', phased, rhs, precision=highest))
        grams = jnp.stack(per_disp, 1)
        item_list.append(grams.reshape(NMOM * NDISP, 2, NEV, NEV))
    elementals = (jnp.concatenate(item_list) * scale).astype(jnp.bfloat16)

    def diagram(entry):
        chosen = elementals[entry[0]].astype(jnp.float32)
        upper_rows = jnp.concatenate([chosen[0], -chosen[1]], 1)
        lower_rows = jnp.concatenate([chosen[1], chosen[0]], 1)
        square = jnp.concatenate([upper_rows, lower_rows], 0)
        tau = perambulators[entry[2]].astype(jnp.float32).reshape(NSPIN, 2 * NEV, NSPIN * NEV)
        blocks = jnp.einsum('ab,sbc->sac', square, tau, precision=highest)
        weights = spin_mix[entry[1]].astype(jnp.float32)
        mixed = weights[:, 0, None, None] * blocks[0][None]
        for spin in range(1, NSPIN):
            mixed = mixed + weights[:, spin, None, None] * blocks[spin][None]
        return mixed.astype(jnp.bfloat16).reshape(NSPIN, 2, NEV, NSPIN * NEV)
    return lax.map(diagram, contraction_list)
```

```python
import functools
import math

import jax
import jax.numpy as jnp
from jax import lax
from jax.experimental import pallas as pl
from jax.experimental.pallas import tpu as pltpu
from jax.sharding import PartitionSpec as P

LX = 16
LY = 16
NDISP = 4
CHUNK = 16
MESH = pl.DeviceIdType.MESH
NT = (((1,), (1,)), ((), ()))
f32 = jnp.float32
bf16 = jnp.bfloat16


def elemental_kernel(
    dims, list_ref, mom_ref, spin_ref, link_ref, eig_hbm, tau_hbm, out_ref, mix_hbm,
    eig_ref, cos_ref, sin_ref, ar_ref, ai_ref, above, fields, plus, minus, tau_ref, mix_ref, lists, table,
    part1, recv1, own, part2, recv2, part3, recv3,
    e_local, t_local, m_local, v_send, v_recv, l_send, l_recv, l_local, s1, r1, s2, r2, s3, r3,
):
    nspace, ndiag, inner, local, slices, nvec, plane, factor = dims
    ndev = nspace * ndiag
    outer = nspace // inner
    space = lax.axis_index("space")
    core = lax.axis_index("diag")
    cfg = lax.axis_index("cfg")
    me = space * ndiag + core
    zpos = space // inner
    ypos = lax.rem(space, inner)

    def device(index):
        return (cfg, index // ndiag, lax.rem(index, ndiag))

    def e_copy(t):
        return pltpu.make_async_copy(eig_hbm.at[t], eig_ref.at[t], e_local.at[t])

    t_copy = pltpu.make_async_copy(tau_hbm, tau_ref, t_local)
    m_copy = pltpu.make_async_copy(mix_ref, mix_hbm, m_local)

    barrier = pltpu.get_barrier_semaphore()

    @pl.loop(1, ndev)
    def _(k):
        pl.semaphore_signal(
            barrier, inc=1, device_id=device(lax.rem(me + k, ndev)), device_id_type=MESH
        )

    for t in range(slices):
        e_copy(t).start()
    t_copy.start()

    column = lax.broadcasted_iota(jnp.int32, (1, 128), 1)
    packed = jnp.zeros((1, 128), jnp.int32)
    for i in range(local):
        packed = jnp.where(column == i, list_ref[i, 0], packed)
    lists[0] = packed

    pl.semaphore_wait(barrier, ndev - 1)

    def v_copy(t):
        return pltpu.make_async_remote_copy(
            src_ref=eig_hbm.at[t], dst_ref=above.at[t],
            send_sem=v_send.at[t], recv_sem=v_recv.at[t],
            device_id=device(lax.rem(me + ndev - 1, ndev)), device_id_type=MESH,
        )

    def l_copy(k):
        return pltpu.make_async_remote_copy(
            src_ref=lists.at[0], dst_ref=lists.at[k],
            send_sem=l_send.at[k], recv_sem=l_recv.at[k],
            device_id=device(lax.rem(me + k, ndev)), device_id_type=MESH,
        )

    for t in range(slices):
        v_copy(t).start()

    @pl.loop(1, ndev)
    def _(k):
        l_copy(k).start()

    nmom = mom_ref.shape[0]
    flat = lax.broadcasted_iota(jnp.int32, (1, plane), 1)
    xcoord = lax.rem(flat, LX).astype(f32)
    ycoord = lax.div(flat, LX).astype(f32)
    zcoord = lax.convert_element_type(me, f32)
    rows, hops = [], []
    for m in range(nmom):
        mom = [mom_ref[m, axis].astype(f32) for axis in range(3)]
        rows.append(
            2.0 * math.pi * (mom[0] * xcoord / LX + mom[1] * ycoord / LY + mom[2] * zcoord / ndev)
        )
        hops.append(jnp.full((1, nvec), math.pi, f32))
        for axis, size in enumerate((LX, LY, ndev)):
            hops.append(jnp.full((1, nvec), mom[axis] * (2.0 * math.pi / size), f32))
    angle = jnp.concatenate(rows, 0)
    cos_ref[...] = jnp.concatenate([jnp.cos(angle)] * 3, 1)
    sin_ref[...] = jnp.concatenate([jnp.sin(angle)] * 3, 1)
    hop = jnp.concatenate(hops, 0)
    plain = lax.rem(lax.broadcasted_iota(jnp.int32, hop.shape, 0), NDISP) == 0
    ar_ref[...] = jnp.where(plain, -1.0, jnp.cos(hop))
    ai_ref[...] = jnp.where(plain, 0.0, -jnp.sin(hop))

    lane = lax.broadcasted_iota(jnp.int32, (CHUNK, plane), 1)
    edge = lax.rem(lane, LX) == LX - 1

    def displace(t, direction, source):
        @pl.loop(0, nvec // CHUNK)
        def _(i):
            rows = pl.multiple_of(i * CHUNK, CHUNK)
            vec = []
            for p in range(2):
                line = []
                for c in range(3):
                    v = source[t, p, c, pl.ds(rows, CHUNK), :].astype(f32)
                    if direction == 0:
                        v = jnp.where(
                            edge, pltpu.roll(v, LX - 1, 1), pltpu.roll(v, plane - 1, 1)
                        )
                    elif direction == 1:
                        v = pltpu.roll(v, plane - LX, 1)
                    line.append(v)
                vec.append(line)
            for row in range(3):
                real = imag = None
                for col in range(3):
                    mr = link_ref[t, direction, 0, row, col]
                    mi = link_ref[t, direction, 1, row, col]
                    re = mr * vec[0][col] - mi * vec[1][col]
                    im = mr * vec[1][col] + mi * vec[0][col]
                    real = re if real is None else real + re
                    imag = im if imag is None else imag + im
                lanes = slice(row * plane, (row + 1) * plane)
                fields[t * NDISP + direction + 1, pl.ds(rows, CHUNK), lanes] = real.astype(bf16)
                fields[
                    t * NDISP + direction + 1, pl.ds(nvec + rows, CHUNK), lanes
                ] = imag.astype(bf16)

    def phases(t):
        @pl.loop(0, nvec // CHUNK)
        def _(i):
            rows = pl.multiple_of(i * CHUNK, CHUNK)
            for c in range(3):
                lanes = slice(c * plane, (c + 1) * plane)
                vr = eig_ref[t, 0, c, pl.ds(rows, CHUNK), :]
                vi = eig_ref[t, 1, c, pl.ds(rows, CHUNK), :]
                fields[t * NDISP, pl.ds(rows, CHUNK), lanes] = vr
                fields[t * NDISP, pl.ds(nvec + rows, CHUNK), lanes] = vi
                vr, vi = vr.astype(f32), vi.astype(f32)
                for m in range(nmom):
                    cosine = cos_ref[m:m + 1, lanes]
                    sine = sin_ref[m:m + 1, lanes]
                    a, b = cosine * vr, sine * vi
                    g, h = cosine * vi, sine * vr
                    plus[t * nmom + m, pl.ds(rows, CHUNK), lanes] = (a - b).astype(bf16)
                    plus[t * nmom + m, pl.ds(nvec + rows, CHUNK), lanes] = (g + h).astype(bf16)
                    minus[t * nmom + m, pl.ds(rows, CHUNK), lanes] = (a + b).astype(bf16)
                    minus[t * nmom + m, pl.ds(nvec + rows, CHUNK), lanes] = (g - h).astype(bf16)

    @pl.loop(0, slices)
    def _(t):
        e_copy(t).wait()
        displace(t, 0, eig_ref)
        displace(t, 1, eig_ref)
        phases(t)

    t_copy.wait()
    count, spins = tau_ref.shape[:2]
    for i in range(local):
        q = lax.rem(list_ref[i, 2], count)
        g = list_ref[i, 1]

        @pl.loop(0, 2 * nvec // CHUNK)
        def _(n):
            rows = pl.multiple_of(n * CHUNK, CHUNK)
            tau = [tau_ref[q, s, pl.ds(rows, CHUNK), :].astype(f32) for s in range(spins)]
            for r in range(spins):
                mixed = spin_ref[r, 0, g] * tau[0]
                for s in range(1, spins):
                    mixed = mixed + spin_ref[r, s, g] * tau[s]
                mix_ref[i, r, pl.ds(rows, CHUNK), :] = mixed.astype(bf16)

    m_copy.start()

    @pl.loop(1, ndev)
    def _(k):
        l_copy(k).wait()

    to_smem = pltpu.make_async_copy(lists, table, l_local)
    to_smem.start()
    to_smem.wait()

    @pl.loop(0, slices)
    def _(t):
        v_copy(t).wait()
        displace(t, 2, above)

    def item(dest, i):
        slot = lax.rem(me + ndev - dest, ndev)
        entry = table[slot, 0, i]
        time = lax.div(entry, nmom * NDISP)
        m = lax.rem(lax.div(entry, NDISP), nmom)
        d = lax.rem(entry, NDISP)
        ar = ar_ref[pl.ds(m * NDISP + d, 1), :]
        ai = ai_ref[pl.ds(m * NDISP + d, 1), :]
        x = fields[time * NDISP + d]
        first = lax.dot_general(plus[time * nmom + m], x, NT, preferred_element_type=f32)
        second = lax.dot_general(x, minus[time * nmom + m], NT, preferred_element_type=f32)
        g1r = first[:nvec, :nvec] + first[nvec:, nvec:]
        g1i = first[:nvec, nvec:] - first[nvec:, :nvec]
        g2r = second[:nvec, :nvec] + second[nvec:, nvec:]
        g2i = second[:nvec, nvec:] - second[nvec:, :nvec]
        return (
            (g1r - (ar * g2r - ai * g2i)) * factor,
            (g1i - (ar * g2i + ai * g2r)) * factor,
        )

    def copy1(n):
        return pltpu.make_async_remote_copy(
            src_ref=part1.at[n], dst_ref=recv1.at[n], send_sem=s1.at[n], recv_sem=r1.at[n],
            device_id=(cfg, space, 1 - core), device_id_type=MESH,
        )

    def copy2(j):
        return pltpu.make_async_remote_copy(
            src_ref=part2.at[j], dst_ref=recv2.at[j], send_sem=s2.at[j], recv_sem=r2.at[j],
            device_id=(cfg, zpos * inner + (1 - ypos), core), device_id_type=MESH,
        )

    low = zpos < outer // 2
    near = jnp.where(low, zpos, outer - 1 - zpos)
    side = jnp.where(low, 1, -1)
    excess = outer - 1 - 2 * near

    def order(j):
        r = j - excess
        ahead = zpos + side * (outer - 1 - near - j)
        turn = side * (2 * lax.rem(r + 2 * outer, 2) - 1)
        back = zpos + turn * (near - (r + 2 * outer) // 2 + outer)
        return jnp.where(r < 0, ahead, back)

    def copy3(j):
        d = order(j)
        up = d > zpos
        step = jnp.where(up, 1, -1)
        slot = jnp.where(jnp.logical_and(d < zpos, d == zpos - 1), outer, d)
        return pltpu.make_async_remote_copy(
            src_ref=part3.at[j], dst_ref=recv3.at[slot], send_sem=s3.at[j], recv_sem=r3.at[slot],
            device_id=(cfg, (zpos + step) * inner + ypos, core), device_id_type=MESH,
        )

    def arrival(slot):
        return pltpu.make_async_remote_copy(
            src_ref=part3.at[0], dst_ref=recv3.at[slot], send_sem=s3.at[0], recv_sem=r3.at[slot],
            device_id=(cfg, space, 1 - core), device_id_type=MESH,
        )

    @pl.loop(0, nspace)
    def _(n):
        last = n == nspace - 1
        across = jnp.logical_or(n == 0, jnp.logical_and(lax.rem(n, 2) == 1, n < nspace - 1))
        kept = jnp.logical_not(across)
        j = jnp.where(across, (n + 1) // 2, jnp.where(last, outer - 1, n // 2 - 1))
        d = order(j)
        chip = (d * inner + jnp.where(across, 1 - ypos, ypos)) * ndiag
        for i in range(local):
            real, imag = item(chip + (1 - core), i)
            part1[n, i, 0] = real.astype(bf16)
            part1[n, i, 1] = imag.astype(bf16)
        copy1(n).start()
        for i in range(local):
            real, imag = item(chip + core, i)
            own[i, 0] = real
            own[i, 1] = imag
        copy1(n).wait()

        @pl.when(across)
        def _():
            part2[j] = (own[...] + recv1[n].astype(f32)).astype(bf16)
            copy2(j).start()

        @pl.when(kept)
        def _():
            copy2(j).wait()
            own[...] = own[...] + recv1[n].astype(f32) + recv2[j].astype(f32)

            @pl.when(jnp.logical_or(
                jnp.logical_and(d >= zpos, zpos > 0),
                jnp.logical_and(d < zpos, zpos < outer - 1),
            ))
            def _():
                arrival(d).wait_recv()
                own[...] = own[...] + recv3[d].astype(f32)

        @pl.when(jnp.logical_and(kept, j < outer - 1))
        def _():
            part3[j] = own[...].astype(bf16)
            copy3(j).start()

    @pl.when(zpos < outer - 1)
    def _():
        arrival(outer).wait_recv()
        own[...] = own[...] + recv3[outer].astype(f32)

    out_ref[...] = own[...].astype(bf16)

    @pl.loop(0, outer - 1)
    def _(j):
        copy3(j).wait_send()

    m_copy.wait()


def diagram_kernel(elem_ref, mix_ref, out_ref):
    er, ei = elem_ref[0, 0], elem_ref[0, 1]
    square = jnp.concatenate(
        [jnp.concatenate([er, -ei], 1), jnp.concatenate([ei, er], 1)], 0
    )
    for r in range(mix_ref.shape[1]):
        out_ref[0, r] = jnp.dot(square, mix_ref[0, r], preferred_element_type=f32).astype(bf16)


def body(eigvecs, gauge_links, momenta, spin_mix, perambulators, contraction_list):
    slices, _, colors, nvec, depth, plane = eigvecs.shape
    assert depth == 1 and colors == 3
    nspace, ndiag = lax.axis_size("space"), lax.axis_size("diag")
    assert ndiag == 2 and nspace % 2 == 0
    inner = 2
    outer = nspace // inner
    ndev = nspace * ndiag
    scale = 1.0 / math.sqrt(3 * plane * ndev)
    nmom = momenta.shape[0]
    local = contraction_list.shape[0]
    count, spins = perambulators.shape[:2]
    width = perambulators.shape[4]
    vmem = pl.BlockSpec(memory_space=pltpu.VMEM)
    smem = pl.BlockSpec(memory_space=pltpu.SMEM)
    hbm = pl.BlockSpec(memory_space=pltpu.HBM)
    tile = (local, 2, nvec, nvec)
    field = (2 * nvec, 3 * plane)
    dma = pltpu.SemaphoreType.DMA
    elem, mixed = pl.pallas_call(
        functools.partial(
            elemental_kernel,
            (nspace, ndiag, inner, local, slices, nvec, plane, 0.5 * scale),
        ),
        out_shape=(
            jax.ShapeDtypeStruct(tile, bf16),
            jax.ShapeDtypeStruct((local, spins, 2 * nvec, width), bf16),
        ),
        in_specs=[smem, smem, smem, vmem, hbm, hbm],
        out_specs=(vmem, hbm),
        scratch_shapes=[
            pltpu.VMEM((slices, 2, 3, nvec, plane), bf16),
            pltpu.VMEM((nmom, 3 * plane), f32),
            pltpu.VMEM((nmom, 3 * plane), f32),
            pltpu.VMEM((nmom * NDISP, nvec), f32),
            pltpu.VMEM((nmom * NDISP, nvec), f32),
            pltpu.VMEM((slices, 2, 3, nvec, plane), bf16),
            pltpu.VMEM((slices * NDISP,) + field, bf16),
            pltpu.VMEM((slices * nmom,) + field, bf16),
            pltpu.VMEM((slices * nmom,) + field, bf16),
            pltpu.VMEM((count, spins, 2 * nvec, width), bf16),
            pltpu.VMEM((local, spins, 2 * nvec, width), bf16),
            pltpu.VMEM((ndev, 1, 128), jnp.int32),
            pltpu.SMEM((ndev, 1, 128), jnp.int32),
            pltpu.VMEM((nspace,) + tile, bf16),
            pltpu.VMEM((nspace,) + tile, bf16),
            pltpu.VMEM(tile, f32),
            pltpu.VMEM((outer,) + tile, bf16),
            pltpu.VMEM((outer,) + tile, bf16),
            pltpu.VMEM((outer - 1,) + tile, bf16),
            pltpu.VMEM((outer + 1,) + tile, bf16),
            dma((slices,)), dma, dma, dma((slices,)), dma((slices,)),
            dma((ndev,)), dma((ndev,)), dma,
            dma((nspace,)), dma((nspace,)),
            dma((outer,)), dma((outer,)),
            dma((outer - 1,)), dma((outer + 1,)),
        ],
        compiler_params=pltpu.CompilerParams(
            collective_id=0, has_side_effects=True, vmem_limit_bytes=63 * 1024 * 1024
        ),
    )(
        contraction_list, momenta, spin_mix.transpose(1, 2, 0), gauge_links,
        eigvecs.reshape(slices, 2, 3, nvec, plane),
        perambulators.reshape(count, spins, 2 * nvec, width),
    )
    group = 2 if spins % 2 == 0 else 1
    out = pl.pallas_call(
        diagram_kernel,
        grid=(local, spins // group),
        in_specs=[
            pl.BlockSpec((1, 2, nvec, nvec), lambda i, h: (i, 0, 0, 0)),
            pl.BlockSpec((1, group, 2 * nvec, width), lambda i, h: (i, h, 0, 0)),
        ],
        out_specs=pl.BlockSpec((1, group, 2 * nvec, width), lambda i, h: (i, h, 0, 0)),
        out_shape=jax.ShapeDtypeStruct((local, spins, 2 * nvec, width), bf16),
    )(elem, mixed)
    return out.reshape(local, spins, 2, nvec, width)


def solution(mesh):
    placed = (
        P("cfg", None, None, None, ("space", "diag"), None),
        P("cfg", None, None, None, None, ("space", "diag"), None),
        P(),
        P(),
        P(("cfg", "space", "diag"), None, None, None, None),
        P(("space", "diag"), None),
    )
    return jax.shard_map(
        body,
        mesh=mesh,
        in_specs=placed,
        out_specs=P(("cfg", "space", "diag"), None, None, None, None),
        check_vma=False,
    )
```

```python
import functools
import math

import jax
import jax.numpy as jnp
from jax import lax
from jax.experimental import pallas as pl
from jax.experimental.pallas import tpu as pltpu
from jax.sharding import PartitionSpec as P

LX = 16
LY = 16
NDISP = 4
CHUNK = 16
MESH = pl.DeviceIdType.MESH
NT = (((1,), (1,)), ((), ()))
f32 = jnp.float32
bf16 = jnp.bfloat16


def elemental_kernel(
    dims, list_ref, mom_ref, spin_ref, link_ref, eig_hbm, tau_hbm, out_ref, mix_hbm,
    eig_ref, cos_ref, sin_ref, ar_ref, ai_ref, above, fields, plus, minus, tau_ref, mix_ref, lists, table,
    part1, recv1, own, part2, recv2, part3, recv3,
    e_local, t_local, m_local, v_send, v_recv, l_send, l_recv, l_local, s1, r1, s2, r2, s3, r3,
):
    nspace, ndiag, inner, local, slices, nvec, plane, factor = dims
    ndev = nspace * ndiag
    outer = nspace // inner
    space = lax.axis_index("space")
    core = lax.axis_index("diag")
    cfg = lax.axis_index("cfg")
    me = space * ndiag + core
    zpos = space // inner
    ypos = lax.rem(space, inner)

    def device(index):
        return (cfg, index // ndiag, lax.rem(index, ndiag))

    def e_copy(t):
        return pltpu.make_async_copy(eig_hbm.at[t], eig_ref.at[t], e_local.at[t])

    t_copy = pltpu.make_async_copy(tau_hbm, tau_ref, t_local)
    m_copy = pltpu.make_async_copy(mix_ref, mix_hbm, m_local)

    barrier = pltpu.get_barrier_semaphore()

    @pl.loop(1, ndev)
    def _(k):
        pl.semaphore_signal(
            barrier, inc=1, device_id=device(lax.rem(me + k, ndev)), device_id_type=MESH
        )

    for t in range(slices):
        e_copy(t).start()
    t_copy.start()

    column = lax.broadcasted_iota(jnp.int32, (1, 128), 1)
    packed = jnp.zeros((1, 128), jnp.int32)
    for i in range(local):
        packed = jnp.where(column == i, list_ref[i, 0], packed)
    lists[0] = packed

    pl.semaphore_wait(barrier, ndev - 1)

    def v_copy(t):
        return pltpu.make_async_remote_copy(
            src_ref=eig_hbm.at[t], dst_ref=above.at[t],
            send_sem=v_send.at[t], recv_sem=v_recv.at[t],
            device_id=device(lax.rem(me + ndev - 1, ndev)), device_id_type=MESH,
        )

    def l_copy(k):
        return pltpu.make_async_remote_copy(
            src_ref=lists.at[0], dst_ref=lists.at[k],
            send_sem=l_send.at[k], recv_sem=l_recv.at[k],
            device_id=device(lax.rem(me + k, ndev)), device_id_type=MESH,
        )

    @pl.loop(1, ndev)
    def _(k):
        l_copy(k).start()

    for t in range(slices):
        v_copy(t).start()

    nmom = mom_ref.shape[0]
    flat = lax.broadcasted_iota(jnp.int32, (1, plane), 1)
    xcoord = lax.rem(flat, LX).astype(f32)
    ycoord = lax.div(flat, LX).astype(f32)
    zcoord = lax.convert_element_type(me, f32)
    rows, hops = [], []
    for m in range(nmom):
        mom = [mom_ref[m, axis].astype(f32) for axis in range(3)]
        rows.append(
            2.0 * math.pi * (mom[0] * xcoord / LX + mom[1] * ycoord / LY + mom[2] * zcoord / ndev)
        )
        hops.append(jnp.full((1, nvec), math.pi, f32))
        for axis, size in enumerate((LX, LY, ndev)):
            hops.append(jnp.full((1, nvec), mom[axis] * (2.0 * math.pi / size), f32))
    angle = jnp.concatenate(rows, 0)
    cos_ref[...] = jnp.concatenate([jnp.cos(angle)] * 3, 1)
    sin_ref[...] = jnp.concatenate([jnp.sin(angle)] * 3, 1)
    hop = jnp.concatenate(hops, 0)
    plain = lax.rem(lax.broadcasted_iota(jnp.int32, hop.shape, 0), NDISP) == 0
    ar_ref[...] = jnp.where(plain, -1.0, jnp.cos(hop))
    ai_ref[...] = jnp.where(plain, 0.0, -jnp.sin(hop))

    lane = lax.broadcasted_iota(jnp.int32, (CHUNK, plane), 1)
    edge = lax.rem(lane, LX) == LX - 1

    def displace(t, direction, source):
        @pl.loop(0, nvec // CHUNK)
        def _(i):
            rows = pl.multiple_of(i * CHUNK, CHUNK)
            vec = []
            for p in range(2):
                line = []
                for c in range(3):
                    v = source[t, p, c, pl.ds(rows, CHUNK), :].astype(f32)
                    if direction == 0:
                        v = jnp.where(
                            edge, pltpu.roll(v, LX - 1, 1), pltpu.roll(v, plane - 1, 1)
                        )
                    elif direction == 1:
                        v = pltpu.roll(v, plane - LX, 1)
                    line.append(v)
                vec.append(line)
            for row in range(3):
                real = imag = None
                for col in range(3):
                    mr = link_ref[t, direction, 0, row, col]
                    mi = link_ref[t, direction, 1, row, col]
                    re = mr * vec[0][col] - mi * vec[1][col]
                    im = mr * vec[1][col] + mi * vec[0][col]
                    real = re if real is None else real + re
                    imag = im if imag is None else imag + im
                lanes = slice(row * plane, (row + 1) * plane)
                fields[t * NDISP + direction + 1, pl.ds(rows, CHUNK), lanes] = real.astype(bf16)
                fields[
                    t * NDISP + direction + 1, pl.ds(nvec + rows, CHUNK), lanes
                ] = imag.astype(bf16)

    def phases(t):
        @pl.loop(0, nvec // CHUNK)
        def _(i):
            rows = pl.multiple_of(i * CHUNK, CHUNK)
            for c in range(3):
                lanes = slice(c * plane, (c + 1) * plane)
                vr = eig_ref[t, 0, c, pl.ds(rows, CHUNK), :]
                vi = eig_ref[t, 1, c, pl.ds(rows, CHUNK), :]
                fields[t * NDISP, pl.ds(rows, CHUNK), lanes] = vr
                fields[t * NDISP, pl.ds(nvec + rows, CHUNK), lanes] = vi
                vr, vi = vr.astype(f32), vi.astype(f32)
                for m in range(nmom):
                    cosine = cos_ref[m:m + 1, lanes]
                    sine = sin_ref[m:m + 1, lanes]
                    a, b = cosine * vr, sine * vi
                    g, h = cosine * vi, sine * vr
                    plus[t * nmom + m, pl.ds(rows, CHUNK), lanes] = (a - b).astype(bf16)
                    plus[t * nmom + m, pl.ds(nvec + rows, CHUNK), lanes] = (g + h).astype(bf16)
                    minus[t * nmom + m, pl.ds(rows, CHUNK), lanes] = (a + b).astype(bf16)
                    minus[t * nmom + m, pl.ds(nvec + rows, CHUNK), lanes] = (g - h).astype(bf16)

    @pl.loop(0, slices)
    def _(t):
        e_copy(t).wait()
        displace(t, 0, eig_ref)
        displace(t, 1, eig_ref)
        phases(t)

    t_copy.wait()
    count, spins = tau_ref.shape[:2]
    for i in range(local):
        q = lax.rem(list_ref[i, 2], count)
        g = list_ref[i, 1]

        @pl.loop(0, 2 * nvec // CHUNK)
        def _(n):
            rows = pl.multiple_of(n * CHUNK, CHUNK)
            tau = [tau_ref[q, s, pl.ds(rows, CHUNK), :].astype(f32) for s in range(spins)]
            for r in range(spins):
                mixed = spin_ref[r, 0, g] * tau[0]
                for s in range(1, spins):
                    mixed = mixed + spin_ref[r, s, g] * tau[s]
                mix_ref[i, r, pl.ds(rows, CHUNK), :] = mixed.astype(bf16)

    m_copy.start()

    @pl.loop(1, ndev)
    def _(k):
        l_copy(k).wait()

    to_smem = pltpu.make_async_copy(lists, table, l_local)
    to_smem.start()
    to_smem.wait()

    @pl.loop(0, slices)
    def _(t):
        v_copy(t).wait()
        displace(t, 2, above)

    def item(dest, i):
        slot = lax.rem(me + ndev - dest, ndev)
        entry = table[slot, 0, i]
        time = lax.div(entry, nmom * NDISP)
        m = lax.rem(lax.div(entry, NDISP), nmom)
        d = lax.rem(entry, NDISP)
        ar = ar_ref[pl.ds(m * NDISP + d, 1), :]
        ai = ai_ref[pl.ds(m * NDISP + d, 1), :]
        x = fields[time * NDISP + d]
        first = lax.dot_general(plus[time * nmom + m], x, NT, preferred_element_type=f32)
        second = lax.dot_general(x, minus[time * nmom + m], NT, preferred_element_type=f32)
        g1r = first[:nvec, :nvec] + first[nvec:, nvec:]
        g1i = first[:nvec, nvec:] - first[nvec:, :nvec]
        g2r = second[:nvec, :nvec] + second[nvec:, nvec:]
        g2i = second[:nvec, nvec:] - second[nvec:, :nvec]
        return (
            (g1r - (ar * g2r - ai * g2i)) * factor,
            (g1i - (ar * g2i + ai * g2r)) * factor,
        )

    levels = outer.bit_length() - 1

    def flip(l):
        size = 1 << l
        return zpos + size * (1 - 2 * lax.rem(zpos // size, 2))

    def away(r):
        row = zpos
        for l in range(levels):
            row = row + lax.rem(r // (1 << l), 2) * (flip(l) - zpos)
        return row

    def copy1(n, i):
        return pltpu.make_async_remote_copy(
            src_ref=part1.at[n, i], dst_ref=recv1.at[n, i], send_sem=s1.at[n, i], recv_sem=r1.at[n, i],
            device_id=(cfg, space, 1 - core), device_id_type=MESH,
        )

    def copy2(n, j, i):
        return pltpu.make_async_remote_copy(
            src_ref=part2.at[n, i], dst_ref=recv2.at[j, i], send_sem=s2.at[j, i], recv_sem=r2.at[j, i],
            device_id=(cfg, zpos * inner + (1 - ypos), core), device_id_type=MESH,
        )

    def copy3(r, i):
        row = flip(levels - 1)
        for l in range(levels - 2, -1, -1):
            row = jnp.where(lax.rem(r, 2 << l) == 1 << l, flip(l), row)
        return pltpu.make_async_remote_copy(
            src_ref=part3.at[r, i], dst_ref=recv3.at[r, i], send_sem=s3.at[r, i], recv_sem=r3.at[r, i],
            device_id=(cfg, row * inner + ypos, core), device_id_type=MESH,
        )

    def unit(n):
        last = n == nspace - 1
        across = jnp.logical_or(n == 0, jnp.logical_and(lax.rem(n, 2) == 1, n < nspace - 1))
        j = jnp.where(across, (n + 1) // 2, jnp.where(last, outer - 1, n // 2 - 1))
        row = away(outer - 1 - j)
        return across, j, (row * inner + jnp.where(across, 1 - ypos, ypos)) * ndiag

    def give(n):
        _, _, chip = unit(n)
        for i in range(local):
            real, imag = item(chip + (1 - core), i)
            part1[n, i, 0] = real.astype(bf16)
            part1[n, i, 1] = imag.astype(bf16)
            copy1(n, i).start()

    def keep(n):
        across, j, chip = unit(n)
        for i in range(local):
            copy1(n, i).wait()
            real, imag = item(chip + core, i)
            real = real + recv1[n, i, 0].astype(f32)
            imag = imag + recv1[n, i, 1].astype(f32)
            own[n, i, 0] = real
            own[n, i, 1] = imag
            part2[n, i, 0] = real.astype(bf16)
            part2[n, i, 1] = imag.astype(bf16)

            @pl.when(across)
            def _():
                copy2(n, j, i).start()

    def collect(q):
        j = q // local
        i = lax.rem(q, local)
        r = outer - 1 - j
        n = jnp.where(j == outer - 1, nspace - 1, 2 * j + 2)
        copy2(0, j, i).wait()
        own[n, i] = own[n, i] + recv2[j, i].astype(f32)
        for l in range(levels):
            @pl.when(lax.rem(r, 2 << l) == 0)
            def _():
                copy3(r + (1 << l), i).wait()
                own[n, i] = own[n, i] + recv3[r + (1 << l), i].astype(f32)

        @pl.when(r > 0)
        def _():
            part3[r, i] = own[n, i].astype(bf16)
            copy3(r, i).start()

    @pl.loop(0, 2 * nspace)
    def _(k):
        gives = jnp.where(core == 0, k < nspace, lax.rem(k, 2) == 0)
        n = jnp.where(core == 0, lax.rem(k, nspace), k // 2)

        @pl.when(gives)
        def _():
            give(n)

        @pl.when(jnp.logical_not(gives))
        def _():
            keep(n)

            @pl.when(n >= 2)
            def _():
                collect(n - 2)

    @pl.loop(nspace - 2, outer * local)
    def _(q):
        collect(q)

    out_ref[...] = own[nspace - 1].astype(bf16)
    m_copy.wait()


def diagram_kernel(elem_ref, mix_hbm, out_hbm, mix_ref, out_ref, load_sem, store_sem):
    local, spins = mix_ref.shape[:2]

    def load(i, r):
        return pltpu.make_async_copy(mix_hbm.at[i, r], mix_ref.at[i, r], load_sem.at[i, r])

    def store(i, r):
        return pltpu.make_async_copy(out_ref.at[i, r], out_hbm.at[i, r], store_sem.at[i, r])

    pairs = [(i, r) for i in range(local) for r in range(spins)]
    for i, r in pairs:
        load(i, r).start()
    for i in range(local):
        er, ei = elem_ref[i, 0], elem_ref[i, 1]
        square = jnp.concatenate(
            [jnp.concatenate([er, -ei], 1), jnp.concatenate([ei, er], 1)], 0
        )
        for r in range(spins):
            load(i, r).wait()
            out_ref[i, r] = jnp.dot(
                square, mix_ref[i, r], preferred_element_type=f32
            ).astype(bf16)
            store(i, r).start()
    for i, r in pairs:
        store(i, r).wait()


def body(eigvecs, gauge_links, momenta, spin_mix, perambulators, contraction_list):
    slices, _, colors, nvec, depth, plane = eigvecs.shape
    assert depth == 1 and colors == 3
    nspace, ndiag = lax.axis_size("space"), lax.axis_size("diag")
    inner = 2
    outer = nspace // inner
    assert ndiag == 2 and inner * outer == nspace
    assert outer & (outer - 1) == 0 and contraction_list.shape[0] >= 2
    ndev = nspace * ndiag
    scale = 1.0 / math.sqrt(3 * plane * ndev)
    nmom = momenta.shape[0]
    local = contraction_list.shape[0]
    count, spins = perambulators.shape[:2]
    width = perambulators.shape[4]
    vmem = pl.BlockSpec(memory_space=pltpu.VMEM)
    smem = pl.BlockSpec(memory_space=pltpu.SMEM)
    hbm = pl.BlockSpec(memory_space=pltpu.HBM)
    tile = (local, 2, nvec, nvec)
    field = (2 * nvec, 3 * plane)
    dma = pltpu.SemaphoreType.DMA
    elem, mixed = pl.pallas_call(
        functools.partial(
            elemental_kernel,
            (nspace, ndiag, inner, local, slices, nvec, plane, 0.5 * scale),
        ),
        out_shape=(
            jax.ShapeDtypeStruct(tile, bf16),
            jax.ShapeDtypeStruct((local, spins, 2 * nvec, width), bf16),
        ),
        in_specs=[smem, smem, smem, vmem, hbm, hbm],
        out_specs=(vmem, hbm),
        scratch_shapes=[
            pltpu.VMEM((slices, 2, 3, nvec, plane), bf16),
            pltpu.VMEM((nmom, 3 * plane), f32),
            pltpu.VMEM((nmom, 3 * plane), f32),
            pltpu.VMEM((nmom * NDISP, nvec), f32),
            pltpu.VMEM((nmom * NDISP, nvec), f32),
            pltpu.VMEM((slices, 2, 3, nvec, plane), bf16),
            pltpu.VMEM((slices * NDISP,) + field, bf16),
            pltpu.VMEM((slices * nmom,) + field, bf16),
            pltpu.VMEM((slices * nmom,) + field, bf16),
            pltpu.VMEM((count, spins, 2 * nvec, width), bf16),
            pltpu.VMEM((local, spins, 2 * nvec, width), bf16),
            pltpu.VMEM((ndev, 1, 128), jnp.int32),
            pltpu.SMEM((ndev, 1, 128), jnp.int32),
            pltpu.VMEM((nspace,) + tile, bf16),
            pltpu.VMEM((nspace,) + tile, bf16),
            pltpu.VMEM((nspace,) + tile, f32),
            pltpu.VMEM((nspace,) + tile, bf16),
            pltpu.VMEM((outer,) + tile, bf16),
            pltpu.VMEM((outer,) + tile, bf16),
            pltpu.VMEM((outer,) + tile, bf16),
            dma((slices,)), dma, dma, dma((slices,)), dma((slices,)),
            dma((ndev,)), dma((ndev,)), dma,
            dma((nspace, local)), dma((nspace, local)),
            dma((outer, local)), dma((outer, local)),
            dma((outer, local)), dma((outer, local)),
        ],
        compiler_params=pltpu.CompilerParams(
            collective_id=0, has_side_effects=True, vmem_limit_bytes=63 * 1024 * 1024
        ),
    )(
        contraction_list, momenta, spin_mix.transpose(1, 2, 0), gauge_links,
        eigvecs.reshape(slices, 2, 3, nvec, plane),
        perambulators.reshape(count, spins, 2 * nvec, width),
    )
    out = pl.pallas_call(
        diagram_kernel,
        in_specs=[vmem, hbm],
        out_specs=hbm,
        out_shape=jax.ShapeDtypeStruct((local, spins, 2 * nvec, width), bf16),
        scratch_shapes=[
            pltpu.VMEM((local, spins, 2 * nvec, width), bf16),
            pltpu.VMEM((local, spins, 2 * nvec, width), bf16),
            dma((local, spins)), dma((local, spins)),
        ],
        compiler_params=pltpu.CompilerParams(vmem_limit_bytes=16 * 1024 * 1024),
    )(elem, mixed)
    return out.reshape(local, spins, 2, nvec, width)


def solution(mesh):
    placed = (
        P("cfg", None, None, None, ("space", "diag"), None),
        P("cfg", None, None, None, None, ("space", "diag"), None),
        P(),
        P(),
        P(("cfg", "space", "diag"), None, None, None, None),
        P(("space", "diag"), None),
    )
    return jax.shard_map(
        body,
        mesh=mesh,
        in_specs=placed,
        out_specs=P(("cfg", "space", "diag"), None, None, None, None),
        check_vma=False,
    )
```

```python
import functools
import math

import jax
import jax.numpy as jnp
from jax import lax
from jax.experimental import pallas as pl
from jax.experimental.pallas import tpu as pltpu
from jax.sharding import PartitionSpec as P

LX = 16
LY = 16
NDISP = 4
CHUNK = 16
MESH = pl.DeviceIdType.MESH
NT = (((1,), (1,)), ((), ()))
f32 = jnp.float32
bf16 = jnp.bfloat16


def elemental_kernel(
    dims, list_ref, mom_ref, spin_ref, link_ref, eig_hbm, tau_hbm, out_ref, mix_hbm,
    eig_ref, cos_ref, sin_ref, ar_ref, ai_ref, above, fields, plus, minus, tau_ref, mix_ref, lists, table,
    part1, recv1, own, part2, recv2, part3, recv3,
    e_local, t_local, m_local, v_send, v_recv, l_send, l_recv, l_local, s1, r1, s2, r2, s3, r3,
):
    nspace, ndiag, inner, local, slices, nvec, plane, factor = dims
    ndev = nspace * ndiag
    outer = nspace // inner
    space = lax.axis_index("space")
    core = lax.axis_index("diag")
    cfg = lax.axis_index("cfg")
    me = space * ndiag + core
    zpos = space // inner
    ypos = lax.rem(space, inner)

    def device(index):
        return (cfg, index // ndiag, lax.rem(index, ndiag))

    def e_copy(t):
        return pltpu.make_async_copy(eig_hbm.at[t], eig_ref.at[t], e_local.at[t])

    t_copy = pltpu.make_async_copy(tau_hbm, tau_ref, t_local)
    m_copy = pltpu.make_async_copy(mix_ref, mix_hbm, m_local)

    barrier = pltpu.get_barrier_semaphore()

    @pl.loop(1, ndev)
    def _(k):
        pl.semaphore_signal(
            barrier, inc=1, device_id=device(lax.rem(me + k, ndev)), device_id_type=MESH
        )

    for t in range(slices):
        e_copy(t).start()
    t_copy.start()

    column = lax.broadcasted_iota(jnp.int32, (1, 128), 1)
    packed = jnp.zeros((1, 128), jnp.int32)
    for i in range(local):
        packed = jnp.where(column == i, list_ref[i, 0], packed)
    lists[0] = packed

    pl.semaphore_wait(barrier, ndev - 1)

    def v_copy(t):
        return pltpu.make_async_remote_copy(
            src_ref=eig_hbm.at[t], dst_ref=above.at[t],
            send_sem=v_send.at[t], recv_sem=v_recv.at[t],
            device_id=device(lax.rem(me + ndev - 1, ndev)), device_id_type=MESH,
        )

    def l_copy(k):
        return pltpu.make_async_remote_copy(
            src_ref=lists.at[0], dst_ref=lists.at[k],
            send_sem=l_send.at[k], recv_sem=l_recv.at[k],
            device_id=device(lax.rem(me + k, ndev)), device_id_type=MESH,
        )

    @pl.loop(1, ndev)
    def _(k):
        l_copy(k).start()

    for t in range(slices):
        v_copy(t).start()

    nmom = mom_ref.shape[0]
    flat = lax.broadcasted_iota(jnp.int32, (1, plane), 1)
    xcoord = lax.rem(flat, LX).astype(f32)
    ycoord = lax.div(flat, LX).astype(f32)
    zcoord = lax.convert_element_type(me, f32)
    rows, hops = [], []
    for m in range(nmom):
        mom = [mom_ref[m, axis].astype(f32) for axis in range(3)]
        rows.append(
            2.0 * math.pi * (mom[0] * xcoord / LX + mom[1] * ycoord / LY + mom[2] * zcoord / ndev)
        )
        hops.append(jnp.full((1, nvec), math.pi, f32))
        for axis, size in enumerate((LX, LY, ndev)):
            hops.append(jnp.full((1, nvec), mom[axis] * (2.0 * math.pi / size), f32))
    angle = jnp.concatenate(rows, 0)
    cos_ref[...] = jnp.concatenate([jnp.cos(angle)] * 3, 1)
    sin_ref[...] = jnp.concatenate([jnp.sin(angle)] * 3, 1)
    hop = jnp.concatenate(hops, 0)
    plain = lax.rem(lax.broadcasted_iota(jnp.int32, hop.shape, 0), NDISP) == 0
    ar_ref[...] = jnp.where(plain, -1.0, jnp.cos(hop))
    ai_ref[...] = jnp.where(plain, 0.0, -jnp.sin(hop))

    lane = lax.broadcasted_iota(jnp.int32, (CHUNK, plane), 1)
    edge = lax.rem(lane, LX) == LX - 1

    def displace(t, direction, source):
        @pl.loop(0, nvec // CHUNK)
        def _(i):
            rows = pl.multiple_of(i * CHUNK, CHUNK)
            vec = []
            for p in range(2):
                line = []
                for c in range(3):
                    v = source[t, p, c, pl.ds(rows, CHUNK), :].astype(f32)
                    if direction == 0:
                        v = jnp.where(
                            edge, pltpu.roll(v, LX - 1, 1), pltpu.roll(v, plane - 1, 1)
                        )
                    elif direction == 1:
                        v = pltpu.roll(v, plane - LX, 1)
                    line.append(v)
                vec.append(line)
            for row in range(3):
                real = imag = None
                for col in range(3):
                    mr = link_ref[t, direction, 0, row, col]
                    mi = link_ref[t, direction, 1, row, col]
                    re = mr * vec[0][col] - mi * vec[1][col]
                    im = mr * vec[1][col] + mi * vec[0][col]
                    real = re if real is None else real + re
                    imag = im if imag is None else imag + im
                lanes = slice(row * plane, (row + 1) * plane)
                fields[t * NDISP + direction + 1, pl.ds(rows, CHUNK), lanes] = real.astype(bf16)
                fields[
                    t * NDISP + direction + 1, pl.ds(nvec + rows, CHUNK), lanes
                ] = imag.astype(bf16)

    def phases(t):
        @pl.loop(0, nvec // CHUNK)
        def _(i):
            rows = pl.multiple_of(i * CHUNK, CHUNK)
            for c in range(3):
                lanes = slice(c * plane, (c + 1) * plane)
                vr = eig_ref[t, 0, c, pl.ds(rows, CHUNK), :]
                vi = eig_ref[t, 1, c, pl.ds(rows, CHUNK), :]
                fields[t * NDISP, pl.ds(rows, CHUNK), lanes] = vr
                fields[t * NDISP, pl.ds(nvec + rows, CHUNK), lanes] = vi
                vr, vi = vr.astype(f32), vi.astype(f32)
                for m in range(nmom):
                    cosine = cos_ref[m:m + 1, lanes]
                    sine = sin_ref[m:m + 1, lanes]
                    a, b = cosine * vr, sine * vi
                    g, h = cosine * vi, sine * vr
                    plus[t * nmom + m, pl.ds(rows, CHUNK), lanes] = (a - b).astype(bf16)
                    plus[t * nmom + m, pl.ds(nvec + rows, CHUNK), lanes] = (g + h).astype(bf16)
                    minus[t * nmom + m, pl.ds(rows, CHUNK), lanes] = (a + b).astype(bf16)
                    minus[t * nmom + m, pl.ds(nvec + rows, CHUNK), lanes] = (g - h).astype(bf16)

    @pl.loop(0, slices)
    def _(t):
        e_copy(t).wait()
        displace(t, 0, eig_ref)
        displace(t, 1, eig_ref)
        phases(t)

    t_copy.wait()
    count, spins = tau_ref.shape[:2]
    for i in range(local):
        q = lax.rem(list_ref[i, 2], count)
        g = list_ref[i, 1]

        @pl.loop(0, 2 * nvec // CHUNK)
        def _(n):
            rows = pl.multiple_of(n * CHUNK, CHUNK)
            tau = [tau_ref[q, s, pl.ds(rows, CHUNK), :].astype(f32) for s in range(spins)]
            for r in range(spins):
                mixed = spin_ref[r, 0, g] * tau[0]
                for s in range(1, spins):
                    mixed = mixed + spin_ref[r, s, g] * tau[s]
                mix_ref[i, r, pl.ds(rows, CHUNK), :] = mixed.astype(bf16)

    m_copy.start()

    @pl.loop(1, ndev)
    def _(k):
        l_copy(k).wait()

    to_smem = pltpu.make_async_copy(lists, table, l_local)
    to_smem.start()
    to_smem.wait()

    @pl.loop(0, slices)
    def _(t):
        v_copy(t).wait()
        displace(t, 2, above)

    def item(dest, i):
        slot = lax.rem(me + ndev - dest, ndev)
        entry = table[slot, 0, i]
        time = lax.div(entry, nmom * NDISP)
        m = lax.rem(lax.div(entry, NDISP), nmom)
        d = lax.rem(entry, NDISP)
        ar = ar_ref[pl.ds(m * NDISP + d, 1), :]
        ai = ai_ref[pl.ds(m * NDISP + d, 1), :]
        x = fields[time * NDISP + d]
        first = lax.dot_general(plus[time * nmom + m], x, NT, preferred_element_type=f32)
        second = lax.dot_general(x, minus[time * nmom + m], NT, preferred_element_type=f32)
        g1r = first[:nvec, :nvec] + first[nvec:, nvec:]
        g1i = first[:nvec, nvec:] - first[nvec:, :nvec]
        g2r = second[:nvec, :nvec] + second[nvec:, nvec:]
        g2i = second[:nvec, nvec:] - second[nvec:, :nvec]
        return (
            (g1r - (ar * g2r - ai * g2i)) * factor,
            (g1i - (ar * g2i + ai * g2r)) * factor,
        )

    levels = outer.bit_length() - 1

    def flip(l):
        size = 1 << l
        return zpos + size * (1 - 2 * lax.rem(zpos // size, 2))

    def away(r):
        row = zpos
        for l in range(levels):
            row = row + lax.rem(r // (1 << l), 2) * (flip(l) - zpos)
        return row

    def copy1(n, i):
        return pltpu.make_async_remote_copy(
            src_ref=part1.at[n, i], dst_ref=recv1.at[n, i], send_sem=s1.at[n, i], recv_sem=r1.at[n, i],
            device_id=(cfg, space, 1 - core), device_id_type=MESH,
        )

    def copy2(n, j, i):
        return pltpu.make_async_remote_copy(
            src_ref=part2.at[n, i], dst_ref=recv2.at[j, i], send_sem=s2.at[j, i], recv_sem=r2.at[j, i],
            device_id=(cfg, zpos * inner + (1 - ypos), core), device_id_type=MESH,
        )

    def copy3(r, i):
        row = flip(levels - 1)
        for l in range(levels - 2, -1, -1):
            row = jnp.where(lax.rem(r, 2 << l) == 1 << l, flip(l), row)
        return pltpu.make_async_remote_copy(
            src_ref=part3.at[r, i], dst_ref=recv3.at[r, i], send_sem=s3.at[r, i], recv_sem=r3.at[r, i],
            device_id=(cfg, row * inner + ypos, core), device_id_type=MESH,
        )

    def unit(n):
        across = jnp.logical_or(n < 3, jnp.logical_and(lax.rem(n, 2) == 0, n < nspace - 2))
        late = jnp.where(n < nspace - 2, (n - 3) // 2, n - outer)
        j = jnp.where(across, jnp.where(n < 3, n, n // 2 + 1), late)
        row = away(outer - 1 - j)
        return across, j, (row * inner + jnp.where(across, 1 - ypos, ypos)) * ndiag

    def give(n):
        _, _, chip = unit(n)
        for i in range(local):
            real, imag = item(chip + (1 - core), i)
            part1[n, i, 0] = real.astype(bf16)
            part1[n, i, 1] = imag.astype(bf16)
            copy1(n, i).start()

    def keep(n):
        _, _, chip = unit(n)
        for i in range(local):
            own[n, i, 0], own[n, i, 1] = item(chip + core, i)

    def join(n):
        across, j, _ = unit(n)
        for i in range(local):
            copy1(n, i).wait_recv()
            total = own[n, i] + recv1[n, i].astype(f32)
            own[n, i] = total
            part2[n, i] = total.astype(bf16)

            @pl.when(across)
            def _():
                copy2(n, j, i).start()

    def collect(q):
        j = q // local
        i = lax.rem(q, local)
        r = outer - 1 - j
        n = jnp.where(j < outer - 2, 2 * j + 3, j + outer)
        copy2(0, j, i).wait()
        own[n, i] = own[n, i] + recv2[j, i].astype(f32)
        for l in range(levels):
            @pl.when(lax.rem(r, 2 << l) == 0)
            def _():
                copy3(r + (1 << l), i).wait()
                own[n, i] = own[n, i] + recv3[r + (1 << l), i].astype(f32)

        @pl.when(r > 0)
        def _():
            part3[r, i] = own[n, i].astype(bf16)
            copy3(r, i).start()

    @pl.loop(0, 3 * nspace)
    def _(k):
        early = core == 0
        kind = jnp.where(early, k // nspace, lax.rem(k + 1, 3))
        n = jnp.where(early, lax.rem(k, nspace), k // 3)

        @pl.when(kind == 0)
        def _():
            give(n)

        @pl.when(kind == 1)
        def _():
            keep(n)

        @pl.when(kind == 2)
        def _():
            join(n)
            first = jnp.where(n == 3, 0, n - 3)
            stop = jnp.where(n == 3, 2, jnp.where(n > 4, n - 2, first))

            @pl.loop(first, stop)
            def _(q):
                collect(q)

    @pl.loop(nspace - 3, outer * local)
    def _(q):
        collect(q)

    out_ref[...] = own[nspace - 1].astype(bf16)

    @pl.loop(0, nspace)
    def _(n):
        for i in range(local):
            copy1(n, i).wait_send()

    m_copy.wait()


def diagram_kernel(elem_ref, mix_hbm, out_hbm, mix_ref, out_ref, load_sem, store_sem):
    local, spins = mix_ref.shape[:2]

    def load(i, r):
        return pltpu.make_async_copy(mix_hbm.at[i, r], mix_ref.at[i, r], load_sem.at[i, r])

    def store(i, r):
        return pltpu.make_async_copy(out_ref.at[i, r], out_hbm.at[i, r], store_sem.at[i, r])

    pairs = [(i, r) for i in range(local) for r in range(spins)]
    for i, r in pairs:
        load(i, r).start()
    for i in range(local):
        er, ei = elem_ref[i, 0], elem_ref[i, 1]
        square = jnp.concatenate(
            [jnp.concatenate([er, -ei], 1), jnp.concatenate([ei, er], 1)], 0
        )
        for r in range(spins):
            load(i, r).wait()
            out_ref[i, r] = jnp.dot(
                square, mix_ref[i, r], preferred_element_type=f32
            ).astype(bf16)
            store(i, r).start()
    for i, r in pairs:
        store(i, r).wait()


def body(eigvecs, gauge_links, momenta, spin_mix, perambulators, contraction_list):
    slices, _, colors, nvec, depth, plane = eigvecs.shape
    assert depth == 1 and colors == 3
    nspace, ndiag = lax.axis_size("space"), lax.axis_size("diag")
    inner = 2
    outer = nspace // inner
    assert ndiag == 2 and inner * outer == nspace
    assert outer >= 4 and outer & (outer - 1) == 0 and contraction_list.shape[0] >= 2
    ndev = nspace * ndiag
    scale = 1.0 / math.sqrt(3 * plane * ndev)
    nmom = momenta.shape[0]
    local = contraction_list.shape[0]
    count, spins = perambulators.shape[:2]
    width = perambulators.shape[4]
    vmem = pl.BlockSpec(memory_space=pltpu.VMEM)
    smem = pl.BlockSpec(memory_space=pltpu.SMEM)
    hbm = pl.BlockSpec(memory_space=pltpu.HBM)
    tile = (local, 2, nvec, nvec)
    field = (2 * nvec, 3 * plane)
    dma = pltpu.SemaphoreType.DMA
    elem, mixed = pl.pallas_call(
        functools.partial(
            elemental_kernel,
            (nspace, ndiag, inner, local, slices, nvec, plane, 0.5 * scale),
        ),
        out_shape=(
            jax.ShapeDtypeStruct(tile, bf16),
            jax.ShapeDtypeStruct((local, spins, 2 * nvec, width), bf16),
        ),
        in_specs=[smem, smem, smem, vmem, hbm, hbm],
        out_specs=(vmem, hbm),
        scratch_shapes=[
            pltpu.VMEM((slices, 2, 3, nvec, plane), bf16),
            pltpu.VMEM((nmom, 3 * plane), f32),
            pltpu.VMEM((nmom, 3 * plane), f32),
            pltpu.VMEM((nmom * NDISP, nvec), f32),
            pltpu.VMEM((nmom * NDISP, nvec), f32),
            pltpu.VMEM((slices, 2, 3, nvec, plane), bf16),
            pltpu.VMEM((slices * NDISP,) + field, bf16),
            pltpu.VMEM((slices * nmom,) + field, bf16),
            pltpu.VMEM((slices * nmom,) + field, bf16),
            pltpu.VMEM((count, spins, 2 * nvec, width), bf16),
            pltpu.VMEM((local, spins, 2 * nvec, width), bf16),
            pltpu.VMEM((ndev, 1, 128), jnp.int32),
            pltpu.SMEM((ndev, 1, 128), jnp.int32),
            pltpu.VMEM((nspace,) + tile, bf16),
            pltpu.VMEM((nspace,) + tile, bf16),
            pltpu.VMEM((nspace,) + tile, f32),
            pltpu.VMEM((nspace,) + tile, bf16),
            pltpu.VMEM((outer,) + tile, bf16),
            pltpu.VMEM((outer,) + tile, bf16),
            pltpu.VMEM((outer,) + tile, bf16),
            dma((slices,)), dma, dma, dma((slices,)), dma((slices,)),
            dma((ndev,)), dma((ndev,)), dma,
            dma((nspace, local)), dma((nspace, local)),
            dma((outer, local)), dma((outer, local)),
            dma((outer, local)), dma((outer, local)),
        ],
        compiler_params=pltpu.CompilerParams(
            collective_id=0, has_side_effects=True, vmem_limit_bytes=63 * 1024 * 1024
        ),
    )(
        contraction_list, momenta, spin_mix.transpose(1, 2, 0), gauge_links,
        eigvecs.reshape(slices, 2, 3, nvec, plane),
        perambulators.reshape(count, spins, 2 * nvec, width),
    )
    out = pl.pallas_call(
        diagram_kernel,
        in_specs=[vmem, hbm],
        out_specs=hbm,
        out_shape=jax.ShapeDtypeStruct((local, spins, 2 * nvec, width), bf16),
        scratch_shapes=[
            pltpu.VMEM((local, spins, 2 * nvec, width), bf16),
            pltpu.VMEM((local, spins, 2 * nvec, width), bf16),
            dma((local, spins)), dma((local, spins)),
        ],
        compiler_params=pltpu.CompilerParams(vmem_limit_bytes=63 * 1024 * 1024),
    )(elem, mixed)
    return out.reshape(local, spins, 2, nvec, width)


def solution(mesh):
    placed = (
        P("cfg", None, None, None, ("space", "diag"), None),
        P("cfg", None, None, None, None, ("space", "diag"), None),
        P(),
        P(),
        P(("cfg", "space", "diag"), None, None, None, None),
        P(("space", "diag"), None),
    )
    return jax.shard_map(
        body,
        mesh=mesh,
        in_specs=placed,
        out_specs=P(("cfg", "space", "diag"), None, None, None, None),
        check_vma=False,
    )
```

```python
import functools
import math

import jax
import jax.numpy as jnp
from jax import lax
from jax.experimental import pallas as pl
from jax.experimental.pallas import tpu as pltpu
from jax.sharding import PartitionSpec as P

LX = 16
LY = 16
NDISP = 4
CHUNK = 16
MESH = pl.DeviceIdType.MESH
NT = (((1,), (1,)), ((), ()))
f32 = jnp.float32
bf16 = jnp.bfloat16


def elemental_kernel(
    dims, list_ref, mom_ref, spin_ref, link_ref, eig_hbm, tau_hbm, out_ref, mix_hbm,
    eig_ref, cos_ref, sin_ref, ar_ref, ai_ref, above, fields, plus, minus, tau_ref, mix_ref, lists, table,
    part1, recv1, own, part2, recv2, part3, recv3,
    e_local, t_local, m_local, v_send, v_recv, l_send, l_recv, l_local, s1, r1, s2, r2, s3, r3,
):
    nspace, ndiag, inner, local, slices, nvec, plane, factor = dims
    ndev = nspace * ndiag
    outer = nspace // inner
    space = lax.axis_index("space")
    core = lax.axis_index("diag")
    cfg = lax.axis_index("cfg")
    me = space * ndiag + core
    zpos = space // inner
    ypos = lax.rem(space, inner)

    def device(index):
        return (cfg, index // ndiag, lax.rem(index, ndiag))

    def e_copy(t):
        return pltpu.make_async_copy(eig_hbm.at[t], eig_ref.at[t], e_local.at[t])

    t_copy = pltpu.make_async_copy(tau_hbm, tau_ref, t_local)
    m_copy = pltpu.make_async_copy(mix_ref, mix_hbm, m_local)

    barrier = pltpu.get_barrier_semaphore()

    @pl.loop(1, ndev)
    def _(k):
        pl.semaphore_signal(
            barrier, inc=1, device_id=device(lax.rem(me + k, ndev)), device_id_type=MESH
        )

    for t in range(slices):
        e_copy(t).start()
    t_copy.start()

    column = lax.broadcasted_iota(jnp.int32, (1, 128), 1)
    packed = jnp.zeros((1, 128), jnp.int32)
    for i in range(local):
        packed = jnp.where(column == i, list_ref[i, 0], packed)
    lists[0] = packed

    pl.semaphore_wait(barrier, ndev - 1)

    def v_copy(t):
        return pltpu.make_async_remote_copy(
            src_ref=eig_hbm.at[t], dst_ref=above.at[t],
            send_sem=v_send.at[t], recv_sem=v_recv.at[t],
            device_id=device(lax.rem(me + ndev - 1, ndev)), device_id_type=MESH,
        )

    def l_copy(k):
        return pltpu.make_async_remote_copy(
            src_ref=lists.at[0], dst_ref=lists.at[k],
            send_sem=l_send.at[k], recv_sem=l_recv.at[k],
            device_id=device(lax.rem(me + k, ndev)), device_id_type=MESH,
        )

    @pl.loop(1, ndev)
    def _(k):
        l_copy(k).start()

    for t in range(slices):
        v_copy(t).start()

    nmom = mom_ref.shape[0]
    flat = lax.broadcasted_iota(jnp.int32, (1, plane), 1)
    xcoord = lax.rem(flat, LX).astype(f32)
    ycoord = lax.div(flat, LX).astype(f32)
    zcoord = lax.convert_element_type(me, f32)
    rows, hops = [], []
    for m in range(nmom):
        mom = [mom_ref[m, axis].astype(f32) for axis in range(3)]
        rows.append(
            2.0 * math.pi * (mom[0] * xcoord / LX + mom[1] * ycoord / LY + mom[2] * zcoord / ndev)
        )
        hops.append(jnp.full((1, nvec), math.pi, f32))
        for axis, size in enumerate((LX, LY, ndev)):
            hops.append(jnp.full((1, nvec), mom[axis] * (2.0 * math.pi / size), f32))
    angle = jnp.concatenate(rows, 0)
    cos_ref[...] = jnp.concatenate([jnp.cos(angle)] * 3, 1)
    sin_ref[...] = jnp.concatenate([jnp.sin(angle)] * 3, 1)
    hop = jnp.concatenate(hops, 0)
    plain = lax.rem(lax.broadcasted_iota(jnp.int32, hop.shape, 0), NDISP) == 0
    ar_ref[...] = jnp.where(plain, -1.0, jnp.cos(hop))
    ai_ref[...] = jnp.where(plain, 0.0, -jnp.sin(hop))

    lane = lax.broadcasted_iota(jnp.int32, (CHUNK, plane), 1)
    edge = lax.rem(lane, LX) == LX - 1

    def displace(t, direction, source):
        @pl.loop(0, nvec // CHUNK)
        def _(i):
            rows = pl.multiple_of(i * CHUNK, CHUNK)
            vec = []
            for p in range(2):
                line = []
                for c in range(3):
                    v = source[t, p, c, pl.ds(rows, CHUNK), :].astype(f32)
                    if direction == 0:
                        v = jnp.where(
                            edge, pltpu.roll(v, LX - 1, 1), pltpu.roll(v, plane - 1, 1)
                        )
                    elif direction == 1:
                        v = pltpu.roll(v, plane - LX, 1)
                    line.append(v)
                vec.append(line)
            for row in range(3):
                real = imag = None
                for col in range(3):
                    mr = link_ref[t, direction, 0, row, col]
                    mi = link_ref[t, direction, 1, row, col]
                    re = mr * vec[0][col] - mi * vec[1][col]
                    im = mr * vec[1][col] + mi * vec[0][col]
                    real = re if real is None else real + re
                    imag = im if imag is None else imag + im
                lanes = slice(row * plane, (row + 1) * plane)
                fields[t * NDISP + direction + 1, pl.ds(rows, CHUNK), lanes] = real.astype(bf16)
                fields[
                    t * NDISP + direction + 1, pl.ds(nvec + rows, CHUNK), lanes
                ] = imag.astype(bf16)

    def phases(t):
        @pl.loop(0, nvec // CHUNK)
        def _(i):
            rows = pl.multiple_of(i * CHUNK, CHUNK)
            for c in range(3):
                lanes = slice(c * plane, (c + 1) * plane)
                vr = eig_ref[t, 0, c, pl.ds(rows, CHUNK), :]
                vi = eig_ref[t, 1, c, pl.ds(rows, CHUNK), :]
                fields[t * NDISP, pl.ds(rows, CHUNK), lanes] = vr
                fields[t * NDISP, pl.ds(nvec + rows, CHUNK), lanes] = vi
                vr, vi = vr.astype(f32), vi.astype(f32)
                for m in range(nmom):
                    cosine = cos_ref[m:m + 1, lanes]
                    sine = sin_ref[m:m + 1, lanes]
                    a, b = cosine * vr, sine * vi
                    g, h = cosine * vi, sine * vr
                    plus[t * nmom + m, pl.ds(rows, CHUNK), lanes] = (a - b).astype(bf16)
                    plus[t * nmom + m, pl.ds(nvec + rows, CHUNK), lanes] = (g + h).astype(bf16)
                    minus[t * nmom + m, pl.ds(rows, CHUNK), lanes] = (a + b).astype(bf16)
                    minus[t * nmom + m, pl.ds(nvec + rows, CHUNK), lanes] = (g - h).astype(bf16)

    @pl.loop(0, slices)
    def _(t):
        e_copy(t).wait()
        displace(t, 0, eig_ref)
        displace(t, 1, eig_ref)
        phases(t)

    t_copy.wait()
    count, spins = tau_ref.shape[:2]
    for i in range(local):
        q = lax.rem(list_ref[i, 2], count)
        g = list_ref[i, 1]

        @pl.loop(0, 2 * nvec // CHUNK)
        def _(n):
            rows = pl.multiple_of(n * CHUNK, CHUNK)
            tau = [tau_ref[q, s, pl.ds(rows, CHUNK), :].astype(f32) for s in range(spins)]
            for r in range(spins):
                mixed = spin_ref[r, 0, g] * tau[0]
                for s in range(1, spins):
                    mixed = mixed + spin_ref[r, s, g] * tau[s]
                mix_ref[i, r, pl.ds(rows, CHUNK), :] = mixed.astype(bf16)

    m_copy.start()

    @pl.loop(1, ndev)
    def _(k):
        l_copy(k).wait()

    to_smem = pltpu.make_async_copy(lists, table, l_local)
    to_smem.start()
    to_smem.wait()

    @pl.loop(0, slices)
    def _(t):
        v_copy(t).wait_recv()
        displace(t, 2, above)

    def item(dest, i):
        slot = lax.rem(me + ndev - dest, ndev)
        entry = table[slot, 0, i]
        time = lax.div(entry, nmom * NDISP)
        m = lax.rem(lax.div(entry, NDISP), nmom)
        d = lax.rem(entry, NDISP)
        ar = ar_ref[pl.ds(m * NDISP + d, 1), :]
        ai = ai_ref[pl.ds(m * NDISP + d, 1), :]
        x = fields[time * NDISP + d]
        first = lax.dot_general(plus[time * nmom + m], x, NT, preferred_element_type=f32)
        second = lax.dot_general(x, minus[time * nmom + m], NT, preferred_element_type=f32)
        g1r = first[:nvec, :nvec] + first[nvec:, nvec:]
        g1i = first[:nvec, nvec:] - first[nvec:, :nvec]
        g2r = second[:nvec, :nvec] + second[nvec:, nvec:]
        g2i = second[:nvec, nvec:] - second[nvec:, :nvec]
        return (
            (g1r - (ar * g2r - ai * g2i)) * factor,
            (g1i - (ar * g2i + ai * g2r)) * factor,
        )

    levels = outer.bit_length() - 1

    def flip(l):
        size = 1 << l
        return zpos + size * (1 - 2 * lax.rem(zpos // size, 2))

    def away(r):
        row = zpos
        for l in range(levels):
            row = row + lax.rem(r // (1 << l), 2) * (flip(l) - zpos)
        return row

    def copy1(n, i):
        return pltpu.make_async_remote_copy(
            src_ref=part1.at[n, i], dst_ref=recv1.at[n, i], send_sem=s1.at[n, i], recv_sem=r1.at[n, i],
            device_id=(cfg, space, 1 - core), device_id_type=MESH,
        )

    def copy2(n, j, i):
        return pltpu.make_async_remote_copy(
            src_ref=part2.at[n, i], dst_ref=recv2.at[j, i], send_sem=s2.at[j, i], recv_sem=r2.at[j, i],
            device_id=(cfg, zpos * inner + (1 - ypos), core), device_id_type=MESH,
        )

    def copy3(r, i):
        row = flip(levels - 1)
        for l in range(levels - 2, -1, -1):
            row = jnp.where(lax.rem(r, 2 << l) == 1 << l, flip(l), row)
        return pltpu.make_async_remote_copy(
            src_ref=part3.at[r, i], dst_ref=recv3.at[r, i], send_sem=s3.at[r, i], recv_sem=r3.at[r, i],
            device_id=(cfg, row * inner + ypos, core), device_id_type=MESH,
        )

    def unit(n):
        across = jnp.logical_or(n < 3, jnp.logical_and(lax.rem(n, 2) == 0, n < nspace - 2))
        late = jnp.where(n < nspace - 2, (n - 3) // 2, n - outer)
        j = jnp.where(across, jnp.where(n < 3, n, n // 2 + 1), late)
        row = away(outer - 1 - j)
        return across, j, (row * inner + jnp.where(across, 1 - ypos, ypos)) * ndiag

    def give(n):
        _, _, chip = unit(n)
        for i in range(local):
            real, imag = item(chip + (1 - core), i)
            part1[n, i, 0] = real.astype(bf16)
            part1[n, i, 1] = imag.astype(bf16)
            copy1(n, i).start()

    def keep(n):
        _, _, chip = unit(n)
        for i in range(local):
            own[n, i, 0], own[n, i, 1] = item(chip + core, i)

    def join(n):
        across, j, _ = unit(n)
        for i in range(local):
            copy1(n, i).wait_recv()
            total = own[n, i] + recv1[n, i].astype(f32)
            own[n, i] = total
            part2[n, i] = total.astype(bf16)

            @pl.when(across)
            def _():
                copy2(n, j, i).start()

    def collect(q):
        j = q // local
        i = lax.rem(q, local)
        r = outer - 1 - j
        n = jnp.where(j < outer - 2, 2 * j + 3, j + outer)
        copy2(0, j, i).wait()
        own[n, i] = own[n, i] + recv2[j, i].astype(f32)
        for l in range(levels):
            @pl.when(lax.rem(r, 2 << l) == 0)
            def _():
                copy3(r + (1 << l), i).wait()
                own[n, i] = own[n, i] + recv3[r + (1 << l), i].astype(f32)

        @pl.when(r > 0)
        def _():
            part3[r, i] = own[n, i].astype(bf16)
            copy3(r, i).start()

    @pl.loop(0, 3 * nspace)
    def _(k):
        early = core == 0
        kind = jnp.where(early, k // nspace, lax.rem(k + 1, 3))
        n = jnp.where(early, lax.rem(k, nspace), k // 3)

        @pl.when(kind == 0)
        def _():
            give(n)

        @pl.when(kind == 1)
        def _():
            keep(n)

        @pl.when(kind == 2)
        def _():
            join(n)
            first = jnp.where(n == 3, 0, n - 3)
            stop = jnp.where(n == 3, 2, jnp.where(n > 4, n - 2, first))

            @pl.loop(first, stop)
            def _(q):
                collect(q)

    @pl.loop(nspace - 3, outer * local)
    def _(q):
        collect(q)

    out_ref[...] = own[nspace - 1].astype(bf16)

    @pl.loop(0, nspace)
    def _(n):
        for i in range(local):
            copy1(n, i).wait_send()

    for t in range(slices):
        v_copy(t).wait_send()
    m_copy.wait()


def diagram_kernel(elem_ref, mix_ref, out_ref):
    er, ei = elem_ref[0, 0], elem_ref[0, 1]
    square = jnp.concatenate(
        [jnp.concatenate([er, -ei], 1), jnp.concatenate([ei, er], 1)], 0
    )
    for r in range(mix_ref.shape[1]):
        out_ref[0, r] = jnp.dot(square, mix_ref[0, r], preferred_element_type=f32).astype(bf16)


def body(eigvecs, gauge_links, momenta, spin_mix, perambulators, contraction_list):
    slices, _, colors, nvec, depth, plane = eigvecs.shape
    assert depth == 1 and colors == 3
    nspace, ndiag = lax.axis_size("space"), lax.axis_size("diag")
    inner = 2
    outer = nspace // inner
    assert ndiag == 2 and inner * outer == nspace
    assert outer >= 4 and outer & (outer - 1) == 0 and contraction_list.shape[0] >= 2
    ndev = nspace * ndiag
    scale = 1.0 / math.sqrt(3 * plane * ndev)
    nmom = momenta.shape[0]
    local = contraction_list.shape[0]
    count, spins = perambulators.shape[:2]
    width = perambulators.shape[4]
    vmem = pl.BlockSpec(memory_space=pltpu.VMEM)
    smem = pl.BlockSpec(memory_space=pltpu.SMEM)
    hbm = pl.BlockSpec(memory_space=pltpu.HBM)
    tile = (local, 2, nvec, nvec)
    field = (2 * nvec, 3 * plane)
    dma = pltpu.SemaphoreType.DMA
    elem, mixed = pl.pallas_call(
        functools.partial(
            elemental_kernel,
            (nspace, ndiag, inner, local, slices, nvec, plane, 0.5 * scale),
        ),
        out_shape=(
            jax.ShapeDtypeStruct(tile, bf16),
            jax.ShapeDtypeStruct((local, spins, 2 * nvec, width), bf16),
        ),
        in_specs=[smem, smem, smem, vmem, hbm, hbm],
        out_specs=(vmem, hbm),
        scratch_shapes=[
            pltpu.VMEM((slices, 2, 3, nvec, plane), bf16),
            pltpu.VMEM((nmom, 3 * plane), f32),
            pltpu.VMEM((nmom, 3 * plane), f32),
            pltpu.VMEM((nmom * NDISP, nvec), f32),
            pltpu.VMEM((nmom * NDISP, nvec), f32),
            pltpu.VMEM((slices, 2, 3, nvec, plane), bf16),
            pltpu.VMEM((slices * NDISP,) + field, bf16),
            pltpu.VMEM((slices * nmom,) + field, bf16),
            pltpu.VMEM((slices * nmom,) + field, bf16),
            pltpu.VMEM((count, spins, 2 * nvec, width), bf16),
            pltpu.VMEM((local, spins, 2 * nvec, width), bf16),
            pltpu.VMEM((ndev, 1, 128), jnp.int32),
            pltpu.SMEM((ndev, 1, 128), jnp.int32),
            pltpu.VMEM((nspace,) + tile, bf16),
            pltpu.VMEM((nspace,) + tile, bf16),
            pltpu.VMEM((nspace,) + tile, f32),
            pltpu.VMEM((nspace,) + tile, bf16),
            pltpu.VMEM((outer,) + tile, bf16),
            pltpu.VMEM((outer,) + tile, bf16),
            pltpu.VMEM((outer,) + tile, bf16),
            dma((slices,)), dma, dma, dma((slices,)), dma((slices,)),
            dma((ndev,)), dma((ndev,)), dma,
            dma((nspace, local)), dma((nspace, local)),
            dma((outer, local)), dma((outer, local)),
            dma((outer, local)), dma((outer, local)),
        ],
        compiler_params=pltpu.CompilerParams(
            collective_id=0, has_side_effects=True, vmem_limit_bytes=63 * 1024 * 1024
        ),
    )(
        contraction_list, momenta, spin_mix.transpose(1, 2, 0), gauge_links,
        eigvecs.reshape(slices, 2, 3, nvec, plane),
        perambulators.reshape(count, spins, 2 * nvec, width),
    )
    out = pl.pallas_call(
        diagram_kernel,
        grid=(local,),
        in_specs=[
            pl.BlockSpec((1, 2, nvec, nvec), lambda i: (i, 0, 0, 0)),
            pl.BlockSpec((1, spins, 2 * nvec, width), lambda i: (i, 0, 0, 0)),
        ],
        out_specs=pl.BlockSpec((1, spins, 2 * nvec, width), lambda i: (i, 0, 0, 0)),
        out_shape=jax.ShapeDtypeStruct((local, spins, 2 * nvec, width), bf16),
    )(elem, mixed)
    return out.reshape(local, spins, 2, nvec, width)


def solution(mesh):
    placed = (
        P("cfg", None, None, None, ("space", "diag"), None),
        P("cfg", None, None, None, None, ("space", "diag"), None),
        P(),
        P(),
        P(("cfg", "space", "diag"), None, None, None, None),
        P(("space", "diag"), None),
    )
    return jax.shard_map(
        body,
        mesh=mesh,
        in_specs=placed,
        out_specs=P(("cfg", "space", "diag"), None, None, None, None),
        check_vma=False,
    )
```

```python
import functools
import math

import jax
import jax.numpy as jnp
from jax import lax
from jax.experimental import pallas as pl
from jax.experimental.pallas import tpu as pltpu
from jax.sharding import PartitionSpec as P

LX = 16
LY = 16
NDISP = 4
CHUNK = 16
MESH = pl.DeviceIdType.MESH
NT = (((1,), (1,)), ((), ()))
f32 = jnp.float32
bf16 = jnp.bfloat16


def elemental_kernel(
    dims, list_ref, mom_ref, spin_ref, link_ref, eig_hbm, tau_hbm, out_ref, mix_hbm,
    eig_ref, cos_ref, sin_ref, ar_ref, ai_ref, above, fields, plus, minus, tau_ref, mix_ref, lists, table,
    part1, recv1, own, part2, recv2, part3, recv3,
    e_local, t_local, m_local, v_send, v_recv, l_send, l_recv, l_local, s1, r1, s2, r2, s3, r3,
):
    nspace, ndiag, inner, local, slices, nvec, plane, factor = dims
    ndev = nspace * ndiag
    outer = nspace // inner
    space = lax.axis_index("space")
    core = lax.axis_index("diag")
    cfg = lax.axis_index("cfg")
    me = space * ndiag + core
    zpos = space // inner
    ypos = lax.rem(space, inner)

    def device(index):
        return (cfg, index // ndiag, lax.rem(index, ndiag))

    def e_copy(t):
        return pltpu.make_async_copy(eig_hbm.at[t], eig_ref.at[t], e_local.at[t])

    t_copy = pltpu.make_async_copy(tau_hbm, tau_ref, t_local)
    m_copy = pltpu.make_async_copy(mix_ref, mix_hbm, m_local)

    barrier = pltpu.get_barrier_semaphore()

    @pl.loop(1, ndev)
    def _(k):
        pl.semaphore_signal(
            barrier, inc=1, device_id=device(lax.rem(me + k, ndev)), device_id_type=MESH
        )

    for t in range(slices):
        e_copy(t).start()
    t_copy.start()

    column = lax.broadcasted_iota(jnp.int32, (1, 128), 1)
    packed = jnp.zeros((1, 128), jnp.int32)
    for i in range(local):
        packed = jnp.where(column == i, list_ref[i, 0], packed)
    lists[0] = packed

    pl.semaphore_wait(barrier, ndev - 1)

    half = nvec // 2

    def v_copy(t, h):
        rows = pl.ds(pl.multiple_of(h * half, half), half)
        return pltpu.make_async_remote_copy(
            src_ref=eig_hbm.at[t, :, :, rows], dst_ref=above.at[t, :, :, rows],
            send_sem=v_send.at[t, h], recv_sem=v_recv.at[t, h],
            device_id=device(lax.rem(me + ndev - 1, ndev)), device_id_type=MESH,
        )

    def l_copy(k):
        return pltpu.make_async_remote_copy(
            src_ref=lists.at[0], dst_ref=lists.at[k],
            send_sem=l_send.at[k], recv_sem=l_recv.at[k],
            device_id=device(lax.rem(me + k, ndev)), device_id_type=MESH,
        )

    @pl.loop(1, ndev)
    def _(k):
        l_copy(k).start()

    for t in range(slices):
        for h in range(2):
            v_copy(t, h).start()

    nmom = mom_ref.shape[0]
    flat = lax.broadcasted_iota(jnp.int32, (1, plane), 1)
    xcoord = lax.rem(flat, LX).astype(f32)
    ycoord = lax.div(flat, LX).astype(f32)
    zcoord = lax.convert_element_type(me, f32)
    rows, hops = [], []
    for m in range(nmom):
        mom = [mom_ref[m, axis].astype(f32) for axis in range(3)]
        rows.append(
            2.0 * math.pi * (mom[0] * xcoord / LX + mom[1] * ycoord / LY + mom[2] * zcoord / ndev)
        )
        hops.append(jnp.full((1, nvec), math.pi, f32))
        for axis, size in enumerate((LX, LY, ndev)):
            hops.append(jnp.full((1, nvec), mom[axis] * (2.0 * math.pi / size), f32))
    angle = jnp.concatenate(rows, 0)
    cos_ref[...] = jnp.concatenate([jnp.cos(angle)] * 3, 1)
    sin_ref[...] = jnp.concatenate([jnp.sin(angle)] * 3, 1)
    hop = jnp.concatenate(hops, 0)
    plain = lax.rem(lax.broadcasted_iota(jnp.int32, hop.shape, 0), NDISP) == 0
    ar_ref[...] = jnp.where(plain, -1.0, jnp.cos(hop))
    ai_ref[...] = jnp.where(plain, 0.0, -jnp.sin(hop))

    lane = lax.broadcasted_iota(jnp.int32, (CHUNK, plane), 1)
    edge = lax.rem(lane, LX) == LX - 1

    def displace(t, direction, source, begin=0, size=nvec):
        @pl.loop(0, size // CHUNK)
        def _(i):
            rows = pl.multiple_of(begin + i * CHUNK, CHUNK)
            vec = []
            for p in range(2):
                line = []
                for c in range(3):
                    v = source[t, p, c, pl.ds(rows, CHUNK), :].astype(f32)
                    if direction == 0:
                        v = jnp.where(
                            edge, pltpu.roll(v, LX - 1, 1), pltpu.roll(v, plane - 1, 1)
                        )
                    elif direction == 1:
                        v = pltpu.roll(v, plane - LX, 1)
                    line.append(v)
                vec.append(line)
            for row in range(3):
                real = imag = None
                for col in range(3):
                    mr = link_ref[t, direction, 0, row, col]
                    mi = link_ref[t, direction, 1, row, col]
                    re = mr * vec[0][col] - mi * vec[1][col]
                    im = mr * vec[1][col] + mi * vec[0][col]
                    real = re if real is None else real + re
                    imag = im if imag is None else imag + im
                lanes = slice(row * plane, (row + 1) * plane)
                fields[t * NDISP + direction + 1, pl.ds(rows, CHUNK), lanes] = real.astype(bf16)
                fields[
                    t * NDISP + direction + 1, pl.ds(nvec + rows, CHUNK), lanes
                ] = imag.astype(bf16)

    def phases(t):
        @pl.loop(0, nvec // CHUNK)
        def _(i):
            rows = pl.multiple_of(i * CHUNK, CHUNK)
            for c in range(3):
                lanes = slice(c * plane, (c + 1) * plane)
                vr = eig_ref[t, 0, c, pl.ds(rows, CHUNK), :]
                vi = eig_ref[t, 1, c, pl.ds(rows, CHUNK), :]
                fields[t * NDISP, pl.ds(rows, CHUNK), lanes] = vr
                fields[t * NDISP, pl.ds(nvec + rows, CHUNK), lanes] = vi
                vr, vi = vr.astype(f32), vi.astype(f32)
                for m in range(nmom):
                    cosine = cos_ref[m:m + 1, lanes]
                    sine = sin_ref[m:m + 1, lanes]
                    a, b = cosine * vr, sine * vi
                    g, h = cosine * vi, sine * vr
                    plus[t * nmom + m, pl.ds(rows, CHUNK), lanes] = (a - b).astype(bf16)
                    plus[t * nmom + m, pl.ds(nvec + rows, CHUNK), lanes] = (g + h).astype(bf16)
                    minus[t * nmom + m, pl.ds(rows, CHUNK), lanes] = (a + b).astype(bf16)
                    minus[t * nmom + m, pl.ds(nvec + rows, CHUNK), lanes] = (g - h).astype(bf16)

    @pl.loop(0, slices)
    def _(t):
        e_copy(t).wait()
        displace(t, 0, eig_ref)
        displace(t, 1, eig_ref)
        phases(t)

    count, spins = tau_ref.shape[:2]

    def mix():
        t_copy.wait()
        for i in range(local):
            q = lax.rem(list_ref[i, 2], count)
            g = list_ref[i, 1]

            @pl.loop(0, 2 * nvec // CHUNK)
            def _(n):
                rows = pl.multiple_of(n * CHUNK, CHUNK)
                tau = [tau_ref[q, s, pl.ds(rows, CHUNK), :].astype(f32) for s in range(spins)]
                for r in range(spins):
                    mixed = spin_ref[r, 0, g] * tau[0]
                    for s in range(1, spins):
                        mixed = mixed + spin_ref[r, s, g] * tau[s]
                    mix_ref[i, r, pl.ds(rows, CHUNK), :] = mixed.astype(bf16)
        m_copy.start()

    @pl.when(core > 0)
    def _():
        mix()

    @pl.loop(1, ndev)
    def _(k):
        l_copy(k).wait()

    to_smem = pltpu.make_async_copy(lists, table, l_local)
    to_smem.start()
    to_smem.wait()

    @pl.loop(0, slices)
    def _(t):
        for h in range(2):
            v_copy(t, h).wait_recv()
            displace(t, 2, above, h * half, half)

    def item(dest, i):
        slot = lax.rem(me + ndev - dest, ndev)
        entry = table[slot, 0, i]
        time = lax.div(entry, nmom * NDISP)
        m = lax.rem(lax.div(entry, NDISP), nmom)
        d = lax.rem(entry, NDISP)
        ar = ar_ref[pl.ds(m * NDISP + d, 1), :]
        ai = ai_ref[pl.ds(m * NDISP + d, 1), :]
        x = fields[time * NDISP + d]
        first = lax.dot_general(plus[time * nmom + m], x, NT, preferred_element_type=f32)
        second = lax.dot_general(x, minus[time * nmom + m], NT, preferred_element_type=f32)
        g1r = first[:nvec, :nvec] + first[nvec:, nvec:]
        g1i = first[:nvec, nvec:] - first[nvec:, :nvec]
        g2r = second[:nvec, :nvec] + second[nvec:, nvec:]
        g2i = second[:nvec, nvec:] - second[nvec:, :nvec]
        return (
            (g1r - (ar * g2r - ai * g2i)) * factor,
            (g1i - (ar * g2i + ai * g2r)) * factor,
        )

    levels = outer.bit_length() - 1

    def flip(l):
        size = 1 << l
        return zpos + size * (1 - 2 * lax.rem(zpos // size, 2))

    def away(r):
        row = zpos
        for l in range(levels):
            row = row + lax.rem(r // (1 << l), 2) * (flip(l) - zpos)
        return row

    def copy1(n, i):
        return pltpu.make_async_remote_copy(
            src_ref=part1.at[n, i], dst_ref=recv1.at[n, i], send_sem=s1.at[n, i], recv_sem=r1.at[n, i],
            device_id=(cfg, space, 1 - core), device_id_type=MESH,
        )

    def copy2(n, j, i):
        return pltpu.make_async_remote_copy(
            src_ref=part2.at[n, i], dst_ref=recv2.at[j, i], send_sem=s2.at[j, i], recv_sem=r2.at[j, i],
            device_id=(cfg, zpos * inner + (1 - ypos), core), device_id_type=MESH,
        )

    def copy3(r, i):
        row = flip(levels - 1)
        for l in range(levels - 2, -1, -1):
            row = jnp.where(lax.rem(r, 2 << l) == 1 << l, flip(l), row)
        return pltpu.make_async_remote_copy(
            src_ref=part3.at[r, i], dst_ref=recv3.at[r, i], send_sem=s3.at[r, i], recv_sem=r3.at[r, i],
            device_id=(cfg, row * inner + ypos, core), device_id_type=MESH,
        )

    def unit(n):
        across = jnp.logical_or(n < 3, jnp.logical_and(lax.rem(n, 2) == 0, n < nspace - 2))
        late = jnp.where(n < nspace - 2, (n - 3) // 2, n - outer)
        j = jnp.where(across, jnp.where(n < 3, n, n // 2 + 1), late)
        row = away(outer - 1 - j)
        return across, j, (row * inner + jnp.where(across, 1 - ypos, ypos)) * ndiag

    def give(n):
        _, _, chip = unit(n)
        for i in range(local):
            real, imag = item(chip + (1 - core), i)
            part1[n, i, 0] = real.astype(bf16)
            part1[n, i, 1] = imag.astype(bf16)
            copy1(n, i).start()

    def keep(n):
        _, _, chip = unit(n)
        for i in range(local):
            own[n, i, 0], own[n, i, 1] = item(chip + core, i)

    def join(n):
        across, j, _ = unit(n)
        for i in range(local):
            copy1(n, i).wait_recv()
            total = own[n, i] + recv1[n, i].astype(f32)
            own[n, i] = total
            part2[n, i] = total.astype(bf16)

            @pl.when(across)
            def _():
                copy2(n, j, i).start()

    def collect(q):
        j = q // local
        i = lax.rem(q, local)
        r = outer - 1 - j
        n = jnp.where(j < outer - 2, 2 * j + 3, j + outer)
        copy2(0, j, i).wait()
        own[n, i] = own[n, i] + recv2[j, i].astype(f32)
        for l in range(levels):
            @pl.when(lax.rem(r, 2 << l) == 0)
            def _():
                copy3(r + (1 << l), i).wait()
                own[n, i] = own[n, i] + recv3[r + (1 << l), i].astype(f32)

        @pl.when(r > 0)
        def _():
            part3[r, i] = own[n, i].astype(bf16)
            copy3(r, i).start()

    @pl.loop(0, 3 * nspace)
    def _(k):
        early = core == 0
        kind = jnp.where(
            early, jnp.where(k < nspace, 0, 1 + lax.rem(k - nspace + 2 * nspace, 2)), lax.rem(k + 1, 3)
        )
        n = jnp.where(early, jnp.where(k < nspace, k, (k - nspace + 2 * nspace) // 2 - nspace), k // 3)

        @pl.when(kind == 0)
        def _():
            give(n)

        @pl.when(kind == 1)
        def _():
            keep(n)

        @pl.when(kind == 2)
        def _():
            join(n)

            @pl.when(jnp.logical_and(early, n == nspace - 4))
            def _():
                mix()

            first = jnp.where(n == 3, 0, n - 3)
            stop = jnp.where(n == 3, 2, jnp.where(n > 4, n - 2, first))

            @pl.loop(first, stop)
            def _(q):
                collect(q)

    @pl.loop(nspace - 3, outer * local)
    def _(q):
        collect(q)

    out_ref[...] = own[nspace - 1].astype(bf16)

    @pl.loop(0, nspace)
    def _(n):
        for i in range(local):
            copy1(n, i).wait_send()

    for t in range(slices):
        for h in range(2):
            v_copy(t, h).wait_send()
    m_copy.wait()


def diagram_kernel(elem_ref, mix_ref, out_ref):
    er, ei = elem_ref[0, 0], elem_ref[0, 1]
    square = jnp.concatenate(
        [jnp.concatenate([er, -ei], 1), jnp.concatenate([ei, er], 1)], 0
    )
    for r in range(mix_ref.shape[1]):
        out_ref[0, r] = jnp.dot(square, mix_ref[0, r], preferred_element_type=f32).astype(bf16)


def body(eigvecs, gauge_links, momenta, spin_mix, perambulators, contraction_list):
    slices, _, colors, nvec, depth, plane = eigvecs.shape
    assert depth == 1 and colors == 3
    nspace, ndiag = lax.axis_size("space"), lax.axis_size("diag")
    inner = 2
    outer = nspace // inner
    assert ndiag == 2 and inner * outer == nspace
    assert outer >= 4 and outer & (outer - 1) == 0 and contraction_list.shape[0] >= 2
    ndev = nspace * ndiag
    scale = 1.0 / math.sqrt(3 * plane * ndev)
    nmom = momenta.shape[0]
    local = contraction_list.shape[0]
    count, spins = perambulators.shape[:2]
    width = perambulators.shape[4]
    vmem = pl.BlockSpec(memory_space=pltpu.VMEM)
    smem = pl.BlockSpec(memory_space=pltpu.SMEM)
    hbm = pl.BlockSpec(memory_space=pltpu.HBM)
    tile = (local, 2, nvec, nvec)
    field = (2 * nvec, 3 * plane)
    dma = pltpu.SemaphoreType.DMA
    elem, mixed = pl.pallas_call(
        functools.partial(
            elemental_kernel,
            (nspace, ndiag, inner, local, slices, nvec, plane, 0.5 * scale),
        ),
        out_shape=(
            jax.ShapeDtypeStruct(tile, bf16),
            jax.ShapeDtypeStruct((local, spins, 2 * nvec, width), bf16),
        ),
        in_specs=[smem, smem, smem, vmem, hbm, hbm],
        out_specs=(vmem, hbm),
        scratch_shapes=[
            pltpu.VMEM((slices, 2, 3, nvec, plane), bf16),
            pltpu.VMEM((nmom, 3 * plane), f32),
            pltpu.VMEM((nmom, 3 * plane), f32),
            pltpu.VMEM((nmom * NDISP, nvec), f32),
            pltpu.VMEM((nmom * NDISP, nvec), f32),
            pltpu.VMEM((slices, 2, 3, nvec, plane), bf16),
            pltpu.VMEM((slices * NDISP,) + field, bf16),
            pltpu.VMEM((slices * nmom,) + field, bf16),
            pltpu.VMEM((slices * nmom,) + field, bf16),
            pltpu.VMEM((count, spins, 2 * nvec, width), bf16),
            pltpu.VMEM((local, spins, 2 * nvec, width), bf16),
            pltpu.VMEM((ndev, 1, 128), jnp.int32),
            pltpu.SMEM((ndev, 1, 128), jnp.int32),
            pltpu.VMEM((nspace,) + tile, bf16),
            pltpu.VMEM((nspace,) + tile, bf16),
            pltpu.VMEM((nspace,) + tile, f32),
            pltpu.VMEM((nspace,) + tile, bf16),
            pltpu.VMEM((outer,) + tile, bf16),
            pltpu.VMEM((outer,) + tile, bf16),
            pltpu.VMEM((outer,) + tile, bf16),
            dma((slices,)), dma, dma, dma((slices, 2)), dma((slices, 2)),
            dma((ndev,)), dma((ndev,)), dma,
            dma((nspace, local)), dma((nspace, local)),
            dma((outer, local)), dma((outer, local)),
            dma((outer, local)), dma((outer, local)),
        ],
        compiler_params=pltpu.CompilerParams(
            collective_id=0, has_side_effects=True, vmem_limit_bytes=63 * 1024 * 1024
        ),
    )(
        contraction_list, momenta, spin_mix.transpose(1, 2, 0), gauge_links,
        eigvecs.reshape(slices, 2, 3, nvec, plane),
        perambulators.reshape(count, spins, 2 * nvec, width),
    )
    out = pl.pallas_call(
        diagram_kernel,
        grid=(local,),
        in_specs=[
            pl.BlockSpec((1, 2, nvec, nvec), lambda i: (i, 0, 0, 0)),
            pl.BlockSpec((1, spins, 2 * nvec, width), lambda i: (i, 0, 0, 0)),
        ],
        out_specs=pl.BlockSpec((1, spins, 2 * nvec, width), lambda i: (i, 0, 0, 0)),
        out_shape=jax.ShapeDtypeStruct((local, spins, 2 * nvec, width), bf16),
    )(elem, mixed)
    return out.reshape(local, spins, 2, nvec, width)


def solution(mesh):
    placed = (
        P("cfg", None, None, None, ("space", "diag"), None),
        P("cfg", None, None, None, None, ("space", "diag"), None),
        P(),
        P(),
        P(("cfg", "space", "diag"), None, None, None, None),
        P(("space", "diag"), None),
    )
    return jax.shard_map(
        body,
        mesh=mesh,
        in_specs=placed,
        out_specs=P(("cfg", "space", "diag"), None, None, None, None),
        check_vma=False,
    )
```

```python
import functools
import math

import jax
import jax.numpy as jnp
from jax import lax
from jax.experimental import pallas as pl
from jax.experimental.pallas import tpu as pltpu
from jax.sharding import PartitionSpec as P

LX = 16
LY = 16
NDISP = 4
CHUNK = 16
MESH = pl.DeviceIdType.MESH
NT = (((1,), (1,)), ((), ()))
f32 = jnp.float32
bf16 = jnp.bfloat16


def elemental_kernel(
    dims, list_ref, mom_ref, spin_ref, link_ref, eig_hbm, tau_hbm, out_ref, mix_hbm,
    eig_ref, cos_ref, sin_ref, ar_ref, ai_ref, above, fields, plus, minus, tau_ref, mix_ref, lists, table,
    part1, recv1, own, part2, recv2, part3, recv3,
    e_local, t_local, m_local, v_send, v_recv, l_send, l_recv, l_local, s1, r1, s2, r2, s3, r3,
):
    nspace, ndiag, inner, local, slices, nvec, plane, factor = dims
    ndev = nspace * ndiag
    outer = nspace // inner
    space = lax.axis_index("space")
    core = lax.axis_index("diag")
    cfg = lax.axis_index("cfg")
    me = space * ndiag + core
    zpos = space // inner
    ypos = lax.rem(space, inner)

    def device(index):
        return (cfg, index // ndiag, lax.rem(index, ndiag))

    def e_copy(t):
        return pltpu.make_async_copy(eig_hbm.at[t], eig_ref.at[t], e_local.at[t])

    t_copy = pltpu.make_async_copy(tau_hbm, tau_ref, t_local)
    m_copy = pltpu.make_async_copy(mix_ref, mix_hbm, m_local)

    barrier = pltpu.get_barrier_semaphore()

    @pl.loop(1, ndev)
    def _(k):
        pl.semaphore_signal(
            barrier, inc=1, device_id=device(lax.rem(me + k, ndev)), device_id_type=MESH
        )

    for t in range(slices):
        e_copy(t).start()
    t_copy.start()

    column = lax.broadcasted_iota(jnp.int32, (1, 128), 1)
    packed = jnp.zeros((1, 128), jnp.int32)
    for i in range(local):
        packed = jnp.where(column == i, list_ref[i, 0], packed)
    lists[0] = packed

    pl.semaphore_wait(barrier, ndev - 1)

    half = nvec // 2

    def v_copy(t, h):
        rows = pl.ds(pl.multiple_of(h * half, half), half)
        return pltpu.make_async_remote_copy(
            src_ref=eig_hbm.at[t, :, :, rows], dst_ref=above.at[t, :, :, rows],
            send_sem=v_send.at[t, h], recv_sem=v_recv.at[t, h],
            device_id=device(lax.rem(me + ndev - 1, ndev)), device_id_type=MESH,
        )

    def l_copy(k):
        return pltpu.make_async_remote_copy(
            src_ref=lists.at[0], dst_ref=lists.at[k],
            send_sem=l_send.at[k], recv_sem=l_recv.at[k],
            device_id=device(lax.rem(me + k, ndev)), device_id_type=MESH,
        )

    @pl.loop(1, ndev)
    def _(k):
        l_copy(k).start()

    for t in range(slices):
        for h in range(2):
            v_copy(t, h).start()

    nmom = mom_ref.shape[0]
    flat = lax.broadcasted_iota(jnp.int32, (1, plane), 1)
    xcoord = lax.rem(flat, LX).astype(f32)
    ycoord = lax.div(flat, LX).astype(f32)
    zcoord = lax.convert_element_type(me, f32)
    rows, hops = [], []
    for m in range(nmom):
        mom = [mom_ref[m, axis].astype(f32) for axis in range(3)]
        rows.append(
            2.0 * math.pi * (mom[0] * xcoord / LX + mom[1] * ycoord / LY + mom[2] * zcoord / ndev)
        )
        hops.append(jnp.full((1, nvec), math.pi, f32))
        for axis, size in enumerate((LX, LY, ndev)):
            hops.append(jnp.full((1, nvec), mom[axis] * (2.0 * math.pi / size), f32))
    angle = jnp.concatenate(rows, 0)
    cos_ref[...] = jnp.concatenate([jnp.cos(angle)] * 3, 1)
    sin_ref[...] = jnp.concatenate([jnp.sin(angle)] * 3, 1)
    hop = jnp.concatenate(hops, 0)
    plain = lax.rem(lax.broadcasted_iota(jnp.int32, hop.shape, 0), NDISP) == 0
    ar_ref[...] = jnp.where(plain, -1.0, jnp.cos(hop))
    ai_ref[...] = jnp.where(plain, 0.0, -jnp.sin(hop))

    lane = lax.broadcasted_iota(jnp.int32, (CHUNK, plane), 1)
    edge = lax.rem(lane, LX) == LX - 1

    def displace(t, direction, source, begin=0, size=nvec):
        @pl.loop(0, size // CHUNK)
        def _(i):
            rows = pl.multiple_of(begin + i * CHUNK, CHUNK)
            vec = []
            for p in range(2):
                line = []
                for c in range(3):
                    v = source[t, p, c, pl.ds(rows, CHUNK), :].astype(f32)
                    if direction == 0:
                        v = jnp.where(
                            edge, pltpu.roll(v, LX - 1, 1), pltpu.roll(v, plane - 1, 1)
                        )
                    elif direction == 1:
                        v = pltpu.roll(v, plane - LX, 1)
                    line.append(v)
                vec.append(line)
            for row in range(3):
                real = imag = None
                for col in range(3):
                    mr = link_ref[t, direction, 0, row, col]
                    mi = link_ref[t, direction, 1, row, col]
                    re = mr * vec[0][col] - mi * vec[1][col]
                    im = mr * vec[1][col] + mi * vec[0][col]
                    real = re if real is None else real + re
                    imag = im if imag is None else imag + im
                lanes = slice(row * plane, (row + 1) * plane)
                fields[t * NDISP + direction + 1, pl.ds(rows, CHUNK), lanes] = real.astype(bf16)
                fields[
                    t * NDISP + direction + 1, pl.ds(nvec + rows, CHUNK), lanes
                ] = imag.astype(bf16)

    def phases(t):
        @pl.loop(0, nvec // CHUNK)
        def _(i):
            rows = pl.multiple_of(i * CHUNK, CHUNK)
            for c in range(3):
                lanes = slice(c * plane, (c + 1) * plane)
                vr = eig_ref[t, 0, c, pl.ds(rows, CHUNK), :]
                vi = eig_ref[t, 1, c, pl.ds(rows, CHUNK), :]
                fields[t * NDISP, pl.ds(rows, CHUNK), lanes] = vr
                fields[t * NDISP, pl.ds(nvec + rows, CHUNK), lanes] = vi
                vr, vi = vr.astype(f32), vi.astype(f32)
                for m in range(nmom):
                    cosine = cos_ref[m:m + 1, lanes]
                    sine = sin_ref[m:m + 1, lanes]
                    a, b = cosine * vr, sine * vi
                    g, h = cosine * vi, sine * vr
                    plus[t * nmom + m, pl.ds(rows, CHUNK), lanes] = (a - b).astype(bf16)
                    plus[t * nmom + m, pl.ds(nvec + rows, CHUNK), lanes] = (g + h).astype(bf16)
                    minus[t * nmom + m, pl.ds(rows, CHUNK), lanes] = (a + b).astype(bf16)
                    minus[t * nmom + m, pl.ds(nvec + rows, CHUNK), lanes] = (g - h).astype(bf16)

    @pl.loop(0, slices)
    def _(t):
        e_copy(t).wait()
        displace(t, 0, eig_ref)
        displace(t, 1, eig_ref)
        phases(t)

    count, spins = tau_ref.shape[:2]

    def mix():
        t_copy.wait()
        for i in range(local):
            q = lax.rem(list_ref[i, 2], count)
            g = list_ref[i, 1]

            @pl.loop(0, 2 * nvec // CHUNK)
            def _(n):
                rows = pl.multiple_of(n * CHUNK, CHUNK)
                tau = [tau_ref[q, s, pl.ds(rows, CHUNK), :].astype(f32) for s in range(spins)]
                for r in range(spins):
                    mixed = spin_ref[r, 0, g] * tau[0]
                    for s in range(1, spins):
                        mixed = mixed + spin_ref[r, s, g] * tau[s]
                    mix_ref[i, r, pl.ds(rows, CHUNK), :] = mixed.astype(bf16)
        m_copy.start()

    @pl.when(core > 0)
    def _():
        mix()

    @pl.loop(1, ndev)
    def _(k):
        l_copy(k).wait()

    to_smem = pltpu.make_async_copy(lists, table, l_local)
    to_smem.start()
    to_smem.wait()

    @pl.loop(0, slices)
    def _(t):
        for h in range(2):
            v_copy(t, h).wait_recv()
            displace(t, 2, above, h * half, half)

    def item(dest, i):
        slot = lax.rem(me + ndev - dest, ndev)
        entry = table[slot, 0, i]
        time = lax.div(entry, nmom * NDISP)
        m = lax.rem(lax.div(entry, NDISP), nmom)
        d = lax.rem(entry, NDISP)
        ar = ar_ref[pl.ds(m * NDISP + d, 1), :]
        ai = ai_ref[pl.ds(m * NDISP + d, 1), :]
        x = fields[time * NDISP + d]
        first = lax.dot_general(plus[time * nmom + m], x, NT, preferred_element_type=f32)
        second = lax.dot_general(x, minus[time * nmom + m], NT, preferred_element_type=f32)
        g1r = first[:nvec, :nvec] + first[nvec:, nvec:]
        g1i = first[:nvec, nvec:] - first[nvec:, :nvec]
        g2r = second[:nvec, :nvec] + second[nvec:, nvec:]
        g2i = second[:nvec, nvec:] - second[nvec:, :nvec]
        return (
            (g1r - (ar * g2r - ai * g2i)) * factor,
            (g1i - (ar * g2i + ai * g2r)) * factor,
        )

    levels = outer.bit_length() - 1

    def flip(l):
        size = 1 << l
        return zpos + size * (1 - 2 * lax.rem(zpos // size, 2))

    def away(r):
        row = zpos
        for l in range(levels):
            row = row + lax.rem(r // (1 << l), 2) * (flip(l) - zpos)
        return row

    def copy1(n, i):
        return pltpu.make_async_remote_copy(
            src_ref=part1.at[n, i], dst_ref=recv1.at[n, i], send_sem=s1.at[n, i], recv_sem=r1.at[n, i],
            device_id=(cfg, space, 1 - core), device_id_type=MESH,
        )

    def copy2(n, j, i):
        return pltpu.make_async_remote_copy(
            src_ref=part2.at[n, i], dst_ref=recv2.at[j, i], send_sem=s2.at[j, i], recv_sem=r2.at[j, i],
            device_id=(cfg, zpos * inner + (1 - ypos), core), device_id_type=MESH,
        )

    def copy3(r, i):
        row = flip(levels - 1)
        for l in range(levels - 2, -1, -1):
            row = jnp.where(lax.rem(r, 2 << l) == 1 << l, flip(l), row)
        return pltpu.make_async_remote_copy(
            src_ref=part3.at[r, i], dst_ref=recv3.at[r, i], send_sem=s3.at[r, i], recv_sem=r3.at[r, i],
            device_id=(cfg, row * inner + ypos, core), device_id_type=MESH,
        )

    def unit(n):
        across = jnp.logical_or(n < 3, jnp.logical_and(lax.rem(n, 2) == 0, n < nspace - 2))
        late = jnp.where(n < nspace - 2, (n - 3) // 2, n - outer)
        j = jnp.where(across, jnp.where(n < 3, n, n // 2 + 1), late)
        row = away(outer - 1 - j)
        return across, j, (row * inner + jnp.where(across, 1 - ypos, ypos)) * ndiag

    def give(n):
        _, _, chip = unit(n)
        for i in range(local):
            real, imag = item(chip + (1 - core), i)
            part1[n, i, 0] = real.astype(bf16)
            part1[n, i, 1] = imag.astype(bf16)
            copy1(n, i).start()

    def keep(n):
        across, j, chip = unit(n)
        for i in range(local):
            real, imag = item(chip + core, i)
            copy1(n, i).wait_recv()
            real = real + recv1[n, i, 0].astype(f32)
            imag = imag + recv1[n, i, 1].astype(f32)
            own[n, i, 0] = real
            own[n, i, 1] = imag
            part2[n, i, 0] = real.astype(bf16)
            part2[n, i, 1] = imag.astype(bf16)

            @pl.when(across)
            def _():
                copy2(n, j, i).start()

    def collect(q):
        j = q // local
        i = lax.rem(q, local)
        r = outer - 1 - j
        n = jnp.where(j < outer - 2, 2 * j + 3, j + outer)
        copy2(0, j, i).wait()
        own[n, i] = own[n, i] + recv2[j, i].astype(f32)
        for l in range(levels):
            @pl.when(lax.rem(r, 2 << l) == 0)
            def _():
                copy3(r + (1 << l), i).wait()
                own[n, i] = own[n, i] + recv3[r + (1 << l), i].astype(f32)

        @pl.when(r > 0)
        def _():
            part3[r, i] = own[n, i].astype(bf16)
            copy3(r, i).start()

    @pl.loop(0, 2 * nspace)
    def _(k):
        early = core == 0
        gives = jnp.where(early, k < nspace, lax.rem(k, 2) == 1)
        n = jnp.where(early, lax.rem(k, nspace), k // 2)

        @pl.when(gives)
        def _():
            give(n)

        @pl.when(jnp.logical_not(gives))
        def _():
            keep(n)

            @pl.when(jnp.logical_and(early, n == nspace - 4))
            def _():
                mix()

            first = jnp.where(n == 3, 0, n - 3)
            stop = jnp.where(n == 3, 2, jnp.where(n > 4, n - 2, first))

            @pl.loop(first, stop)
            def _(q):
                collect(q)

    @pl.loop(nspace - 3, outer * local)
    def _(q):
        collect(q)

    out_ref[...] = own[nspace - 1].astype(bf16)

    @pl.loop(0, nspace)
    def _(n):
        for i in range(local):
            copy1(n, i).wait_send()

    for t in range(slices):
        for h in range(2):
            v_copy(t, h).wait_send()
    m_copy.wait()


def diagram_kernel(elem_ref, mix_ref, out_ref):
    er, ei = elem_ref[0, 0], elem_ref[0, 1]
    square = jnp.concatenate(
        [jnp.concatenate([er, -ei], 1), jnp.concatenate([ei, er], 1)], 0
    )
    for r in range(mix_ref.shape[1]):
        out_ref[0, r] = jnp.dot(square, mix_ref[0, r], preferred_element_type=f32).astype(bf16)


def body(eigvecs, gauge_links, momenta, spin_mix, perambulators, contraction_list):
    slices, _, colors, nvec, depth, plane = eigvecs.shape
    assert depth == 1 and colors == 3
    nspace, ndiag = lax.axis_size("space"), lax.axis_size("diag")
    inner = 2
    outer = nspace // inner
    assert ndiag == 2 and inner * outer == nspace
    assert outer >= 4 and outer & (outer - 1) == 0 and contraction_list.shape[0] >= 2
    ndev = nspace * ndiag
    scale = 1.0 / math.sqrt(3 * plane * ndev)
    nmom = momenta.shape[0]
    local = contraction_list.shape[0]
    count, spins = perambulators.shape[:2]
    width = perambulators.shape[4]
    vmem = pl.BlockSpec(memory_space=pltpu.VMEM)
    smem = pl.BlockSpec(memory_space=pltpu.SMEM)
    hbm = pl.BlockSpec(memory_space=pltpu.HBM)
    tile = (local, 2, nvec, nvec)
    field = (2 * nvec, 3 * plane)
    dma = pltpu.SemaphoreType.DMA
    elem, mixed = pl.pallas_call(
        functools.partial(
            elemental_kernel,
            (nspace, ndiag, inner, local, slices, nvec, plane, 0.5 * scale),
        ),
        out_shape=(
            jax.ShapeDtypeStruct(tile, bf16),
            jax.ShapeDtypeStruct((local, spins, 2 * nvec, width), bf16),
        ),
        in_specs=[smem, smem, smem, vmem, hbm, hbm],
        out_specs=(vmem, hbm),
        scratch_shapes=[
            pltpu.VMEM((slices, 2, 3, nvec, plane), bf16),
            pltpu.VMEM((nmom, 3 * plane), f32),
            pltpu.VMEM((nmom, 3 * plane), f32),
            pltpu.VMEM((nmom * NDISP, nvec), f32),
            pltpu.VMEM((nmom * NDISP, nvec), f32),
            pltpu.VMEM((slices, 2, 3, nvec, plane), bf16),
            pltpu.VMEM((slices * NDISP,) + field, bf16),
            pltpu.VMEM((slices * nmom,) + field, bf16),
            pltpu.VMEM((slices * nmom,) + field, bf16),
            pltpu.VMEM((count, spins, 2 * nvec, width), bf16),
            pltpu.VMEM((local, spins, 2 * nvec, width), bf16),
            pltpu.VMEM((ndev, 1, 128), jnp.int32),
            pltpu.SMEM((ndev, 1, 128), jnp.int32),
            pltpu.VMEM((nspace,) + tile, bf16),
            pltpu.VMEM((nspace,) + tile, bf16),
            pltpu.VMEM((nspace,) + tile, f32),
            pltpu.VMEM((nspace,) + tile, bf16),
            pltpu.VMEM((outer,) + tile, bf16),
            pltpu.VMEM((outer,) + tile, bf16),
            pltpu.VMEM((outer,) + tile, bf16),
            dma((slices,)), dma, dma, dma((slices, 2)), dma((slices, 2)),
            dma((ndev,)), dma((ndev,)), dma,
            dma((nspace, local)), dma((nspace, local)),
            dma((outer, local)), dma((outer, local)),
            dma((outer, local)), dma((outer, local)),
        ],
        compiler_params=pltpu.CompilerParams(
            collective_id=0, has_side_effects=True, vmem_limit_bytes=63 * 1024 * 1024
        ),
    )(
        contraction_list, momenta, spin_mix.transpose(1, 2, 0), gauge_links,
        eigvecs.reshape(slices, 2, 3, nvec, plane),
        perambulators.reshape(count, spins, 2 * nvec, width),
    )
    out = pl.pallas_call(
        diagram_kernel,
        grid=(local,),
        in_specs=[
            pl.BlockSpec((1, 2, nvec, nvec), lambda i: (i, 0, 0, 0)),
            pl.BlockSpec((1, spins, 2 * nvec, width), lambda i: (i, 0, 0, 0)),
        ],
        out_specs=pl.BlockSpec((1, spins, 2 * nvec, width), lambda i: (i, 0, 0, 0)),
        out_shape=jax.ShapeDtypeStruct((local, spins, 2 * nvec, width), bf16),
    )(elem, mixed)
    return out.reshape(local, spins, 2, nvec, width)


def solution(mesh):
    placed = (
        P("cfg", None, None, None, ("space", "diag"), None),
        P("cfg", None, None, None, None, ("space", "diag"), None),
        P(),
        P(),
        P(("cfg", "space", "diag"), None, None, None, None),
        P(("space", "diag"), None),
    )
    return jax.shard_map(
        body,
        mesh=mesh,
        in_specs=placed,
        out_specs=P(("cfg", "space", "diag"), None, None, None, None),
        check_vma=False,
    )
```

```python
import functools
import math

import jax
import jax.numpy as jnp
from jax import lax
from jax.experimental import pallas as pl
from jax.experimental.pallas import tpu as pltpu
from jax.sharding import PartitionSpec as P

LX = 16
LY = 16
NDISP = 4
CHUNK = 16
MESH = pl.DeviceIdType.MESH
NT = (((1,), (1,)), ((), ()))
f32 = jnp.float32
bf16 = jnp.bfloat16


def elemental_kernel(
    dims, list_ref, mom_ref, spin_ref, link_ref, eig_hbm, tau_hbm, out_ref, mix_hbm,
    eig_ref, cos_ref, sin_ref, ar_ref, ai_ref, above, fields, plus, minus, tau_ref, mix_ref, lists, table,
    part1, recv1, own, part2, recv2, part3, recv3,
    e_local, t_local, m_local, v_send, v_recv, l_send, l_recv, l_local, s1, r1, s2, r2, s3, r3,
):
    nspace, ndiag, inner, local, slices, nvec, plane, factor = dims
    ndev = nspace * ndiag
    outer = nspace // inner
    space = lax.axis_index("space")
    core = lax.axis_index("diag")
    cfg = lax.axis_index("cfg")
    me = space * ndiag + core
    zpos = space // inner
    ypos = lax.rem(space, inner)

    def device(index):
        return (cfg, index // ndiag, lax.rem(index, ndiag))

    def e_copy(t):
        return pltpu.make_async_copy(eig_hbm.at[t], eig_ref.at[t], e_local.at[t])

    t_copy = pltpu.make_async_copy(tau_hbm, tau_ref, t_local)
    m_copy = pltpu.make_async_copy(mix_ref, mix_hbm, m_local)

    barrier = pltpu.get_barrier_semaphore()

    @pl.loop(1, ndev)
    def _(k):
        pl.semaphore_signal(
            barrier, inc=1, device_id=device(lax.rem(me + k, ndev)), device_id_type=MESH
        )

    for t in range(slices):
        e_copy(t).start()
    t_copy.start()

    column = lax.broadcasted_iota(jnp.int32, (1, 128), 1)
    packed = jnp.zeros((1, 128), jnp.int32)
    for i in range(local):
        packed = jnp.where(column == i, list_ref[i, 0], packed)
    lists[0] = packed

    pl.semaphore_wait(barrier, ndev - 1)

    half = nvec // 2

    def v_copy(t, h):
        rows = pl.ds(pl.multiple_of(h * half, half), half)
        return pltpu.make_async_remote_copy(
            src_ref=eig_hbm.at[t, :, :, rows], dst_ref=above.at[t, :, :, rows],
            send_sem=v_send.at[t, h], recv_sem=v_recv.at[t, h],
            device_id=device(lax.rem(me + ndev - 1, ndev)), device_id_type=MESH,
        )

    def l_copy(k):
        return pltpu.make_async_remote_copy(
            src_ref=lists.at[0], dst_ref=lists.at[k],
            send_sem=l_send.at[k], recv_sem=l_recv.at[k],
            device_id=device(lax.rem(me + k, ndev)), device_id_type=MESH,
        )

    for h in range(2):
        v_copy(0, h).start()

    @pl.loop(1, ndev)
    def _(k):
        l_copy(k).start()

    for t in range(1, slices):
        for h in range(2):
            v_copy(t, h).start()

    nmom = mom_ref.shape[0]
    flat = lax.broadcasted_iota(jnp.int32, (1, plane), 1)
    xcoord = lax.rem(flat, LX).astype(f32)
    ycoord = lax.div(flat, LX).astype(f32)
    zcoord = lax.convert_element_type(me, f32)
    rows, hops = [], []
    for m in range(nmom):
        mom = [mom_ref[m, axis].astype(f32) for axis in range(3)]
        rows.append(
            2.0 * math.pi * (mom[0] * xcoord / LX + mom[1] * ycoord / LY + mom[2] * zcoord / ndev)
        )
        hops.append(jnp.full((1, nvec), math.pi, f32))
        for axis, size in enumerate((LX, LY, ndev)):
            hops.append(jnp.full((1, nvec), mom[axis] * (2.0 * math.pi / size), f32))
    angle = jnp.concatenate(rows, 0)
    cos_ref[...] = jnp.concatenate([jnp.cos(angle)] * 3, 1)
    sin_ref[...] = jnp.concatenate([jnp.sin(angle)] * 3, 1)
    hop = jnp.concatenate(hops, 0)
    plain = lax.rem(lax.broadcasted_iota(jnp.int32, hop.shape, 0), NDISP) == 0
    ar_ref[...] = jnp.where(plain, -1.0, jnp.cos(hop))
    ai_ref[...] = jnp.where(plain, 0.0, -jnp.sin(hop))

    lane = lax.broadcasted_iota(jnp.int32, (CHUNK, plane), 1)
    edge = lax.rem(lane, LX) == LX - 1

    def displace(t, direction, source, begin=0, size=nvec):
        @pl.loop(0, size // CHUNK)
        def _(i):
            rows = pl.multiple_of(begin + i * CHUNK, CHUNK)
            vec = []
            for p in range(2):
                line = []
                for c in range(3):
                    v = source[t, p, c, pl.ds(rows, CHUNK), :].astype(f32)
                    if direction == 0:
                        v = jnp.where(
                            edge, pltpu.roll(v, LX - 1, 1), pltpu.roll(v, plane - 1, 1)
                        )
                    elif direction == 1:
                        v = pltpu.roll(v, plane - LX, 1)
                    line.append(v)
                vec.append(line)
            for row in range(3):
                real = imag = None
                for col in range(3):
                    mr = link_ref[t, direction, 0, row, col]
                    mi = link_ref[t, direction, 1, row, col]
                    re = mr * vec[0][col] - mi * vec[1][col]
                    im = mr * vec[1][col] + mi * vec[0][col]
                    real = re if real is None else real + re
                    imag = im if imag is None else imag + im
                lanes = slice(row * plane, (row + 1) * plane)
                fields[t * NDISP + direction + 1, pl.ds(rows, CHUNK), lanes] = real.astype(bf16)
                fields[
                    t * NDISP + direction + 1, pl.ds(nvec + rows, CHUNK), lanes
                ] = imag.astype(bf16)

    def phases(t):
        @pl.loop(0, nvec // CHUNK)
        def _(i):
            rows = pl.multiple_of(i * CHUNK, CHUNK)
            for c in range(3):
                lanes = slice(c * plane, (c + 1) * plane)
                vr = eig_ref[t, 0, c, pl.ds(rows, CHUNK), :]
                vi = eig_ref[t, 1, c, pl.ds(rows, CHUNK), :]
                fields[t * NDISP, pl.ds(rows, CHUNK), lanes] = vr
                fields[t * NDISP, pl.ds(nvec + rows, CHUNK), lanes] = vi
                vr, vi = vr.astype(f32), vi.astype(f32)
                for m in range(nmom):
                    cosine = cos_ref[m:m + 1, lanes]
                    sine = sin_ref[m:m + 1, lanes]
                    a, b = cosine * vr, sine * vi
                    g, h = cosine * vi, sine * vr
                    plus[t * nmom + m, pl.ds(rows, CHUNK), lanes] = (a - b).astype(bf16)
                    plus[t * nmom + m, pl.ds(nvec + rows, CHUNK), lanes] = (g + h).astype(bf16)
                    minus[t * nmom + m, pl.ds(rows, CHUNK), lanes] = (a + b).astype(bf16)
                    minus[t * nmom + m, pl.ds(nvec + rows, CHUNK), lanes] = (g - h).astype(bf16)

    @pl.loop(0, slices)
    def _(t):
        e_copy(t).wait()
        displace(t, 0, eig_ref)
        displace(t, 1, eig_ref)
        phases(t)

    count, spins = tau_ref.shape[:2]

    def mix():
        t_copy.wait()
        for i in range(local):
            q = lax.rem(list_ref[i, 2], count)
            g = list_ref[i, 1]

            @pl.loop(0, 2 * nvec // CHUNK)
            def _(n):
                rows = pl.multiple_of(n * CHUNK, CHUNK)
                tau = [tau_ref[q, s, pl.ds(rows, CHUNK), :].astype(f32) for s in range(spins)]
                for r in range(spins):
                    mixed = spin_ref[r, 0, g] * tau[0]
                    for s in range(1, spins):
                        mixed = mixed + spin_ref[r, s, g] * tau[s]
                    mix_ref[i, r, pl.ds(rows, CHUNK), :] = mixed.astype(bf16)
        m_copy.start()

    @pl.when(core > 0)
    def _():
        mix()

    @pl.loop(1, ndev)
    def _(k):
        l_copy(k).wait()

    to_smem = pltpu.make_async_copy(lists, table, l_local)
    to_smem.start()
    to_smem.wait()

    @pl.loop(0, slices)
    def _(t):
        for h in range(2):
            v_copy(t, h).wait_recv()
            displace(t, 2, above, h * half, half)

    def item(dest, i):
        slot = lax.rem(me + ndev - dest, ndev)
        entry = table[slot, 0, i]
        time = lax.div(entry, nmom * NDISP)
        m = lax.rem(lax.div(entry, NDISP), nmom)
        d = lax.rem(entry, NDISP)
        ar = ar_ref[pl.ds(m * NDISP + d, 1), :]
        ai = ai_ref[pl.ds(m * NDISP + d, 1), :]
        x = fields[time * NDISP + d]
        first = lax.dot_general(plus[time * nmom + m], x, NT, preferred_element_type=f32)
        second = lax.dot_general(x, minus[time * nmom + m], NT, preferred_element_type=f32)
        g1r = first[:nvec, :nvec] + first[nvec:, nvec:]
        g1i = first[:nvec, nvec:] - first[nvec:, :nvec]
        g2r = second[:nvec, :nvec] + second[nvec:, nvec:]
        g2i = second[:nvec, nvec:] - second[nvec:, :nvec]
        return (
            (g1r - (ar * g2r - ai * g2i)) * factor,
            (g1i - (ar * g2i + ai * g2r)) * factor,
        )

    levels = outer.bit_length() - 1

    def flip(l):
        size = 1 << l
        return zpos + size * (1 - 2 * lax.rem(zpos // size, 2))

    def away(r):
        row = zpos
        for l in range(levels):
            row = row + lax.rem(r // (1 << l), 2) * (flip(l) - zpos)
        return row

    def copy1(n, i):
        return pltpu.make_async_remote_copy(
            src_ref=part1.at[n, i], dst_ref=recv1.at[n, i], send_sem=s1.at[n, i], recv_sem=r1.at[n, i],
            device_id=(cfg, space, 1 - core), device_id_type=MESH,
        )

    def copy2(n, j, i):
        return pltpu.make_async_remote_copy(
            src_ref=part2.at[n, i], dst_ref=recv2.at[j, i], send_sem=s2.at[j, i], recv_sem=r2.at[j, i],
            device_id=(cfg, zpos * inner + (1 - ypos), core), device_id_type=MESH,
        )

    def copy3(r, i):
        row = flip(levels - 1)
        for l in range(levels - 2, -1, -1):
            row = jnp.where(lax.rem(r, 2 << l) == 1 << l, flip(l), row)
        return pltpu.make_async_remote_copy(
            src_ref=part3.at[r, i], dst_ref=recv3.at[r, i], send_sem=s3.at[r, i], recv_sem=r3.at[r, i],
            device_id=(cfg, row * inner + ypos, core), device_id_type=MESH,
        )

    def unit(n):
        across = jnp.logical_or(n < 3, jnp.logical_and(lax.rem(n, 2) == 0, n < nspace - 2))
        late = jnp.where(n < nspace - 2, (n - 3) // 2, n - outer)
        j = jnp.where(across, jnp.where(n < 3, n, n // 2 + 1), late)
        row = away(outer - 1 - j)
        return across, j, (row * inner + jnp.where(across, 1 - ypos, ypos)) * ndiag

    def give(n):
        _, _, chip = unit(n)
        for i in range(local):
            real, imag = item(chip + (1 - core), i)
            part1[n, i, 0] = real.astype(bf16)
            part1[n, i, 1] = imag.astype(bf16)
            copy1(n, i).start()

    def keep(n):
        _, _, chip = unit(n)
        for i in range(local):
            own[n, i, 0], own[n, i, 1] = item(chip + core, i)

    def join(n):
        across, j, _ = unit(n)
        for i in range(local):
            copy1(n, i).wait_recv()
            total = own[n, i] + recv1[n, i].astype(f32)
            own[n, i] = total
            part2[n, i] = total.astype(bf16)

            @pl.when(across)
            def _():
                copy2(n, j, i).start()

    def collect(q):
        j = q // local
        i = lax.rem(q, local)
        r = outer - 1 - j
        n = jnp.where(j < outer - 2, 2 * j + 3, j + outer)
        copy2(0, j, i).wait()
        own[n, i] = own[n, i] + recv2[j, i].astype(f32)
        for l in range(levels):
            @pl.when(lax.rem(r, 2 << l) == 0)
            def _():
                copy3(r + (1 << l), i).wait()
                own[n, i] = own[n, i] + recv3[r + (1 << l), i].astype(f32)

        @pl.when(r > 0)
        def _():
            part3[r, i] = own[n, i].astype(bf16)
            copy3(r, i).start()

    @pl.loop(0, 3 * nspace)
    def _(k):
        early = core == 0
        kind = jnp.where(
            early, jnp.where(k < nspace, 0, 1 + lax.rem(k - nspace + 2 * nspace, 2)), lax.rem(k + 1, 3)
        )
        n = jnp.where(early, jnp.where(k < nspace, k, (k - nspace + 2 * nspace) // 2 - nspace), k // 3)

        @pl.when(kind == 0)
        def _():
            give(n)

        @pl.when(kind == 1)
        def _():
            keep(n)

        @pl.when(kind == 2)
        def _():
            join(n)

            @pl.when(jnp.logical_and(early, n == nspace - 4))
            def _():
                mix()

            first = jnp.where(n == 3, 0, n - 3)
            stop = jnp.where(n == 3, 2, jnp.where(n > 4, n - 2, first))

            @pl.loop(first, stop)
            def _(q):
                collect(q)

    @pl.loop(nspace - 3, outer * local)
    def _(q):
        collect(q)

    out_ref[...] = own[nspace - 1].astype(bf16)

    @pl.loop(0, nspace)
    def _(n):
        for i in range(local):
            copy1(n, i).wait_send()

    for t in range(slices):
        for h in range(2):
            v_copy(t, h).wait_send()
    m_copy.wait()


def diagram_kernel(elem_ref, mix_ref, out_hbm, out_ref, store_sem):
    local, spins = mix_ref.shape[:2]
    group = 2 if spins % 2 == 0 else 1

    def store(i, h):
        some = pl.ds(h * group, group)
        return pltpu.make_async_copy(out_ref.at[i, some], out_hbm.at[i, some], store_sem.at[i, h])

    pieces = [(i, h) for i in range(local) for h in range(spins // group)]
    for i, h in pieces:
        if h == 0:
            er, ei = elem_ref[i, 0], elem_ref[i, 1]
            square = jnp.concatenate(
                [jnp.concatenate([er, -ei], 1), jnp.concatenate([ei, er], 1)], 0
            )
        for r in range(h * group, (h + 1) * group):
            out_ref[i, r] = jnp.dot(
                square, mix_ref[i, r], preferred_element_type=f32
            ).astype(bf16)
        store(i, h).start()
    for i, h in pieces:
        store(i, h).wait()


def body(eigvecs, gauge_links, momenta, spin_mix, perambulators, contraction_list):
    slices, _, colors, nvec, depth, plane = eigvecs.shape
    assert depth == 1 and colors == 3
    nspace, ndiag = lax.axis_size("space"), lax.axis_size("diag")
    inner = 2
    outer = nspace // inner
    assert ndiag == 2 and inner * outer == nspace
    assert outer >= 4 and outer & (outer - 1) == 0 and contraction_list.shape[0] >= 2
    ndev = nspace * ndiag
    scale = 1.0 / math.sqrt(3 * plane * ndev)
    nmom = momenta.shape[0]
    local = contraction_list.shape[0]
    count, spins = perambulators.shape[:2]
    width = perambulators.shape[4]
    vmem = pl.BlockSpec(memory_space=pltpu.VMEM)
    smem = pl.BlockSpec(memory_space=pltpu.SMEM)
    hbm = pl.BlockSpec(memory_space=pltpu.HBM)
    tile = (local, 2, nvec, nvec)
    field = (2 * nvec, 3 * plane)
    dma = pltpu.SemaphoreType.DMA
    elem, mixed = pl.pallas_call(
        functools.partial(
            elemental_kernel,
            (nspace, ndiag, inner, local, slices, nvec, plane, 0.5 * scale),
        ),
        out_shape=(
            jax.ShapeDtypeStruct(tile, bf16),
            jax.ShapeDtypeStruct((local, spins, 2 * nvec, width), bf16),
        ),
        in_specs=[smem, smem, smem, vmem, hbm, hbm],
        out_specs=(vmem, pl.BlockSpec(memory_space=pl.ANY)),
        scratch_shapes=[
            pltpu.VMEM((slices, 2, 3, nvec, plane), bf16),
            pltpu.VMEM((nmom, 3 * plane), f32),
            pltpu.VMEM((nmom, 3 * plane), f32),
            pltpu.VMEM((nmom * NDISP, nvec), f32),
            pltpu.VMEM((nmom * NDISP, nvec), f32),
            pltpu.VMEM((slices, 2, 3, nvec, plane), bf16),
            pltpu.VMEM((slices * NDISP,) + field, bf16),
            pltpu.VMEM((slices * nmom,) + field, bf16),
            pltpu.VMEM((slices * nmom,) + field, bf16),
            pltpu.VMEM((count, spins, 2 * nvec, width), bf16),
            pltpu.VMEM((local, spins, 2 * nvec, width), bf16),
            pltpu.VMEM((ndev, 1, 128), jnp.int32),
            pltpu.SMEM((ndev, 1, 128), jnp.int32),
            pltpu.VMEM((nspace,) + tile, bf16),
            pltpu.VMEM((nspace,) + tile, bf16),
            pltpu.VMEM((nspace,) + tile, f32),
            pltpu.VMEM((nspace,) + tile, bf16),
            pltpu.VMEM((outer,) + tile, bf16),
            pltpu.VMEM((outer,) + tile, bf16),
            pltpu.VMEM((outer,) + tile, bf16),
            dma((slices,)), dma, dma, dma((slices, 2)), dma((slices, 2)),
            dma((ndev,)), dma((ndev,)), dma,
            dma((nspace, local)), dma((nspace, local)),
            dma((outer, local)), dma((outer, local)),
            dma((outer, local)), dma((outer, local)),
        ],
        compiler_params=pltpu.CompilerParams(
            collective_id=0, has_side_effects=True, vmem_limit_bytes=52 * 1024 * 1024
        ),
    )(*(
        pltpu.with_memory_space_constraint(x, pltpu.HBM) for x in (
            contraction_list, momenta, spin_mix.transpose(1, 2, 0), gauge_links,
            eigvecs.reshape(slices, 2, 3, nvec, plane),
            perambulators.reshape(count, spins, 2 * nvec, width),
        )
    ))
    out = pl.pallas_call(
        diagram_kernel,
        in_specs=[vmem, vmem],
        out_specs=hbm,
        out_shape=jax.ShapeDtypeStruct((local, spins, 2 * nvec, width), bf16),
        scratch_shapes=[
            pltpu.VMEM((local, spins, 2 * nvec, width), bf16), dma((local, spins)),
        ],
        compiler_params=pltpu.CompilerParams(vmem_limit_bytes=24 * 1024 * 1024),
    )(elem, mixed)
    return out.reshape(local, spins, 2, nvec, width)


def solution(mesh):
    placed = (
        P("cfg", None, None, None, ("space", "diag"), None),
        P("cfg", None, None, None, None, ("space", "diag"), None),
        P(),
        P(),
        P(("cfg", "space", "diag"), None, None, None, None),
        P(("space", "diag"), None),
    )
    return jax.shard_map(
        body,
        mesh=mesh,
        in_specs=placed,
        out_specs=P(("cfg", "space", "diag"), None, None, None, None),
        check_vma=False,
    )
```

```python
import functools
import math

import jax
import jax.numpy as jnp
from jax import lax
from jax.experimental import pallas as pl
from jax.experimental.pallas import tpu as pltpu
from jax.sharding import PartitionSpec as P

LX = 16
LY = 16
NDISP = 4
CHUNK = 16
MESH = pl.DeviceIdType.MESH
NT = (((1,), (1,)), ((), ()))
f32 = jnp.float32
bf16 = jnp.bfloat16


def elemental_kernel(
    dims, list_ref, mom_ref, spin_ref, link_ref, eig_hbm, tau_hbm, out_ref, mix_hbm,
    eig_ref, cos_ref, sin_ref, ar_ref, ai_ref, above, fields, plus, minus, tau_ref, mix_ref, lists, table,
    part1, recv1, own, part2, recv2, part3, recv3,
    e_local, t_local, m_local, v_send, v_recv, l_send, l_recv, l_local, s1, r1, s2, r2, s3, r3,
):
    nspace, ndiag, inner, local, slices, nvec, plane, factor = dims
    ndev = nspace * ndiag
    outer = nspace // inner
    space = lax.axis_index("space")
    core = lax.axis_index("diag")
    cfg = lax.axis_index("cfg")
    me = space * ndiag + core
    zpos = space // inner
    ypos = lax.rem(space, inner)

    def device(index):
        return (cfg, index // ndiag, lax.rem(index, ndiag))

    def e_copy(t):
        return pltpu.make_async_copy(eig_hbm.at[t], eig_ref.at[t], e_local.at[t])

    t_copy = pltpu.make_async_copy(tau_hbm, tau_ref, t_local)
    m_copy = pltpu.make_async_copy(mix_ref, mix_hbm, m_local)

    barrier = pltpu.get_barrier_semaphore()

    @pl.loop(1, ndev)
    def _(k):
        pl.semaphore_signal(
            barrier, inc=1, device_id=device(lax.rem(me + k, ndev)), device_id_type=MESH
        )

    for t in range(slices):
        e_copy(t).start()
    t_copy.start()

    column = lax.broadcasted_iota(jnp.int32, (1, 128), 1)
    packed = jnp.zeros((1, 128), jnp.int32)
    for i in range(local):
        packed = jnp.where(column == i, list_ref[i, 0], packed)
    lists[0] = packed

    pl.semaphore_wait(barrier, ndev - 1)

    half = nvec // 2

    def v_copy(t, h):
        rows = pl.ds(pl.multiple_of(h * half, half), half)
        return pltpu.make_async_remote_copy(
            src_ref=eig_hbm.at[t, :, :, rows], dst_ref=above.at[t, :, :, rows],
            send_sem=v_send.at[t, h], recv_sem=v_recv.at[t, h],
            device_id=device(lax.rem(me + ndev - 1, ndev)), device_id_type=MESH,
        )

    def l_copy(k):
        return pltpu.make_async_remote_copy(
            src_ref=lists.at[0], dst_ref=lists.at[k],
            send_sem=l_send.at[k], recv_sem=l_recv.at[k],
            device_id=device(lax.rem(me + k, ndev)), device_id_type=MESH,
        )

    for h in range(2):
        v_copy(0, h).start()

    @pl.loop(1, ndev)
    def _(k):
        l_copy(k).start()

    for t in range(1, slices):
        for h in range(2):
            v_copy(t, h).start()

    nmom = mom_ref.shape[0]
    flat = lax.broadcasted_iota(jnp.int32, (1, plane), 1)
    xcoord = lax.rem(flat, LX).astype(f32)
    ycoord = lax.div(flat, LX).astype(f32)
    zcoord = lax.convert_element_type(me, f32)
    rows, hops = [], []
    for m in range(nmom):
        mom = [mom_ref[m, axis].astype(f32) for axis in range(3)]
        rows.append(
            2.0 * math.pi * (mom[0] * xcoord / LX + mom[1] * ycoord / LY + mom[2] * zcoord / ndev)
        )
        hops.append(jnp.full((1, nvec), math.pi, f32))
        for axis, size in enumerate((LX, LY, ndev)):
            hops.append(jnp.full((1, nvec), mom[axis] * (2.0 * math.pi / size), f32))
    angle = jnp.concatenate(rows, 0)
    cos_ref[...] = jnp.concatenate([jnp.cos(angle)] * 3, 1)
    sin_ref[...] = jnp.concatenate([jnp.sin(angle)] * 3, 1)
    hop = jnp.concatenate(hops, 0)
    plain = lax.rem(lax.broadcasted_iota(jnp.int32, hop.shape, 0), NDISP) == 0
    ar_ref[...] = jnp.where(plain, -1.0, jnp.cos(hop))
    ai_ref[...] = jnp.where(plain, 0.0, -jnp.sin(hop))

    lane = lax.broadcasted_iota(jnp.int32, (CHUNK, plane), 1)
    edge = lax.rem(lane, LX) == LX - 1

    def displace(t, direction, source, begin=0, size=nvec):
        @pl.loop(0, size // CHUNK)
        def _(i):
            rows = pl.multiple_of(begin + i * CHUNK, CHUNK)
            vec = []
            for p in range(2):
                line = []
                for c in range(3):
                    v = source[t, p, c, pl.ds(rows, CHUNK), :].astype(f32)
                    if direction == 0:
                        v = jnp.where(
                            edge, pltpu.roll(v, LX - 1, 1), pltpu.roll(v, plane - 1, 1)
                        )
                    elif direction == 1:
                        v = pltpu.roll(v, plane - LX, 1)
                    line.append(v)
                vec.append(line)
            for row in range(3):
                real = imag = None
                for col in range(3):
                    mr = link_ref[t, direction, 0, row, col]
                    mi = link_ref[t, direction, 1, row, col]
                    re = mr * vec[0][col] - mi * vec[1][col]
                    im = mr * vec[1][col] + mi * vec[0][col]
                    real = re if real is None else real + re
                    imag = im if imag is None else imag + im
                lanes = slice(row * plane, (row + 1) * plane)
                fields[t * NDISP + direction + 1, pl.ds(rows, CHUNK), lanes] = real.astype(bf16)
                fields[
                    t * NDISP + direction + 1, pl.ds(nvec + rows, CHUNK), lanes
                ] = imag.astype(bf16)

    def phases(t):
        @pl.loop(0, nvec // CHUNK)
        def _(i):
            rows = pl.multiple_of(i * CHUNK, CHUNK)
            for c in range(3):
                lanes = slice(c * plane, (c + 1) * plane)
                vr = eig_ref[t, 0, c, pl.ds(rows, CHUNK), :]
                vi = eig_ref[t, 1, c, pl.ds(rows, CHUNK), :]
                fields[t * NDISP, pl.ds(rows, CHUNK), lanes] = vr
                fields[t * NDISP, pl.ds(nvec + rows, CHUNK), lanes] = vi
                vr, vi = vr.astype(f32), vi.astype(f32)
                for m in range(nmom):
                    cosine = cos_ref[m:m + 1, lanes]
                    sine = sin_ref[m:m + 1, lanes]
                    a, b = cosine * vr, sine * vi
                    g, h = cosine * vi, sine * vr
                    plus[t * nmom + m, pl.ds(rows, CHUNK), lanes] = (a - b).astype(bf16)
                    plus[t * nmom + m, pl.ds(nvec + rows, CHUNK), lanes] = (g + h).astype(bf16)
                    minus[t * nmom + m, pl.ds(rows, CHUNK), lanes] = (a + b).astype(bf16)
                    minus[t * nmom + m, pl.ds(nvec + rows, CHUNK), lanes] = (g - h).astype(bf16)

    @pl.loop(0, slices)
    def _(t):
        e_copy(t).wait()
        displace(t, 0, eig_ref)
        displace(t, 1, eig_ref)
        phases(t)

    count, spins = tau_ref.shape[:2]

    def mix():
        t_copy.wait()
        for i in range(local):
            q = lax.rem(list_ref[i, 2], count)
            g = list_ref[i, 1]

            @pl.loop(0, 2 * nvec // CHUNK)
            def _(n):
                rows = pl.multiple_of(n * CHUNK, CHUNK)
                tau = [tau_ref[q, s, pl.ds(rows, CHUNK), :].astype(f32) for s in range(spins)]
                for r in range(spins):
                    mixed = spin_ref[r, 0, g] * tau[0]
                    for s in range(1, spins):
                        mixed = mixed + spin_ref[r, s, g] * tau[s]
                    mix_ref[i, r, pl.ds(rows, CHUNK), :] = mixed.astype(bf16)
        m_copy.start()

    @pl.when(core > 0)
    def _():
        mix()

    @pl.loop(1, ndev)
    def _(k):
        l_copy(k).wait()

    to_smem = pltpu.make_async_copy(lists, table, l_local)
    to_smem.start()
    to_smem.wait()

    @pl.loop(0, slices)
    def _(t):
        for h in range(2):
            v_copy(t, h).wait_recv()
            displace(t, 2, above, h * half, half)

    def item(dest, i):
        slot = lax.rem(me + ndev - dest, ndev)
        entry = table[slot, 0, i]
        time = lax.div(entry, nmom * NDISP)
        m = lax.rem(lax.div(entry, NDISP), nmom)
        d = lax.rem(entry, NDISP)
        ar = ar_ref[pl.ds(m * NDISP + d, 1), :]
        ai = ai_ref[pl.ds(m * NDISP + d, 1), :]
        x = fields[time * NDISP + d]
        first = lax.dot_general(plus[time * nmom + m], x, NT, preferred_element_type=f32)
        second = lax.dot_general(x, minus[time * nmom + m], NT, preferred_element_type=f32)
        g1r = first[:nvec, :nvec] + first[nvec:, nvec:]
        g1i = first[:nvec, nvec:] - first[nvec:, :nvec]
        g2r = second[:nvec, :nvec] + second[nvec:, nvec:]
        g2i = second[:nvec, nvec:] - second[nvec:, :nvec]
        return (
            (g1r - (ar * g2r - ai * g2i)) * factor,
            (g1i - (ar * g2i + ai * g2r)) * factor,
        )

    levels = outer.bit_length() - 1

    def flip(l):
        size = 1 << l
        return zpos + size * (1 - 2 * lax.rem(zpos // size, 2))

    def away(r):
        row = zpos
        for l in range(levels):
            row = row + lax.rem(r // (1 << l), 2) * (flip(l) - zpos)
        return row

    def copy1(n, i):
        return pltpu.make_async_remote_copy(
            src_ref=part1.at[n, i], dst_ref=recv1.at[n, i], send_sem=s1.at[n, i], recv_sem=r1.at[n, i],
            device_id=(cfg, space, 1 - core), device_id_type=MESH,
        )

    def copy2(n, j, i):
        return pltpu.make_async_remote_copy(
            src_ref=part2.at[n, i], dst_ref=recv2.at[j, i], send_sem=s2.at[j, i], recv_sem=r2.at[j, i],
            device_id=(cfg, zpos * inner + (1 - ypos), core), device_id_type=MESH,
        )

    def copy3(r, i):
        row = flip(levels - 1)
        for l in range(levels - 2, -1, -1):
            row = jnp.where(lax.rem(r, 2 << l) == 1 << l, flip(l), row)
        return pltpu.make_async_remote_copy(
            src_ref=part3.at[r, i], dst_ref=recv3.at[r, i], send_sem=s3.at[r, i], recv_sem=r3.at[r, i],
            device_id=(cfg, row * inner + ypos, core), device_id_type=MESH,
        )

    def unit(n):
        across = jnp.logical_or(n < 3, jnp.logical_and(lax.rem(n, 2) == 0, n < nspace - 2))
        late = jnp.where(n < nspace - 2, (n - 3) // 2, n - outer)
        j = jnp.where(across, jnp.where(n < 3, n, n // 2 + 1), late)
        row = away(outer - 1 - j)
        return across, j, (row * inner + jnp.where(across, 1 - ypos, ypos)) * ndiag

    def give(n):
        _, _, chip = unit(n)
        for i in range(local):
            real, imag = item(chip + (1 - core), i)
            part1[n, i, 0] = real.astype(bf16)
            part1[n, i, 1] = imag.astype(bf16)
            copy1(n, i).start()

    def keep(n):
        _, _, chip = unit(n)
        for i in range(local):
            own[n, i, 0], own[n, i, 1] = item(chip + core, i)

    def join(n):
        across, j, _ = unit(n)
        for i in range(local):
            copy1(n, i).wait_recv()
            total = own[n, i] + recv1[n, i].astype(f32)
            own[n, i] = total
            part2[n, i] = total.astype(bf16)

            @pl.when(across)
            def _():
                copy2(n, j, i).start()

    def collect(q):
        j = q // local
        i = lax.rem(q, local)
        r = outer - 1 - j
        n = jnp.where(j < outer - 2, 2 * j + 3, j + outer)
        copy2(0, j, i).wait()
        own[n, i] = own[n, i] + recv2[j, i].astype(f32)
        for l in range(levels):
            @pl.when(lax.rem(r, 2 << l) == 0)
            def _():
                copy3(r + (1 << l), i).wait()
                own[n, i] = own[n, i] + recv3[r + (1 << l), i].astype(f32)

        @pl.when(r > 0)
        def _():
            part3[r, i] = own[n, i].astype(bf16)
            copy3(r, i).start()

    @pl.loop(0, 3 * nspace)
    def _(k):
        early = core == 0
        kind = jnp.where(
            early, jnp.where(k < nspace, 0, 1 + lax.rem(k - nspace + 2 * nspace, 2)), lax.rem(k + 1, 3)
        )
        n = jnp.where(early, jnp.where(k < nspace, k, (k - nspace + 2 * nspace) // 2 - nspace), k // 3)

        @pl.when(kind == 0)
        def _():
            give(n)

        @pl.when(kind == 1)
        def _():
            keep(n)

        @pl.when(kind == 2)
        def _():
            join(n)

            @pl.when(jnp.logical_and(early, n == nspace - 4))
            def _():
                mix()

            first = jnp.where(n == 3, 0, n - 3)
            stop = jnp.where(n == 3, 2, jnp.where(n > 4, n - 2, first))

            @pl.loop(first, stop)
            def _(q):
                collect(q)

    @pl.loop(nspace - 3, outer * local)
    def _(q):
        collect(q)

    out_ref[...] = own[nspace - 1].astype(bf16)

    @pl.loop(0, nspace)
    def _(n):
        for i in range(local):
            copy1(n, i).wait_send()

    for t in range(slices):
        for h in range(2):
            v_copy(t, h).wait_send()
    m_copy.wait()


def diagram_kernel(elem_ref, mix_ref, out_hbm, out_ref, store_sem):
    local, spins = mix_ref.shape[:2]
    group = 2 if spins % 2 == 0 else 1

    def store(i, h):
        some = pl.ds(h * group, group)
        return pltpu.make_async_copy(out_ref.at[i, some], out_hbm.at[i, some], store_sem.at[i, h])

    pieces = [(i, h) for i in range(local) for h in range(spins // group)]
    for i, h in pieces:
        if h == 0:
            er, ei = elem_ref[i, 0], elem_ref[i, 1]
            square = jnp.concatenate(
                [jnp.concatenate([er, -ei], 1), jnp.concatenate([ei, er], 1)], 0
            )
        for r in range(h * group, (h + 1) * group):
            out_ref[i, r] = jnp.dot(
                square, mix_ref[i, r], preferred_element_type=f32
            ).astype(bf16)
        store(i, h).start()
    for i, h in pieces:
        store(i, h).wait()


def body(eigvecs, gauge_links, momenta, spin_mix, perambulators, contraction_list):
    slices, _, colors, nvec, depth, plane = eigvecs.shape
    assert depth == 1 and colors == 3
    nspace, ndiag = lax.axis_size("space"), lax.axis_size("diag")
    inner = 2
    outer = nspace // inner
    assert ndiag == 2 and inner * outer == nspace
    assert outer >= 4 and outer & (outer - 1) == 0 and contraction_list.shape[0] >= 2
    ndev = nspace * ndiag
    scale = 1.0 / math.sqrt(3 * plane * ndev)
    nmom = momenta.shape[0]
    local = contraction_list.shape[0]
    count, spins = perambulators.shape[:2]
    width = perambulators.shape[4]
    vmem = pl.BlockSpec(memory_space=pltpu.VMEM)
    smem = pl.BlockSpec(memory_space=pltpu.SMEM)
    hbm = pl.BlockSpec(memory_space=pltpu.HBM)
    tile = (local, 2, nvec, nvec)
    field = (2 * nvec, 3 * plane)
    dma = pltpu.SemaphoreType.DMA
    elem, mixed = pl.pallas_call(
        functools.partial(
            elemental_kernel,
            (nspace, ndiag, inner, local, slices, nvec, plane, 0.5 * scale),
        ),
        out_shape=(
            jax.ShapeDtypeStruct(tile, bf16),
            jax.ShapeDtypeStruct((local, spins, 2 * nvec, width), bf16),
        ),
        in_specs=[smem, smem, smem, vmem, hbm, hbm],
        out_specs=(vmem, pl.BlockSpec(memory_space=pl.ANY)),
        scratch_shapes=[
            pltpu.VMEM((slices, 2, 3, nvec, plane), bf16),
            pltpu.VMEM((nmom, 3 * plane), f32),
            pltpu.VMEM((nmom, 3 * plane), f32),
            pltpu.VMEM((nmom * NDISP, nvec), f32),
            pltpu.VMEM((nmom * NDISP, nvec), f32),
            pltpu.VMEM((slices, 2, 3, nvec, plane), bf16),
            pltpu.VMEM((slices * NDISP,) + field, bf16),
            pltpu.VMEM((slices * nmom,) + field, bf16),
            pltpu.VMEM((slices * nmom,) + field, bf16),
            pltpu.VMEM((count, spins, 2 * nvec, width), bf16),
            pltpu.VMEM((local, spins, 2 * nvec, width), bf16),
            pltpu.VMEM((ndev, 1, 128), jnp.int32),
            pltpu.SMEM((ndev, 1, 128), jnp.int32),
            pltpu.VMEM((nspace,) + tile, bf16),
            pltpu.VMEM((nspace,) + tile, bf16),
            pltpu.VMEM((nspace,) + tile, f32),
            pltpu.VMEM((nspace,) + tile, bf16),
            pltpu.VMEM((outer,) + tile, bf16),
            pltpu.VMEM((outer,) + tile, bf16),
            pltpu.VMEM((outer,) + tile, bf16),
            dma((slices,)), dma, dma, dma((slices, 2)), dma((slices, 2)),
            dma((ndev,)), dma((ndev,)), dma,
            dma((nspace, local)), dma((nspace, local)),
            dma((outer, local)), dma((outer, local)),
            dma((outer, local)), dma((outer, local)),
        ],
        compiler_params=pltpu.CompilerParams(
            collective_id=0, has_side_effects=True, vmem_limit_bytes=44 * 1024 * 1024
        ),
    )(*(
        pltpu.with_memory_space_constraint(x, pltpu.HBM) for x in (
            contraction_list, momenta, spin_mix.transpose(1, 2, 0), gauge_links,
            eigvecs.reshape(slices, 2, 3, nvec, plane),
            perambulators.reshape(count, spins, 2 * nvec, width),
        )
    ))
    out = pl.pallas_call(
        diagram_kernel,
        in_specs=[vmem, vmem],
        out_specs=hbm,
        out_shape=jax.ShapeDtypeStruct((local, spins, 2 * nvec, width), bf16),
        scratch_shapes=[
            pltpu.VMEM((local, spins, 2 * nvec, width), bf16), dma((local, spins)),
        ],
        compiler_params=pltpu.CompilerParams(vmem_limit_bytes=24 * 1024 * 1024),
    )(elem, mixed)
    return out.reshape(local, spins, 2, nvec, width)


def solution(mesh):
    placed = (
        P("cfg", None, None, None, ("space", "diag"), None),
        P("cfg", None, None, None, None, ("space", "diag"), None),
        P(),
        P(),
        P(("cfg", "space", "diag"), None, None, None, None),
        P(("space", "diag"), None),
    )
    return jax.shard_map(
        body,
        mesh=mesh,
        in_specs=placed,
        out_specs=P(("cfg", "space", "diag"), None, None, None, None),
        check_vma=False,
    )
```

```python
import functools
import math

import jax
import jax.numpy as jnp
from jax import lax
from jax.experimental import pallas as pl
from jax.experimental.pallas import tpu as pltpu
from jax.sharding import PartitionSpec as P

LX = 16
LY = 16
NDISP = 4
CHUNK = 16
MESH = pl.DeviceIdType.MESH
NT = (((1,), (1,)), ((), ()))
f32 = jnp.float32
bf16 = jnp.bfloat16


def elemental_kernel(
    dims, list_ref, mom_ref, spin_ref, link_ref, eig_hbm, tau_hbm, out_ref, mix_hbm,
    eig_ref, cos_ref, sin_ref, ar_ref, ai_ref, above, fields, plus, minus, tau_ref, mix_ref, lists, table,
    part1, recv1, own, part2, recv2, part3, recv3,
    e_local, t_local, m_local, v_send, v_recv, l_send, l_recv, l_local, s1, r1, s2, r2, s3, r3,
):
    nspace, ndiag, inner, local, slices, nvec, plane, factor = dims
    ndev = nspace * ndiag
    outer = nspace // inner
    space = lax.axis_index("space")
    core = lax.axis_index("diag")
    cfg = lax.axis_index("cfg")
    me = space * ndiag + core
    zpos = space // inner
    ypos = lax.rem(space, inner)

    def device(index):
        return (cfg, index // ndiag, lax.rem(index, ndiag))

    def e_copy(t):
        return pltpu.make_async_copy(eig_hbm.at[t], eig_ref.at[t], e_local.at[t])

    t_copy = pltpu.make_async_copy(tau_hbm, tau_ref, t_local)
    m_copy = pltpu.make_async_copy(mix_ref, mix_hbm, m_local)

    barrier = pltpu.get_barrier_semaphore()

    @pl.loop(1, ndev)
    def _(k):
        pl.semaphore_signal(
            barrier, inc=1, device_id=device(lax.rem(me + k, ndev)), device_id_type=MESH
        )

    for t in range(slices):
        e_copy(t).start()
    t_copy.start()

    column = lax.broadcasted_iota(jnp.int32, (1, 128), 1)
    packed = jnp.zeros((1, 128), jnp.int32)
    for i in range(local):
        packed = jnp.where(column == i, list_ref[i, 0], packed)
    lists[0] = packed

    pl.semaphore_wait(barrier, ndev - 1)

    half = nvec // 2

    def v_copy(t, h):
        rows = pl.ds(pl.multiple_of(h * half, half), half)
        return pltpu.make_async_remote_copy(
            src_ref=eig_hbm.at[t, :, :, rows], dst_ref=above.at[t, :, :, rows],
            send_sem=v_send.at[t, h], recv_sem=v_recv.at[t, h],
            device_id=device(lax.rem(me + ndev - 1, ndev)), device_id_type=MESH,
        )

    def l_copy(k):
        return pltpu.make_async_remote_copy(
            src_ref=lists.at[0], dst_ref=lists.at[k],
            send_sem=l_send.at[k], recv_sem=l_recv.at[k],
            device_id=device(lax.rem(me + k, ndev)), device_id_type=MESH,
        )

    for h in range(2):
        v_copy(0, h).start()

    @pl.loop(1, ndev)
    def _(k):
        l_copy(k).start()

    for t in range(1, slices):
        for h in range(2):
            v_copy(t, h).start()

    nmom = mom_ref.shape[0]
    flat = lax.broadcasted_iota(jnp.int32, (1, plane), 1)
    xcoord = lax.rem(flat, LX).astype(f32)
    ycoord = lax.div(flat, LX).astype(f32)
    zcoord = lax.convert_element_type(me, f32)
    rows, hops = [], []
    for m in range(nmom):
        mom = [mom_ref[m, axis].astype(f32) for axis in range(3)]
        rows.append(
            2.0 * math.pi * (mom[0] * xcoord / LX + mom[1] * ycoord / LY + mom[2] * zcoord / ndev)
        )
        hops.append(jnp.full((1, nvec), math.pi, f32))
        for axis, size in enumerate((LX, LY, ndev)):
            hops.append(jnp.full((1, nvec), mom[axis] * (2.0 * math.pi / size), f32))
    angle = jnp.concatenate(rows, 0)
    cos_ref[...] = jnp.concatenate([jnp.cos(angle)] * 3, 1)
    sin_ref[...] = jnp.concatenate([jnp.sin(angle)] * 3, 1)
    hop = jnp.concatenate(hops, 0)
    plain = lax.rem(lax.broadcasted_iota(jnp.int32, hop.shape, 0), NDISP) == 0
    ar_ref[...] = jnp.where(plain, -1.0, jnp.cos(hop))
    ai_ref[...] = jnp.where(plain, 0.0, -jnp.sin(hop))

    lane = lax.broadcasted_iota(jnp.int32, (CHUNK, plane), 1)
    edge = lax.rem(lane, LX) == LX - 1

    def displace(t, direction, source, begin=0, size=nvec):
        @pl.loop(0, size // CHUNK)
        def _(i):
            rows = pl.multiple_of(begin + i * CHUNK, CHUNK)
            vec = []
            for p in range(2):
                line = []
                for c in range(3):
                    v = source[t, p, c, pl.ds(rows, CHUNK), :].astype(f32)
                    if direction == 0:
                        v = jnp.where(
                            edge, pltpu.roll(v, LX - 1, 1), pltpu.roll(v, plane - 1, 1)
                        )
                    elif direction == 1:
                        v = pltpu.roll(v, plane - LX, 1)
                    line.append(v)
                vec.append(line)
            for row in range(3):
                real = imag = None
                for col in range(3):
                    mr = link_ref[t, direction, 0, row, col]
                    mi = link_ref[t, direction, 1, row, col]
                    re = mr * vec[0][col] - mi * vec[1][col]
                    im = mr * vec[1][col] + mi * vec[0][col]
                    real = re if real is None else real + re
                    imag = im if imag is None else imag + im
                lanes = slice(row * plane, (row + 1) * plane)
                fields[t * NDISP + direction + 1, pl.ds(rows, CHUNK), lanes] = real.astype(bf16)
                fields[
                    t * NDISP + direction + 1, pl.ds(nvec + rows, CHUNK), lanes
                ] = imag.astype(bf16)

    def phases(t):
        @pl.loop(0, nvec // CHUNK)
        def _(i):
            rows = pl.multiple_of(i * CHUNK, CHUNK)
            for c in range(3):
                lanes = slice(c * plane, (c + 1) * plane)
                vr = eig_ref[t, 0, c, pl.ds(rows, CHUNK), :]
                vi = eig_ref[t, 1, c, pl.ds(rows, CHUNK), :]
                fields[t * NDISP, pl.ds(rows, CHUNK), lanes] = vr
                fields[t * NDISP, pl.ds(nvec + rows, CHUNK), lanes] = vi
                vr, vi = vr.astype(f32), vi.astype(f32)
                for m in range(nmom):
                    cosine = cos_ref[m:m + 1, lanes]
                    sine = sin_ref[m:m + 1, lanes]
                    a, b = cosine * vr, sine * vi
                    g, h = cosine * vi, sine * vr
                    plus[t * nmom + m, pl.ds(rows, CHUNK), lanes] = (a - b).astype(bf16)
                    plus[t * nmom + m, pl.ds(nvec + rows, CHUNK), lanes] = (g + h).astype(bf16)
                    minus[t * nmom + m, pl.ds(rows, CHUNK), lanes] = (a + b).astype(bf16)
                    minus[t * nmom + m, pl.ds(nvec + rows, CHUNK), lanes] = (g - h).astype(bf16)

    @pl.loop(0, slices)
    def _(t):
        e_copy(t).wait()
        displace(t, 0, eig_ref)
        displace(t, 1, eig_ref)
        phases(t)

    count, spins = tau_ref.shape[:2]

    def mix():
        t_copy.wait()
        for i in range(local):
            q = lax.rem(list_ref[i, 2], count)
            g = list_ref[i, 1]

            @pl.loop(0, 2 * nvec // CHUNK)
            def _(n):
                rows = pl.multiple_of(n * CHUNK, CHUNK)
                tau = [tau_ref[q, s, pl.ds(rows, CHUNK), :].astype(f32) for s in range(spins)]
                for r in range(spins):
                    mixed = spin_ref[r, 0, g] * tau[0]
                    for s in range(1, spins):
                        mixed = mixed + spin_ref[r, s, g] * tau[s]
                    mix_ref[i, r, pl.ds(rows, CHUNK), :] = mixed.astype(bf16)
        m_copy.start()

    @pl.when(core > 0)
    def _():
        mix()

    @pl.loop(1, ndev)
    def _(k):
        l_copy(k).wait()

    to_smem = pltpu.make_async_copy(lists, table, l_local)
    to_smem.start()
    to_smem.wait()

    @pl.loop(0, slices)
    def _(t):
        for h in range(2):
            v_copy(t, h).wait_recv()
            displace(t, 2, above, h * half, half)

    def item(dest, i):
        slot = lax.rem(me + ndev - dest, ndev)
        entry = table[slot, 0, i]
        time = lax.div(entry, nmom * NDISP)
        m = lax.rem(lax.div(entry, NDISP), nmom)
        d = lax.rem(entry, NDISP)
        ar = ar_ref[pl.ds(m * NDISP + d, 1), :]
        ai = ai_ref[pl.ds(m * NDISP + d, 1), :]
        x = fields[time * NDISP + d]
        first = lax.dot_general(plus[time * nmom + m], x, NT, preferred_element_type=f32)
        second = lax.dot_general(x, minus[time * nmom + m], NT, preferred_element_type=f32)
        g1r = first[:nvec, :nvec] + first[nvec:, nvec:]
        g1i = first[:nvec, nvec:] - first[nvec:, :nvec]
        g2r = second[:nvec, :nvec] + second[nvec:, nvec:]
        g2i = second[:nvec, nvec:] - second[nvec:, :nvec]
        return (
            (g1r - (ar * g2r - ai * g2i)) * factor,
            (g1i - (ar * g2i + ai * g2r)) * factor,
        )

    levels = outer.bit_length() - 1

    def flip(l):
        size = 1 << l
        return zpos + size * (1 - 2 * lax.rem(zpos // size, 2))

    def away(r):
        row = zpos
        for l in range(levels):
            row = row + lax.rem(r // (1 << l), 2) * (flip(l) - zpos)
        return row

    def copy1(n, i):
        return pltpu.make_async_remote_copy(
            src_ref=part1.at[n, i], dst_ref=recv1.at[n, i], send_sem=s1.at[n, i], recv_sem=r1.at[n, i],
            device_id=(cfg, space, 1 - core), device_id_type=MESH,
        )

    def copy2(n, j, i):
        return pltpu.make_async_remote_copy(
            src_ref=part2.at[n, i], dst_ref=recv2.at[j, i], send_sem=s2.at[j, i], recv_sem=r2.at[j, i],
            device_id=(cfg, zpos * inner + (1 - ypos), core), device_id_type=MESH,
        )

    def copy3(r, i):
        row = flip(levels - 1)
        for l in range(levels - 2, -1, -1):
            row = jnp.where(lax.rem(r, 2 << l) == 1 << l, flip(l), row)
        return pltpu.make_async_remote_copy(
            src_ref=part3.at[r, i], dst_ref=recv3.at[r, i], send_sem=s3.at[r, i], recv_sem=r3.at[r, i],
            device_id=(cfg, row * inner + ypos, core), device_id_type=MESH,
        )

    def unit(n):
        last = n == nspace - 1
        across = jnp.logical_or(n == 0, jnp.logical_and(lax.rem(n, 2) == 1, n < nspace - 1))
        j = jnp.where(across, (n + 1) // 2, jnp.where(last, outer - 1, n // 2 - 1))
        row = away(outer - 1 - j)
        return across, j, (row * inner + jnp.where(across, 1 - ypos, ypos)) * ndiag

    def give(n):
        _, _, chip = unit(n)
        for i in range(local):
            real, imag = item(chip + (1 - core), i)
            part1[n, i, 0] = real.astype(bf16)
            part1[n, i, 1] = imag.astype(bf16)
            copy1(n, i).start()

    def keep(n):
        _, _, chip = unit(n)
        for i in range(local):
            own[n, i, 0], own[n, i, 1] = item(chip + core, i)

    def join(n):
        across, j, _ = unit(n)
        for i in range(local):
            copy1(n, i).wait_recv()
            total = own[n, i] + recv1[n, i].astype(f32)
            own[n, i] = total
            part2[n, i] = total.astype(bf16)

            @pl.when(across)
            def _():
                copy2(n, j, i).start()

    def collect(q):
        j = q // local
        i = lax.rem(q, local)
        r = outer - 1 - j
        n = jnp.where(j == outer - 1, nspace - 1, 2 * j + 2)
        copy2(0, j, i).wait()
        own[n, i] = own[n, i] + recv2[j, i].astype(f32)
        for l in range(levels):
            @pl.when(lax.rem(r, 2 << l) == 0)
            def _():
                copy3(r + (1 << l), i).wait()
                own[n, i] = own[n, i] + recv3[r + (1 << l), i].astype(f32)

        @pl.when(r > 0)
        def _():
            part3[r, i] = own[n, i].astype(bf16)
            copy3(r, i).start()

    @pl.loop(0, 3 * nspace)
    def _(k):
        early = core == 0
        kind = jnp.where(
            early, jnp.where(k < nspace, 0, 1 + lax.rem(k - nspace + 2 * nspace, 2)), lax.rem(k, 3)
        )
        n = jnp.where(early, jnp.where(k < nspace, k, (k - nspace + 2 * nspace) // 2 - nspace), k // 3)

        @pl.when(kind == 0)
        def _():
            give(n)

        @pl.when(kind == 1)
        def _():
            keep(n)

        @pl.when(kind == 2)
        def _():
            join(n)

            first = jnp.where(n == 5, 2, n - 2)
            stop = jnp.where(jnp.logical_or(n < 2, n == 4), first, n - 1)

            @pl.loop(first, stop)
            def _(q):
                collect(q)

    @pl.loop(nspace - 2, (outer - 1) * local)
    def _(q):
        collect(q)

    @pl.when(core == 0)
    def _():
        mix()

    @pl.loop((outer - 1) * local, outer * local)
    def _(q):
        collect(q)

    out_ref[...] = own[nspace - 1].astype(bf16)

    @pl.loop(0, nspace)
    def _(n):
        for i in range(local):
            copy1(n, i).wait_send()

    for t in range(slices):
        for h in range(2):
            v_copy(t, h).wait_send()
    m_copy.wait()


def diagram_kernel(elem_ref, mix_ref, out_hbm, out_ref, store_sem):
    local, spins = mix_ref.shape[:2]
    group = 2 if spins % 2 == 0 else 1

    def store(i, h):
        some = pl.ds(h * group, group)
        return pltpu.make_async_copy(out_ref.at[i, some], out_hbm.at[i, some], store_sem.at[i, h])

    pieces = [(i, h) for i in range(local) for h in range(spins // group)]
    for i, h in pieces:
        if h == 0:
            er, ei = elem_ref[i, 0], elem_ref[i, 1]
            square = jnp.concatenate(
                [jnp.concatenate([er, -ei], 1), jnp.concatenate([ei, er], 1)], 0
            )
        for r in range(h * group, (h + 1) * group):
            out_ref[i, r] = jnp.dot(
                square, mix_ref[i, r], preferred_element_type=f32
            ).astype(bf16)
        store(i, h).start()
    for i, h in pieces:
        store(i, h).wait()


def body(eigvecs, gauge_links, momenta, spin_mix, perambulators, contraction_list):
    slices, _, colors, nvec, depth, plane = eigvecs.shape
    assert depth == 1 and colors == 3
    nspace, ndiag = lax.axis_size("space"), lax.axis_size("diag")
    inner = 2
    outer = nspace // inner
    assert ndiag == 2 and inner * outer == nspace
    assert outer >= 4 and outer & (outer - 1) == 0 and contraction_list.shape[0] == 2
    ndev = nspace * ndiag
    scale = 1.0 / math.sqrt(3 * plane * ndev)
    nmom = momenta.shape[0]
    local = contraction_list.shape[0]
    count, spins = perambulators.shape[:2]
    width = perambulators.shape[4]
    vmem = pl.BlockSpec(memory_space=pltpu.VMEM)
    smem = pl.BlockSpec(memory_space=pltpu.SMEM)
    hbm = pl.BlockSpec(memory_space=pltpu.HBM)
    tile = (local, 2, nvec, nvec)
    field = (2 * nvec, 3 * plane)
    dma = pltpu.SemaphoreType.DMA
    elem, mixed = pl.pallas_call(
        functools.partial(
            elemental_kernel,
            (nspace, ndiag, inner, local, slices, nvec, plane, 0.5 * scale),
        ),
        out_shape=(
            jax.ShapeDtypeStruct(tile, bf16),
            jax.ShapeDtypeStruct((local, spins, 2 * nvec, width), bf16),
        ),
        in_specs=[smem, smem, smem, vmem, hbm, hbm],
        out_specs=(vmem, pl.BlockSpec(memory_space=pl.ANY)),
        scratch_shapes=[
            pltpu.VMEM((slices, 2, 3, nvec, plane), bf16),
            pltpu.VMEM((nmom, 3 * plane), f32),
            pltpu.VMEM((nmom, 3 * plane), f32),
            pltpu.VMEM((nmom * NDISP, nvec), f32),
            pltpu.VMEM((nmom * NDISP, nvec), f32),
            pltpu.VMEM((slices, 2, 3, nvec, plane), bf16),
            pltpu.VMEM((slices * NDISP,) + field, bf16),
            pltpu.VMEM((slices * nmom,) + field, bf16),
            pltpu.VMEM((slices * nmom,) + field, bf16),
            pltpu.VMEM((count, spins, 2 * nvec, width), bf16),
            pltpu.VMEM((local, spins, 2 * nvec, width), bf16),
            pltpu.VMEM((ndev, 1, 128), jnp.int32),
            pltpu.SMEM((ndev, 1, 128), jnp.int32),
            pltpu.VMEM((nspace,) + tile, bf16),
            pltpu.VMEM((nspace,) + tile, bf16),
            pltpu.VMEM((nspace,) + tile, f32),
            pltpu.VMEM((nspace,) + tile, bf16),
            pltpu.VMEM((outer,) + tile, bf16),
            pltpu.VMEM((outer,) + tile, bf16),
            pltpu.VMEM((outer,) + tile, bf16),
            dma((slices,)), dma, dma, dma((slices, 2)), dma((slices, 2)),
            dma((ndev,)), dma((ndev,)), dma,
            dma((nspace, local)), dma((nspace, local)),
            dma((outer, local)), dma((outer, local)),
            dma((outer, local)), dma((outer, local)),
        ],
        compiler_params=pltpu.CompilerParams(
            collective_id=0, has_side_effects=True, vmem_limit_bytes=44 * 1024 * 1024
        ),
    )(*(
        pltpu.with_memory_space_constraint(x, pltpu.HBM) for x in (
            contraction_list, momenta, spin_mix.transpose(1, 2, 0), gauge_links,
            eigvecs.reshape(slices, 2, 3, nvec, plane),
            perambulators.reshape(count, spins, 2 * nvec, width),
        )
    ))
    out = pl.pallas_call(
        diagram_kernel,
        in_specs=[vmem, vmem],
        out_specs=hbm,
        out_shape=jax.ShapeDtypeStruct((local, spins, 2 * nvec, width), bf16),
        scratch_shapes=[
            pltpu.VMEM((local, spins, 2 * nvec, width), bf16), dma((local, spins)),
        ],
        compiler_params=pltpu.CompilerParams(vmem_limit_bytes=24 * 1024 * 1024),
    )(elem, mixed)
    return out.reshape(local, spins, 2, nvec, width)


def solution(mesh):
    placed = (
        P("cfg", None, None, None, ("space", "diag"), None),
        P("cfg", None, None, None, None, ("space", "diag"), None),
        P(),
        P(),
        P(("cfg", "space", "diag"), None, None, None, None),
        P(("space", "diag"), None),
    )
    return jax.shard_map(
        body,
        mesh=mesh,
        in_specs=placed,
        out_specs=P(("cfg", "space", "diag"), None, None, None, None),
        check_vma=False,
    )
```

```python
import functools
import math

import jax
import jax.numpy as jnp
from jax import lax
from jax.experimental import pallas as pl
from jax.experimental.pallas import tpu as pltpu
from jax.sharding import PartitionSpec as P

LX = 16
LY = 16
NDISP = 4
CHUNK = 16
MESH = pl.DeviceIdType.MESH
NT = (((1,), (1,)), ((), ()))
f32 = jnp.float32
bf16 = jnp.bfloat16


def elemental_kernel(
    dims, list_ref, mom_ref, spin_ref, link_ref, eig_hbm, tau_hbm, out_ref, mix_hbm,
    eig_ref, cos_ref, sin_ref, ar_ref, ai_ref, above, fields, plus, minus, tau_ref, mix_ref, lists, table,
    part1, recv1, own, early, part2, recv2, part3, recv3,
    e_local, t_local, m_local, v_send, v_recv, l_send, l_recv, l_local, s1, r1, s2, r2, s3, r3,
):
    nspace, ndiag, inner, local, slices, nvec, plane, factor = dims
    ndev = nspace * ndiag
    outer = nspace // inner
    space = lax.axis_index("space")
    core = lax.axis_index("diag")
    cfg = lax.axis_index("cfg")
    me = space * ndiag + core
    zpos = space // inner
    ypos = lax.rem(space, inner)

    def device(index):
        return (cfg, index // ndiag, lax.rem(index, ndiag))

    def e_copy(t):
        return pltpu.make_async_copy(eig_hbm.at[t], eig_ref.at[t], e_local.at[t])

    t_copy = pltpu.make_async_copy(tau_hbm, tau_ref, t_local)
    m_copy = pltpu.make_async_copy(mix_ref, mix_hbm, m_local)

    barrier = pltpu.get_barrier_semaphore()

    @pl.loop(1, ndev)
    def _(k):
        pl.semaphore_signal(
            barrier, inc=1, device_id=device(lax.rem(me + k, ndev)), device_id_type=MESH
        )

    for t in range(slices):
        e_copy(t).start()
    t_copy.start()

    column = lax.broadcasted_iota(jnp.int32, (1, 128), 1)
    packed = jnp.zeros((1, 128), jnp.int32)
    for i in range(local):
        packed = jnp.where(column == i, list_ref[i, 0], packed)
    lists[0] = packed

    pl.semaphore_wait(barrier, ndev - 1)

    half = nvec // 2

    def v_copy(t, h):
        rows = pl.ds(pl.multiple_of(h * half, half), half)
        return pltpu.make_async_remote_copy(
            src_ref=eig_hbm.at[t, :, :, rows], dst_ref=above.at[t, :, :, rows],
            send_sem=v_send.at[t, h], recv_sem=v_recv.at[t, h],
            device_id=device(lax.rem(me + ndev - 1, ndev)), device_id_type=MESH,
        )

    def l_copy(k):
        return pltpu.make_async_remote_copy(
            src_ref=lists.at[0], dst_ref=lists.at[k],
            send_sem=l_send.at[k], recv_sem=l_recv.at[k],
            device_id=device(lax.rem(me + k, ndev)), device_id_type=MESH,
        )

    for h in range(2):
        v_copy(0, h).start()

    @pl.loop(1, ndev)
    def _(k):
        l_copy(k).start()

    for t in range(1, slices):
        for h in range(2):
            v_copy(t, h).start()

    nmom = mom_ref.shape[0]
    flat = lax.broadcasted_iota(jnp.int32, (1, plane), 1)
    xcoord = lax.rem(flat, LX).astype(f32)
    ycoord = lax.div(flat, LX).astype(f32)
    zcoord = lax.convert_element_type(me, f32)
    rows, hops = [], []
    for m in range(nmom):
        mom = [mom_ref[m, axis].astype(f32) for axis in range(3)]
        rows.append(
            2.0 * math.pi * (mom[0] * xcoord / LX + mom[1] * ycoord / LY + mom[2] * zcoord / ndev)
        )
        hops.append(jnp.full((1, nvec), math.pi, f32))
        for axis, size in enumerate((LX, LY, ndev)):
            hops.append(jnp.full((1, nvec), mom[axis] * (2.0 * math.pi / size), f32))
    angle = jnp.concatenate(rows, 0)
    cos_ref[...] = jnp.concatenate([jnp.cos(angle)] * 3, 1)
    sin_ref[...] = jnp.concatenate([jnp.sin(angle)] * 3, 1)
    hop = jnp.concatenate(hops, 0)
    plain = lax.rem(lax.broadcasted_iota(jnp.int32, hop.shape, 0), NDISP) == 0
    ar_ref[...] = jnp.where(plain, -1.0, jnp.cos(hop))
    ai_ref[...] = jnp.where(plain, 0.0, -jnp.sin(hop))

    lane = lax.broadcasted_iota(jnp.int32, (CHUNK, plane), 1)
    edge = lax.rem(lane, LX) == LX - 1

    def displace(t, direction, source, begin=0, size=nvec):
        @pl.loop(0, size // CHUNK)
        def _(i):
            rows = pl.multiple_of(begin + i * CHUNK, CHUNK)
            vec = []
            for p in range(2):
                line = []
                for c in range(3):
                    v = source[t, p, c, pl.ds(rows, CHUNK), :].astype(f32)
                    if direction == 0:
                        v = jnp.where(
                            edge, pltpu.roll(v, LX - 1, 1), pltpu.roll(v, plane - 1, 1)
                        )
                    elif direction == 1:
                        v = pltpu.roll(v, plane - LX, 1)
                    line.append(v)
                vec.append(line)
            for row in range(3):
                real = imag = None
                for col in range(3):
                    mr = link_ref[t, direction, 0, row, col]
                    mi = link_ref[t, direction, 1, row, col]
                    re = mr * vec[0][col] - mi * vec[1][col]
                    im = mr * vec[1][col] + mi * vec[0][col]
                    real = re if real is None else real + re
                    imag = im if imag is None else imag + im
                lanes = slice(row * plane, (row + 1) * plane)
                fields[t * NDISP + direction + 1, pl.ds(rows, CHUNK), lanes] = real.astype(bf16)
                fields[
                    t * NDISP + direction + 1, pl.ds(nvec + rows, CHUNK), lanes
                ] = imag.astype(bf16)

    def phases(t):
        @pl.loop(0, nvec // CHUNK)
        def _(i):
            rows = pl.multiple_of(i * CHUNK, CHUNK)
            for c in range(3):
                lanes = slice(c * plane, (c + 1) * plane)
                vr = eig_ref[t, 0, c, pl.ds(rows, CHUNK), :]
                vi = eig_ref[t, 1, c, pl.ds(rows, CHUNK), :]
                fields[t * NDISP, pl.ds(rows, CHUNK), lanes] = vr
                fields[t * NDISP, pl.ds(nvec + rows, CHUNK), lanes] = vi
                vr, vi = vr.astype(f32), vi.astype(f32)
                for m in range(nmom):
                    cosine = cos_ref[m:m + 1, lanes]
                    sine = sin_ref[m:m + 1, lanes]
                    a, b = cosine * vr, sine * vi
                    g, h = cosine * vi, sine * vr
                    plus[t * nmom + m, pl.ds(rows, CHUNK), lanes] = (a - b).astype(bf16)
                    plus[t * nmom + m, pl.ds(nvec + rows, CHUNK), lanes] = (g + h).astype(bf16)
                    minus[t * nmom + m, pl.ds(rows, CHUNK), lanes] = (a + b).astype(bf16)
                    minus[t * nmom + m, pl.ds(nvec + rows, CHUNK), lanes] = (g - h).astype(bf16)

    @pl.loop(0, slices)
    def _(t):
        e_copy(t).wait()
        displace(t, 0, eig_ref)
        displace(t, 1, eig_ref)
        phases(t)

    count, spins = tau_ref.shape[:2]

    def mix():
        t_copy.wait()
        for i in range(local):
            q = lax.rem(list_ref[i, 2], count)
            g = list_ref[i, 1]

            @pl.loop(0, 2 * nvec // CHUNK)
            def _(n):
                rows = pl.multiple_of(n * CHUNK, CHUNK)
                tau = [tau_ref[q, s, pl.ds(rows, CHUNK), :].astype(f32) for s in range(spins)]
                for r in range(spins):
                    mixed = spin_ref[r, 0, g] * tau[0]
                    for s in range(1, spins):
                        mixed = mixed + spin_ref[r, s, g] * tau[s]
                    mix_ref[i, r, pl.ds(rows, CHUNK), :] = mixed.astype(bf16)
        m_copy.start()

    @pl.loop(1, ndev)
    def _(k):
        l_copy(k).wait()

    to_smem = pltpu.make_async_copy(lists, table, l_local)
    to_smem.start()
    to_smem.wait()

    def entry_of(dest, i):
        return table[lax.rem(me + ndev - dest, ndev), 0, i]

    def item(entry):
        time = lax.div(entry, nmom * NDISP)
        m = lax.rem(lax.div(entry, NDISP), nmom)
        d = lax.rem(entry, NDISP)
        ar = ar_ref[pl.ds(m * NDISP + d, 1), :]
        ai = ai_ref[pl.ds(m * NDISP + d, 1), :]
        x = fields[time * NDISP + d]
        first = lax.dot_general(plus[time * nmom + m], x, NT, preferred_element_type=f32)
        second = lax.dot_general(x, minus[time * nmom + m], NT, preferred_element_type=f32)
        g1r = first[:nvec, :nvec] + first[nvec:, nvec:]
        g1i = first[:nvec, nvec:] - first[nvec:, :nvec]
        g2r = second[:nvec, :nvec] + second[nvec:, nvec:]
        g2i = second[:nvec, nvec:] - second[nvec:, :nvec]
        return (
            (g1r - (ar * g2r - ai * g2i)) * factor,
            (g1i - (ar * g2i + ai * g2r)) * factor,
        )

    levels = outer.bit_length() - 1

    def flip(l):
        size = 1 << l
        return zpos + size * (1 - 2 * lax.rem(zpos // size, 2))

    def away(r):
        row = zpos
        for l in range(levels):
            row = row + lax.rem(r // (1 << l), 2) * (flip(l) - zpos)
        return row

    def copy1(n, i):
        return pltpu.make_async_remote_copy(
            src_ref=part1.at[n, i], dst_ref=recv1.at[n, i], send_sem=s1.at[n, i], recv_sem=r1.at[n, i],
            device_id=(cfg, space, 1 - core), device_id_type=MESH,
        )

    def copy2(n, j, i):
        return pltpu.make_async_remote_copy(
            src_ref=part2.at[n, i], dst_ref=recv2.at[j, i], send_sem=s2.at[j, i], recv_sem=r2.at[j, i],
            device_id=(cfg, zpos * inner + (1 - ypos), core), device_id_type=MESH,
        )

    def copy3(r, i):
        row = flip(levels - 1)
        for l in range(levels - 2, -1, -1):
            row = jnp.where(lax.rem(r, 2 << l) == 1 << l, flip(l), row)
        return pltpu.make_async_remote_copy(
            src_ref=part3.at[r, i], dst_ref=recv3.at[r, i], send_sem=s3.at[r, i], recv_sem=r3.at[r, i],
            device_id=(cfg, row * inner + ypos, core), device_id_type=MESH,
        )

    def unit(n):
        last = n == nspace - 1
        across = jnp.logical_or(n == 0, jnp.logical_and(lax.rem(n, 2) == 1, n < nspace - 1))
        j = jnp.where(across, (n + 1) // 2, jnp.where(last, outer - 1, n // 2 - 1))
        row = away(outer - 1 - j)
        return across, j, (row * inner + jnp.where(across, 1 - ypos, ypos)) * ndiag

    ahead = nspace - 3

    def stored(n):
        return jnp.logical_and(core > 0, n >= ahead)

    def found(n, dest, side, i):
        entry = entry_of(dest, i)
        m = lax.rem(lax.div(entry, NDISP), nmom)
        final = jnp.logical_and(
            lax.div(entry, nmom * NDISP) == slices - 1, lax.rem(entry, NDISP) == NDISP - 1
        )
        return jnp.where(final, 6 * local + m, ((n - ahead) * 2 + side) * local + i)

    def prepare(n):
        _, _, chip = unit(n)
        for side in range(2):
            for i in range(local):
                place = ((n - ahead) * 2 + side) * local + i
                dest = chip + (1 - core if side == 0 else core)
                early[place, 0], early[place, 1] = item(entry_of(dest, i))

    def complete(m):
        early[6 * local + m, 0], early[6 * local + m, 1] = item(
            ((slices - 1) * nmom + m) * NDISP + NDISP - 1
        )

    def give(n):
        _, _, chip = unit(n)

        @pl.when(stored(n))
        def _():
            for i in range(local):
                part1[n, i] = early[found(n, chip + (1 - core), 0, i)].astype(bf16)
                copy1(n, i).start()

        @pl.when(jnp.logical_not(stored(n)))
        def _():
            for i in range(local):
                real, imag = item(entry_of(chip + (1 - core), i))
                part1[n, i, 0] = real.astype(bf16)
                part1[n, i, 1] = imag.astype(bf16)
                copy1(n, i).start()

    def keep(n):
        _, _, chip = unit(n)

        @pl.when(stored(n))
        def _():
            for i in range(local):
                own[n, i] = early[found(n, chip + core, 1, i)]

        @pl.when(jnp.logical_not(stored(n)))
        def _():
            for i in range(local):
                own[n, i, 0], own[n, i, 1] = item(entry_of(chip + core, i))

    def join(n):
        across, j, _ = unit(n)
        for i in range(local):
            copy1(n, i).wait_recv()
            total = own[n, i] + recv1[n, i].astype(f32)
            own[n, i] = total
            part2[n, i] = total.astype(bf16)

            @pl.when(across)
            def _():
                copy2(n, j, i).start()

    def collect(q):
        j = q // local
        i = lax.rem(q, local)
        r = outer - 1 - j
        n = jnp.where(j == outer - 1, nspace - 1, 2 * j + 2)
        copy2(0, j, i).wait()
        own[n, i] = own[n, i] + recv2[j, i].astype(f32)
        for l in range(levels):
            @pl.when(lax.rem(r, 2 << l) == 0)
            def _():
                copy3(r + (1 << l), i).wait()
                own[n, i] = own[n, i] + recv3[r + (1 << l), i].astype(f32)

        @pl.when(r > 0)
        def _():
            part3[r, i] = own[n, i].astype(bf16)
            copy3(r, i).start()

    def halo(t):
        for h in range(2):
            v_copy(t, h).wait_recv()
            displace(t, 2, above, h * half, half)

    @pl.loop(0, slices - 1)
    def _(t):
        halo(t)

    @pl.when(core > 0)
    def _():
        @pl.loop(ahead, nspace)
        def _(n):
            prepare(n)

    halo(slices - 1)

    @pl.loop(0, 3 * nspace)
    def _(k):
        first_core = core == 0
        kind = jnp.where(
            first_core, jnp.where(k < nspace, 0, 1 + lax.rem(k - nspace + 2 * nspace, 2)), lax.rem(k, 3)
        )
        n = jnp.where(first_core, jnp.where(k < nspace, k, (k - nspace + 2 * nspace) // 2 - nspace), k // 3)

        @pl.when(jnp.logical_and(kind == 0, jnp.logical_and(core > 0, n == ahead)))
        def _():
            @pl.loop(0, nmom // 2)
            def _(m):
                complete(2 * m)
                complete(2 * m + 1)

        @pl.when(kind == 0)
        def _():
            give(n)

        @pl.when(kind == 1)
        def _():
            keep(n)

        @pl.when(kind == 2)
        def _():
            join(n)

            first = jnp.where(n == 5, 2, n - 2)
            stop = jnp.where(jnp.logical_or(n < 2, n == 4), first, n - 1)

            @pl.loop(first, stop)
            def _(q):
                collect(q)

    @pl.loop(nspace - 2, (outer - 1) * local)
    def _(q):
        collect(q)

    mix()

    @pl.loop((outer - 1) * local, outer * local)
    def _(q):
        collect(q)

    out_ref[...] = own[nspace - 1].astype(bf16)

    @pl.loop(0, nspace)
    def _(n):
        for i in range(local):
            copy1(n, i).wait_send()

    for t in range(slices):
        for h in range(2):
            v_copy(t, h).wait_send()
    m_copy.wait()


def diagram_kernel(elem_ref, mix_ref, out_hbm, out_ref, store_sem):
    local, spins = mix_ref.shape[:2]
    group = 2 if spins % 2 == 0 else 1

    def store(i, h):
        some = pl.ds(h * group, group)
        return pltpu.make_async_copy(out_ref.at[i, some], out_hbm.at[i, some], store_sem.at[i, h])

    pieces = [(i, h) for i in range(local) for h in range(spins // group)]
    for i, h in pieces:
        if h == 0:
            er, ei = elem_ref[i, 0], elem_ref[i, 1]
            square = jnp.concatenate(
                [jnp.concatenate([er, -ei], 1), jnp.concatenate([ei, er], 1)], 0
            )
        for r in range(h * group, (h + 1) * group):
            out_ref[i, r] = jnp.dot(
                square, mix_ref[i, r], preferred_element_type=f32
            ).astype(bf16)
        store(i, h).start()
    for i, h in pieces:
        store(i, h).wait()


def body(eigvecs, gauge_links, momenta, spin_mix, perambulators, contraction_list):
    slices, _, colors, nvec, depth, plane = eigvecs.shape
    assert depth == 1 and colors == 3
    nspace, ndiag = lax.axis_size("space"), lax.axis_size("diag")
    inner = 2
    outer = nspace // inner
    assert ndiag == 2 and inner * outer == nspace
    assert momenta.shape[0] % 2 == 0 and outer >= 4 and outer & (outer - 1) == 0 and contraction_list.shape[0] == 2
    ndev = nspace * ndiag
    scale = 1.0 / math.sqrt(3 * plane * ndev)
    nmom = momenta.shape[0]
    local = contraction_list.shape[0]
    count, spins = perambulators.shape[:2]
    width = perambulators.shape[4]
    vmem = pl.BlockSpec(memory_space=pltpu.VMEM)
    smem = pl.BlockSpec(memory_space=pltpu.SMEM)
    hbm = pl.BlockSpec(memory_space=pltpu.HBM)
    tile = (local, 2, nvec, nvec)
    field = (2 * nvec, 3 * plane)
    dma = pltpu.SemaphoreType.DMA
    elem, mixed = pl.pallas_call(
        functools.partial(
            elemental_kernel,
            (nspace, ndiag, inner, local, slices, nvec, plane, 0.5 * scale),
        ),
        out_shape=(
            jax.ShapeDtypeStruct(tile, bf16),
            jax.ShapeDtypeStruct((local, spins, 2 * nvec, width), bf16),
        ),
        in_specs=[smem, smem, smem, vmem, hbm, hbm],
        out_specs=(vmem, pl.BlockSpec(memory_space=pl.ANY)),
        scratch_shapes=[
            pltpu.VMEM((slices, 2, 3, nvec, plane), bf16),
            pltpu.VMEM((nmom, 3 * plane), f32),
            pltpu.VMEM((nmom, 3 * plane), f32),
            pltpu.VMEM((nmom * NDISP, nvec), f32),
            pltpu.VMEM((nmom * NDISP, nvec), f32),
            pltpu.VMEM((slices, 2, 3, nvec, plane), bf16),
            pltpu.VMEM((slices * NDISP,) + field, bf16),
            pltpu.VMEM((slices * nmom,) + field, bf16),
            pltpu.VMEM((slices * nmom,) + field, bf16),
            pltpu.VMEM((count, spins, 2 * nvec, width), bf16),
            pltpu.VMEM((local, spins, 2 * nvec, width), bf16),
            pltpu.VMEM((ndev, 1, 128), jnp.int32),
            pltpu.SMEM((ndev, 1, 128), jnp.int32),
            pltpu.VMEM((nspace,) + tile, bf16),
            pltpu.VMEM((nspace,) + tile, bf16),
            pltpu.VMEM((nspace,) + tile, f32),
            pltpu.VMEM((6 * local + nmom,) + tile[1:], f32),
            pltpu.VMEM((nspace,) + tile, bf16),
            pltpu.VMEM((outer,) + tile, bf16),
            pltpu.VMEM((outer,) + tile, bf16),
            pltpu.VMEM((outer,) + tile, bf16),
            dma((slices,)), dma, dma, dma((slices, 2)), dma((slices, 2)),
            dma((ndev,)), dma((ndev,)), dma,
            dma((nspace, local)), dma((nspace, local)),
            dma((outer, local)), dma((outer, local)),
            dma((outer, local)), dma((outer, local)),
        ],
        compiler_params=pltpu.CompilerParams(
            collective_id=0, has_side_effects=True, vmem_limit_bytes=44 * 1024 * 1024
        ),
    )(*(
        pltpu.with_memory_space_constraint(x, pltpu.HBM) for x in (
            contraction_list, momenta, spin_mix.transpose(1, 2, 0), gauge_links,
            eigvecs.reshape(slices, 2, 3, nvec, plane),
            perambulators.reshape(count, spins, 2 * nvec, width),
        )
    ))
    out = pl.pallas_call(
        diagram_kernel,
        in_specs=[vmem, vmem],
        out_specs=hbm,
        out_shape=jax.ShapeDtypeStruct((local, spins, 2 * nvec, width), bf16),
        scratch_shapes=[
            pltpu.VMEM((local, spins, 2 * nvec, width), bf16), dma((local, spins)),
        ],
        compiler_params=pltpu.CompilerParams(vmem_limit_bytes=24 * 1024 * 1024),
    )(elem, mixed)
    return out.reshape(local, spins, 2, nvec, width)


def solution(mesh):
    placed = (
        P("cfg", None, None, None, ("space", "diag"), None),
        P("cfg", None, None, None, None, ("space", "diag"), None),
        P(),
        P(),
        P(("cfg", "space", "diag"), None, None, None, None),
        P(("space", "diag"), None),
    )
    return jax.shard_map(
        body,
        mesh=mesh,
        in_specs=placed,
        out_specs=P(("cfg", "space", "diag"), None, None, None, None),
        check_vma=False,
    )
```

```python
import functools
import math

import jax
import jax.numpy as jnp
from jax import lax
from jax.experimental import pallas as pl
from jax.experimental.pallas import tpu as pltpu
from jax.sharding import PartitionSpec as P

LX = 16
LY = 16
NDISP = 4
CHUNK = 16
MESH = pl.DeviceIdType.MESH
NT = (((1,), (1,)), ((), ()))
f32 = jnp.float32
bf16 = jnp.bfloat16


def elemental_kernel(
    dims, list_hbm, mom_hbm, spin_hbm, link_hbm, eig_hbm, tau_hbm, out_ref, mix_hbm,
    list_ref, mom_ref, spin_ref, link_ref,
    eig_ref, cos_ref, sin_ref, ar_ref, ai_ref, above, fields, plus, minus, tau_ref, mix_ref, lists, table,
    part1, recv1, own, early, part2, recv2, part3, recv3,
    small_local, link_local, e_local, t_local, m_local, v_send, v_recv, l_send, l_recv, l_local, s1, r1, s2, r2, s3, r3,
):
    nspace, ndiag, inner, local, slices, nvec, plane, factor = dims
    ndev = nspace * ndiag
    outer = nspace // inner
    space = lax.axis_index("space")
    core = lax.axis_index("diag")
    cfg = lax.axis_index("cfg")
    me = space * ndiag + core
    zpos = space // inner
    ypos = lax.rem(space, inner)

    def device(index):
        return (cfg, index // ndiag, lax.rem(index, ndiag))

    def e_copy(t):
        return pltpu.make_async_copy(eig_hbm.at[t], eig_ref.at[t], e_local.at[t])

    t_copy = pltpu.make_async_copy(tau_hbm, tau_ref, t_local)
    m_copy = pltpu.make_async_copy(mix_ref, mix_hbm, m_local)

    barrier = pltpu.get_barrier_semaphore()

    @pl.loop(1, ndev)
    def _(k):
        pl.semaphore_signal(
            barrier, inc=1, device_id=device(lax.rem(me + k, ndev)), device_id_type=MESH
        )

    small = [
        pltpu.make_async_copy(src, dst, small_local.at[k])
        for k, (src, dst) in enumerate(
            ((list_hbm, list_ref), (mom_hbm, mom_ref), (spin_hbm, spin_ref))
        )
    ]
    link_copy = pltpu.make_async_copy(link_hbm, link_ref, link_local)
    for copy in small:
        copy.start()
    link_copy.start()
    for t in range(slices):
        e_copy(t).start()
    t_copy.start()

    pl.semaphore_wait(barrier, ndev - 1)

    half = nvec // 2

    def v_copy(t, h):
        rows = pl.ds(pl.multiple_of(h * half, half), half)
        return pltpu.make_async_remote_copy(
            src_ref=eig_hbm.at[t, :, :, rows], dst_ref=above.at[t, :, :, rows],
            send_sem=v_send.at[t, h], recv_sem=v_recv.at[t, h],
            device_id=device(lax.rem(me + ndev - 1, ndev)), device_id_type=MESH,
        )

    def l_copy(k):
        return pltpu.make_async_remote_copy(
            src_ref=lists.at[0], dst_ref=lists.at[k],
            send_sem=l_send.at[k], recv_sem=l_recv.at[k],
            device_id=device(lax.rem(me + k, ndev)), device_id_type=MESH,
        )

    for h in range(2):
        v_copy(0, h).start()

    for copy in small:
        copy.wait()
    column = lax.broadcasted_iota(jnp.int32, (1, 128), 1)
    packed = jnp.zeros((1, 128), jnp.int32)
    for i in range(local):
        packed = jnp.where(column == i, list_ref[i, 0], packed)
    lists[0] = packed

    @pl.loop(1, ndev)
    def _(k):
        l_copy(k).start()

    for t in range(1, slices):
        for h in range(2):
            v_copy(t, h).start()

    nmom = mom_ref.shape[0]
    flat = lax.broadcasted_iota(jnp.int32, (1, plane), 1)
    xcoord = lax.rem(flat, LX).astype(f32)
    ycoord = lax.div(flat, LX).astype(f32)
    zcoord = lax.convert_element_type(me, f32)
    rows, hops = [], []
    for m in range(nmom):
        mom = [mom_ref[m, axis].astype(f32) for axis in range(3)]
        rows.append(
            2.0 * math.pi * (mom[0] * xcoord / LX + mom[1] * ycoord / LY + mom[2] * zcoord / ndev)
        )
        hops.append(jnp.full((1, nvec), math.pi, f32))
        for axis, size in enumerate((LX, LY, ndev)):
            hops.append(jnp.full((1, nvec), mom[axis] * (2.0 * math.pi / size), f32))
    angle = jnp.concatenate(rows, 0)
    cos_ref[...] = jnp.concatenate([jnp.cos(angle)] * 3, 1)
    sin_ref[...] = jnp.concatenate([jnp.sin(angle)] * 3, 1)
    hop = jnp.concatenate(hops, 0)
    plain = lax.rem(lax.broadcasted_iota(jnp.int32, hop.shape, 0), NDISP) == 0
    ar_ref[...] = jnp.where(plain, -1.0, jnp.cos(hop))
    ai_ref[...] = jnp.where(plain, 0.0, -jnp.sin(hop))

    lane = lax.broadcasted_iota(jnp.int32, (CHUNK, plane), 1)
    edge = lax.rem(lane, LX) == LX - 1

    def displace(t, direction, source, begin=0, size=nvec):
        @pl.loop(0, size // CHUNK)
        def _(i):
            rows = pl.multiple_of(begin + i * CHUNK, CHUNK)
            vec = []
            for p in range(2):
                line = []
                for c in range(3):
                    v = source[t, p, c, pl.ds(rows, CHUNK), :].astype(f32)
                    if direction == 0:
                        v = jnp.where(
                            edge, pltpu.roll(v, LX - 1, 1), pltpu.roll(v, plane - 1, 1)
                        )
                    elif direction == 1:
                        v = pltpu.roll(v, plane - LX, 1)
                    line.append(v)
                vec.append(line)
            for row in range(3):
                real = imag = None
                for col in range(3):
                    mr = link_ref[t, direction, 0, row, col]
                    mi = link_ref[t, direction, 1, row, col]
                    re = mr * vec[0][col] - mi * vec[1][col]
                    im = mr * vec[1][col] + mi * vec[0][col]
                    real = re if real is None else real + re
                    imag = im if imag is None else imag + im
                lanes = slice(row * plane, (row + 1) * plane)
                fields[t * NDISP + direction + 1, pl.ds(rows, CHUNK), lanes] = real.astype(bf16)
                fields[
                    t * NDISP + direction + 1, pl.ds(nvec + rows, CHUNK), lanes
                ] = imag.astype(bf16)

    def phases(t):
        @pl.loop(0, nvec // CHUNK)
        def _(i):
            rows = pl.multiple_of(i * CHUNK, CHUNK)
            for c in range(3):
                lanes = slice(c * plane, (c + 1) * plane)
                vr = eig_ref[t, 0, c, pl.ds(rows, CHUNK), :]
                vi = eig_ref[t, 1, c, pl.ds(rows, CHUNK), :]
                fields[t * NDISP, pl.ds(rows, CHUNK), lanes] = vr
                fields[t * NDISP, pl.ds(nvec + rows, CHUNK), lanes] = vi
                vr, vi = vr.astype(f32), vi.astype(f32)
                for m in range(nmom):
                    cosine = cos_ref[m:m + 1, lanes]
                    sine = sin_ref[m:m + 1, lanes]
                    a, b = cosine * vr, sine * vi
                    g, h = cosine * vi, sine * vr
                    plus[t * nmom + m, pl.ds(rows, CHUNK), lanes] = (a - b).astype(bf16)
                    plus[t * nmom + m, pl.ds(nvec + rows, CHUNK), lanes] = (g + h).astype(bf16)
                    minus[t * nmom + m, pl.ds(rows, CHUNK), lanes] = (a + b).astype(bf16)
                    minus[t * nmom + m, pl.ds(nvec + rows, CHUNK), lanes] = (g - h).astype(bf16)

    link_copy.wait()

    @pl.loop(0, slices)
    def _(t):
        e_copy(t).wait()
        displace(t, 0, eig_ref)
        displace(t, 1, eig_ref)
        phases(t)

    count, spins = tau_ref.shape[:2]

    def mix():
        t_copy.wait()
        for i in range(local):
            q = lax.rem(list_ref[i, 2], count)
            g = list_ref[i, 1]

            @pl.loop(0, 2 * nvec // CHUNK)
            def _(n):
                rows = pl.multiple_of(n * CHUNK, CHUNK)
                tau = [tau_ref[q, s, pl.ds(rows, CHUNK), :].astype(f32) for s in range(spins)]
                for r in range(spins):
                    mixed = spin_ref[r, 0, g] * tau[0]
                    for s in range(1, spins):
                        mixed = mixed + spin_ref[r, s, g] * tau[s]
                    mix_ref[i, r, pl.ds(rows, CHUNK), :] = mixed.astype(bf16)
        m_copy.start()

    @pl.loop(1, ndev)
    def _(k):
        l_copy(k).wait()

    to_smem = pltpu.make_async_copy(lists, table, l_local)
    to_smem.start()
    to_smem.wait()

    def entry_of(dest, i):
        return table[lax.rem(me + ndev - dest, ndev), 0, i]

    def item(entry):
        time = lax.div(entry, nmom * NDISP)
        m = lax.rem(lax.div(entry, NDISP), nmom)
        d = lax.rem(entry, NDISP)
        ar = ar_ref[pl.ds(m * NDISP + d, 1), :]
        ai = ai_ref[pl.ds(m * NDISP + d, 1), :]
        x = fields[time * NDISP + d]
        first = lax.dot_general(plus[time * nmom + m], x, NT, preferred_element_type=f32)
        second = lax.dot_general(x, minus[time * nmom + m], NT, preferred_element_type=f32)
        g1r = first[:nvec, :nvec] + first[nvec:, nvec:]
        g1i = first[:nvec, nvec:] - first[nvec:, :nvec]
        g2r = second[:nvec, :nvec] + second[nvec:, nvec:]
        g2i = second[:nvec, nvec:] - second[nvec:, :nvec]
        return (
            (g1r - (ar * g2r - ai * g2i)) * factor,
            (g1i - (ar * g2i + ai * g2r)) * factor,
        )

    levels = outer.bit_length() - 1

    def flip(l):
        size = 1 << l
        return zpos + size * (1 - 2 * lax.rem(zpos // size, 2))

    def away(r):
        row = zpos
        for l in range(levels):
            row = row + lax.rem(r // (1 << l), 2) * (flip(l) - zpos)
        return row

    def copy1(n, i):
        return pltpu.make_async_remote_copy(
            src_ref=part1.at[n, i], dst_ref=recv1.at[n, i], send_sem=s1.at[n, i], recv_sem=r1.at[n, i],
            device_id=(cfg, space, 1 - core), device_id_type=MESH,
        )

    def copy2(n, j, i):
        return pltpu.make_async_remote_copy(
            src_ref=part2.at[n, i], dst_ref=recv2.at[j, i], send_sem=s2.at[j, i], recv_sem=r2.at[j, i],
            device_id=(cfg, zpos * inner + (1 - ypos), core), device_id_type=MESH,
        )

    def copy3(r, i):
        row = flip(levels - 1)
        for l in range(levels - 2, -1, -1):
            row = jnp.where(lax.rem(r, 2 << l) == 1 << l, flip(l), row)
        return pltpu.make_async_remote_copy(
            src_ref=part3.at[r, i], dst_ref=recv3.at[r, i], send_sem=s3.at[r, i], recv_sem=r3.at[r, i],
            device_id=(cfg, row * inner + ypos, core), device_id_type=MESH,
        )

    def unit(n):
        last = n == nspace - 1
        across = jnp.logical_or(n == 0, jnp.logical_and(lax.rem(n, 2) == 1, n < nspace - 1))
        j = jnp.where(across, (n + 1) // 2, jnp.where(last, outer - 1, n // 2 - 1))
        row = away(outer - 1 - j)
        return across, j, (row * inner + jnp.where(across, 1 - ypos, ypos)) * ndiag

    ahead = nspace - 3

    def stored(n):
        return jnp.logical_and(core > 0, n >= ahead)

    def found(n, dest, side, i):
        entry = entry_of(dest, i)
        m = lax.rem(lax.div(entry, NDISP), nmom)
        final = jnp.logical_and(
            lax.div(entry, nmom * NDISP) == slices - 1, lax.rem(entry, NDISP) == NDISP - 1
        )
        return jnp.where(final, 6 * local + m, ((n - ahead) * 2 + side) * local + i)

    def prepare(n):
        _, _, chip = unit(n)
        for side in range(2):
            for i in range(local):
                place = ((n - ahead) * 2 + side) * local + i
                dest = chip + (1 - core if side == 0 else core)
                early[place, 0], early[place, 1] = item(entry_of(dest, i))

    def complete(m):
        early[6 * local + m, 0], early[6 * local + m, 1] = item(
            ((slices - 1) * nmom + m) * NDISP + NDISP - 1
        )

    def give(n):
        _, _, chip = unit(n)

        @pl.when(stored(n))
        def _():
            for i in range(local):
                part1[n, i] = early[found(n, chip + (1 - core), 0, i)].astype(bf16)
                copy1(n, i).start()

        @pl.when(jnp.logical_not(stored(n)))
        def _():
            for i in range(local):
                real, imag = item(entry_of(chip + (1 - core), i))
                part1[n, i, 0] = real.astype(bf16)
                part1[n, i, 1] = imag.astype(bf16)
                copy1(n, i).start()

    def keep(n):
        _, _, chip = unit(n)

        @pl.when(stored(n))
        def _():
            for i in range(local):
                own[n, i] = early[found(n, chip + core, 1, i)]

        @pl.when(jnp.logical_not(stored(n)))
        def _():
            for i in range(local):
                own[n, i, 0], own[n, i, 1] = item(entry_of(chip + core, i))

    def join(n):
        across, j, _ = unit(n)
        for i in range(local):
            copy1(n, i).wait_recv()
            total = own[n, i] + recv1[n, i].astype(f32)
            own[n, i] = total
            part2[n, i] = total.astype(bf16)

            @pl.when(across)
            def _():
                copy2(n, j, i).start()

    def collect(q):
        j = q // local
        i = lax.rem(q, local)
        r = outer - 1 - j
        n = jnp.where(j == outer - 1, nspace - 1, 2 * j + 2)
        copy2(0, j, i).wait()
        own[n, i] = own[n, i] + recv2[j, i].astype(f32)
        for l in range(levels):
            @pl.when(lax.rem(r, 2 << l) == 0)
            def _():
                copy3(r + (1 << l), i).wait()
                own[n, i] = own[n, i] + recv3[r + (1 << l), i].astype(f32)

        @pl.when(r > 0)
        def _():
            part3[r, i] = own[n, i].astype(bf16)
            copy3(r, i).start()

    def halo(t):
        for h in range(2):
            v_copy(t, h).wait_recv()
            displace(t, 2, above, h * half, half)

    @pl.loop(0, slices - 1)
    def _(t):
        halo(t)

    @pl.when(core > 0)
    def _():
        @pl.loop(ahead, nspace)
        def _(n):
            prepare(n)

    halo(slices - 1)

    @pl.loop(0, 3 * nspace)
    def _(k):
        first_core = core == 0
        kind = jnp.where(
            first_core, jnp.where(k < nspace, 0, 1 + lax.rem(k - nspace + 2 * nspace, 2)), lax.rem(k, 3)
        )
        n = jnp.where(first_core, jnp.where(k < nspace, k, (k - nspace + 2 * nspace) // 2 - nspace), k // 3)

        @pl.when(jnp.logical_and(kind == 0, jnp.logical_and(core > 0, n == ahead)))
        def _():
            @pl.loop(0, nmom // 2)
            def _(m):
                complete(2 * m)
                complete(2 * m + 1)

        @pl.when(kind == 0)
        def _():
            give(n)

        @pl.when(kind == 1)
        def _():
            keep(n)

        @pl.when(kind == 2)
        def _():
            join(n)

            first = jnp.where(n == 5, 2, n - 2)
            stop = jnp.where(jnp.logical_or(n < 2, n == 4), first, n - 1)

            @pl.loop(first, stop)
            def _(q):
                collect(q)

    @pl.loop(nspace - 2, (outer - 1) * local)
    def _(q):
        collect(q)

    mix()

    @pl.loop((outer - 1) * local, outer * local)
    def _(q):
        collect(q)

    out_ref[...] = own[nspace - 1].astype(bf16)

    @pl.loop(0, nspace)
    def _(n):
        for i in range(local):
            copy1(n, i).wait_send()

    for t in range(slices):
        for h in range(2):
            v_copy(t, h).wait_send()
    m_copy.wait()


def diagram_kernel(elem_ref, mix_ref, out_hbm, out_ref, store_sem):
    local, spins = mix_ref.shape[:2]
    group = 2 if spins % 2 == 0 else 1

    def store(i, h):
        some = pl.ds(h * group, group)
        return pltpu.make_async_copy(out_ref.at[i, some], out_hbm.at[i, some], store_sem.at[i, h])

    pieces = [(i, h) for i in range(local) for h in range(spins // group)]
    for i, h in pieces:
        if h == 0:
            er, ei = elem_ref[i, 0], elem_ref[i, 1]
            square = jnp.concatenate(
                [jnp.concatenate([er, -ei], 1), jnp.concatenate([ei, er], 1)], 0
            )
        for r in range(h * group, (h + 1) * group):
            out_ref[i, r] = jnp.dot(
                square, mix_ref[i, r], preferred_element_type=f32
            ).astype(bf16)
        store(i, h).start()
    for i, h in pieces:
        store(i, h).wait()


def body(eigvecs, gauge_links, momenta, spin_mix, perambulators, contraction_list):
    slices, _, colors, nvec, depth, plane = eigvecs.shape
    assert depth == 1 and colors == 3
    nspace, ndiag = lax.axis_size("space"), lax.axis_size("diag")
    inner = 2
    outer = nspace // inner
    assert ndiag == 2 and inner * outer == nspace
    assert momenta.shape[0] % 2 == 0 and outer >= 4 and outer & (outer - 1) == 0 and contraction_list.shape[0] == 2
    ndev = nspace * ndiag
    scale = 1.0 / math.sqrt(3 * plane * ndev)
    nmom = momenta.shape[0]
    local = contraction_list.shape[0]
    count, spins = perambulators.shape[:2]
    width = perambulators.shape[4]
    vmem = pl.BlockSpec(memory_space=pltpu.VMEM)
    hbm = pl.BlockSpec(memory_space=pltpu.HBM)
    tile = (local, 2, nvec, nvec)
    field = (2 * nvec, 3 * plane)
    dma = pltpu.SemaphoreType.DMA
    elem, mixed = pl.pallas_call(
        functools.partial(
            elemental_kernel,
            (nspace, ndiag, inner, local, slices, nvec, plane, 0.5 * scale),
        ),
        out_shape=(
            jax.ShapeDtypeStruct(tile, bf16),
            jax.ShapeDtypeStruct((local, spins, 2 * nvec, width), bf16),
        ),
        in_specs=[hbm] * 6,
        out_specs=(vmem, pl.BlockSpec(memory_space=pl.ANY)),
        scratch_shapes=[
            pltpu.SMEM(contraction_list.shape, jnp.int32),
            pltpu.SMEM(momenta.shape, jnp.int32),
            pltpu.SMEM((spins, spins, spin_mix.shape[0]), f32),
            pltpu.VMEM(gauge_links.shape, f32),
            pltpu.VMEM((slices, 2, 3, nvec, plane), bf16),
            pltpu.VMEM((nmom, 3 * plane), f32),
            pltpu.VMEM((nmom, 3 * plane), f32),
            pltpu.VMEM((nmom * NDISP, nvec), f32),
            pltpu.VMEM((nmom * NDISP, nvec), f32),
            pltpu.VMEM((slices, 2, 3, nvec, plane), bf16),
            pltpu.VMEM((slices * NDISP,) + field, bf16),
            pltpu.VMEM((slices * nmom,) + field, bf16),
            pltpu.VMEM((slices * nmom,) + field, bf16),
            pltpu.VMEM((count, spins, 2 * nvec, width), bf16),
            pltpu.VMEM((local, spins, 2 * nvec, width), bf16),
            pltpu.VMEM((ndev, 1, 128), jnp.int32),
            pltpu.SMEM((ndev, 1, 128), jnp.int32),
            pltpu.VMEM((nspace,) + tile, bf16),
            pltpu.VMEM((nspace,) + tile, bf16),
            pltpu.VMEM((nspace,) + tile, f32),
            pltpu.VMEM((6 * local + nmom,) + tile[1:], f32),
            pltpu.VMEM((nspace,) + tile, bf16),
            pltpu.VMEM((outer,) + tile, bf16),
            pltpu.VMEM((outer,) + tile, bf16),
            pltpu.VMEM((outer,) + tile, bf16),
            dma((3,)), dma, dma((slices,)), dma, dma, dma((slices, 2)), dma((slices, 2)),
            dma((ndev,)), dma((ndev,)), dma,
            dma((nspace, local)), dma((nspace, local)),
            dma((outer, local)), dma((outer, local)),
            dma((outer, local)), dma((outer, local)),
        ],
        compiler_params=pltpu.CompilerParams(
            collective_id=0, has_side_effects=True, vmem_limit_bytes=44 * 1024 * 1024
        ),
    )(*(
        pltpu.with_memory_space_constraint(x, pltpu.HBM) for x in (
            contraction_list, momenta, spin_mix.transpose(1, 2, 0), gauge_links,
            eigvecs.reshape(slices, 2, 3, nvec, plane),
            perambulators.reshape(count, spins, 2 * nvec, width),
        )
    ))
    out = pl.pallas_call(
        diagram_kernel,
        in_specs=[vmem, vmem],
        out_specs=hbm,
        out_shape=jax.ShapeDtypeStruct((local, spins, 2 * nvec, width), bf16),
        scratch_shapes=[
            pltpu.VMEM((local, spins, 2 * nvec, width), bf16), dma((local, spins)),
        ],
        compiler_params=pltpu.CompilerParams(vmem_limit_bytes=24 * 1024 * 1024),
    )(elem, mixed)
    return out.reshape(local, spins, 2, nvec, width)


def solution(mesh):
    placed = (
        P("cfg", None, None, None, ("space", "diag"), None),
        P("cfg", None, None, None, None, ("space", "diag"), None),
        P(),
        P(),
        P(("cfg", "space", "diag"), None, None, None, None),
        P(("space", "diag"), None),
    )
    return jax.shard_map(
        body,
        mesh=mesh,
        in_specs=placed,
        out_specs=P(("cfg", "space", "diag"), None, None, None, None),
        check_vma=False,
    )
```

```python
import functools
import math

import jax
import jax.numpy as jnp
from jax import lax
from jax.experimental import pallas as pl
from jax.experimental.pallas import tpu as pltpu
from jax.sharding import PartitionSpec as P

LX = 16
LY = 16
NDISP = 4
CHUNK = 16
MESH = pl.DeviceIdType.MESH
NT = (((1,), (1,)), ((), ()))
f32 = jnp.float32
bf16 = jnp.bfloat16


def elemental_kernel(
    dims, list_hbm, mom_hbm, spin_hbm, link_hbm, eig_hbm, tau_hbm, out_ref, mix_hbm,
    list_ref, mom_ref, spin_ref, link_ref,
    eig_ref, cos_ref, sin_ref, ar_ref, ai_ref, above, fields, plus, minus, tau_ref, mix_ref, lists, table,
    part1, recv1, own, early, part2, recv2, part3, recv3,
    small_local, link_local, e_local, t_local, m_local, v_send, v_recv, l_send, l_recv, l_local, s1, r1, s2, r2, s3, r3,
):
    nspace, ndiag, inner, local, slices, nvec, plane, factor = dims
    ndev = nspace * ndiag
    outer = nspace // inner
    space = lax.axis_index("space")
    core = lax.axis_index("diag")
    cfg = lax.axis_index("cfg")
    me = space * ndiag + core
    zpos = space // inner
    ypos = lax.rem(space, inner)

    def device(index):
        return (cfg, index // ndiag, lax.rem(index, ndiag))

    def e_copy(t):
        return pltpu.make_async_copy(eig_hbm.at[t], eig_ref.at[t], e_local.at[t])

    t_copy = pltpu.make_async_copy(tau_hbm, tau_ref, t_local)
    m_copy = pltpu.make_async_copy(mix_ref, mix_hbm, m_local)

    barrier = pltpu.get_barrier_semaphore()

    @pl.loop(1, ndev)
    def _(k):
        pl.semaphore_signal(
            barrier, inc=1, device_id=device(lax.rem(me + k, ndev)), device_id_type=MESH
        )

    small = [
        pltpu.make_async_copy(src, dst, small_local.at[k])
        for k, (src, dst) in enumerate(
            ((list_hbm, list_ref), (mom_hbm, mom_ref), (spin_hbm, spin_ref))
        )
    ]
    link_copy = pltpu.make_async_copy(link_hbm, link_ref, link_local)
    for copy in small:
        copy.start()
    link_copy.start()
    for t in range(slices):
        e_copy(t).start()
    t_copy.start()

    pl.semaphore_wait(barrier, ndev - 1)

    half = nvec // 2

    def v_copy(t, h):
        rows = pl.ds(pl.multiple_of(h * half, half), half)
        return pltpu.make_async_remote_copy(
            src_ref=eig_hbm.at[t, :, :, rows], dst_ref=above.at[t, :, :, rows],
            send_sem=v_send.at[t, h], recv_sem=v_recv.at[t, h],
            device_id=device(lax.rem(me + ndev - 1, ndev)), device_id_type=MESH,
        )

    def l_copy(k):
        return pltpu.make_async_remote_copy(
            src_ref=lists.at[0], dst_ref=lists.at[k],
            send_sem=l_send.at[k], recv_sem=l_recv.at[k],
            device_id=device(lax.rem(me + k, ndev)), device_id_type=MESH,
        )

    for h in range(2):
        v_copy(0, h).start()

    for copy in small:
        copy.wait()
    column = lax.broadcasted_iota(jnp.int32, (1, 128), 1)
    packed = jnp.zeros((1, 128), jnp.int32)
    for i in range(local):
        packed = jnp.where(column == i, list_ref[i, 0], packed)
    lists[0] = packed

    @pl.loop(1, ndev)
    def _(k):
        l_copy(k).start()

    for t in range(1, slices):
        for h in range(2):
            v_copy(t, h).start()

    nmom = mom_ref.shape[0]
    flat = lax.broadcasted_iota(jnp.int32, (1, plane), 1)
    xcoord = lax.rem(flat, LX).astype(f32)
    ycoord = lax.div(flat, LX).astype(f32)
    zcoord = lax.convert_element_type(me, f32)
    rows, hops = [], []
    for m in range(nmom):
        mom = [mom_ref[m, axis].astype(f32) for axis in range(3)]
        rows.append(
            2.0 * math.pi * (mom[0] * xcoord / LX + mom[1] * ycoord / LY + mom[2] * zcoord / ndev)
        )
        hops.append(jnp.full((1, nvec), math.pi, f32))
        for axis, size in enumerate((LX, LY, ndev)):
            hops.append(jnp.full((1, nvec), mom[axis] * (2.0 * math.pi / size), f32))
    angle = jnp.concatenate(rows, 0)
    cos_ref[...] = jnp.concatenate([jnp.cos(angle)] * 3, 1)
    sin_ref[...] = jnp.concatenate([jnp.sin(angle)] * 3, 1)
    hop = jnp.concatenate(hops, 0)
    plain = lax.rem(lax.broadcasted_iota(jnp.int32, hop.shape, 0), NDISP) == 0
    ar_ref[...] = jnp.where(plain, -1.0, jnp.cos(hop))
    ai_ref[...] = jnp.where(plain, 0.0, -jnp.sin(hop))

    lane = lax.broadcasted_iota(jnp.int32, (CHUNK, plane), 1)
    edge = lax.rem(lane, LX) == LX - 1

    def displace(t, direction, source, begin=0, size=nvec):
        @pl.loop(0, size // CHUNK)
        def _(i):
            rows = pl.multiple_of(begin + i * CHUNK, CHUNK)
            vec = []
            for p in range(2):
                line = []
                for c in range(3):
                    v = source[t, p, c, pl.ds(rows, CHUNK), :].astype(f32)
                    if direction == 0:
                        v = jnp.where(
                            edge, pltpu.roll(v, LX - 1, 1), pltpu.roll(v, plane - 1, 1)
                        )
                    elif direction == 1:
                        v = pltpu.roll(v, plane - LX, 1)
                    line.append(v)
                vec.append(line)
            for row in range(3):
                real = imag = None
                for col in range(3):
                    mr = link_ref[t, direction, 0, row, col]
                    mi = link_ref[t, direction, 1, row, col]
                    re = mr * vec[0][col] - mi * vec[1][col]
                    im = mr * vec[1][col] + mi * vec[0][col]
                    real = re if real is None else real + re
                    imag = im if imag is None else imag + im
                lanes = slice(row * plane, (row + 1) * plane)
                fields[t * NDISP + direction + 1, pl.ds(rows, CHUNK), lanes] = real.astype(bf16)
                fields[
                    t * NDISP + direction + 1, pl.ds(nvec + rows, CHUNK), lanes
                ] = imag.astype(bf16)

    def phases(t):
        @pl.loop(0, nvec // CHUNK)
        def _(i):
            rows = pl.multiple_of(i * CHUNK, CHUNK)
            for c in range(3):
                lanes = slice(c * plane, (c + 1) * plane)
                vr = eig_ref[t, 0, c, pl.ds(rows, CHUNK), :]
                vi = eig_ref[t, 1, c, pl.ds(rows, CHUNK), :]
                fields[t * NDISP, pl.ds(rows, CHUNK), lanes] = vr
                fields[t * NDISP, pl.ds(nvec + rows, CHUNK), lanes] = vi
                vr, vi = vr.astype(f32), vi.astype(f32)
                for m in range(nmom):
                    cosine = cos_ref[m:m + 1, lanes]
                    sine = sin_ref[m:m + 1, lanes]
                    a, b = cosine * vr, sine * vi
                    g, h = cosine * vi, sine * vr
                    plus[t * nmom + m, pl.ds(rows, CHUNK), lanes] = (a - b).astype(bf16)
                    plus[t * nmom + m, pl.ds(nvec + rows, CHUNK), lanes] = (g + h).astype(bf16)
                    minus[t * nmom + m, pl.ds(rows, CHUNK), lanes] = (a + b).astype(bf16)
                    minus[t * nmom + m, pl.ds(nvec + rows, CHUNK), lanes] = (g - h).astype(bf16)

    link_copy.wait()

    @pl.loop(0, slices)
    def _(t):
        e_copy(t).wait()
        displace(t, 0, eig_ref)
        displace(t, 1, eig_ref)
        phases(t)

    count, spins = tau_ref.shape[:2]

    def mix():
        t_copy.wait()
        for i in range(local):
            q = lax.rem(list_ref[i, 2], count)
            g = list_ref[i, 1]

            @pl.loop(0, 2 * nvec // CHUNK)
            def _(n):
                rows = pl.multiple_of(n * CHUNK, CHUNK)
                tau = [tau_ref[q, s, pl.ds(rows, CHUNK), :].astype(f32) for s in range(spins)]
                for r in range(spins):
                    mixed = spin_ref[r, 0, g] * tau[0]
                    for s in range(1, spins):
                        mixed = mixed + spin_ref[r, s, g] * tau[s]
                    mix_ref[i, r, pl.ds(rows, CHUNK), :] = mixed.astype(bf16)
        m_copy.start()

    @pl.loop(1, ndev)
    def _(k):
        l_copy(k).wait()

    to_smem = pltpu.make_async_copy(lists, table, l_local)
    to_smem.start()
    to_smem.wait()

    def entry_of(dest, i):
        return table[lax.rem(me + ndev - dest, ndev), 0, i]

    def item(entry):
        time = lax.div(entry, nmom * NDISP)
        m = lax.rem(lax.div(entry, NDISP), nmom)
        d = lax.rem(entry, NDISP)
        ar = ar_ref[pl.ds(m * NDISP + d, 1), :]
        ai = ai_ref[pl.ds(m * NDISP + d, 1), :]
        x = fields[time * NDISP + d]
        first = lax.dot_general(plus[time * nmom + m], x, NT, preferred_element_type=f32)
        second = lax.dot_general(x, minus[time * nmom + m], NT, preferred_element_type=f32)
        g1r = first[:nvec, :nvec] + first[nvec:, nvec:]
        g1i = first[:nvec, nvec:] - first[nvec:, :nvec]
        g2r = second[:nvec, :nvec] + second[nvec:, nvec:]
        g2i = second[:nvec, nvec:] - second[nvec:, :nvec]
        return (
            (g1r - (ar * g2r - ai * g2i)) * factor,
            (g1i - (ar * g2i + ai * g2r)) * factor,
        )

    levels = outer.bit_length() - 1

    def flip(l):
        size = 1 << l
        return zpos + size * (1 - 2 * lax.rem(zpos // size, 2))

    def away(r):
        row = zpos
        for l in range(levels):
            row = row + lax.rem(r // (1 << l), 2) * (flip(l) - zpos)
        return row

    def copy1(n, i):
        return pltpu.make_async_remote_copy(
            src_ref=part1.at[n, i], dst_ref=recv1.at[n, i], send_sem=s1.at[n, i], recv_sem=r1.at[n, i],
            device_id=(cfg, space, 1 - core), device_id_type=MESH,
        )

    def copy2(n, j, i):
        return pltpu.make_async_remote_copy(
            src_ref=part2.at[n, i], dst_ref=recv2.at[j, i], send_sem=s2.at[j, i], recv_sem=r2.at[j, i],
            device_id=(cfg, zpos * inner + (1 - ypos), core), device_id_type=MESH,
        )

    def copy3(r, i):
        row = flip((r & -r).bit_length() - 1)
        return pltpu.make_async_remote_copy(
            src_ref=part3.at[r, i], dst_ref=recv3.at[r, i], send_sem=s3.at[r, i], recv_sem=r3.at[r, i],
            device_id=(cfg, row * inner + ypos, core), device_id_type=MESH,
        )

    def unit(n):
        last = n == nspace - 1
        across = jnp.logical_or(n == 0, jnp.logical_and(lax.rem(n, 2) == 1, n < nspace - 1))
        j = jnp.where(across, (n + 1) // 2, jnp.where(last, outer - 1, n // 2 - 1))
        row = away(outer - 1 - j)
        return across, j, (row * inner + jnp.where(across, 1 - ypos, ypos)) * ndiag

    ahead = nspace - 3

    def stored(n):
        return jnp.logical_and(core > 0, n >= ahead)

    def found(n, dest, side, i):
        entry = entry_of(dest, i)
        m = lax.rem(lax.div(entry, NDISP), nmom)
        final = jnp.logical_and(
            lax.div(entry, nmom * NDISP) == slices - 1, lax.rem(entry, NDISP) == NDISP - 1
        )
        return jnp.where(final, 6 * local + m, ((n - ahead) * 2 + side) * local + i)

    def prepare(n):
        _, _, chip = unit(n)
        for side in range(2):
            for i in range(local):
                place = ((n - ahead) * 2 + side) * local + i
                dest = chip + (1 - core if side == 0 else core)
                early[place, 0], early[place, 1] = item(entry_of(dest, i))

    def complete(m):
        early[6 * local + m, 0], early[6 * local + m, 1] = item(
            ((slices - 1) * nmom + m) * NDISP + NDISP - 1
        )

    def give(n):
        _, _, chip = unit(n)

        @pl.when(stored(n))
        def _():
            for i in range(local):
                part1[n, i] = early[found(n, chip + (1 - core), 0, i)].astype(bf16)
                copy1(n, i).start()

        @pl.when(jnp.logical_not(stored(n)))
        def _():
            for i in range(local):
                real, imag = item(entry_of(chip + (1 - core), i))
                part1[n, i, 0] = real.astype(bf16)
                part1[n, i, 1] = imag.astype(bf16)
                copy1(n, i).start()

    def keep(n):
        _, _, chip = unit(n)

        @pl.when(stored(n))
        def _():
            for i in range(local):
                own[n, i] = early[found(n, chip + core, 1, i)]

        @pl.when(jnp.logical_not(stored(n)))
        def _():
            for i in range(local):
                own[n, i, 0], own[n, i, 1] = item(entry_of(chip + core, i))

    def join(n):
        across, j, _ = unit(n)
        for i in range(local):
            copy1(n, i).wait_recv()
            total = own[n, i] + recv1[n, i].astype(f32)
            own[n, i] = total
            part2[n, i] = total.astype(bf16)

            @pl.when(across)
            def _():
                copy2(n, j, i).start()

    def collect_row(r, i):
        j = outer - 1 - r
        n = nspace - 1 if r == 0 else 2 * j + 2
        sources = [r + (1 << l) for l in range(levels) if r % (2 << l) == 0]
        copy2(0, j, i).wait()
        for source in sources:
            copy3(source, i).wait()
        total = own[n, i] + recv2[j, i].astype(f32)
        for source in sources:
            total = total + recv3[source, i].astype(f32)
        if r == 0:
            out_ref[i] = total.astype(bf16)
        else:
            part3[r, i] = total.astype(bf16)
            copy3(r, i).start()

    def collect(q):
        for r in range(outer - 1, -1, -1):
            @pl.when(outer - 1 - q // local == r)
            def _():
                collect_row(r, lax.rem(q, local))

    def halo(t):
        for h in range(2):
            v_copy(t, h).wait_recv()
            displace(t, 2, above, h * half, half)

    @pl.loop(0, slices - 1)
    def _(t):
        halo(t)

    @pl.when(core > 0)
    def _():
        @pl.loop(ahead, nspace)
        def _(n):
            prepare(n)

    halo(slices - 1)

    @pl.loop(0, 3 * nspace)
    def _(k):
        first_core = core == 0
        kind = jnp.where(
            first_core, jnp.where(k < nspace, 0, 1 + lax.rem(k - nspace + 2 * nspace, 2)), lax.rem(k, 3)
        )
        n = jnp.where(first_core, jnp.where(k < nspace, k, (k - nspace + 2 * nspace) // 2 - nspace), k // 3)

        @pl.when(jnp.logical_and(kind == 0, jnp.logical_and(core > 0, n == ahead)))
        def _():
            @pl.loop(0, nmom // 2)
            def _(m):
                complete(2 * m)
                complete(2 * m + 1)

        @pl.when(kind == 0)
        def _():
            give(n)

        @pl.when(kind == 1)
        def _():
            keep(n)

        @pl.when(kind == 2)
        def _():
            join(n)

            first = jnp.where(n == 5, 2, n - 2)
            stop = jnp.where(jnp.logical_or(n < 2, n == 4), first, n - 1)

            @pl.loop(first, stop)
            def _(q):
                collect(q)

    @pl.loop(nspace - 2, (outer - 1) * local)
    def _(q):
        collect(q)

    mix()

    for i in range(local):
        collect_row(0, i)

    @pl.loop(0, nspace)
    def _(n):
        for i in range(local):
            copy1(n, i).wait_send()

    for t in range(slices):
        for h in range(2):
            v_copy(t, h).wait_send()
    m_copy.wait()


def diagram_kernel(elem_ref, mix_ref, out_hbm, out_ref, store_sem):
    local, spins = mix_ref.shape[:2]
    group = 1

    def store(i, h):
        some = pl.ds(h * group, group)
        return pltpu.make_async_copy(out_ref.at[i, some], out_hbm.at[i, some], store_sem.at[i, h])

    pieces = [(i, h) for i in range(local) for h in range(spins // group)]
    for i, h in pieces:
        if h == 0:
            er, ei = elem_ref[i, 0], elem_ref[i, 1]
            square = jnp.concatenate(
                [jnp.concatenate([er, -ei], 1), jnp.concatenate([ei, er], 1)], 0
            )
        for r in range(h * group, (h + 1) * group):
            out_ref[i, r] = jnp.dot(
                square, mix_ref[i, r], preferred_element_type=f32
            ).astype(bf16)
        store(i, h).start()
    for i, h in pieces:
        store(i, h).wait()


def body(eigvecs, gauge_links, momenta, spin_mix, perambulators, contraction_list):
    slices, _, colors, nvec, depth, plane = eigvecs.shape
    assert depth == 1 and colors == 3
    nspace, ndiag = lax.axis_size("space"), lax.axis_size("diag")
    inner = 2
    outer = nspace // inner
    assert ndiag == 2 and inner * outer == nspace
    assert momenta.shape[0] % 2 == 0 and outer >= 4 and outer & (outer - 1) == 0 and contraction_list.shape[0] == 2
    ndev = nspace * ndiag
    scale = 1.0 / math.sqrt(3 * plane * ndev)
    nmom = momenta.shape[0]
    local = contraction_list.shape[0]
    count, spins = perambulators.shape[:2]
    width = perambulators.shape[4]
    vmem = pl.BlockSpec(memory_space=pltpu.VMEM)
    hbm = pl.BlockSpec(memory_space=pltpu.HBM)
    tile = (local, 2, nvec, nvec)
    field = (2 * nvec, 3 * plane)
    dma = pltpu.SemaphoreType.DMA
    elem, mixed = pl.pallas_call(
        functools.partial(
            elemental_kernel,
            (nspace, ndiag, inner, local, slices, nvec, plane, 0.5 * scale),
        ),
        out_shape=(
            jax.ShapeDtypeStruct(tile, bf16),
            jax.ShapeDtypeStruct((local, spins, 2 * nvec, width), bf16),
        ),
        in_specs=[hbm] * 6,
        out_specs=(vmem, pl.BlockSpec(memory_space=pl.ANY)),
        scratch_shapes=[
            pltpu.SMEM(contraction_list.shape, jnp.int32),
            pltpu.SMEM(momenta.shape, jnp.int32),
            pltpu.SMEM((spins, spins, spin_mix.shape[0]), f32),
            pltpu.VMEM(gauge_links.shape, f32),
            pltpu.VMEM((slices, 2, 3, nvec, plane), bf16),
            pltpu.VMEM((nmom, 3 * plane), f32),
            pltpu.VMEM((nmom, 3 * plane), f32),
            pltpu.VMEM((nmom * NDISP, nvec), f32),
            pltpu.VMEM((nmom * NDISP, nvec), f32),
            pltpu.VMEM((slices, 2, 3, nvec, plane), bf16),
            pltpu.VMEM((slices * NDISP,) + field, bf16),
            pltpu.VMEM((slices * nmom,) + field, bf16),
            pltpu.VMEM((slices * nmom,) + field, bf16),
            pltpu.VMEM((count, spins, 2 * nvec, width), bf16),
            pltpu.VMEM((local, spins, 2 * nvec, width), bf16),
            pltpu.VMEM((ndev, 1, 128), jnp.int32),
            pltpu.SMEM((ndev, 1, 128), jnp.int32),
            pltpu.VMEM((nspace,) + tile, bf16),
            pltpu.VMEM((nspace,) + tile, bf16),
            pltpu.VMEM((nspace,) + tile, f32),
            pltpu.VMEM((6 * local + nmom,) + tile[1:], f32),
            pltpu.VMEM((nspace,) + tile, bf16),
            pltpu.VMEM((outer,) + tile, bf16),
            pltpu.VMEM((outer,) + tile, bf16),
            pltpu.VMEM((outer,) + tile, bf16),
            dma((3,)), dma, dma((slices,)), dma, dma, dma((slices, 2)), dma((slices, 2)),
            dma((ndev,)), dma((ndev,)), dma,
            dma((nspace, local)), dma((nspace, local)),
            dma((outer, local)), dma((outer, local)),
            dma((outer, local)), dma((outer, local)),
        ],
        compiler_params=pltpu.CompilerParams(
            collective_id=0, has_side_effects=True, vmem_limit_bytes=44 * 1024 * 1024
        ),
    )(*(
        pltpu.with_memory_space_constraint(x, pltpu.HBM) for x in (
            contraction_list, momenta, spin_mix.transpose(1, 2, 0), gauge_links,
            eigvecs.reshape(slices, 2, 3, nvec, plane),
            perambulators.reshape(count, spins, 2 * nvec, width),
        )
    ))
    out = pl.pallas_call(
        diagram_kernel,
        in_specs=[vmem, vmem],
        out_specs=hbm,
        out_shape=jax.ShapeDtypeStruct((local, spins, 2 * nvec, width), bf16),
        scratch_shapes=[
            pltpu.VMEM((local, spins, 2 * nvec, width), bf16), dma((local, spins)),
        ],
        compiler_params=pltpu.CompilerParams(vmem_limit_bytes=24 * 1024 * 1024),
    )(elem, mixed)
    return out.reshape(local, spins, 2, nvec, width)


def solution(mesh):
    placed = (
        P("cfg", None, None, None, ("space", "diag"), None),
        P("cfg", None, None, None, None, ("space", "diag"), None),
        P(),
        P(),
        P(("cfg", "space", "diag"), None, None, None, None),
        P(("space", "diag"), None),
    )
    return jax.shard_map(
        body,
        mesh=mesh,
        in_specs=placed,
        out_specs=P(("cfg", "space", "diag"), None, None, None, None),
        check_vma=False,
    )
```

```python
import functools
import math

import jax
import jax.numpy as jnp
from jax import lax
from jax.experimental import pallas as pl
from jax.experimental.pallas import tpu as pltpu
from jax.sharding import PartitionSpec as P

LX = 16
LY = 16
NDISP = 4
CHUNK = 16
MESH = pl.DeviceIdType.MESH
NT = (((1,), (1,)), ((), ()))
f32 = jnp.float32
bf16 = jnp.bfloat16


def elemental_kernel(
    dims, list_hbm, mom_hbm, spin_hbm, link_hbm, eig_hbm, tau_hbm, out_ref, mix_hbm,
    list_ref, mom_ref, spin_ref, link_ref,
    eig_ref, cos_ref, sin_ref, ar_ref, ai_ref, above, fields, plus, minus, tau_ref, mix_ref, lists, table,
    part1, recv1, own, early, part2, recv2, part3, recv3,
    small_local, link_local, e_local, t_local, m_local, v_send, v_recv, l_send, l_recv, l_local, s1, r1, s2, r2, s3, r3,
):
    nspace, ndiag, inner, local, slices, nvec, plane, factor = dims
    ndev = nspace * ndiag
    outer = nspace // inner
    space = lax.axis_index("space")
    core = lax.axis_index("diag")
    cfg = lax.axis_index("cfg")
    me = space * ndiag + core
    zpos = space // inner
    ypos = lax.rem(space, inner)

    def device(index):
        return (cfg, index // ndiag, lax.rem(index, ndiag))

    def e_copy(t):
        return pltpu.make_async_copy(eig_hbm.at[t], eig_ref.at[t], e_local.at[t])

    t_copy = pltpu.make_async_copy(tau_hbm, tau_ref, t_local)

    def m_copy(i):
        return pltpu.make_async_copy(mix_ref.at[i], mix_hbm.at[i], m_local.at[i])

    barrier = pltpu.get_barrier_semaphore()

    @pl.loop(1, ndev)
    def _(k):
        pl.semaphore_signal(
            barrier, inc=1, device_id=device(lax.rem(me + k, ndev)), device_id_type=MESH
        )

    small = [
        pltpu.make_async_copy(src, dst, small_local.at[k])
        for k, (src, dst) in enumerate(
            ((list_hbm, list_ref), (mom_hbm, mom_ref), (spin_hbm, spin_ref))
        )
    ]
    link_copy = pltpu.make_async_copy(link_hbm, link_ref, link_local)
    for copy in small:
        copy.start()
    link_copy.start()
    for t in range(slices):
        e_copy(t).start()
    t_copy.start()

    pl.semaphore_wait(barrier, ndev - 1)

    half = nvec // 2

    def v_copy(t, h):
        rows = pl.ds(pl.multiple_of(h * half, half), half)
        return pltpu.make_async_remote_copy(
            src_ref=eig_hbm.at[t, :, :, rows], dst_ref=above.at[t, :, :, rows],
            send_sem=v_send.at[t, h], recv_sem=v_recv.at[t, h],
            device_id=device(lax.rem(me + ndev - 1, ndev)), device_id_type=MESH,
        )

    def l_copy(k):
        return pltpu.make_async_remote_copy(
            src_ref=lists.at[0], dst_ref=lists.at[k],
            send_sem=l_send.at[k], recv_sem=l_recv.at[k],
            device_id=device(lax.rem(me + k, ndev)), device_id_type=MESH,
        )

    for h in range(2):
        v_copy(0, h).start()

    for copy in small:
        copy.wait()
    column = lax.broadcasted_iota(jnp.int32, (1, 128), 1)
    packed = jnp.zeros((1, 128), jnp.int32)
    for i in range(local):
        packed = jnp.where(column == i, list_ref[i, 0], packed)
    lists[0] = packed

    @pl.loop(1, ndev)
    def _(k):
        l_copy(k).start()

    for t in range(1, slices):
        for h in range(2):
            v_copy(t, h).start()

    nmom = mom_ref.shape[0]
    flat = lax.broadcasted_iota(jnp.int32, (1, plane), 1)
    xcoord = lax.rem(flat, LX).astype(f32)
    ycoord = lax.div(flat, LX).astype(f32)
    zcoord = lax.convert_element_type(me, f32)
    rows, hops = [], []
    for m in range(nmom):
        mom = [mom_ref[m, axis].astype(f32) for axis in range(3)]
        rows.append(
            2.0 * math.pi * (mom[0] * xcoord / LX + mom[1] * ycoord / LY + mom[2] * zcoord / ndev)
        )
        hops.append(jnp.full((1, nvec), math.pi, f32))
        for axis, size in enumerate((LX, LY, ndev)):
            hops.append(jnp.full((1, nvec), mom[axis] * (2.0 * math.pi / size), f32))
    angle = jnp.concatenate(rows, 0)
    cos_ref[...] = jnp.concatenate([jnp.cos(angle)] * 3, 1)
    sin_ref[...] = jnp.concatenate([jnp.sin(angle)] * 3, 1)
    hop = jnp.concatenate(hops, 0)
    plain = lax.rem(lax.broadcasted_iota(jnp.int32, hop.shape, 0), NDISP) == 0
    ar_ref[...] = jnp.where(plain, -1.0, jnp.cos(hop))
    ai_ref[...] = jnp.where(plain, 0.0, -jnp.sin(hop))

    lane = lax.broadcasted_iota(jnp.int32, (CHUNK, plane), 1)
    edge = lax.rem(lane, LX) == LX - 1

    def displace(t, direction, source, begin=0, size=nvec):
        @pl.loop(0, size // CHUNK)
        def _(i):
            rows = pl.multiple_of(begin + i * CHUNK, CHUNK)
            vec = []
            for p in range(2):
                line = []
                for c in range(3):
                    v = source[t, p, c, pl.ds(rows, CHUNK), :].astype(f32)
                    if direction == 0:
                        v = jnp.where(
                            edge, pltpu.roll(v, LX - 1, 1), pltpu.roll(v, plane - 1, 1)
                        )
                    elif direction == 1:
                        v = pltpu.roll(v, plane - LX, 1)
                    line.append(v)
                vec.append(line)
            for row in range(3):
                real = imag = None
                for col in range(3):
                    mr = link_ref[t, direction, 0, row, col]
                    mi = link_ref[t, direction, 1, row, col]
                    re = mr * vec[0][col] - mi * vec[1][col]
                    im = mr * vec[1][col] + mi * vec[0][col]
                    real = re if real is None else real + re
                    imag = im if imag is None else imag + im
                lanes = slice(row * plane, (row + 1) * plane)
                fields[t * NDISP + direction + 1, pl.ds(rows, CHUNK), lanes] = real.astype(bf16)
                fields[
                    t * NDISP + direction + 1, pl.ds(nvec + rows, CHUNK), lanes
                ] = imag.astype(bf16)

    def phases(t):
        @pl.loop(0, nvec // CHUNK)
        def _(i):
            rows = pl.multiple_of(i * CHUNK, CHUNK)
            for c in range(3):
                lanes = slice(c * plane, (c + 1) * plane)
                vr = eig_ref[t, 0, c, pl.ds(rows, CHUNK), :]
                vi = eig_ref[t, 1, c, pl.ds(rows, CHUNK), :]
                fields[t * NDISP, pl.ds(rows, CHUNK), lanes] = vr
                fields[t * NDISP, pl.ds(nvec + rows, CHUNK), lanes] = vi
                vr, vi = vr.astype(f32), vi.astype(f32)
                for m in range(nmom):
                    cosine = cos_ref[m:m + 1, lanes]
                    sine = sin_ref[m:m + 1, lanes]
                    a, b = cosine * vr, sine * vi
                    g, h = cosine * vi, sine * vr
                    plus[t * nmom + m, pl.ds(rows, CHUNK), lanes] = (a - b).astype(bf16)
                    plus[t * nmom + m, pl.ds(nvec + rows, CHUNK), lanes] = (g + h).astype(bf16)
                    minus[t * nmom + m, pl.ds(rows, CHUNK), lanes] = (a + b).astype(bf16)
                    minus[t * nmom + m, pl.ds(nvec + rows, CHUNK), lanes] = (g - h).astype(bf16)

    link_copy.wait()

    @pl.loop(0, slices)
    def _(t):
        e_copy(t).wait()
        displace(t, 0, eig_ref)
        displace(t, 1, eig_ref)
        phases(t)

    count, spins = tau_ref.shape[:2]

    def mix(i):
        q = lax.rem(list_ref[i, 2], count)
        g = list_ref[i, 1]

        @pl.loop(0, 2 * nvec // CHUNK)
        def _(n):
            rows = pl.multiple_of(n * CHUNK, CHUNK)
            tau = [tau_ref[q, s, pl.ds(rows, CHUNK), :].astype(f32) for s in range(spins)]
            for r in range(spins):
                mixed = spin_ref[r, 0, g] * tau[0]
                for s in range(1, spins):
                    mixed = mixed + spin_ref[r, s, g] * tau[s]
                mix_ref[i, r, pl.ds(rows, CHUNK), :] = mixed.astype(bf16)

        m_copy(i).start()

    @pl.loop(1, ndev)
    def _(k):
        l_copy(k).wait()

    to_smem = pltpu.make_async_copy(lists, table, l_local)
    to_smem.start()
    to_smem.wait()

    def entry_of(dest, i):
        return table[lax.rem(me + ndev - dest, ndev), 0, i]

    def item(entry):
        time = lax.div(entry, nmom * NDISP)
        m = lax.rem(lax.div(entry, NDISP), nmom)
        d = lax.rem(entry, NDISP)
        ar = ar_ref[pl.ds(m * NDISP + d, 1), :]
        ai = ai_ref[pl.ds(m * NDISP + d, 1), :]
        x = fields[time * NDISP + d]
        first = lax.dot_general(plus[time * nmom + m], x, NT, preferred_element_type=f32)
        second = lax.dot_general(x, minus[time * nmom + m], NT, preferred_element_type=f32)
        g1r = first[:nvec, :nvec] + first[nvec:, nvec:]
        g1i = first[:nvec, nvec:] - first[nvec:, :nvec]
        g2r = second[:nvec, :nvec] + second[nvec:, nvec:]
        g2i = second[:nvec, nvec:] - second[nvec:, :nvec]
        return (
            (g1r - (ar * g2r - ai * g2i)) * factor,
            (g1i - (ar * g2i + ai * g2r)) * factor,
        )

    levels = outer.bit_length() - 1

    def flip(l):
        size = 1 << l
        return zpos + size * (1 - 2 * lax.rem(zpos // size, 2))

    def away(r):
        row = zpos
        for l in range(levels):
            row = row + lax.rem(r // (1 << l), 2) * (flip(l) - zpos)
        return row

    def copy1(n, i):
        return pltpu.make_async_remote_copy(
            src_ref=part1.at[n, i], dst_ref=recv1.at[n, i], send_sem=s1.at[n, i], recv_sem=r1.at[n, i],
            device_id=(cfg, space, 1 - core), device_id_type=MESH,
        )

    def copy2(n, j, i):
        return pltpu.make_async_remote_copy(
            src_ref=part2.at[n, i], dst_ref=recv2.at[j, i], send_sem=s2.at[j, i], recv_sem=r2.at[j, i],
            device_id=(cfg, zpos * inner + (1 - ypos), core), device_id_type=MESH,
        )

    def copy3(r, i):
        row = flip((r & -r).bit_length() - 1)
        return pltpu.make_async_remote_copy(
            src_ref=part3.at[r, i], dst_ref=recv3.at[r, i], send_sem=s3.at[r, i], recv_sem=r3.at[r, i],
            device_id=(cfg, row * inner + ypos, core), device_id_type=MESH,
        )

    def unit(n):
        last = n == nspace - 1
        across = jnp.logical_or(n == 0, jnp.logical_and(lax.rem(n, 2) == 1, n < nspace - 1))
        j = jnp.where(across, (n + 1) // 2, jnp.where(last, outer - 1, n // 2 - 1))
        row = away(outer - 1 - j)
        return across, j, (row * inner + jnp.where(across, 1 - ypos, ypos)) * ndiag

    ahead = nspace - 3

    def stored(n):
        return jnp.logical_and(core > 0, n >= ahead)

    def found(n, dest, side, i):
        entry = entry_of(dest, i)
        m = lax.rem(lax.div(entry, NDISP), nmom)
        final = jnp.logical_and(
            lax.div(entry, nmom * NDISP) == slices - 1, lax.rem(entry, NDISP) == NDISP - 1
        )
        return jnp.where(final, 6 * local + m, ((n - ahead) * 2 + side) * local + i)

    def prepare(n):
        _, _, chip = unit(n)
        for side in range(2):
            for i in range(local):
                place = ((n - ahead) * 2 + side) * local + i
                dest = chip + (1 - core if side == 0 else core)
                early[place, 0], early[place, 1] = item(entry_of(dest, i))

    def complete(m):
        early[6 * local + m, 0], early[6 * local + m, 1] = item(
            ((slices - 1) * nmom + m) * NDISP + NDISP - 1
        )

    def give(n):
        _, _, chip = unit(n)

        @pl.when(stored(n))
        def _():
            for i in range(local):
                part1[n, i] = early[found(n, chip + (1 - core), 0, i)].astype(bf16)
                copy1(n, i).start()

        @pl.when(jnp.logical_not(stored(n)))
        def _():
            for i in range(local):
                real, imag = item(entry_of(chip + (1 - core), i))
                part1[n, i, 0] = real.astype(bf16)
                part1[n, i, 1] = imag.astype(bf16)
                copy1(n, i).start()

    def keep(n):
        _, _, chip = unit(n)

        @pl.when(stored(n))
        def _():
            for i in range(local):
                own[n, i] = early[found(n, chip + core, 1, i)]

        @pl.when(jnp.logical_not(stored(n)))
        def _():
            for i in range(local):
                own[n, i, 0], own[n, i, 1] = item(entry_of(chip + core, i))

    def join(n):
        across, j, _ = unit(n)
        for i in range(local):
            copy1(n, i).wait_recv()
            total = own[n, i] + recv1[n, i].astype(f32)
            own[n, i] = total
            part2[n, i] = total.astype(bf16)

            @pl.when(across)
            def _():
                copy2(n, j, i).start()

    def collect_row(r, i):
        j = outer - 1 - r
        n = nspace - 1 if r == 0 else 2 * j + 2
        sources = [r + (1 << l) for l in range(levels) if r % (2 << l) == 0]
        copy2(0, j, i).wait()
        for source in sources:
            copy3(source, i).wait()
        total = own[n, i] + recv2[j, i].astype(f32)
        for source in sources:
            total = total + recv3[source, i].astype(f32)
        if r == 0:
            out_ref[i] = total.astype(bf16)
        else:
            part3[r, i] = total.astype(bf16)
            copy3(r, i).start()

    def collect(q):
        for r in range(outer - 1, -1, -1):
            @pl.when(outer - 1 - q // local == r)
            def _():
                collect_row(r, lax.rem(q, local))

    def halo(t):
        for h in range(2):
            v_copy(t, h).wait_recv()
            displace(t, 2, above, h * half, half)

    @pl.loop(0, slices - 1)
    def _(t):
        halo(t)

    @pl.when(core > 0)
    def _():
        @pl.loop(ahead, nspace)
        def _(n):
            prepare(n)

    halo(slices - 1)

    @pl.loop(0, 3 * nspace)
    def _(k):
        first_core = core == 0
        kind = jnp.where(
            first_core, jnp.where(k < nspace, 0, 1 + lax.rem(k - nspace + 2 * nspace, 2)), jnp.where(k < 3, lax.rem(k + 1, 3), lax.rem(k, 3))
        )
        n = jnp.where(first_core, jnp.where(k < nspace, k, (k - nspace + 2 * nspace) // 2 - nspace), k // 3)

        @pl.when(jnp.logical_and(kind == 0, jnp.logical_and(core > 0, n == ahead)))
        def _():
            @pl.loop(0, nmom // 2)
            def _(m):
                complete(2 * m)
                complete(2 * m + 1)

        @pl.when(kind == 0)
        def _():
            give(n)

        @pl.when(kind == 1)
        def _():
            keep(n)

        @pl.when(kind == 2)
        def _():
            join(n)

            @pl.when(n == jnp.where(first_core, 1, nspace - 2))
            def _():
                t_copy.wait()
                mix(0)

            @pl.when(n == jnp.where(first_core, 4, nspace - 1))
            def _():
                mix(1)

            first = jnp.where(n == 5, 2, n - 2)
            stop = jnp.where(jnp.logical_or(n < 2, n == 4), first, n - 1)

            @pl.loop(first, stop)
            def _(q):
                collect(q)

    @pl.loop(nspace - 2, (outer - 1) * local)
    def _(q):
        collect(q)

    for i in range(local):
        collect_row(0, i)

    @pl.loop(0, nspace)
    def _(n):
        for i in range(local):
            copy1(n, i).wait_send()

    for t in range(slices):
        for h in range(2):
            v_copy(t, h).wait_send()
    for i in range(local):
        m_copy(i).wait()


def diagram_kernel(elem_ref, mix_ref, out_hbm, out_ref, store_sem):
    local, spins = mix_ref.shape[:2]
    group = 1

    def store(i, h):
        some = pl.ds(h * group, group)
        return pltpu.make_async_copy(out_ref.at[i, some], out_hbm.at[i, some], store_sem.at[i, h])

    pieces = [(i, h) for i in range(local) for h in range(spins // group)]
    for i, h in pieces:
        if h == 0:
            er, ei = elem_ref[i, 0], elem_ref[i, 1]
            square = jnp.concatenate(
                [jnp.concatenate([er, -ei], 1), jnp.concatenate([ei, er], 1)], 0
            )
        for r in range(h * group, (h + 1) * group):
            out_ref[i, r] = jnp.dot(
                square, mix_ref[i, r], preferred_element_type=f32
            ).astype(bf16)
        store(i, h).start()
    for i, h in pieces:
        store(i, h).wait()


def body(eigvecs, gauge_links, momenta, spin_mix, perambulators, contraction_list):
    slices, _, colors, nvec, depth, plane = eigvecs.shape
    assert depth == 1 and colors == 3
    nspace, ndiag = lax.axis_size("space"), lax.axis_size("diag")
    inner = 2
    outer = nspace // inner
    assert ndiag == 2 and inner * outer == nspace
    assert momenta.shape[0] % 2 == 0 and outer >= 4 and outer & (outer - 1) == 0 and contraction_list.shape[0] == 2
    ndev = nspace * ndiag
    scale = 1.0 / math.sqrt(3 * plane * ndev)
    nmom = momenta.shape[0]
    local = contraction_list.shape[0]
    count, spins = perambulators.shape[:2]
    width = perambulators.shape[4]
    vmem = pl.BlockSpec(memory_space=pltpu.VMEM)
    hbm = pl.BlockSpec(memory_space=pltpu.HBM)
    tile = (local, 2, nvec, nvec)
    field = (2 * nvec, 3 * plane)
    dma = pltpu.SemaphoreType.DMA
    elem, mixed = pl.pallas_call(
        functools.partial(
            elemental_kernel,
            (nspace, ndiag, inner, local, slices, nvec, plane, 0.5 * scale),
        ),
        out_shape=(
            jax.ShapeDtypeStruct(tile, bf16),
            jax.ShapeDtypeStruct((local, spins, 2 * nvec, width), bf16),
        ),
        in_specs=[hbm] * 6,
        out_specs=(vmem, pl.BlockSpec(memory_space=pl.ANY)),
        scratch_shapes=[
            pltpu.SMEM(contraction_list.shape, jnp.int32),
            pltpu.SMEM(momenta.shape, jnp.int32),
            pltpu.SMEM((spins, spins, spin_mix.shape[0]), f32),
            pltpu.VMEM(gauge_links.shape, f32),
            pltpu.VMEM((slices, 2, 3, nvec, plane), bf16),
            pltpu.VMEM((nmom, 3 * plane), f32),
            pltpu.VMEM((nmom, 3 * plane), f32),
            pltpu.VMEM((nmom * NDISP, nvec), f32),
            pltpu.VMEM((nmom * NDISP, nvec), f32),
            pltpu.VMEM((slices, 2, 3, nvec, plane), bf16),
            pltpu.VMEM((slices * NDISP,) + field, bf16),
            pltpu.VMEM((slices * nmom,) + field, bf16),
            pltpu.VMEM((slices * nmom,) + field, bf16),
            pltpu.VMEM((count, spins, 2 * nvec, width), bf16),
            pltpu.VMEM((local, spins, 2 * nvec, width), bf16),
            pltpu.VMEM((ndev, 1, 128), jnp.int32),
            pltpu.SMEM((ndev, 1, 128), jnp.int32),
            pltpu.VMEM((nspace,) + tile, bf16),
            pltpu.VMEM((nspace,) + tile, bf16),
            pltpu.VMEM((nspace,) + tile, f32),
            pltpu.VMEM((6 * local + nmom,) + tile[1:], f32),
            pltpu.VMEM((nspace,) + tile, bf16),
            pltpu.VMEM((outer,) + tile, bf16),
            pltpu.VMEM((outer,) + tile, bf16),
            pltpu.VMEM((outer,) + tile, bf16),
            dma((3,)), dma, dma((slices,)), dma, dma((local,)), dma((slices, 2)), dma((slices, 2)),
            dma((ndev,)), dma((ndev,)), dma,
            dma((nspace, local)), dma((nspace, local)),
            dma((outer, local)), dma((outer, local)),
            dma((outer, local)), dma((outer, local)),
        ],
        compiler_params=pltpu.CompilerParams(
            collective_id=0, has_side_effects=True, vmem_limit_bytes=44 * 1024 * 1024
        ),
    )(*(
        pltpu.with_memory_space_constraint(x, pltpu.HBM) for x in (
            contraction_list, momenta, spin_mix.transpose(1, 2, 0), gauge_links,
            eigvecs.reshape(slices, 2, 3, nvec, plane),
            perambulators.reshape(count, spins, 2 * nvec, width),
        )
    ))
    out = pl.pallas_call(
        diagram_kernel,
        in_specs=[vmem, vmem],
        out_specs=hbm,
        out_shape=jax.ShapeDtypeStruct((local, spins, 2 * nvec, width), bf16),
        scratch_shapes=[
            pltpu.VMEM((local, spins, 2 * nvec, width), bf16), dma((local, spins)),
        ],
        compiler_params=pltpu.CompilerParams(vmem_limit_bytes=24 * 1024 * 1024),
    )(elem, mixed)
    return out.reshape(local, spins, 2, nvec, width)


def solution(mesh):
    placed = (
        P("cfg", None, None, None, ("space", "diag"), None),
        P("cfg", None, None, None, None, ("space", "diag"), None),
        P(),
        P(),
        P(("cfg", "space", "diag"), None, None, None, None),
        P(("space", "diag"), None),
    )
    return jax.shard_map(
        body,
        mesh=mesh,
        in_specs=placed,
        out_specs=P(("cfg", "space", "diag"), None, None, None, None),
        check_vma=False,
    )
```

```python
import functools
import math

import jax
import jax.numpy as jnp
from jax import lax
from jax.experimental import pallas as pl
from jax.experimental.pallas import tpu as pltpu
from jax.sharding import PartitionSpec as P

LX = 16
LY = 16
NDISP = 4
CHUNK = 16
MESH = pl.DeviceIdType.MESH
NT = (((1,), (1,)), ((), ()))
f32 = jnp.float32
bf16 = jnp.bfloat16


def elemental_kernel(
    dims, list_hbm, mom_hbm, spin_hbm, link_hbm, eig_hbm, tau_hbm, out_ref, mix_hbm,
    list_ref, mom_ref, spin_ref, link_ref,
    eig_ref, cos_ref, sin_ref, ar_ref, ai_ref, above, fields, plus, minus, tau_ref, mix_ref, lists, table,
    part1, recv1, own, early, part2, recv2, part3, recv3,
    small_local, link_local, e_local, t_local, m_local, v_send, v_recv, l_send, l_recv, l_local, s1, r1, s2, r2, s3, r3,
):
    nspace, ndiag, inner, local, slices, nvec, plane, factor = dims
    ndev = nspace * ndiag
    outer = nspace // inner
    space = lax.axis_index("space")
    core = lax.axis_index("diag")
    cfg = lax.axis_index("cfg")
    me = space * ndiag + core
    zpos = space // inner
    ypos = lax.rem(space, inner)

    def device(index):
        return (cfg, index // ndiag, lax.rem(index, ndiag))

    def e_copy(t):
        return pltpu.make_async_copy(eig_hbm.at[t], eig_ref.at[t], e_local.at[t])

    t_copy = pltpu.make_async_copy(tau_hbm, tau_ref, t_local)

    def m_copy(i):
        return pltpu.make_async_copy(mix_ref.at[i], mix_hbm.at[i], m_local.at[i])

    barrier = pltpu.get_barrier_semaphore()

    @pl.loop(1, ndev)
    def _(k):
        pl.semaphore_signal(
            barrier, inc=1, device_id=device(lax.rem(me + k, ndev)), device_id_type=MESH
        )

    small = [
        pltpu.make_async_copy(src, dst, small_local.at[k])
        for k, (src, dst) in enumerate(
            ((list_hbm, list_ref), (mom_hbm, mom_ref), (spin_hbm, spin_ref))
        )
    ]
    link_copy = pltpu.make_async_copy(link_hbm, link_ref, link_local)
    for copy in small:
        copy.start()
    link_copy.start()
    for t in range(slices):
        e_copy(t).start()
    t_copy.start()

    pl.semaphore_wait(barrier, ndev - 1)

    half = nvec // 2

    def v_copy(t, h):
        rows = pl.ds(pl.multiple_of(h * half, half), half)
        return pltpu.make_async_remote_copy(
            src_ref=eig_hbm.at[t, :, :, rows], dst_ref=above.at[t, :, :, rows],
            send_sem=v_send.at[t, h], recv_sem=v_recv.at[t, h],
            device_id=device(lax.rem(me + ndev - 1, ndev)), device_id_type=MESH,
        )

    def l_copy(k):
        return pltpu.make_async_remote_copy(
            src_ref=lists.at[0], dst_ref=lists.at[k],
            send_sem=l_send.at[k], recv_sem=l_recv.at[k],
            device_id=device(lax.rem(me + k, ndev)), device_id_type=MESH,
        )

    for h in range(2):
        v_copy(0, h).start()

    for copy in small:
        copy.wait()
    column = lax.broadcasted_iota(jnp.int32, (1, 128), 1)
    packed = jnp.zeros((1, 128), jnp.int32)
    for i in range(local):
        packed = jnp.where(column == i, list_ref[i, 0], packed)
    lists[0] = packed

    @pl.loop(1, ndev)
    def _(k):
        l_copy(k).start()

    for t in range(1, slices):
        for h in range(2):
            v_copy(t, h).start()

    nmom = mom_ref.shape[0]
    flat = lax.broadcasted_iota(jnp.int32, (1, plane), 1)
    xcoord = lax.rem(flat, LX).astype(f32)
    ycoord = lax.div(flat, LX).astype(f32)
    zcoord = lax.convert_element_type(me, f32)
    rows, hops = [], []
    for m in range(nmom):
        mom = [mom_ref[m, axis].astype(f32) for axis in range(3)]
        rows.append(
            2.0 * math.pi * (mom[0] * xcoord / LX + mom[1] * ycoord / LY + mom[2] * zcoord / ndev)
        )
        hops.append(jnp.full((1, nvec), math.pi, f32))
        for axis, size in enumerate((LX, LY, ndev)):
            hops.append(jnp.full((1, nvec), mom[axis] * (2.0 * math.pi / size), f32))
    angle = jnp.concatenate(rows, 0)
    cos_ref[...] = jnp.concatenate([jnp.cos(angle)] * 3, 1)
    sin_ref[...] = jnp.concatenate([jnp.sin(angle)] * 3, 1)
    hop = jnp.concatenate(hops, 0)
    plain = lax.rem(lax.broadcasted_iota(jnp.int32, hop.shape, 0), NDISP) == 0
    ar_ref[...] = jnp.where(plain, -1.0, jnp.cos(hop))
    ai_ref[...] = jnp.where(plain, 0.0, -jnp.sin(hop))

    lane = lax.broadcasted_iota(jnp.int32, (CHUNK, plane), 1)
    edge = lax.rem(lane, LX) == LX - 1

    def displace(t, direction, source, begin=0, size=nvec):
        @pl.loop(0, size // CHUNK)
        def _(i):
            rows = pl.multiple_of(begin + i * CHUNK, CHUNK)
            vec = []
            for p in range(2):
                line = []
                for c in range(3):
                    v = source[t, p, c, pl.ds(rows, CHUNK), :].astype(f32)
                    if direction == 0:
                        v = jnp.where(
                            edge, pltpu.roll(v, LX - 1, 1), pltpu.roll(v, plane - 1, 1)
                        )
                    elif direction == 1:
                        v = pltpu.roll(v, plane - LX, 1)
                    line.append(v)
                vec.append(line)
            for row in range(3):
                real = imag = None
                for col in range(3):
                    mr = link_ref[t, direction, 0, row, col]
                    mi = link_ref[t, direction, 1, row, col]
                    re = mr * vec[0][col] - mi * vec[1][col]
                    im = mr * vec[1][col] + mi * vec[0][col]
                    real = re if real is None else real + re
                    imag = im if imag is None else imag + im
                lanes = slice(row * plane, (row + 1) * plane)
                fields[t * NDISP + direction + 1, pl.ds(rows, CHUNK), lanes] = real.astype(bf16)
                fields[
                    t * NDISP + direction + 1, pl.ds(nvec + rows, CHUNK), lanes
                ] = imag.astype(bf16)

    def phases(t):
        @pl.loop(0, nvec // CHUNK)
        def _(i):
            rows = pl.multiple_of(i * CHUNK, CHUNK)
            for c in range(3):
                lanes = slice(c * plane, (c + 1) * plane)
                vr = eig_ref[t, 0, c, pl.ds(rows, CHUNK), :]
                vi = eig_ref[t, 1, c, pl.ds(rows, CHUNK), :]
                fields[t * NDISP, pl.ds(rows, CHUNK), lanes] = vr
                fields[t * NDISP, pl.ds(nvec + rows, CHUNK), lanes] = vi
                vr, vi = vr.astype(f32), vi.astype(f32)
                for m in range(nmom):
                    cosine = cos_ref[m:m + 1, lanes]
                    sine = sin_ref[m:m + 1, lanes]
                    a, b = cosine * vr, sine * vi
                    g, h = cosine * vi, sine * vr
                    plus[t * nmom + m, pl.ds(rows, CHUNK), lanes] = (a - b).astype(bf16)
                    plus[t * nmom + m, pl.ds(nvec + rows, CHUNK), lanes] = (g + h).astype(bf16)
                    minus[t * nmom + m, pl.ds(rows, CHUNK), lanes] = (a + b).astype(bf16)
                    minus[t * nmom + m, pl.ds(nvec + rows, CHUNK), lanes] = (g - h).astype(bf16)

    link_copy.wait()

    @pl.loop(0, slices)
    def _(t):
        e_copy(t).wait()
        displace(t, 0, eig_ref)
        displace(t, 1, eig_ref)
        phases(t)

    count, spins = tau_ref.shape[:2]

    def mix(i):
        q = lax.rem(list_ref[i, 2], count)
        g = list_ref[i, 1]

        @pl.loop(0, 2 * nvec // CHUNK)
        def _(n):
            rows = pl.multiple_of(n * CHUNK, CHUNK)
            tau = [tau_ref[q, s, pl.ds(rows, CHUNK), :].astype(f32) for s in range(spins)]
            for r in range(spins):
                mixed = spin_ref[r, 0, g] * tau[0]
                for s in range(1, spins):
                    mixed = mixed + spin_ref[r, s, g] * tau[s]
                mix_ref[i, r, pl.ds(rows, CHUNK), :] = mixed.astype(bf16)

        m_copy(i).start()

    @pl.loop(1, ndev)
    def _(k):
        l_copy(k).wait()

    to_smem = pltpu.make_async_copy(lists, table, l_local)
    to_smem.start()
    to_smem.wait()

    def entry_of(dest, i):
        return table[lax.rem(me + ndev - dest, ndev), 0, i]

    def item(entry):
        time = lax.div(entry, nmom * NDISP)
        m = lax.rem(lax.div(entry, NDISP), nmom)
        d = lax.rem(entry, NDISP)
        ar = ar_ref[pl.ds(m * NDISP + d, 1), :]
        ai = ai_ref[pl.ds(m * NDISP + d, 1), :]
        x = fields[time * NDISP + d]
        first = lax.dot_general(plus[time * nmom + m], x, NT, preferred_element_type=f32)
        second = lax.dot_general(x, minus[time * nmom + m], NT, preferred_element_type=f32)
        g1r = first[:nvec, :nvec] + first[nvec:, nvec:]
        g1i = first[:nvec, nvec:] - first[nvec:, :nvec]
        g2r = second[:nvec, :nvec] + second[nvec:, nvec:]
        g2i = second[:nvec, nvec:] - second[nvec:, :nvec]
        return (
            (g1r - (ar * g2r - ai * g2i)) * factor,
            (g1i - (ar * g2i + ai * g2r)) * factor,
        )

    levels = outer.bit_length() - 1

    def flip(l):
        size = 1 << l
        return zpos + size * (1 - 2 * lax.rem(zpos // size, 2))

    def away(r):
        row = zpos
        for l in range(levels):
            row = row + lax.rem(r // (1 << l), 2) * (flip(l) - zpos)
        return row

    def copy1(n, i):
        return pltpu.make_async_remote_copy(
            src_ref=part1.at[n, i], dst_ref=recv1.at[n, i], send_sem=s1.at[n, i], recv_sem=r1.at[n, i],
            device_id=(cfg, space, 1 - core), device_id_type=MESH,
        )

    def copy2(n, j, i):
        return pltpu.make_async_remote_copy(
            src_ref=part2.at[n, i], dst_ref=recv2.at[j, i], send_sem=s2.at[j, i], recv_sem=r2.at[j, i],
            device_id=(cfg, zpos * inner + (1 - ypos), core), device_id_type=MESH,
        )

    def copy3(r, i):
        row = flip((r & -r).bit_length() - 1)
        return pltpu.make_async_remote_copy(
            src_ref=part3.at[r, i], dst_ref=recv3.at[r, i], send_sem=s3.at[r, i], recv_sem=r3.at[r, i],
            device_id=(cfg, row * inner + ypos, core), device_id_type=MESH,
        )

    def unit(n):
        last = n == nspace - 1
        across = jnp.logical_or(n == 0, jnp.logical_and(lax.rem(n, 2) == 1, n < nspace - 1))
        j = jnp.where(across, (n + 1) // 2, jnp.where(last, outer - 1, n // 2 - 1))
        row = away(outer - 1 - j)
        return across, j, (row * inner + jnp.where(across, 1 - ypos, ypos)) * ndiag

    ahead = nspace - 3

    def stored(n):
        return jnp.logical_and(core > 0, n >= ahead)

    def found(n, dest, side, i):
        entry = entry_of(dest, i)
        m = lax.rem(lax.div(entry, NDISP), nmom)
        final = jnp.logical_and(
            lax.div(entry, nmom * NDISP) == slices - 1, lax.rem(entry, NDISP) == NDISP - 1
        )
        return jnp.where(final, 6 * local + m, ((n - ahead) * 2 + side) * local + i)

    def prepare(n):
        _, _, chip = unit(n)
        for side in range(2):
            for i in range(local):
                place = ((n - ahead) * 2 + side) * local + i
                dest = chip + (1 - core if side == 0 else core)
                early[place, 0], early[place, 1] = item(entry_of(dest, i))

    def complete(m):
        early[6 * local + m, 0], early[6 * local + m, 1] = item(
            ((slices - 1) * nmom + m) * NDISP + NDISP - 1
        )

    def give(n):
        _, _, chip = unit(n)

        @pl.when(stored(n))
        def _():
            for i in range(local):
                part1[n, i] = early[found(n, chip + (1 - core), 0, i)].astype(bf16)
                copy1(n, i).start()

        @pl.when(jnp.logical_not(stored(n)))
        def _():
            for i in range(local):
                real, imag = item(entry_of(chip + (1 - core), i))
                part1[n, i, 0] = real.astype(bf16)
                part1[n, i, 1] = imag.astype(bf16)
                copy1(n, i).start()

    def keep(n):
        _, _, chip = unit(n)

        @pl.when(stored(n))
        def _():
            for i in range(local):
                own[n, i] = early[found(n, chip + core, 1, i)]

        @pl.when(jnp.logical_not(stored(n)))
        def _():
            for i in range(local):
                own[n, i, 0], own[n, i, 1] = item(entry_of(chip + core, i))

    def join(n):
        across, j, _ = unit(n)
        for i in range(local):
            copy1(n, i).wait_recv()
            total = own[n, i] + recv1[n, i].astype(f32)
            own[n, i] = total
            part2[n, i] = total.astype(bf16)

            @pl.when(across)
            def _():
                copy2(n, j, i).start()

    def collect_row(r, i):
        j = outer - 1 - r
        n = nspace - 1 if r == 0 else 2 * j + 2
        sources = [r + (1 << l) for l in range(levels) if r % (2 << l) == 0]
        copy2(0, j, i).wait()
        for source in sources:
            copy3(source, i).wait()
        total = own[n, i] + recv2[j, i].astype(f32)
        for source in sources:
            total = total + recv3[source, i].astype(f32)
        if r == 0:
            out_ref[i] = total.astype(bf16)
        else:
            part3[r, i] = total.astype(bf16)
            copy3(r, i).start()

    def collect(q):
        for r in range(outer - 1, -1, -1):
            @pl.when(outer - 1 - q // local == r)
            def _():
                collect_row(r, lax.rem(q, local))

    def halo(t):
        for h in range(2):
            v_copy(t, h).wait_recv()
            displace(t, 2, above, h * half, half)

    @pl.loop(0, slices - 1)
    def _(t):
        halo(t)

    @pl.when(core > 0)
    def _():
        @pl.loop(ahead, nspace)
        def _(n):
            prepare(n)

    halo(slices - 1)

    @pl.loop(0, 3 * nspace)
    def _(k):
        first_core = core == 0
        kind = jnp.where(
            first_core, jnp.where(k < nspace, 0, 1 + lax.rem(k - nspace + 2 * nspace, 2)), jnp.where(k < 3, lax.rem(k + 1, 3), lax.rem(k, 3))
        )
        n = jnp.where(first_core, jnp.where(k < nspace, k, (k - nspace + 2 * nspace) // 2 - nspace), k // 3)

        @pl.when(jnp.logical_and(kind == 0, jnp.logical_and(core > 0, n == ahead)))
        def _():
            @pl.loop(0, nmom // 2)
            def _(m):
                complete(2 * m)
                complete(2 * m + 1)

        @pl.when(kind == 0)
        def _():
            give(n)

        @pl.when(kind == 1)
        def _():
            keep(n)

        @pl.when(kind == 2)
        def _():
            join(n)

            waits = jnp.logical_not(first_core)
            first = jnp.where(jnp.logical_and(waits, n == 5), 2, n - 2)
            stop = jnp.where(
                jnp.logical_or(n < 2, jnp.logical_and(waits, n == 4)), first, n - 1
            )

            @pl.loop(first, stop)
            def _(q):
                collect(q)

            @pl.when(n == jnp.where(first_core, 1, nspace - 1))
            def _():
                t_copy.wait()
                mix(0)

            @pl.when(n == jnp.where(first_core, 3, nspace - 1))
            def _():
                mix(1)

    @pl.loop(nspace - 2, (outer - 1) * local)
    def _(q):
        collect(q)

    for i in range(local):
        collect_row(0, i)

    @pl.loop(0, nspace)
    def _(n):
        for i in range(local):
            copy1(n, i).wait_send()

    for t in range(slices):
        for h in range(2):
            v_copy(t, h).wait_send()
    for i in range(local):
        m_copy(i).wait()


def diagram_kernel(elem_ref, mix_ref, out_hbm, out_ref, store_sem):
    local, spins = mix_ref.shape[:2]
    group = 1

    def store(i, h):
        some = pl.ds(h * group, group)
        return pltpu.make_async_copy(out_ref.at[i, some], out_hbm.at[i, some], store_sem.at[i, h])

    pieces = [(i, h) for i in range(local) for h in range(spins // group)]
    for i, h in pieces:
        if h == 0:
            er, ei = elem_ref[i, 0], elem_ref[i, 1]
            square = jnp.concatenate(
                [jnp.concatenate([er, -ei], 1), jnp.concatenate([ei, er], 1)], 0
            )
        for r in range(h * group, (h + 1) * group):
            out_ref[i, r] = jnp.dot(
                square, mix_ref[i, r], preferred_element_type=f32
            ).astype(bf16)
        store(i, h).start()
    for i, h in pieces:
        store(i, h).wait()


def body(eigvecs, gauge_links, momenta, spin_mix, perambulators, contraction_list):
    slices, _, colors, nvec, depth, plane = eigvecs.shape
    assert depth == 1 and colors == 3
    nspace, ndiag = lax.axis_size("space"), lax.axis_size("diag")
    inner = 2
    outer = nspace // inner
    assert ndiag == 2 and inner * outer == nspace
    assert momenta.shape[0] % 2 == 0 and outer >= 4 and outer & (outer - 1) == 0 and contraction_list.shape[0] == 2
    ndev = nspace * ndiag
    scale = 1.0 / math.sqrt(3 * plane * ndev)
    nmom = momenta.shape[0]
    local = contraction_list.shape[0]
    count, spins = perambulators.shape[:2]
    width = perambulators.shape[4]
    vmem = pl.BlockSpec(memory_space=pltpu.VMEM)
    hbm = pl.BlockSpec(memory_space=pltpu.HBM)
    tile = (local, 2, nvec, nvec)
    field = (2 * nvec, 3 * plane)
    dma = pltpu.SemaphoreType.DMA
    elem, mixed = pl.pallas_call(
        functools.partial(
            elemental_kernel,
            (nspace, ndiag, inner, local, slices, nvec, plane, 0.5 * scale),
        ),
        out_shape=(
            jax.ShapeDtypeStruct(tile, bf16),
            jax.ShapeDtypeStruct((local, spins, 2 * nvec, width), bf16),
        ),
        in_specs=[hbm] * 6,
        out_specs=(vmem, pl.BlockSpec(memory_space=pl.ANY)),
        scratch_shapes=[
            pltpu.SMEM(contraction_list.shape, jnp.int32),
            pltpu.SMEM(momenta.shape, jnp.int32),
            pltpu.SMEM((spins, spins, spin_mix.shape[0]), f32),
            pltpu.VMEM(gauge_links.shape, f32),
            pltpu.VMEM((slices, 2, 3, nvec, plane), bf16),
            pltpu.VMEM((nmom, 3 * plane), f32),
            pltpu.VMEM((nmom, 3 * plane), f32),
            pltpu.VMEM((nmom * NDISP, nvec), f32),
            pltpu.VMEM((nmom * NDISP, nvec), f32),
            pltpu.VMEM((slices, 2, 3, nvec, plane), bf16),
            pltpu.VMEM((slices * NDISP,) + field, bf16),
            pltpu.VMEM((slices * nmom,) + field, bf16),
            pltpu.VMEM((slices * nmom,) + field, bf16),
            pltpu.VMEM((count, spins, 2 * nvec, width), bf16),
            pltpu.VMEM((local, spins, 2 * nvec, width), bf16),
            pltpu.VMEM((ndev, 1, 128), jnp.int32),
            pltpu.SMEM((ndev, 1, 128), jnp.int32),
            pltpu.VMEM((nspace,) + tile, bf16),
            pltpu.VMEM((nspace,) + tile, bf16),
            pltpu.VMEM((nspace,) + tile, f32),
            pltpu.VMEM((6 * local + nmom,) + tile[1:], f32),
            pltpu.VMEM((nspace,) + tile, bf16),
            pltpu.VMEM((outer,) + tile, bf16),
            pltpu.VMEM((outer,) + tile, bf16),
            pltpu.VMEM((outer,) + tile, bf16),
            dma((3,)), dma, dma((slices,)), dma, dma((local,)), dma((slices, 2)), dma((slices, 2)),
            dma((ndev,)), dma((ndev,)), dma,
            dma((nspace, local)), dma((nspace, local)),
            dma((outer, local)), dma((outer, local)),
            dma((outer, local)), dma((outer, local)),
        ],
        compiler_params=pltpu.CompilerParams(
            collective_id=0, has_side_effects=True, vmem_limit_bytes=44 * 1024 * 1024
        ),
    )(*(
        pltpu.with_memory_space_constraint(x, pltpu.HBM) for x in (
            contraction_list, momenta, spin_mix.transpose(1, 2, 0), gauge_links,
            eigvecs.reshape(slices, 2, 3, nvec, plane),
            perambulators.reshape(count, spins, 2 * nvec, width),
        )
    ))
    out = pl.pallas_call(
        diagram_kernel,
        in_specs=[vmem, vmem],
        out_specs=hbm,
        out_shape=jax.ShapeDtypeStruct((local, spins, 2 * nvec, width), bf16),
        scratch_shapes=[
            pltpu.VMEM((local, spins, 2 * nvec, width), bf16), dma((local, spins)),
        ],
        compiler_params=pltpu.CompilerParams(vmem_limit_bytes=24 * 1024 * 1024),
    )(elem, mixed)
    return out.reshape(local, spins, 2, nvec, width)


def solution(mesh):
    placed = (
        P("cfg", None, None, None, ("space", "diag"), None),
        P("cfg", None, None, None, None, ("space", "diag"), None),
        P(),
        P(),
        P(("cfg", "space", "diag"), None, None, None, None),
        P(("space", "diag"), None),
    )
    return jax.shard_map(
        body,
        mesh=mesh,
        in_specs=placed,
        out_specs=P(("cfg", "space", "diag"), None, None, None, None),
        check_vma=False,
    )
```

```python
import functools
import math

import jax
import jax.numpy as jnp
from jax import lax
from jax.experimental import pallas as pl
from jax.experimental.pallas import tpu as pltpu
from jax.sharding import PartitionSpec as P

LX = 16
LY = 16
NDISP = 4
CHUNK = 16
MESH = pl.DeviceIdType.MESH
NT = (((1,), (1,)), ((), ()))
f32 = jnp.float32
bf16 = jnp.bfloat16


def elemental_kernel(
    dims, list_hbm, mom_hbm, spin_hbm, link_hbm, eig_hbm, tau_hbm, out_ref, mix_hbm,
    list_ref, mom_ref, spin_ref, link_ref,
    eig_ref, cos_ref, sin_ref, ar_ref, ai_ref, above, fields, plus, minus, tau_ref, mix_ref, lists, table,
    part1, recv1, own, early, part2, recv2, part3, recv3,
    small_local, link_local, e_local, t_local, m_local, v_send, v_recv, l_send, l_recv, l_local, s1, r1, s2, r2, s3, r3,
):
    nspace, ndiag, inner, local, slices, nvec, plane, factor = dims
    ndev = nspace * ndiag
    outer = nspace // inner
    space = lax.axis_index("space")
    core = lax.axis_index("diag")
    cfg = lax.axis_index("cfg")
    me = space * ndiag + core
    zpos = space // inner
    ypos = lax.rem(space, inner)

    def device(index):
        return (cfg, index // ndiag, lax.rem(index, ndiag))

    def e_copy(t):
        return pltpu.make_async_copy(eig_hbm.at[t], eig_ref.at[t], e_local.at[t])

    t_copy = pltpu.make_async_copy(tau_hbm, tau_ref, t_local)

    def m_copy(i):
        return pltpu.make_async_copy(mix_ref.at[i], mix_hbm.at[i], m_local.at[i])

    barrier = pltpu.get_barrier_semaphore()

    @pl.loop(1, ndev)
    def _(k):
        pl.semaphore_signal(
            barrier, inc=1, device_id=device(lax.rem(me + k, ndev)), device_id_type=MESH
        )

    small = [
        pltpu.make_async_copy(src, dst, small_local.at[k])
        for k, (src, dst) in enumerate(
            ((list_hbm, list_ref), (mom_hbm, mom_ref), (spin_hbm, spin_ref))
        )
    ]
    link_copy = pltpu.make_async_copy(link_hbm, link_ref, link_local)
    for copy in small:
        copy.start()
    link_copy.start()
    for t in range(slices):
        e_copy(t).start()
    t_copy.start()

    pl.semaphore_wait(barrier, ndev - 1)

    def v_copy(t, h, pieces=2):
        size = nvec // pieces
        rows = pl.ds(pl.multiple_of(h * size, size), size)
        return pltpu.make_async_remote_copy(
            src_ref=eig_hbm.at[t, :, :, rows], dst_ref=above.at[t, :, :, rows],
            send_sem=v_send.at[t, h], recv_sem=v_recv.at[t, h],
            device_id=device(lax.rem(me + ndev - 1, ndev)), device_id_type=MESH,
        )

    def l_copy(k):
        return pltpu.make_async_remote_copy(
            src_ref=lists.at[0], dst_ref=lists.at[k],
            send_sem=l_send.at[k], recv_sem=l_recv.at[k],
            device_id=device(lax.rem(me + k, ndev)), device_id_type=MESH,
        )

    for h in range(2):
        v_copy(0, h).start()

    for copy in small:
        copy.wait()
    column = lax.broadcasted_iota(jnp.int32, (1, 128), 1)
    packed = jnp.zeros((1, 128), jnp.int32)
    for i in range(local):
        packed = jnp.where(column == i, list_ref[i, 0], packed)
    lists[0] = packed

    @pl.loop(1, ndev)
    def _(k):
        l_copy(k).start()

    for t in range(1, slices - 1):
        for h in range(2):
            v_copy(t, h).start()
    for h in range(4):
        v_copy(slices - 1, h, 4).start()

    nmom = mom_ref.shape[0]
    flat = lax.broadcasted_iota(jnp.int32, (1, plane), 1)
    xcoord = lax.rem(flat, LX).astype(f32)
    ycoord = lax.div(flat, LX).astype(f32)
    zcoord = lax.convert_element_type(me, f32)
    rows, hops = [], []
    for m in range(nmom):
        mom = [mom_ref[m, axis].astype(f32) for axis in range(3)]
        rows.append(
            2.0 * math.pi * (mom[0] * xcoord / LX + mom[1] * ycoord / LY + mom[2] * zcoord / ndev)
        )
        hops.append(jnp.full((1, nvec), math.pi, f32))
        for axis, size in enumerate((LX, LY, ndev)):
            hops.append(jnp.full((1, nvec), mom[axis] * (2.0 * math.pi / size), f32))
    angle = jnp.concatenate(rows, 0)
    cos_ref[...] = jnp.concatenate([jnp.cos(angle)] * 3, 1)
    sin_ref[...] = jnp.concatenate([jnp.sin(angle)] * 3, 1)
    hop = jnp.concatenate(hops, 0)
    plain = lax.rem(lax.broadcasted_iota(jnp.int32, hop.shape, 0), NDISP) == 0
    ar_ref[...] = jnp.where(plain, -1.0, jnp.cos(hop))
    ai_ref[...] = jnp.where(plain, 0.0, -jnp.sin(hop))

    lane = lax.broadcasted_iota(jnp.int32, (CHUNK, plane), 1)
    edge = lax.rem(lane, LX) == LX - 1

    def displace(t, direction, source, begin=0, size=nvec):
        @pl.loop(0, size // CHUNK)
        def _(i):
            rows = pl.multiple_of(begin + i * CHUNK, CHUNK)
            vec = []
            for p in range(2):
                line = []
                for c in range(3):
                    v = source[t, p, c, pl.ds(rows, CHUNK), :].astype(f32)
                    if direction == 0:
                        v = jnp.where(
                            edge, pltpu.roll(v, LX - 1, 1), pltpu.roll(v, plane - 1, 1)
                        )
                    elif direction == 1:
                        v = pltpu.roll(v, plane - LX, 1)
                    line.append(v)
                vec.append(line)
            for row in range(3):
                real = imag = None
                for col in range(3):
                    mr = link_ref[t, direction, 0, row, col]
                    mi = link_ref[t, direction, 1, row, col]
                    re = mr * vec[0][col] - mi * vec[1][col]
                    im = mr * vec[1][col] + mi * vec[0][col]
                    real = re if real is None else real + re
                    imag = im if imag is None else imag + im
                lanes = slice(row * plane, (row + 1) * plane)
                fields[t * NDISP + direction + 1, pl.ds(rows, CHUNK), lanes] = real.astype(bf16)
                fields[
                    t * NDISP + direction + 1, pl.ds(nvec + rows, CHUNK), lanes
                ] = imag.astype(bf16)

    def phases(t):
        @pl.loop(0, nvec // CHUNK)
        def _(i):
            rows = pl.multiple_of(i * CHUNK, CHUNK)
            for c in range(3):
                lanes = slice(c * plane, (c + 1) * plane)
                vr = eig_ref[t, 0, c, pl.ds(rows, CHUNK), :]
                vi = eig_ref[t, 1, c, pl.ds(rows, CHUNK), :]
                fields[t * NDISP, pl.ds(rows, CHUNK), lanes] = vr
                fields[t * NDISP, pl.ds(nvec + rows, CHUNK), lanes] = vi
                vr, vi = vr.astype(f32), vi.astype(f32)
                for m in range(nmom):
                    cosine = cos_ref[m:m + 1, lanes]
                    sine = sin_ref[m:m + 1, lanes]
                    a, b = cosine * vr, sine * vi
                    g, h = cosine * vi, sine * vr
                    plus[t * nmom + m, pl.ds(rows, CHUNK), lanes] = (a - b).astype(bf16)
                    plus[t * nmom + m, pl.ds(nvec + rows, CHUNK), lanes] = (g + h).astype(bf16)
                    minus[t * nmom + m, pl.ds(rows, CHUNK), lanes] = (a + b).astype(bf16)
                    minus[t * nmom + m, pl.ds(nvec + rows, CHUNK), lanes] = (g - h).astype(bf16)

    link_copy.wait()

    @pl.loop(0, slices)
    def _(t):
        e_copy(t).wait()
        displace(t, 0, eig_ref)
        displace(t, 1, eig_ref)
        phases(t)

    count, spins = tau_ref.shape[:2]

    def mix(i):
        q = lax.rem(list_ref[i, 2], count)
        g = list_ref[i, 1]

        @pl.loop(0, 2 * nvec // CHUNK)
        def _(n):
            rows = pl.multiple_of(n * CHUNK, CHUNK)
            tau = [tau_ref[q, s, pl.ds(rows, CHUNK), :].astype(f32) for s in range(spins)]
            for r in range(spins):
                mixed = spin_ref[r, 0, g] * tau[0]
                for s in range(1, spins):
                    mixed = mixed + spin_ref[r, s, g] * tau[s]
                mix_ref[i, r, pl.ds(rows, CHUNK), :] = mixed.astype(bf16)

        m_copy(i).start()

    @pl.loop(1, ndev)
    def _(k):
        l_copy(k).wait()

    to_smem = pltpu.make_async_copy(lists, table, l_local)
    to_smem.start()
    to_smem.wait()

    def entry_of(dest, i):
        return table[lax.rem(me + ndev - dest, ndev), 0, i]

    def item(entry):
        time = lax.div(entry, nmom * NDISP)
        m = lax.rem(lax.div(entry, NDISP), nmom)
        d = lax.rem(entry, NDISP)
        ar = ar_ref[pl.ds(m * NDISP + d, 1), :]
        ai = ai_ref[pl.ds(m * NDISP + d, 1), :]
        x = fields[time * NDISP + d]
        first = lax.dot_general(plus[time * nmom + m], x, NT, preferred_element_type=f32)
        second = lax.dot_general(x, minus[time * nmom + m], NT, preferred_element_type=f32)
        g1r = first[:nvec, :nvec] + first[nvec:, nvec:]
        g1i = first[:nvec, nvec:] - first[nvec:, :nvec]
        g2r = second[:nvec, :nvec] + second[nvec:, nvec:]
        g2i = second[:nvec, nvec:] - second[nvec:, :nvec]
        return (
            (g1r - (ar * g2r - ai * g2i)) * factor,
            (g1i - (ar * g2i + ai * g2r)) * factor,
        )

    levels = outer.bit_length() - 1

    def flip(l):
        size = 1 << l
        return zpos + size * (1 - 2 * lax.rem(zpos // size, 2))

    def away(r):
        row = zpos
        for l in range(levels):
            row = row + lax.rem(r // (1 << l), 2) * (flip(l) - zpos)
        return row

    def copy1(n, i):
        return pltpu.make_async_remote_copy(
            src_ref=part1.at[n, i], dst_ref=recv1.at[n, i], send_sem=s1.at[n, i], recv_sem=r1.at[n, i],
            device_id=(cfg, space, 1 - core), device_id_type=MESH,
        )

    def copy2(n, j, i):
        return pltpu.make_async_remote_copy(
            src_ref=part2.at[n, i], dst_ref=recv2.at[j, i], send_sem=s2.at[j, i], recv_sem=r2.at[j, i],
            device_id=(cfg, zpos * inner + (1 - ypos), core), device_id_type=MESH,
        )

    def copy3(r, i):
        row = flip((r & -r).bit_length() - 1)
        return pltpu.make_async_remote_copy(
            src_ref=part3.at[r, i], dst_ref=recv3.at[r, i], send_sem=s3.at[r, i], recv_sem=r3.at[r, i],
            device_id=(cfg, row * inner + ypos, core), device_id_type=MESH,
        )

    def unit(n):
        last = n == nspace - 1
        across = jnp.logical_or(n == 0, jnp.logical_and(lax.rem(n, 2) == 1, n < nspace - 1))
        j = jnp.where(across, (n + 1) // 2, jnp.where(last, outer - 1, n // 2 - 1))
        row = away(outer - 1 - j)
        return across, j, (row * inner + jnp.where(across, 1 - ypos, ypos)) * ndiag

    ahead = nspace - 3

    def stored(n):
        return jnp.logical_and(core > 0, n >= ahead)

    def found(n, dest, side, i):
        entry = entry_of(dest, i)
        m = lax.rem(lax.div(entry, NDISP), nmom)
        final = jnp.logical_and(
            lax.div(entry, nmom * NDISP) == slices - 1, lax.rem(entry, NDISP) == NDISP - 1
        )
        return jnp.where(final, 6 * local + m, ((n - ahead) * 2 + side) * local + i)

    def prepare(n):
        _, _, chip = unit(n)
        for side in range(2):
            for i in range(local):
                place = ((n - ahead) * 2 + side) * local + i
                dest = chip + (1 - core if side == 0 else core)
                early[place, 0], early[place, 1] = item(entry_of(dest, i))

    def complete(m):
        early[6 * local + m, 0], early[6 * local + m, 1] = item(
            ((slices - 1) * nmom + m) * NDISP + NDISP - 1
        )

    def give(n):
        _, _, chip = unit(n)

        @pl.when(stored(n))
        def _():
            for i in range(local):
                part1[n, i] = early[found(n, chip + (1 - core), 0, i)].astype(bf16)
                copy1(n, i).start()

        @pl.when(jnp.logical_not(stored(n)))
        def _():
            for i in range(local):
                real, imag = item(entry_of(chip + (1 - core), i))
                part1[n, i, 0] = real.astype(bf16)
                part1[n, i, 1] = imag.astype(bf16)
                copy1(n, i).start()

    def keep(n):
        _, _, chip = unit(n)

        @pl.when(stored(n))
        def _():
            for i in range(local):
                own[n, i] = early[found(n, chip + core, 1, i)]

        @pl.when(jnp.logical_not(stored(n)))
        def _():
            for i in range(local):
                own[n, i, 0], own[n, i, 1] = item(entry_of(chip + core, i))

    def join(n, i):
        across, j, _ = unit(n)
        copy1(n, i).wait_recv()
        total = own[n, i] + recv1[n, i].astype(f32)
        own[n, i] = total
        part2[n, i] = total.astype(bf16)

        @pl.when(across)
        def _():
            copy2(n, j, i).start()

    def keep_first():
        _, _, chip = unit(0)
        for i in range(local):
            own[0, i, 0], own[0, i, 1] = item(entry_of(chip + core, i))
            join(0, i)

    def collect_row(r, i):
        j = outer - 1 - r
        n = nspace - 1 if r == 0 else 2 * j + 2
        sources = [r + (1 << l) for l in range(levels) if r % (2 << l) == 0]
        copy2(0, j, i).wait()
        for source in sources:
            copy3(source, i).wait()
        total = own[n, i] + recv2[j, i].astype(f32)
        for source in sources:
            total = total + recv3[source, i].astype(f32)
        if r == 0:
            out_ref[i] = total.astype(bf16)
        else:
            part3[r, i] = total.astype(bf16)
            copy3(r, i).start()

    def collect(q):
        for r in range(outer - 1, -1, -1):
            @pl.when(outer - 1 - q // local == r)
            def _():
                collect_row(r, lax.rem(q, local))

    def halo(t, pieces=2):
        for h in range(pieces):
            v_copy(t, h, pieces).wait_recv()
            displace(t, 2, above, h * (nvec // pieces), nvec // pieces)

    @pl.loop(0, slices - 1)
    def _(t):
        halo(t)

    @pl.when(core > 0)
    def _():
        @pl.loop(ahead, nspace)
        def _(n):
            prepare(n)

    halo(slices - 1, 4)

    @pl.loop(0, 3 * nspace)
    def _(k):
        first_core = core == 0
        kind = jnp.where(
            first_core, jnp.where(k < nspace, 0, 1 + lax.rem(k - nspace + 2 * nspace, 2)), jnp.where(k < 3, lax.rem(k + 1, 3), lax.rem(k, 3))
        )
        n = jnp.where(first_core, jnp.where(k < nspace, k, (k - nspace + 2 * nspace) // 2 - nspace), k // 3)

        @pl.when(jnp.logical_and(kind == 0, jnp.logical_and(core > 0, n == ahead)))
        def _():
            @pl.loop(0, nmom // 2)
            def _(m):
                complete(2 * m)
                complete(2 * m + 1)

        @pl.when(kind == 0)
        def _():
            give(n)

        alone = jnp.logical_and(core > 0, n == 0)

        @pl.when(jnp.logical_and(kind == 1, alone))
        def _():
            keep_first()

        @pl.when(jnp.logical_and(kind == 1, jnp.logical_not(alone)))
        def _():
            keep(n)

        @pl.when(jnp.logical_and(kind == 2, jnp.logical_not(alone)))
        def _():
            for i in range(local):
                join(n, i)

        @pl.when(kind == 2)
        def _():
            waits = jnp.logical_not(first_core)
            first = jnp.where(jnp.logical_and(waits, n == 5), 2, n - 2)
            stop = jnp.where(
                jnp.logical_or(n < 2, jnp.logical_and(waits, n == 4)), first, n - 1
            )

            @pl.loop(first, stop)
            def _(q):
                collect(q)

            @pl.when(n == jnp.where(first_core, 1, nspace - 1))
            def _():
                t_copy.wait()
                mix(0)

            @pl.when(n == jnp.where(first_core, 3, nspace - 1))
            def _():
                mix(1)

    @pl.loop(nspace - 2, (outer - 1) * local)
    def _(q):
        collect(q)

    for i in range(local):
        collect_row(0, i)

    @pl.loop(0, nspace)
    def _(n):
        for i in range(local):
            copy1(n, i).wait_send()

    for t in range(slices):
        pieces = 2 if t < slices - 1 else 4
        for h in range(pieces):
            v_copy(t, h, pieces).wait_send()
    for i in range(local):
        m_copy(i).wait()


def diagram_kernel(elem_ref, mix_ref, out_hbm, out_ref, store_sem):
    local, spins = mix_ref.shape[:2]
    group = 1

    def store(i, h):
        some = pl.ds(h * group, group)
        return pltpu.make_async_copy(out_ref.at[i, some], out_hbm.at[i, some], store_sem.at[i, h])

    pieces = [(i, h) for i in range(local) for h in range(spins // group)]
    for i, h in pieces:
        if h == 0:
            er, ei = elem_ref[i, 0], elem_ref[i, 1]
            square = jnp.concatenate(
                [jnp.concatenate([er, -ei], 1), jnp.concatenate([ei, er], 1)], 0
            )
        for r in range(h * group, (h + 1) * group):
            out_ref[i, r] = jnp.dot(
                square, mix_ref[i, r], preferred_element_type=f32
            ).astype(bf16)
        store(i, h).start()
    for i, h in pieces:
        store(i, h).wait()


def body(eigvecs, gauge_links, momenta, spin_mix, perambulators, contraction_list):
    slices, _, colors, nvec, depth, plane = eigvecs.shape
    assert depth == 1 and colors == 3
    nspace, ndiag = lax.axis_size("space"), lax.axis_size("diag")
    inner = 2
    outer = nspace // inner
    assert ndiag == 2 and inner * outer == nspace
    assert momenta.shape[0] % 2 == 0 and outer >= 4 and outer & (outer - 1) == 0 and contraction_list.shape[0] == 2
    ndev = nspace * ndiag
    scale = 1.0 / math.sqrt(3 * plane * ndev)
    nmom = momenta.shape[0]
    local = contraction_list.shape[0]
    count, spins = perambulators.shape[:2]
    width = perambulators.shape[4]
    vmem = pl.BlockSpec(memory_space=pltpu.VMEM)
    hbm = pl.BlockSpec(memory_space=pltpu.HBM)
    tile = (local, 2, nvec, nvec)
    field = (2 * nvec, 3 * plane)
    dma = pltpu.SemaphoreType.DMA
    elem, mixed = pl.pallas_call(
        functools.partial(
            elemental_kernel,
            (nspace, ndiag, inner, local, slices, nvec, plane, 0.5 * scale),
        ),
        out_shape=(
            jax.ShapeDtypeStruct(tile, bf16),
            jax.ShapeDtypeStruct((local, spins, 2 * nvec, width), bf16),
        ),
        in_specs=[hbm] * 6,
        out_specs=(vmem, pl.BlockSpec(memory_space=pl.ANY)),
        scratch_shapes=[
            pltpu.SMEM(contraction_list.shape, jnp.int32),
            pltpu.SMEM(momenta.shape, jnp.int32),
            pltpu.SMEM((spins, spins, spin_mix.shape[0]), f32),
            pltpu.VMEM(gauge_links.shape, f32),
            pltpu.VMEM((slices, 2, 3, nvec, plane), bf16),
            pltpu.VMEM((nmom, 3 * plane), f32),
            pltpu.VMEM((nmom, 3 * plane), f32),
            pltpu.VMEM((nmom * NDISP, nvec), f32),
            pltpu.VMEM((nmom * NDISP, nvec), f32),
            pltpu.VMEM((slices, 2, 3, nvec, plane), bf16),
            pltpu.VMEM((slices * NDISP,) + field, bf16),
            pltpu.VMEM((slices * nmom,) + field, bf16),
            pltpu.VMEM((slices * nmom,) + field, bf16),
            pltpu.VMEM((count, spins, 2 * nvec, width), bf16),
            pltpu.VMEM((local, spins, 2 * nvec, width), bf16),
            pltpu.VMEM((ndev, 1, 128), jnp.int32),
            pltpu.SMEM((ndev, 1, 128), jnp.int32),
            pltpu.VMEM((nspace,) + tile, bf16),
            pltpu.VMEM((nspace,) + tile, bf16),
            pltpu.VMEM((nspace,) + tile, f32),
            pltpu.VMEM((6 * local + nmom,) + tile[1:], f32),
            pltpu.VMEM((nspace,) + tile, bf16),
            pltpu.VMEM((outer,) + tile, bf16),
            pltpu.VMEM((outer,) + tile, bf16),
            pltpu.VMEM((outer,) + tile, bf16),
            dma((3,)), dma, dma((slices,)), dma, dma((local,)), dma((slices, 4)), dma((slices, 4)),
            dma((ndev,)), dma((ndev,)), dma,
            dma((nspace, local)), dma((nspace, local)),
            dma((outer, local)), dma((outer, local)),
            dma((outer, local)), dma((outer, local)),
        ],
        compiler_params=pltpu.CompilerParams(
            collective_id=0, has_side_effects=True, vmem_limit_bytes=44 * 1024 * 1024
        ),
    )(*(
        pltpu.with_memory_space_constraint(x, pltpu.HBM) for x in (
            contraction_list, momenta, spin_mix.transpose(1, 2, 0), gauge_links,
            eigvecs.reshape(slices, 2, 3, nvec, plane),
            perambulators.reshape(count, spins, 2 * nvec, width),
        )
    ))
    out = pl.pallas_call(
        diagram_kernel,
        in_specs=[vmem, vmem],
        out_specs=hbm,
        out_shape=jax.ShapeDtypeStruct((local, spins, 2 * nvec, width), bf16),
        scratch_shapes=[
            pltpu.VMEM((local, spins, 2 * nvec, width), bf16), dma((local, spins)),
        ],
        compiler_params=pltpu.CompilerParams(vmem_limit_bytes=24 * 1024 * 1024),
    )(elem, mixed)
    return out.reshape(local, spins, 2, nvec, width)


def solution(mesh):
    placed = (
        P("cfg", None, None, None, ("space", "diag"), None),
        P("cfg", None, None, None, None, ("space", "diag"), None),
        P(),
        P(),
        P(("cfg", "space", "diag"), None, None, None, None),
        P(("space", "diag"), None),
    )
    return jax.shard_map(
        body,
        mesh=mesh,
        in_specs=placed,
        out_specs=P(("cfg", "space", "diag"), None, None, None, None),
        check_vma=False,
    )
```

```python
import functools
import math

import jax
import jax.numpy as jnp
from jax import lax
from jax.experimental import pallas as pl
from jax.experimental.pallas import tpu as pltpu
from jax.sharding import PartitionSpec as P

LX = 16
LY = 16
NDISP = 4
CHUNK = 16
MESH = pl.DeviceIdType.MESH
NT = (((1,), (1,)), ((), ()))
f32 = jnp.float32
bf16 = jnp.bfloat16


def elemental_kernel(
    dims, list_hbm, mom_hbm, spin_hbm, link_hbm, eig_hbm, tau_hbm, out_ref, mix_hbm,
    list_ref, mom_ref, spin_ref, link_ref,
    eig_ref, cos_ref, sin_ref, ar_ref, ai_ref, above, fields, plus, minus, tau_ref, mix_ref, lists, table,
    part1, recv1, own, early, part2, recv2, part3, recv3,
    small_local, link_local, e_local, t_local, m_local, v_send, v_recv, l_send, l_recv, l_local, s1, r1, s2, r2, s3, r3,
):
    nspace, ndiag, inner, local, slices, nvec, plane, factor = dims
    ndev = nspace * ndiag
    outer = nspace // inner
    space = lax.axis_index("space")
    core = lax.axis_index("diag")
    cfg = lax.axis_index("cfg")
    me = space * ndiag + core
    zpos = space // inner
    ypos = lax.rem(space, inner)

    def device(index):
        return (cfg, index // ndiag, lax.rem(index, ndiag))

    def e_copy(t):
        return pltpu.make_async_copy(eig_hbm.at[t], eig_ref.at[t], e_local.at[t])

    t_copy = pltpu.make_async_copy(tau_hbm, tau_ref, t_local)

    def m_copy(i):
        return pltpu.make_async_copy(mix_ref.at[i], mix_hbm.at[i], m_local.at[i])

    barrier = pltpu.get_barrier_semaphore()

    @pl.loop(1, ndev)
    def _(k):
        pl.semaphore_signal(
            barrier, inc=1, device_id=device(lax.rem(me + k, ndev)), device_id_type=MESH
        )

    small = [
        pltpu.make_async_copy(src, dst, small_local.at[k])
        for k, (src, dst) in enumerate(
            ((list_hbm, list_ref), (mom_hbm, mom_ref), (spin_hbm, spin_ref))
        )
    ]
    link_copy = pltpu.make_async_copy(link_hbm, link_ref, link_local)
    for copy in small:
        copy.start()
    link_copy.start()
    for t in range(slices):
        e_copy(t).start()
    t_copy.start()

    pl.semaphore_wait(barrier, ndev - 1)

    def v_copy(t, h, pieces=1):
        size = nvec // pieces
        rows = pl.ds(h * size, size)
        whole = pieces == 1
        return pltpu.make_async_remote_copy(
            src_ref=eig_hbm.at[t] if whole else eig_hbm.at[t, :, :, rows],
            dst_ref=above.at[t] if whole else above.at[t, :, :, rows],
            send_sem=v_send.at[t, h], recv_sem=v_recv.at[t, h],
            device_id=device(lax.rem(me + ndev - 1, ndev)), device_id_type=MESH,
        )

    def l_copy(k):
        return pltpu.make_async_remote_copy(
            src_ref=lists.at[0], dst_ref=lists.at[k],
            send_sem=l_send.at[k], recv_sem=l_recv.at[k],
            device_id=device(lax.rem(me + k, ndev)), device_id_type=MESH,
        )

    v_copy(0, 0).start()

    for copy in small:
        copy.wait()
    column = lax.broadcasted_iota(jnp.int32, (1, 128), 1)
    packed = jnp.zeros((1, 128), jnp.int32)
    for i in range(local):
        packed = jnp.where(column == i, list_ref[i, 0], packed)
    lists[0] = packed

    @pl.loop(1, ndev)
    def _(k):
        l_copy(k).start()

    for t in range(1, slices - 1):
        v_copy(t, 0).start()
    for h in range(2):
        v_copy(slices - 1, h, 2).start()

    nmom = mom_ref.shape[0]
    flat = lax.broadcasted_iota(jnp.int32, (1, plane), 1)
    xcoord = lax.rem(flat, LX).astype(f32)
    ycoord = lax.div(flat, LX).astype(f32)
    zcoord = lax.convert_element_type(me, f32)
    rows, hops = [], []
    for m in range(nmom):
        mom = [mom_ref[m, axis].astype(f32) for axis in range(3)]
        rows.append(
            2.0 * math.pi * (mom[0] * xcoord / LX + mom[1] * ycoord / LY + mom[2] * zcoord / ndev)
        )
        hops.append(jnp.full((1, nvec), math.pi, f32))
        for axis, size in enumerate((LX, LY, ndev)):
            hops.append(jnp.full((1, nvec), mom[axis] * (2.0 * math.pi / size), f32))
    angle = jnp.concatenate(rows, 0)
    cos_ref[...] = jnp.concatenate([jnp.cos(angle)] * 3, 1)
    sin_ref[...] = jnp.concatenate([jnp.sin(angle)] * 3, 1)
    hop = jnp.concatenate(hops, 0)
    plain = lax.rem(lax.broadcasted_iota(jnp.int32, hop.shape, 0), NDISP) == 0
    ar_ref[...] = jnp.where(plain, -1.0, jnp.cos(hop))
    ai_ref[...] = jnp.where(plain, 0.0, -jnp.sin(hop))

    lane = lax.broadcasted_iota(jnp.int32, (CHUNK, plane), 1)
    edge = lax.rem(lane, LX) == LX - 1

    def displace(t, direction, source, begin=0, size=nvec):
        @pl.loop(0, size // CHUNK)
        def _(i):
            rows = pl.multiple_of(begin + i * CHUNK, CHUNK)
            vec = []
            for p in range(2):
                line = []
                for c in range(3):
                    v = source[t, p, c, pl.ds(rows, CHUNK), :].astype(f32)
                    if direction == 0:
                        v = jnp.where(
                            edge, pltpu.roll(v, LX - 1, 1), pltpu.roll(v, plane - 1, 1)
                        )
                    elif direction == 1:
                        v = pltpu.roll(v, plane - LX, 1)
                    line.append(v)
                vec.append(line)
            for row in range(3):
                real = imag = None
                for col in range(3):
                    mr = link_ref[t, direction, 0, row, col]
                    mi = link_ref[t, direction, 1, row, col]
                    re = mr * vec[0][col] - mi * vec[1][col]
                    im = mr * vec[1][col] + mi * vec[0][col]
                    real = re if real is None else real + re
                    imag = im if imag is None else imag + im
                lanes = slice(row * plane, (row + 1) * plane)
                fields[t * NDISP + direction + 1, pl.ds(rows, CHUNK), lanes] = real.astype(bf16)
                fields[
                    t * NDISP + direction + 1, pl.ds(nvec + rows, CHUNK), lanes
                ] = imag.astype(bf16)

    def phases(t):
        @pl.loop(0, nvec // CHUNK)
        def _(i):
            rows = pl.multiple_of(i * CHUNK, CHUNK)
            for c in range(3):
                lanes = slice(c * plane, (c + 1) * plane)
                vr = eig_ref[t, 0, c, pl.ds(rows, CHUNK), :]
                vi = eig_ref[t, 1, c, pl.ds(rows, CHUNK), :]
                fields[t * NDISP, pl.ds(rows, CHUNK), lanes] = vr
                fields[t * NDISP, pl.ds(nvec + rows, CHUNK), lanes] = vi
                vr, vi = vr.astype(f32), vi.astype(f32)
                for m in range(nmom):
                    cosine = cos_ref[m:m + 1, lanes]
                    sine = sin_ref[m:m + 1, lanes]
                    a, b = cosine * vr, sine * vi
                    g, h = cosine * vi, sine * vr
                    plus[t * nmom + m, pl.ds(rows, CHUNK), lanes] = (a - b).astype(bf16)
                    plus[t * nmom + m, pl.ds(nvec + rows, CHUNK), lanes] = (g + h).astype(bf16)
                    minus[t * nmom + m, pl.ds(rows, CHUNK), lanes] = (a + b).astype(bf16)
                    minus[t * nmom + m, pl.ds(nvec + rows, CHUNK), lanes] = (g - h).astype(bf16)

    link_copy.wait()

    @pl.loop(0, slices)
    def _(t):
        e_copy(t).wait()
        displace(t, 0, eig_ref)
        displace(t, 1, eig_ref)
        phases(t)

    count, spins = tau_ref.shape[:2]

    def mix(i):
        q = lax.rem(list_ref[i, 2], count)
        g = list_ref[i, 1]

        @pl.loop(0, 2 * nvec // CHUNK)
        def _(n):
            rows = pl.multiple_of(n * CHUNK, CHUNK)
            tau = [tau_ref[q, s, pl.ds(rows, CHUNK), :].astype(f32) for s in range(spins)]
            for r in range(spins):
                mixed = spin_ref[r, 0, g] * tau[0]
                for s in range(1, spins):
                    mixed = mixed + spin_ref[r, s, g] * tau[s]
                mix_ref[i, r, pl.ds(rows, CHUNK), :] = mixed.astype(bf16)

        m_copy(i).start()

    @pl.loop(1, ndev)
    def _(k):
        l_copy(k).wait()

    to_smem = pltpu.make_async_copy(lists, table, l_local)
    to_smem.start()
    to_smem.wait()

    def entry_of(dest, i):
        return table[lax.rem(me + ndev - dest, ndev), 0, i]

    def item(entry):
        time = lax.div(entry, nmom * NDISP)
        m = lax.rem(lax.div(entry, NDISP), nmom)
        d = lax.rem(entry, NDISP)
        ar = ar_ref[pl.ds(m * NDISP + d, 1), :]
        ai = ai_ref[pl.ds(m * NDISP + d, 1), :]
        x = fields[time * NDISP + d]
        first = lax.dot_general(plus[time * nmom + m], x, NT, preferred_element_type=f32)
        second = lax.dot_general(x, minus[time * nmom + m], NT, preferred_element_type=f32)
        g1r = first[:nvec, :nvec] + first[nvec:, nvec:]
        g1i = first[:nvec, nvec:] - first[nvec:, :nvec]
        g2r = second[:nvec, :nvec] + second[nvec:, nvec:]
        g2i = second[:nvec, nvec:] - second[nvec:, :nvec]
        return (
            (g1r - (ar * g2r - ai * g2i)) * factor,
            (g1i - (ar * g2i + ai * g2r)) * factor,
        )

    levels = outer.bit_length() - 1

    def flip(l):
        size = 1 << l
        return zpos + size * (1 - 2 * lax.rem(zpos // size, 2))

    def away(r):
        row = zpos
        for l in range(levels):
            row = row + lax.rem(r // (1 << l), 2) * (flip(l) - zpos)
        return row

    def copy1(n, i):
        return pltpu.make_async_remote_copy(
            src_ref=part1.at[n, i], dst_ref=recv1.at[n, i], send_sem=s1.at[n, i], recv_sem=r1.at[n, i],
            device_id=(cfg, space, 1 - core), device_id_type=MESH,
        )

    def copy2(n, j, i):
        return pltpu.make_async_remote_copy(
            src_ref=part2.at[n, i], dst_ref=recv2.at[j, i], send_sem=s2.at[j, i], recv_sem=r2.at[j, i],
            device_id=(cfg, zpos * inner + (1 - ypos), core), device_id_type=MESH,
        )

    def copy3(r, i):
        row = flip((r & -r).bit_length() - 1)
        return pltpu.make_async_remote_copy(
            src_ref=part3.at[r, i], dst_ref=recv3.at[r, i], send_sem=s3.at[r, i], recv_sem=r3.at[r, i],
            device_id=(cfg, row * inner + ypos, core), device_id_type=MESH,
        )

    def unit(n):
        last = n == nspace - 1
        across = jnp.logical_or(n == 0, jnp.logical_and(lax.rem(n, 2) == 1, n < nspace - 1))
        j = jnp.where(across, (n + 1) // 2, jnp.where(last, outer - 1, n // 2 - 1))
        row = away(outer - 1 - j)
        return across, j, (row * inner + jnp.where(across, 1 - ypos, ypos)) * ndiag

    ahead = nspace - 3

    def stored(n):
        return jnp.logical_and(core > 0, n >= ahead)

    def found(n, dest, side, i):
        entry = entry_of(dest, i)
        m = lax.rem(lax.div(entry, NDISP), nmom)
        final = jnp.logical_and(
            lax.div(entry, nmom * NDISP) == slices - 1, lax.rem(entry, NDISP) == NDISP - 1
        )
        return jnp.where(final, 6 * local + m, ((n - ahead) * 2 + side) * local + i)

    def prepare(n):
        _, _, chip = unit(n)
        for side in range(2):
            for i in range(local):
                place = ((n - ahead) * 2 + side) * local + i
                dest = chip + (1 - core if side == 0 else core)
                early[place, 0], early[place, 1] = item(entry_of(dest, i))

    def complete(m):
        early[6 * local + m, 0], early[6 * local + m, 1] = item(
            ((slices - 1) * nmom + m) * NDISP + NDISP - 1
        )

    def give(n):
        _, _, chip = unit(n)

        @pl.when(stored(n))
        def _():
            for i in range(local):
                part1[n, i] = early[found(n, chip + (1 - core), 0, i)].astype(bf16)
                copy1(n, i).start()

        @pl.when(jnp.logical_not(stored(n)))
        def _():
            for i in range(local):
                real, imag = item(entry_of(chip + (1 - core), i))
                part1[n, i, 0] = real.astype(bf16)
                part1[n, i, 1] = imag.astype(bf16)
                copy1(n, i).start()

    def keep(n):
        _, _, chip = unit(n)

        @pl.when(stored(n))
        def _():
            for i in range(local):
                own[n, i] = early[found(n, chip + core, 1, i)]

        @pl.when(jnp.logical_not(stored(n)))
        def _():
            for i in range(local):
                own[n, i, 0], own[n, i, 1] = item(entry_of(chip + core, i))

    def join(n):
        across, j, _ = unit(n)
        for i in range(local):
            copy1(n, i).wait_recv()
            total = own[n, i] + recv1[n, i].astype(f32)
            own[n, i] = total
            part2[n, i] = total.astype(bf16)

            @pl.when(across)
            def _():
                copy2(n, j, i).start()

    def collect_row(r, i):
        j = outer - 1 - r
        n = nspace - 1 if r == 0 else 2 * j + 2
        sources = [r + (1 << l) for l in range(levels) if r % (2 << l) == 0]
        copy2(0, j, i).wait()
        for source in sources:
            copy3(source, i).wait()
        total = own[n, i] + recv2[j, i].astype(f32)
        for source in sources:
            total = total + recv3[source, i].astype(f32)
        if r == 0:
            out_ref[i] = total.astype(bf16)
        else:
            part3[r, i] = total.astype(bf16)
            copy3(r, i).start()

    def collect(q):
        for r in range(outer - 1, -1, -1):
            @pl.when(outer - 1 - q // local == r)
            def _():
                collect_row(r, lax.rem(q, local))

    def halo(t, pieces=1):
        for h in range(pieces):
            v_copy(t, h, pieces).wait_recv()
            displace(t, 2, above, h * (nvec // pieces), nvec // pieces)

    @pl.loop(0, slices - 1)
    def _(t):
        halo(t)

    @pl.when(core > 0)
    def _():
        @pl.loop(ahead, nspace)
        def _(n):
            prepare(n)

    halo(slices - 1, 2)

    @pl.loop(0, 3 * nspace)
    def _(k):
        first_core = core == 0
        kind = jnp.where(
            first_core, jnp.where(k < nspace, 0, 1 + lax.rem(k - nspace + 2 * nspace, 2)), jnp.where(k < 3, lax.rem(k + 1, 3), lax.rem(k, 3))
        )
        n = jnp.where(first_core, jnp.where(k < nspace, k, (k - nspace + 2 * nspace) // 2 - nspace), k // 3)

        @pl.when(jnp.logical_and(kind == 0, jnp.logical_and(core > 0, n == ahead)))
        def _():
            @pl.loop(0, nmom // 2)
            def _(m):
                complete(2 * m)
                complete(2 * m + 1)

        @pl.when(kind == 0)
        def _():
            give(n)

        @pl.when(kind == 1)
        def _():
            keep(n)

        @pl.when(kind == 2)
        def _():
            join(n)

            waits = jnp.logical_not(first_core)
            first = jnp.where(jnp.logical_and(waits, n == 5), 2, n - 2)
            stop = jnp.where(
                jnp.logical_or(n < 2, jnp.logical_and(waits, n == 4)), first, n - 1
            )

            @pl.loop(first, stop)
            def _(q):
                collect(q)

            @pl.when(n == jnp.where(first_core, 1, nspace - 1))
            def _():
                t_copy.wait()
                mix(0)

            @pl.when(n == jnp.where(first_core, 3, nspace - 1))
            def _():
                mix(1)

    @pl.loop(nspace - 2, (outer - 1) * local)
    def _(q):
        collect(q)

    for i in range(local):
        collect_row(0, i)

    @pl.loop(0, nspace)
    def _(n):
        for i in range(local):
            copy1(n, i).wait_send()

    for t in range(slices):
        pieces = 1 if t < slices - 1 else 2
        for h in range(pieces):
            v_copy(t, h, pieces).wait_send()
    for i in range(local):
        m_copy(i).wait()


def diagram_kernel(elem_ref, mix_ref, out_hbm, out_ref, store_sem):
    local, spins = mix_ref.shape[:2]
    group = 1

    def store(i, h):
        some = pl.ds(h * group, group)
        return pltpu.make_async_copy(out_ref.at[i, some], out_hbm.at[i, some], store_sem.at[i, h])

    pieces = [(i, h) for i in range(local) for h in range(spins // group)]
    for i, h in pieces:
        if h == 0:
            er, ei = elem_ref[i, 0], elem_ref[i, 1]
            square = jnp.concatenate(
                [jnp.concatenate([er, -ei], 1), jnp.concatenate([ei, er], 1)], 0
            )
        for r in range(h * group, (h + 1) * group):
            out_ref[i, r] = jnp.dot(
                square, mix_ref[i, r], preferred_element_type=f32
            ).astype(bf16)
        store(i, h).start()
    for i, h in pieces:
        store(i, h).wait()


def body(eigvecs, gauge_links, momenta, spin_mix, perambulators, contraction_list):
    slices, _, colors, nvec, depth, plane = eigvecs.shape
    assert depth == 1 and colors == 3
    nspace, ndiag = lax.axis_size("space"), lax.axis_size("diag")
    inner = 2
    outer = nspace // inner
    assert ndiag == 2 and inner * outer == nspace
    assert momenta.shape[0] % 2 == 0 and outer >= 4 and outer & (outer - 1) == 0 and contraction_list.shape[0] == 2
    ndev = nspace * ndiag
    scale = 1.0 / math.sqrt(3 * plane * ndev)
    nmom = momenta.shape[0]
    local = contraction_list.shape[0]
    count, spins = perambulators.shape[:2]
    width = perambulators.shape[4]
    vmem = pl.BlockSpec(memory_space=pltpu.VMEM)
    hbm = pl.BlockSpec(memory_space=pltpu.HBM)
    tile = (local, 2, nvec, nvec)
    field = (2 * nvec, 3 * plane)
    dma = pltpu.SemaphoreType.DMA
    elem, mixed = pl.pallas_call(
        functools.partial(
            elemental_kernel,
            (nspace, ndiag, inner, local, slices, nvec, plane, 0.5 * scale),
        ),
        out_shape=(
            jax.ShapeDtypeStruct(tile, bf16),
            jax.ShapeDtypeStruct((local, spins, 2 * nvec, width), bf16),
        ),
        in_specs=[hbm] * 6,
        out_specs=(vmem, pl.BlockSpec(memory_space=pl.ANY)),
        scratch_shapes=[
            pltpu.SMEM(contraction_list.shape, jnp.int32),
            pltpu.SMEM(momenta.shape, jnp.int32),
            pltpu.SMEM((spins, spins, spin_mix.shape[0]), f32),
            pltpu.VMEM(gauge_links.shape, f32),
            pltpu.VMEM((slices, 2, 3, nvec, plane), bf16),
            pltpu.VMEM((nmom, 3 * plane), f32),
            pltpu.VMEM((nmom, 3 * plane), f32),
            pltpu.VMEM((nmom * NDISP, nvec), f32),
            pltpu.VMEM((nmom * NDISP, nvec), f32),
            pltpu.VMEM((slices, 2, 3, nvec, plane), bf16),
            pltpu.VMEM((slices * NDISP,) + field, bf16),
            pltpu.VMEM((slices * nmom,) + field, bf16),
            pltpu.VMEM((slices * nmom,) + field, bf16),
            pltpu.VMEM((count, spins, 2 * nvec, width), bf16),
            pltpu.VMEM((local, spins, 2 * nvec, width), bf16),
            pltpu.VMEM((ndev, 1, 128), jnp.int32),
            pltpu.SMEM((ndev, 1, 128), jnp.int32),
            pltpu.VMEM((nspace,) + tile, bf16),
            pltpu.VMEM((nspace,) + tile, bf16),
            pltpu.VMEM((nspace,) + tile, f32),
            pltpu.VMEM((6 * local + nmom,) + tile[1:], f32),
            pltpu.VMEM((nspace,) + tile, bf16),
            pltpu.VMEM((outer,) + tile, bf16),
            pltpu.VMEM((outer,) + tile, bf16),
            pltpu.VMEM((outer,) + tile, bf16),
            dma((3,)), dma, dma((slices,)), dma, dma((local,)), dma((slices, 2)), dma((slices, 2)),
            dma((ndev,)), dma((ndev,)), dma,
            dma((nspace, local)), dma((nspace, local)),
            dma((outer, local)), dma((outer, local)),
            dma((outer, local)), dma((outer, local)),
        ],
        compiler_params=pltpu.CompilerParams(
            collective_id=0, has_side_effects=True, vmem_limit_bytes=44 * 1024 * 1024
        ),
    )(*(
        pltpu.with_memory_space_constraint(x, pltpu.HBM) for x in (
            contraction_list, momenta, spin_mix.transpose(1, 2, 0), gauge_links,
            eigvecs.reshape(slices, 2, 3, nvec, plane),
            perambulators.reshape(count, spins, 2 * nvec, width),
        )
    ))
    out = pl.pallas_call(
        diagram_kernel,
        in_specs=[vmem, vmem],
        out_specs=hbm,
        out_shape=jax.ShapeDtypeStruct((local, spins, 2 * nvec, width), bf16),
        scratch_shapes=[
            pltpu.VMEM((local, spins, 2 * nvec, width), bf16), dma((local, spins)),
        ],
        compiler_params=pltpu.CompilerParams(vmem_limit_bytes=24 * 1024 * 1024),
    )(elem, mixed)
    return out.reshape(local, spins, 2, nvec, width)


def solution(mesh):
    placed = (
        P("cfg", None, None, None, ("space", "diag"), None),
        P("cfg", None, None, None, None, ("space", "diag"), None),
        P(),
        P(),
        P(("cfg", "space", "diag"), None, None, None, None),
        P(("space", "diag"), None),
    )
    return jax.shard_map(
        body,
        mesh=mesh,
        in_specs=placed,
        out_specs=P(("cfg", "space", "diag"), None, None, None, None),
        check_vma=False,
    )
```

```python
import functools
import math

import jax
import jax.numpy as jnp
from jax import lax
from jax.experimental import pallas as pl
from jax.experimental.pallas import tpu as pltpu
from jax.sharding import PartitionSpec as P

LX = 16
LY = 16
NDISP = 4
CHUNK = 16
MESH = pl.DeviceIdType.MESH
NT = (((1,), (1,)), ((), ()))
f32 = jnp.float32
bf16 = jnp.bfloat16


def elemental_kernel(
    dims, list_hbm, mom_hbm, spin_hbm, link_hbm, eig_hbm, tau_hbm, out_ref, mix_hbm,
    list_ref, mom_ref, spin_ref, link_ref,
    eig_ref, cos_ref, sin_ref, ar_ref, ai_ref, above, fields, plus, minus, tau_ref, mix_ref, lists, table,
    part1, recv1, own, early, part2, recv2, part3, recv3,
    small_local, link_local, e_local, t_local, m_local, v_send, v_recv, l_send, l_recv, l_local, s1, r1, s2, r2, s3, r3,
):
    nspace, ndiag, inner, local, slices, nvec, plane, factor = dims
    ndev = nspace * ndiag
    outer = nspace // inner
    space = lax.axis_index("space")
    core = lax.axis_index("diag")
    cfg = lax.axis_index("cfg")
    me = space * ndiag + core
    zpos = space // inner
    ypos = lax.rem(space, inner)

    def device(index):
        return (cfg, index // ndiag, lax.rem(index, ndiag))

    def e_copy(t):
        return pltpu.make_async_copy(eig_hbm.at[t], eig_ref.at[t], e_local.at[t])

    t_copy = pltpu.make_async_copy(tau_hbm, tau_ref, t_local)

    def m_copy(i):
        return pltpu.make_async_copy(mix_ref.at[i], mix_hbm.at[i], m_local.at[i])

    barrier = pltpu.get_barrier_semaphore()

    @pl.loop(1, ndev)
    def _(k):
        pl.semaphore_signal(
            barrier, inc=1, device_id=device(lax.rem(me + k, ndev)), device_id_type=MESH
        )

    small = [
        pltpu.make_async_copy(src, dst, small_local.at[k])
        for k, (src, dst) in enumerate(
            ((list_hbm, list_ref), (mom_hbm, mom_ref), (spin_hbm, spin_ref))
        )
    ]
    link_copy = pltpu.make_async_copy(link_hbm, link_ref, link_local)
    for copy in small:
        copy.start()
    link_copy.start()
    for t in range(slices):
        e_copy(t).start()
    t_copy.start()

    pl.semaphore_wait(barrier, ndev - 1)

    half = nvec // 2

    def v_copy(t, h):
        rows = pl.ds(pl.multiple_of(h * half, half), half)
        return pltpu.make_async_remote_copy(
            src_ref=eig_hbm.at[t, :, :, rows], dst_ref=above.at[t, :, :, rows],
            send_sem=v_send.at[t, h], recv_sem=v_recv.at[t, h],
            device_id=device(lax.rem(me + ndev - 1, ndev)), device_id_type=MESH,
        )

    def l_copy(k):
        return pltpu.make_async_remote_copy(
            src_ref=lists.at[0], dst_ref=lists.at[k],
            send_sem=l_send.at[k], recv_sem=l_recv.at[k],
            device_id=device(lax.rem(me + k, ndev)), device_id_type=MESH,
        )

    for h in range(2):
        v_copy(0, h).start()

    for copy in small:
        copy.wait()
    column = lax.broadcasted_iota(jnp.int32, (1, 128), 1)
    packed = jnp.zeros((1, 128), jnp.int32)
    for i in range(local):
        packed = jnp.where(column == i, list_ref[i, 0], packed)
    lists[0] = packed

    @pl.loop(1, ndev)
    def _(k):
        l_copy(k).start()

    for t in range(1, slices):
        for h in range(2):
            v_copy(t, h).start()

    nmom = mom_ref.shape[0]
    flat = lax.broadcasted_iota(jnp.int32, (1, plane), 1)
    xcoord = lax.rem(flat, LX).astype(f32)
    ycoord = lax.div(flat, LX).astype(f32)
    zcoord = lax.convert_element_type(me, f32)
    rows, hops = [], []
    for m in range(nmom):
        mom = [mom_ref[m, axis].astype(f32) for axis in range(3)]
        rows.append(
            2.0 * math.pi * (mom[0] * xcoord / LX + mom[1] * ycoord / LY + mom[2] * zcoord / ndev)
        )
        hops.append(jnp.full((1, nvec), math.pi, f32))
        for axis, size in enumerate((LX, LY, ndev)):
            hops.append(jnp.full((1, nvec), mom[axis] * (2.0 * math.pi / size), f32))
    angle = jnp.concatenate(rows, 0)
    cos_ref[...] = jnp.concatenate([jnp.cos(angle)] * 3, 1)
    sin_ref[...] = jnp.concatenate([jnp.sin(angle)] * 3, 1)
    hop = jnp.concatenate(hops, 0)
    plain = lax.rem(lax.broadcasted_iota(jnp.int32, hop.shape, 0), NDISP) == 0
    ar_ref[...] = jnp.where(plain, -1.0, jnp.cos(hop))
    ai_ref[...] = jnp.where(plain, 0.0, -jnp.sin(hop))

    lane = lax.broadcasted_iota(jnp.int32, (CHUNK, plane), 1)
    edge = lax.rem(lane, LX) == LX - 1

    def displace(t, direction, source, begin=0, size=nvec):
        @pl.loop(0, size // CHUNK)
        def _(i):
            rows = pl.multiple_of(begin + i * CHUNK, CHUNK)
            vec = []
            for p in range(2):
                line = []
                for c in range(3):
                    v = source[t, p, c, pl.ds(rows, CHUNK), :].astype(f32)
                    if direction == 0:
                        v = jnp.where(
                            edge, pltpu.roll(v, LX - 1, 1), pltpu.roll(v, plane - 1, 1)
                        )
                    elif direction == 1:
                        v = pltpu.roll(v, plane - LX, 1)
                    line.append(v)
                vec.append(line)
            for row in range(3):
                real = imag = None
                for col in range(3):
                    mr = link_ref[t, direction, 0, row, col]
                    mi = link_ref[t, direction, 1, row, col]
                    re = mr * vec[0][col] - mi * vec[1][col]
                    im = mr * vec[1][col] + mi * vec[0][col]
                    real = re if real is None else real + re
                    imag = im if imag is None else imag + im
                lanes = slice(row * plane, (row + 1) * plane)
                fields[t * NDISP + direction + 1, pl.ds(rows, CHUNK), lanes] = real.astype(bf16)
                fields[
                    t * NDISP + direction + 1, pl.ds(nvec + rows, CHUNK), lanes
                ] = imag.astype(bf16)

    def phases(t):
        @pl.loop(0, nvec // CHUNK)
        def _(i):
            rows = pl.multiple_of(i * CHUNK, CHUNK)
            for c in range(3):
                lanes = slice(c * plane, (c + 1) * plane)
                vr = eig_ref[t, 0, c, pl.ds(rows, CHUNK), :]
                vi = eig_ref[t, 1, c, pl.ds(rows, CHUNK), :]
                fields[t * NDISP, pl.ds(rows, CHUNK), lanes] = vr
                fields[t * NDISP, pl.ds(nvec + rows, CHUNK), lanes] = vi
                vr, vi = vr.astype(f32), vi.astype(f32)
                for m in range(nmom):
                    cosine = cos_ref[m:m + 1, lanes]
                    sine = sin_ref[m:m + 1, lanes]
                    a, b = cosine * vr, sine * vi
                    g, h = cosine * vi, sine * vr
                    plus[t * nmom + m, pl.ds(rows, CHUNK), lanes] = (a - b).astype(bf16)
                    plus[t * nmom + m, pl.ds(nvec + rows, CHUNK), lanes] = (g + h).astype(bf16)
                    minus[t * nmom + m, pl.ds(rows, CHUNK), lanes] = (a + b).astype(bf16)
                    minus[t * nmom + m, pl.ds(nvec + rows, CHUNK), lanes] = (g - h).astype(bf16)

    link_copy.wait()

    @pl.loop(0, slices)
    def _(t):
        e_copy(t).wait()
        displace(t, 0, eig_ref)
        displace(t, 1, eig_ref)
        phases(t)

    count, spins = tau_ref.shape[:2]

    def mix(i):
        q = lax.rem(list_ref[i, 2], count)
        g = list_ref[i, 1]

        @pl.loop(0, 2 * nvec // CHUNK)
        def _(n):
            rows = pl.multiple_of(n * CHUNK, CHUNK)
            tau = [tau_ref[q, s, pl.ds(rows, CHUNK), :].astype(f32) for s in range(spins)]
            for r in range(spins):
                mixed = spin_ref[r, 0, g] * tau[0]
                for s in range(1, spins):
                    mixed = mixed + spin_ref[r, s, g] * tau[s]
                mix_ref[i, r, pl.ds(rows, CHUNK), :] = mixed.astype(bf16)

        m_copy(i).start()

    @pl.loop(1, ndev)
    def _(k):
        l_copy(k).wait()

    to_smem = pltpu.make_async_copy(lists, table, l_local)
    to_smem.start()
    to_smem.wait()

    def entry_of(dest, i):
        return table[lax.rem(me + ndev - dest, ndev), 0, i]

    def item(entry):
        time = lax.div(entry, nmom * NDISP)
        m = lax.rem(lax.div(entry, NDISP), nmom)
        d = lax.rem(entry, NDISP)
        ar = ar_ref[pl.ds(m * NDISP + d, 1), :]
        ai = ai_ref[pl.ds(m * NDISP + d, 1), :]
        x = fields[time * NDISP + d]
        first = lax.dot_general(plus[time * nmom + m], x, NT, preferred_element_type=f32)
        second = lax.dot_general(x, minus[time * nmom + m], NT, preferred_element_type=f32)
        g1r = first[:nvec, :nvec] + first[nvec:, nvec:]
        g1i = first[:nvec, nvec:] - first[nvec:, :nvec]
        g2r = second[:nvec, :nvec] + second[nvec:, nvec:]
        g2i = second[:nvec, nvec:] - second[nvec:, :nvec]
        return (
            (g1r - (ar * g2r - ai * g2i)) * factor,
            (g1i - (ar * g2i + ai * g2r)) * factor,
        )

    levels = outer.bit_length() - 1

    def flip(l):
        size = 1 << l
        return zpos + size * (1 - 2 * lax.rem(zpos // size, 2))

    def away(r):
        row = zpos
        for l in range(levels):
            row = row + lax.rem(r // (1 << l), 2) * (flip(l) - zpos)
        return row

    def copy1(n):
        return pltpu.make_async_remote_copy(
            src_ref=part1.at[n], dst_ref=recv1.at[n], send_sem=s1.at[n], recv_sem=r1.at[n],
            device_id=(cfg, space, 1 - core), device_id_type=MESH,
        )

    def copy2(n, j, i):
        return pltpu.make_async_remote_copy(
            src_ref=part2.at[n, i], dst_ref=recv2.at[j, i], send_sem=s2.at[j, i], recv_sem=r2.at[j, i],
            device_id=(cfg, zpos * inner + (1 - ypos), core), device_id_type=MESH,
        )

    def copy3(r, i):
        row = flip((r & -r).bit_length() - 1)
        return pltpu.make_async_remote_copy(
            src_ref=part3.at[r, i], dst_ref=recv3.at[r, i], send_sem=s3.at[r, i], recv_sem=r3.at[r, i],
            device_id=(cfg, row * inner + ypos, core), device_id_type=MESH,
        )

    def unit(n):
        last = n == nspace - 1
        across = jnp.logical_or(n == 0, jnp.logical_and(lax.rem(n, 2) == 1, n < nspace - 1))
        j = jnp.where(across, (n + 1) // 2, jnp.where(last, outer - 1, n // 2 - 1))
        row = away(outer - 1 - j)
        return across, j, (row * inner + jnp.where(across, 1 - ypos, ypos)) * ndiag

    ahead = nspace - 3

    def stored(n):
        return jnp.logical_and(core > 0, n >= ahead)

    def found(n, dest, side, i):
        entry = entry_of(dest, i)
        m = lax.rem(lax.div(entry, NDISP), nmom)
        final = jnp.logical_and(
            lax.div(entry, nmom * NDISP) == slices - 1, lax.rem(entry, NDISP) == NDISP - 1
        )
        return jnp.where(final, 6 * local + m, ((n - ahead) * 2 + side) * local + i)

    def prepare(n):
        _, _, chip = unit(n)
        for side in range(2):
            for i in range(local):
                place = ((n - ahead) * 2 + side) * local + i
                dest = chip + (1 - core if side == 0 else core)
                early[place, 0], early[place, 1] = item(entry_of(dest, i))

    def complete(m):
        early[6 * local + m, 0], early[6 * local + m, 1] = item(
            ((slices - 1) * nmom + m) * NDISP + NDISP - 1
        )

    def give(n):
        _, _, chip = unit(n)

        @pl.when(stored(n))
        def _():
            for i in range(local):
                part1[n, i] = early[found(n, chip + (1 - core), 0, i)].astype(bf16)
            copy1(n).start()

        @pl.when(jnp.logical_not(stored(n)))
        def _():
            for i in range(local):
                real, imag = item(entry_of(chip + (1 - core), i))
                part1[n, i, 0] = real.astype(bf16)
                part1[n, i, 1] = imag.astype(bf16)
            copy1(n).start()

    def keep(n):
        _, _, chip = unit(n)

        @pl.when(stored(n))
        def _():
            for i in range(local):
                own[n, i] = early[found(n, chip + core, 1, i)]

        @pl.when(jnp.logical_not(stored(n)))
        def _():
            for i in range(local):
                own[n, i, 0], own[n, i, 1] = item(entry_of(chip + core, i))

    def join(n):
        across, j, _ = unit(n)
        copy1(n).wait_recv()
        for i in range(local):
            total = own[n, i] + recv1[n, i].astype(f32)
            own[n, i] = total
            part2[n, i] = total.astype(bf16)

            @pl.when(across)
            def _():
                copy2(n, j, i).start()

    def collect_row(r, i):
        j = outer - 1 - r
        n = nspace - 1 if r == 0 else 2 * j + 2
        sources = [r + (1 << l) for l in range(levels) if r % (2 << l) == 0]
        copy2(0, j, i).wait()
        for source in sources:
            copy3(source, i).wait()
        total = own[n, i] + recv2[j, i].astype(f32)
        for source in sources:
            total = total + recv3[source, i].astype(f32)
        if r == 0:
            out_ref[i] = total.astype(bf16)
        else:
            part3[r, i] = total.astype(bf16)
            copy3(r, i).start()

    def collect(q):
        for r in range(outer - 1, -1, -1):
            @pl.when(outer - 1 - q // local == r)
            def _():
                collect_row(r, lax.rem(q, local))

    def halo(t):
        for h in range(2):
            v_copy(t, h).wait_recv()
            displace(t, 2, above, h * half, half)

    @pl.loop(0, slices - 1)
    def _(t):
        halo(t)

    @pl.when(core > 0)
    def _():
        @pl.loop(ahead, nspace)
        def _(n):
            prepare(n)

    halo(slices - 1)

    @pl.loop(0, 3 * nspace)
    def _(k):
        first_core = core == 0
        kind = jnp.where(
            first_core, jnp.where(k < nspace, 0, 1 + lax.rem(k - nspace + 2 * nspace, 2)), lax.rem(k, 3)
        )
        n = jnp.where(first_core, jnp.where(k < nspace, k, (k - nspace + 2 * nspace) // 2 - nspace), k // 3)

        @pl.when(jnp.logical_and(kind == 0, jnp.logical_and(core > 0, n == ahead)))
        def _():
            @pl.loop(0, nmom // 2)
            def _(m):
                complete(2 * m)
                complete(2 * m + 1)

        @pl.when(kind == 0)
        def _():
            give(n)

        @pl.when(kind == 1)
        def _():
            keep(n)

        @pl.when(kind == 2)
        def _():
            join(n)

            waits = jnp.logical_not(first_core)
            first = jnp.where(jnp.logical_and(waits, n == 5), 2, n - 2)
            stop = jnp.where(
                jnp.logical_or(n < 2, jnp.logical_and(waits, n == 4)), first, n - 1
            )

            @pl.loop(first, stop)
            def _(q):
                collect(q)

            @pl.when(n == jnp.where(first_core, 1, nspace - 1))
            def _():
                t_copy.wait()
                mix(0)

            @pl.when(n == jnp.where(first_core, 3, nspace - 1))
            def _():
                mix(1)

    @pl.loop(nspace - 2, (outer - 1) * local)
    def _(q):
        collect(q)

    for i in range(local):
        collect_row(0, i)

    @pl.loop(0, nspace)
    def _(n):
        copy1(n).wait_send()

    for t in range(slices):
        for h in range(2):
            v_copy(t, h).wait_send()
    for i in range(local):
        m_copy(i).wait()


def diagram_kernel(elem_ref, mix_ref, out_hbm, out_ref, store_sem):
    local, spins = mix_ref.shape[:2]
    group = 1

    def store(i, h):
        some = pl.ds(h * group, group)
        return pltpu.make_async_copy(out_ref.at[i, some], out_hbm.at[i, some], store_sem.at[i, h])

    pieces = [(i, h) for i in range(local) for h in range(spins // group)]
    for i, h in pieces:
        if h == 0:
            er, ei = elem_ref[i, 0], elem_ref[i, 1]
            square = jnp.concatenate(
                [jnp.concatenate([er, -ei], 1), jnp.concatenate([ei, er], 1)], 0
            )
        for r in range(h * group, (h + 1) * group):
            out_ref[i, r] = jnp.dot(
                square, mix_ref[i, r], preferred_element_type=f32
            ).astype(bf16)
        store(i, h).start()
    for i, h in pieces:
        store(i, h).wait()


def body(eigvecs, gauge_links, momenta, spin_mix, perambulators, contraction_list):
    slices, _, colors, nvec, depth, plane = eigvecs.shape
    assert depth == 1 and colors == 3
    nspace, ndiag = lax.axis_size("space"), lax.axis_size("diag")
    inner = 2
    outer = nspace // inner
    assert ndiag == 2 and inner * outer == nspace
    assert momenta.shape[0] % 2 == 0 and outer >= 4 and outer & (outer - 1) == 0 and contraction_list.shape[0] == 2
    ndev = nspace * ndiag
    scale = 1.0 / math.sqrt(3 * plane * ndev)
    nmom = momenta.shape[0]
    local = contraction_list.shape[0]
    count, spins = perambulators.shape[:2]
    width = perambulators.shape[4]
    vmem = pl.BlockSpec(memory_space=pltpu.VMEM)
    hbm = pl.BlockSpec(memory_space=pltpu.HBM)
    tile = (local, 2, nvec, nvec)
    field = (2 * nvec, 3 * plane)
    dma = pltpu.SemaphoreType.DMA
    elem, mixed = pl.pallas_call(
        functools.partial(
            elemental_kernel,
            (nspace, ndiag, inner, local, slices, nvec, plane, 0.5 * scale),
        ),
        out_shape=(
            jax.ShapeDtypeStruct(tile, bf16),
            jax.ShapeDtypeStruct((local, spins, 2 * nvec, width), bf16),
        ),
        in_specs=[hbm] * 6,
        out_specs=(vmem, pl.BlockSpec(memory_space=pl.ANY)),
        scratch_shapes=[
            pltpu.SMEM(contraction_list.shape, jnp.int32),
            pltpu.SMEM(momenta.shape, jnp.int32),
            pltpu.SMEM((spins, spins, spin_mix.shape[0]), f32),
            pltpu.VMEM(gauge_links.shape, f32),
            pltpu.VMEM((slices, 2, 3, nvec, plane), bf16),
            pltpu.VMEM((nmom, 3 * plane), f32),
            pltpu.VMEM((nmom, 3 * plane), f32),
            pltpu.VMEM((nmom * NDISP, nvec), f32),
            pltpu.VMEM((nmom * NDISP, nvec), f32),
            pltpu.VMEM((slices, 2, 3, nvec, plane), bf16),
            pltpu.VMEM((slices * NDISP,) + field, bf16),
            pltpu.VMEM((slices * nmom,) + field, bf16),
            pltpu.VMEM((slices * nmom,) + field, bf16),
            pltpu.VMEM((count, spins, 2 * nvec, width), bf16),
            pltpu.VMEM((local, spins, 2 * nvec, width), bf16),
            pltpu.VMEM((ndev, 1, 128), jnp.int32),
            pltpu.SMEM((ndev, 1, 128), jnp.int32),
            pltpu.VMEM((nspace,) + tile, bf16),
            pltpu.VMEM((nspace,) + tile, bf16),
            pltpu.VMEM((nspace,) + tile, f32),
            pltpu.VMEM((6 * local + nmom,) + tile[1:], f32),
            pltpu.VMEM((nspace,) + tile, bf16),
            pltpu.VMEM((outer,) + tile, bf16),
            pltpu.VMEM((outer,) + tile, bf16),
            pltpu.VMEM((outer,) + tile, bf16),
            dma((3,)), dma, dma((slices,)), dma, dma((local,)), dma((slices, 2)), dma((slices, 2)),
            dma((ndev,)), dma((ndev,)), dma,
            dma((nspace,)), dma((nspace,)),
            dma((outer, local)), dma((outer, local)),
            dma((outer, local)), dma((outer, local)),
        ],
        compiler_params=pltpu.CompilerParams(
            collective_id=0, has_side_effects=True, vmem_limit_bytes=44 * 1024 * 1024
        ),
    )(*(
        pltpu.with_memory_space_constraint(x, pltpu.HBM) for x in (
            contraction_list, momenta, spin_mix.transpose(1, 2, 0), gauge_links,
            eigvecs.reshape(slices, 2, 3, nvec, plane),
            perambulators.reshape(count, spins, 2 * nvec, width),
        )
    ))
    out = pl.pallas_call(
        diagram_kernel,
        in_specs=[vmem, vmem],
        out_specs=hbm,
        out_shape=jax.ShapeDtypeStruct((local, spins, 2 * nvec, width), bf16),
        scratch_shapes=[
            pltpu.VMEM((local, spins, 2 * nvec, width), bf16), dma((local, spins)),
        ],
        compiler_params=pltpu.CompilerParams(vmem_limit_bytes=24 * 1024 * 1024),
    )(elem, mixed)
    return out.reshape(local, spins, 2, nvec, width)


def solution(mesh):
    placed = (
        P("cfg", None, None, None, ("space", "diag"), None),
        P("cfg", None, None, None, None, ("space", "diag"), None),
        P(),
        P(),
        P(("cfg", "space", "diag"), None, None, None, None),
        P(("space", "diag"), None),
    )
    return jax.shard_map(
        body,
        mesh=mesh,
        in_specs=placed,
        out_specs=P(("cfg", "space", "diag"), None, None, None, None),
        check_vma=False,
    )
```

```python
import functools
import math

import jax
import jax.numpy as jnp
from jax import lax
from jax.experimental import pallas as pl
from jax.experimental.pallas import tpu as pltpu
from jax.sharding import PartitionSpec as P

LX = 16
LY = 16
NDISP = 4
CHUNK = 16
MESH = pl.DeviceIdType.MESH
NT = (((1,), (1,)), ((), ()))
f32 = jnp.float32
bf16 = jnp.bfloat16


def elemental_kernel(
    dims, list_hbm, mom_hbm, spin_hbm, link_hbm, eig_hbm, tau_hbm, out_ref, mix_hbm,
    list_ref, mom_ref, spin_ref, link_ref,
    eig_ref, cos_ref, sin_ref, ar_ref, ai_ref, above, fields, plus, minus, tau_ref, mix_ref, lists, table,
    part1, recv1, own, early, part2, recv2, part3, recv3,
    small_local, link_local, e_local, t_local, m_local, v_send, v_recv, l_send, l_recv, l_local, s1, r1, s2, r2, s3, r3,
):
    nspace, ndiag, inner, local, slices, nvec, plane, factor = dims
    ndev = nspace * ndiag
    outer = nspace // inner
    space = lax.axis_index("space")
    core = lax.axis_index("diag")
    cfg = lax.axis_index("cfg")
    me = space * ndiag + core
    zpos = space // inner
    ypos = lax.rem(space, inner)

    def device(index):
        return (cfg, index // ndiag, lax.rem(index, ndiag))

    def e_copy(t):
        return pltpu.make_async_copy(eig_hbm.at[t], eig_ref.at[t], e_local.at[t])

    t_copy = pltpu.make_async_copy(tau_hbm, tau_ref, t_local)

    def m_copy(i):
        return pltpu.make_async_copy(mix_ref.at[i], mix_hbm.at[i], m_local.at[i])

    barrier = pltpu.get_barrier_semaphore()

    for k in range(1, ndev):
        pl.semaphore_signal(
            barrier, inc=1, device_id=device(lax.rem(me + k, ndev)), device_id_type=MESH
        )

    small = [
        pltpu.make_async_copy(src, dst, small_local.at[k])
        for k, (src, dst) in enumerate(
            ((list_hbm, list_ref), (mom_hbm, mom_ref), (spin_hbm, spin_ref))
        )
    ]
    link_copy = pltpu.make_async_copy(link_hbm, link_ref, link_local)
    for copy in small:
        copy.start()
    link_copy.start()
    for t in range(slices):
        e_copy(t).start()
    t_copy.start()

    pl.semaphore_wait(barrier, ndev - 1)

    half = nvec // 2

    def v_copy(t, h):
        rows = pl.ds(pl.multiple_of(h * half, half), half)
        return pltpu.make_async_remote_copy(
            src_ref=eig_hbm.at[t, :, :, rows], dst_ref=above.at[t, :, :, rows],
            send_sem=v_send.at[t, h], recv_sem=v_recv.at[t, h],
            device_id=device(lax.rem(me + ndev - 1, ndev)), device_id_type=MESH,
        )

    def l_copy(k):
        return pltpu.make_async_remote_copy(
            src_ref=lists.at[0], dst_ref=lists.at[k],
            send_sem=l_send.at[k], recv_sem=l_recv.at[k],
            device_id=device(lax.rem(me + k, ndev)), device_id_type=MESH,
        )

    for h in range(2):
        v_copy(0, h).start()

    for copy in small:
        copy.wait()
    column = lax.broadcasted_iota(jnp.int32, (1, 128), 1)
    packed = jnp.zeros((1, 128), jnp.int32)
    for i in range(local):
        packed = jnp.where(column == i, list_ref[i, 0], packed)
    lists[0] = packed

    @pl.loop(1, ndev)
    def _(k):
        l_copy(k).start()

    for t in range(1, slices):
        for h in range(2):
            v_copy(t, h).start()

    nmom = mom_ref.shape[0]
    flat = lax.broadcasted_iota(jnp.int32, (1, plane), 1)
    xcoord = lax.rem(flat, LX).astype(f32)
    ycoord = lax.div(flat, LX).astype(f32)
    zcoord = lax.convert_element_type(me, f32)
    rows, hops = [], []
    for m in range(nmom):
        mom = [mom_ref[m, axis].astype(f32) for axis in range(3)]
        rows.append(
            2.0 * math.pi * (mom[0] * xcoord / LX + mom[1] * ycoord / LY + mom[2] * zcoord / ndev)
        )
        hops.append(jnp.full((1, nvec), math.pi, f32))
        for axis, size in enumerate((LX, LY, ndev)):
            hops.append(jnp.full((1, nvec), mom[axis] * (2.0 * math.pi / size), f32))
    angle = jnp.concatenate(rows, 0)
    cos_ref[...] = jnp.concatenate([jnp.cos(angle)] * 3, 1)
    sin_ref[...] = jnp.concatenate([jnp.sin(angle)] * 3, 1)
    hop = jnp.concatenate(hops, 0)
    plain = lax.rem(lax.broadcasted_iota(jnp.int32, hop.shape, 0), NDISP) == 0
    ar_ref[...] = jnp.where(plain, -1.0, jnp.cos(hop))
    ai_ref[...] = jnp.where(plain, 0.0, -jnp.sin(hop))

    lane = lax.broadcasted_iota(jnp.int32, (CHUNK, plane), 1)
    edge = lax.rem(lane, LX) == LX - 1

    def displace(t, direction, source, begin=0, size=nvec):
        @pl.loop(0, size // CHUNK)
        def _(i):
            rows = pl.multiple_of(begin + i * CHUNK, CHUNK)
            vec = []
            for p in range(2):
                line = []
                for c in range(3):
                    v = source[t, p, c, pl.ds(rows, CHUNK), :].astype(f32)
                    if direction == 0:
                        v = jnp.where(
                            edge, pltpu.roll(v, LX - 1, 1), pltpu.roll(v, plane - 1, 1)
                        )
                    elif direction == 1:
                        v = pltpu.roll(v, plane - LX, 1)
                    line.append(v)
                vec.append(line)
            for row in range(3):
                real = imag = None
                for col in range(3):
                    mr = link_ref[t, direction, 0, row, col]
                    mi = link_ref[t, direction, 1, row, col]
                    re = mr * vec[0][col] - mi * vec[1][col]
                    im = mr * vec[1][col] + mi * vec[0][col]
                    real = re if real is None else real + re
                    imag = im if imag is None else imag + im
                lanes = slice(row * plane, (row + 1) * plane)
                fields[t * NDISP + direction + 1, pl.ds(rows, CHUNK), lanes] = real.astype(bf16)
                fields[
                    t * NDISP + direction + 1, pl.ds(nvec + rows, CHUNK), lanes
                ] = imag.astype(bf16)

    def phases(t):
        @pl.loop(0, nvec // CHUNK)
        def _(i):
            rows = pl.multiple_of(i * CHUNK, CHUNK)
            for c in range(3):
                lanes = slice(c * plane, (c + 1) * plane)
                vr = eig_ref[t, 0, c, pl.ds(rows, CHUNK), :]
                vi = eig_ref[t, 1, c, pl.ds(rows, CHUNK), :]
                fields[t * NDISP, pl.ds(rows, CHUNK), lanes] = vr
                fields[t * NDISP, pl.ds(nvec + rows, CHUNK), lanes] = vi
                vr, vi = vr.astype(f32), vi.astype(f32)
                for m in range(nmom):
                    cosine = cos_ref[m:m + 1, lanes]
                    sine = sin_ref[m:m + 1, lanes]
                    a, b = cosine * vr, sine * vi
                    g, h = cosine * vi, sine * vr
                    plus[t * nmom + m, pl.ds(rows, CHUNK), lanes] = (a - b).astype(bf16)
                    plus[t * nmom + m, pl.ds(nvec + rows, CHUNK), lanes] = (g + h).astype(bf16)
                    minus[t * nmom + m, pl.ds(rows, CHUNK), lanes] = (a + b).astype(bf16)
                    minus[t * nmom + m, pl.ds(nvec + rows, CHUNK), lanes] = (g - h).astype(bf16)

    link_copy.wait()

    @pl.loop(0, slices)
    def _(t):
        e_copy(t).wait()
        displace(t, 0, eig_ref)
        displace(t, 1, eig_ref)
        phases(t)

    count, spins = tau_ref.shape[:2]

    def mix(i):
        q = lax.rem(list_ref[i, 2], count)
        g = list_ref[i, 1]

        @pl.loop(0, 2 * nvec // CHUNK)
        def _(n):
            rows = pl.multiple_of(n * CHUNK, CHUNK)
            tau = [tau_ref[q, s, pl.ds(rows, CHUNK), :].astype(f32) for s in range(spins)]
            for r in range(spins):
                mixed = spin_ref[r, 0, g] * tau[0]
                for s in range(1, spins):
                    mixed = mixed + spin_ref[r, s, g] * tau[s]
                mix_ref[i, r, pl.ds(rows, CHUNK), :] = mixed.astype(bf16)

        m_copy(i).start()

    @pl.loop(1, ndev)
    def _(k):
        l_copy(k).wait()

    to_smem = pltpu.make_async_copy(lists, table, l_local)
    to_smem.start()
    to_smem.wait()

    def entry_of(dest, i):
        return table[lax.rem(me + ndev - dest, ndev), 0, i]

    def item(entry):
        time = lax.div(entry, nmom * NDISP)
        m = lax.rem(lax.div(entry, NDISP), nmom)
        d = lax.rem(entry, NDISP)
        ar = ar_ref[pl.ds(m * NDISP + d, 1), :]
        ai = ai_ref[pl.ds(m * NDISP + d, 1), :]
        x = fields[time * NDISP + d]
        first = lax.dot_general(plus[time * nmom + m], x, NT, preferred_element_type=f32)
        second = lax.dot_general(x, minus[time * nmom + m], NT, preferred_element_type=f32)
        g1r = first[:nvec, :nvec] + first[nvec:, nvec:]
        g1i = first[:nvec, nvec:] - first[nvec:, :nvec]
        g2r = second[:nvec, :nvec] + second[nvec:, nvec:]
        g2i = second[:nvec, nvec:] - second[nvec:, :nvec]
        return (
            (g1r - (ar * g2r - ai * g2i)) * factor,
            (g1i - (ar * g2i + ai * g2r)) * factor,
        )

    levels = outer.bit_length() - 1

    def flip(l):
        size = 1 << l
        return zpos + size * (1 - 2 * lax.rem(zpos // size, 2))

    def away(r):
        row = zpos
        for l in range(levels):
            row = row + lax.rem(r // (1 << l), 2) * (flip(l) - zpos)
        return row

    def copy1(n, i):
        return pltpu.make_async_remote_copy(
            src_ref=part1.at[n, i], dst_ref=recv1.at[n, i], send_sem=s1.at[n, i], recv_sem=r1.at[n, i],
            device_id=(cfg, space, 1 - core), device_id_type=MESH,
        )

    def copy2(n, j, i):
        return pltpu.make_async_remote_copy(
            src_ref=part2.at[n, i], dst_ref=recv2.at[j, i], send_sem=s2.at[j, i], recv_sem=r2.at[j, i],
            device_id=(cfg, zpos * inner + (1 - ypos), core), device_id_type=MESH,
        )

    def copy3(r, i):
        row = flip((r & -r).bit_length() - 1)
        return pltpu.make_async_remote_copy(
            src_ref=part3.at[r, i], dst_ref=recv3.at[r, i], send_sem=s3.at[r, i], recv_sem=r3.at[r, i],
            device_id=(cfg, row * inner + ypos, core), device_id_type=MESH,
        )

    def unit(n):
        last = n == nspace - 1
        across = jnp.logical_or(n == 0, jnp.logical_and(lax.rem(n, 2) == 1, n < nspace - 1))
        j = jnp.where(across, (n + 1) // 2, jnp.where(last, outer - 1, n // 2 - 1))
        row = away(outer - 1 - j)
        return across, j, (row * inner + jnp.where(across, 1 - ypos, ypos)) * ndiag

    ahead = nspace - 3

    def stored(n):
        return jnp.logical_and(core > 0, n >= ahead)

    def found(n, dest, side, i):
        entry = entry_of(dest, i)
        m = lax.rem(lax.div(entry, NDISP), nmom)
        final = jnp.logical_and(
            lax.div(entry, nmom * NDISP) == slices - 1, lax.rem(entry, NDISP) == NDISP - 1
        )
        return jnp.where(final, 6 * local + m, ((n - ahead) * 2 + side) * local + i)

    def prepare(n):
        _, _, chip = unit(n)
        for side in range(2):
            for i in range(local):
                place = ((n - ahead) * 2 + side) * local + i
                dest = chip + (1 - core if side == 0 else core)
                early[place, 0], early[place, 1] = item(entry_of(dest, i))

    def complete(m):
        early[6 * local + m, 0], early[6 * local + m, 1] = item(
            ((slices - 1) * nmom + m) * NDISP + NDISP - 1
        )

    def give(n):
        _, _, chip = unit(n)

        @pl.when(stored(n))
        def _():
            for i in range(local):
                part1[n, i] = early[found(n, chip + (1 - core), 0, i)].astype(bf16)
                copy1(n, i).start()

        @pl.when(jnp.logical_not(stored(n)))
        def _():
            for i in range(local):
                real, imag = item(entry_of(chip + (1 - core), i))
                part1[n, i, 0] = real.astype(bf16)
                part1[n, i, 1] = imag.astype(bf16)
                copy1(n, i).start()

    def keep(n):
        _, _, chip = unit(n)

        @pl.when(stored(n))
        def _():
            for i in range(local):
                own[n, i] = early[found(n, chip + core, 1, i)]

        @pl.when(jnp.logical_not(stored(n)))
        def _():
            for i in range(local):
                own[n, i, 0], own[n, i, 1] = item(entry_of(chip + core, i))

    def join(n):
        across, j, _ = unit(n)
        for i in range(local):
            copy1(n, i).wait_recv()
            total = own[n, i] + recv1[n, i].astype(f32)
            own[n, i] = total
            part2[n, i] = total.astype(bf16)

            @pl.when(across)
            def _():
                copy2(n, j, i).start()

    def collect_row(r, i):
        j = outer - 1 - r
        n = nspace - 1 if r == 0 else 2 * j + 2
        sources = [r + (1 << l) for l in range(levels) if r % (2 << l) == 0]
        copy2(0, j, i).wait()
        for source in sources:
            copy3(source, i).wait()
        total = own[n, i] + recv2[j, i].astype(f32)
        for source in sources:
            total = total + recv3[source, i].astype(f32)
        if r == 0:
            out_ref[i] = total.astype(bf16)
        else:
            part3[r, i] = total.astype(bf16)
            copy3(r, i).start()

    def collect(q):
        for r in range(outer - 1, -1, -1):
            @pl.when(outer - 1 - q // local == r)
            def _():
                collect_row(r, lax.rem(q, local))

    def halo(t):
        for h in range(2):
            v_copy(t, h).wait_recv()
            displace(t, 2, above, h * half, half)

    @pl.loop(0, slices - 1)
    def _(t):
        halo(t)

    @pl.when(core > 0)
    def _():
        @pl.loop(ahead, nspace)
        def _(n):
            prepare(n)

    halo(slices - 1)

    @pl.loop(0, 3 * nspace)
    def _(k):
        first_core = core == 0
        kind = jnp.where(
            first_core, jnp.where(k < nspace, 0, 1 + lax.rem(k - nspace + 2 * nspace, 2)), jnp.where(k < 3, lax.rem(k + 1, 3), lax.rem(k, 3))
        )
        n = jnp.where(first_core, jnp.where(k < nspace, k, (k - nspace + 2 * nspace) // 2 - nspace), k // 3)

        @pl.when(jnp.logical_and(kind == 0, jnp.logical_and(core > 0, n == ahead)))
        def _():
            @pl.loop(0, nmom // 2)
            def _(m):
                complete(2 * m)
                complete(2 * m + 1)

        @pl.when(kind == 0)
        def _():
            give(n)

        @pl.when(kind == 1)
        def _():
            keep(n)

        @pl.when(kind == 2)
        def _():
            join(n)

            waits = jnp.logical_not(first_core)
            first = jnp.where(jnp.logical_and(waits, n == 5), 2, n - 2)
            stop = jnp.where(
                jnp.logical_or(n < 2, jnp.logical_and(waits, n == 4)), first, n - 1
            )

            @pl.loop(first, stop)
            def _(q):
                collect(q)

            @pl.when(n == jnp.where(first_core, 1, nspace - 1))
            def _():
                t_copy.wait()
                mix(0)

            @pl.when(n == jnp.where(first_core, 3, nspace - 1))
            def _():
                mix(1)

    @pl.loop(nspace - 2, (outer - 1) * local)
    def _(q):
        collect(q)

    for i in range(local):
        collect_row(0, i)

    @pl.loop(0, nspace)
    def _(n):
        for i in range(local):
            copy1(n, i).wait_send()

    for t in range(slices):
        for h in range(2):
            v_copy(t, h).wait_send()
    for i in range(local):
        m_copy(i).wait()


def diagram_kernel(elem_ref, mix_ref, out_hbm, out_ref, store_sem):
    local, spins = mix_ref.shape[:2]
    group = 1

    def store(i, h):
        some = pl.ds(h * group, group)
        return pltpu.make_async_copy(out_ref.at[i, some], out_hbm.at[i, some], store_sem.at[i, h])

    pieces = [(i, h) for i in range(local) for h in range(spins // group)]
    for i, h in pieces:
        if h == 0:
            er, ei = elem_ref[i, 0], elem_ref[i, 1]
            square = jnp.concatenate(
                [jnp.concatenate([er, -ei], 1), jnp.concatenate([ei, er], 1)], 0
            )
        for r in range(h * group, (h + 1) * group):
            out_ref[i, r] = jnp.dot(
                square, mix_ref[i, r], preferred_element_type=f32
            ).astype(bf16)
        store(i, h).start()
    for i, h in pieces:
        store(i, h).wait()


def body(eigvecs, gauge_links, momenta, spin_mix, perambulators, contraction_list):
    slices, _, colors, nvec, depth, plane = eigvecs.shape
    assert depth == 1 and colors == 3
    nspace, ndiag = lax.axis_size("space"), lax.axis_size("diag")
    inner = 2
    outer = nspace // inner
    assert ndiag == 2 and inner * outer == nspace
    assert momenta.shape[0] % 2 == 0 and outer >= 4 and outer & (outer - 1) == 0 and contraction_list.shape[0] == 2
    ndev = nspace * ndiag
    scale = 1.0 / math.sqrt(3 * plane * ndev)
    nmom = momenta.shape[0]
    local = contraction_list.shape[0]
    count, spins = perambulators.shape[:2]
    width = perambulators.shape[4]
    vmem = pl.BlockSpec(memory_space=pltpu.VMEM)
    hbm = pl.BlockSpec(memory_space=pltpu.HBM)
    tile = (local, 2, nvec, nvec)
    field = (2 * nvec, 3 * plane)
    dma = pltpu.SemaphoreType.DMA
    elem, mixed = pl.pallas_call(
        functools.partial(
            elemental_kernel,
            (nspace, ndiag, inner, local, slices, nvec, plane, 0.5 * scale),
        ),
        out_shape=(
            jax.ShapeDtypeStruct(tile, bf16),
            jax.ShapeDtypeStruct((local, spins, 2 * nvec, width), bf16),
        ),
        in_specs=[hbm] * 6,
        out_specs=(vmem, pl.BlockSpec(memory_space=pl.ANY)),
        scratch_shapes=[
            pltpu.SMEM(contraction_list.shape, jnp.int32),
            pltpu.SMEM(momenta.shape, jnp.int32),
            pltpu.SMEM((spins, spins, spin_mix.shape[0]), f32),
            pltpu.VMEM(gauge_links.shape, f32),
            pltpu.VMEM((slices, 2, 3, nvec, plane), bf16),
            pltpu.VMEM((nmom, 3 * plane), f32),
            pltpu.VMEM((nmom, 3 * plane), f32),
            pltpu.VMEM((nmom * NDISP, nvec), f32),
            pltpu.VMEM((nmom * NDISP, nvec), f32),
            pltpu.VMEM((slices, 2, 3, nvec, plane), bf16),
            pltpu.VMEM((slices * NDISP,) + field, bf16),
            pltpu.VMEM((slices * nmom,) + field, bf16),
            pltpu.VMEM((slices * nmom,) + field, bf16),
            pltpu.VMEM((count, spins, 2 * nvec, width), bf16),
            pltpu.VMEM((local, spins, 2 * nvec, width), bf16),
            pltpu.VMEM((ndev, 1, 128), jnp.int32),
            pltpu.SMEM((ndev, 1, 128), jnp.int32),
            pltpu.VMEM((nspace,) + tile, bf16),
            pltpu.VMEM((nspace,) + tile, bf16),
            pltpu.VMEM((nspace,) + tile, f32),
            pltpu.VMEM((6 * local + nmom,) + tile[1:], f32),
            pltpu.VMEM((nspace,) + tile, bf16),
            pltpu.VMEM((outer,) + tile, bf16),
            pltpu.VMEM((outer,) + tile, bf16),
            pltpu.VMEM((outer,) + tile, bf16),
            dma((3,)), dma, dma((slices,)), dma, dma((local,)), dma((slices, 2)), dma((slices, 2)),
            dma((ndev,)), dma((ndev,)), dma,
            dma((nspace, local)), dma((nspace, local)),
            dma((outer, local)), dma((outer, local)),
            dma((outer, local)), dma((outer, local)),
        ],
        compiler_params=pltpu.CompilerParams(
            collective_id=0, has_side_effects=True, vmem_limit_bytes=44 * 1024 * 1024
        ),
    )(*(
        pltpu.with_memory_space_constraint(x, pltpu.HBM) for x in (
            contraction_list, momenta, spin_mix.transpose(1, 2, 0), gauge_links,
            eigvecs.reshape(slices, 2, 3, nvec, plane),
            perambulators.reshape(count, spins, 2 * nvec, width),
        )
    ))
    out = pl.pallas_call(
        diagram_kernel,
        in_specs=[vmem, vmem],
        out_specs=hbm,
        out_shape=jax.ShapeDtypeStruct((local, spins, 2 * nvec, width), bf16),
        scratch_shapes=[
            pltpu.VMEM((local, spins, 2 * nvec, width), bf16), dma((local, spins)),
        ],
        compiler_params=pltpu.CompilerParams(vmem_limit_bytes=24 * 1024 * 1024),
    )(elem, mixed)
    return out.reshape(local, spins, 2, nvec, width)


def solution(mesh):
    placed = (
        P("cfg", None, None, None, ("space", "diag"), None),
        P("cfg", None, None, None, None, ("space", "diag"), None),
        P(),
        P(),
        P(("cfg", "space", "diag"), None, None, None, None),
        P(("space", "diag"), None),
    )
    return jax.shard_map(
        body,
        mesh=mesh,
        in_specs=placed,
        out_specs=P(("cfg", "space", "diag"), None, None, None, None),
        check_vma=False,
    )
```

```python
import functools
import math

import jax
import jax.numpy as jnp
from jax import lax
from jax.experimental import pallas as pl
from jax.experimental.pallas import tpu as pltpu
from jax.sharding import PartitionSpec as P

LX = 16
LY = 16
NDISP = 4
CHUNK = 32
MESH = pl.DeviceIdType.MESH
NT = (((1,), (1,)), ((), ()))
f32 = jnp.float32
bf16 = jnp.bfloat16


def elemental_kernel(
    dims, list_hbm, mom_hbm, spin_hbm, link_hbm, eig_hbm, tau_hbm, out_ref, mix_hbm,
    list_ref, mom_ref, spin_ref, link_ref,
    eig_ref, cos_ref, sin_ref, ar_ref, ai_ref, above, fields, plus, minus, tau_ref, mix_ref, lists, table,
    part1, recv1, own, early, part2, recv2, part3, recv3,
    small_local, link_local, e_local, t_local, m_local, v_send, v_recv, l_send, l_recv, l_local, s1, r1, s2, r2, s3, r3,
):
    nspace, ndiag, inner, local, slices, nvec, plane, factor = dims
    ndev = nspace * ndiag
    outer = nspace // inner
    space = lax.axis_index("space")
    core = lax.axis_index("diag")
    cfg = lax.axis_index("cfg")
    me = space * ndiag + core
    zpos = space // inner
    ypos = lax.rem(space, inner)

    def device(index):
        return (cfg, index // ndiag, lax.rem(index, ndiag))

    def e_copy(t):
        return pltpu.make_async_copy(eig_hbm.at[t], eig_ref.at[t], e_local.at[t])

    t_copy = pltpu.make_async_copy(tau_hbm, tau_ref, t_local)

    def m_copy(i):
        return pltpu.make_async_copy(mix_ref.at[i], mix_hbm.at[i], m_local.at[i])

    barrier = pltpu.get_barrier_semaphore()

    @pl.loop(1, ndev)
    def _(k):
        pl.semaphore_signal(
            barrier, inc=1, device_id=device(lax.rem(me + k, ndev)), device_id_type=MESH
        )

    small = [
        pltpu.make_async_copy(src, dst, small_local.at[k])
        for k, (src, dst) in enumerate(
            ((list_hbm, list_ref), (mom_hbm, mom_ref), (spin_hbm, spin_ref))
        )
    ]
    link_copy = pltpu.make_async_copy(link_hbm, link_ref, link_local)
    for copy in small:
        copy.start()
    link_copy.start()
    for t in range(slices):
        e_copy(t).start()
    t_copy.start()

    pl.semaphore_wait(barrier, ndev - 1)

    half = nvec // 2

    def v_copy(t, h):
        rows = pl.ds(pl.multiple_of(h * half, half), half)
        return pltpu.make_async_remote_copy(
            src_ref=eig_hbm.at[t, :, :, rows], dst_ref=above.at[t, :, :, rows],
            send_sem=v_send.at[t, h], recv_sem=v_recv.at[t, h],
            device_id=device(lax.rem(me + ndev - 1, ndev)), device_id_type=MESH,
        )

    def l_copy(k):
        return pltpu.make_async_remote_copy(
            src_ref=lists.at[0], dst_ref=lists.at[k],
            send_sem=l_send.at[k], recv_sem=l_recv.at[k],
            device_id=device(lax.rem(me + k, ndev)), device_id_type=MESH,
        )

    for h in range(2):
        v_copy(0, h).start()

    for copy in small:
        copy.wait()
    column = lax.broadcasted_iota(jnp.int32, (1, 128), 1)
    packed = jnp.zeros((1, 128), jnp.int32)
    for i in range(local):
        packed = jnp.where(column == i, list_ref[i, 0], packed)
    lists[0] = packed

    @pl.loop(1, ndev)
    def _(k):
        l_copy(k).start()

    for t in range(1, slices):
        for h in range(2):
            v_copy(t, h).start()

    nmom = mom_ref.shape[0]
    flat = lax.broadcasted_iota(jnp.int32, (1, plane), 1)
    xcoord = lax.rem(flat, LX).astype(f32)
    ycoord = lax.div(flat, LX).astype(f32)
    zcoord = lax.convert_element_type(me, f32)
    rows, hops = [], []
    for m in range(nmom):
        mom = [mom_ref[m, axis].astype(f32) for axis in range(3)]
        rows.append(
            2.0 * math.pi * (mom[0] * xcoord / LX + mom[1] * ycoord / LY + mom[2] * zcoord / ndev)
        )
        hops.append(jnp.full((1, nvec), math.pi, f32))
        for axis, size in enumerate((LX, LY, ndev)):
            hops.append(jnp.full((1, nvec), mom[axis] * (2.0 * math.pi / size), f32))
    angle = jnp.concatenate(rows, 0)
    cos_ref[...] = jnp.concatenate([jnp.cos(angle)] * 3, 1)
    sin_ref[...] = jnp.concatenate([jnp.sin(angle)] * 3, 1)
    hop = jnp.concatenate(hops, 0)
    plain = lax.rem(lax.broadcasted_iota(jnp.int32, hop.shape, 0), NDISP) == 0
    ar_ref[...] = jnp.where(plain, -1.0, jnp.cos(hop))
    ai_ref[...] = jnp.where(plain, 0.0, -jnp.sin(hop))

    lane = lax.broadcasted_iota(jnp.int32, (CHUNK, plane), 1)
    edge = lax.rem(lane, LX) == LX - 1

    def displace(t, direction, source, begin=0, size=nvec):
        @pl.loop(0, size // CHUNK)
        def _(i):
            rows = pl.multiple_of(begin + i * CHUNK, CHUNK)
            vec = []
            for p in range(2):
                line = []
                for c in range(3):
                    v = source[t, p, c, pl.ds(rows, CHUNK), :].astype(f32)
                    if direction == 0:
                        v = jnp.where(
                            edge, pltpu.roll(v, LX - 1, 1), pltpu.roll(v, plane - 1, 1)
                        )
                    elif direction == 1:
                        v = pltpu.roll(v, plane - LX, 1)
                    line.append(v)
                vec.append(line)
            for row in range(3):
                real = imag = None
                for col in range(3):
                    mr = link_ref[t, direction, 0, row, col]
                    mi = link_ref[t, direction, 1, row, col]
                    re = mr * vec[0][col] - mi * vec[1][col]
                    im = mr * vec[1][col] + mi * vec[0][col]
                    real = re if real is None else real + re
                    imag = im if imag is None else imag + im
                lanes = slice(row * plane, (row + 1) * plane)
                fields[t * NDISP + direction + 1, pl.ds(rows, CHUNK), lanes] = real.astype(bf16)
                fields[
                    t * NDISP + direction + 1, pl.ds(nvec + rows, CHUNK), lanes
                ] = imag.astype(bf16)

    def phases(t):
        @pl.loop(0, nvec // CHUNK)
        def _(i):
            rows = pl.multiple_of(i * CHUNK, CHUNK)
            for c in range(3):
                lanes = slice(c * plane, (c + 1) * plane)
                vr = eig_ref[t, 0, c, pl.ds(rows, CHUNK), :]
                vi = eig_ref[t, 1, c, pl.ds(rows, CHUNK), :]
                fields[t * NDISP, pl.ds(rows, CHUNK), lanes] = vr
                fields[t * NDISP, pl.ds(nvec + rows, CHUNK), lanes] = vi
                vr, vi = vr.astype(f32), vi.astype(f32)
                for m in range(nmom):
                    cosine = cos_ref[m:m + 1, lanes]
                    sine = sin_ref[m:m + 1, lanes]
                    a, b = cosine * vr, sine * vi
                    g, h = cosine * vi, sine * vr
                    plus[t * nmom + m, pl.ds(rows, CHUNK), lanes] = (a - b).astype(bf16)
                    plus[t * nmom + m, pl.ds(nvec + rows, CHUNK), lanes] = (g + h).astype(bf16)
                    minus[t * nmom + m, pl.ds(rows, CHUNK), lanes] = (a + b).astype(bf16)
                    minus[t * nmom + m, pl.ds(nvec + rows, CHUNK), lanes] = (g - h).astype(bf16)

    link_copy.wait()

    @pl.loop(0, slices)
    def _(t):
        e_copy(t).wait()
        displace(t, 0, eig_ref)
        displace(t, 1, eig_ref)
        phases(t)

    count, spins = tau_ref.shape[:2]

    def mix(i):
        q = lax.rem(list_ref[i, 2], count)
        g = list_ref[i, 1]

        @pl.loop(0, 2 * nvec // CHUNK)
        def _(n):
            rows = pl.multiple_of(n * CHUNK, CHUNK)
            tau = [tau_ref[q, s, pl.ds(rows, CHUNK), :].astype(f32) for s in range(spins)]
            for r in range(spins):
                mixed = spin_ref[r, 0, g] * tau[0]
                for s in range(1, spins):
                    mixed = mixed + spin_ref[r, s, g] * tau[s]
                mix_ref[i, r, pl.ds(rows, CHUNK), :] = mixed.astype(bf16)

        m_copy(i).start()

    @pl.loop(1, ndev)
    def _(k):
        l_copy(k).wait()

    to_smem = pltpu.make_async_copy(lists, table, l_local)
    to_smem.start()
    to_smem.wait()

    def entry_of(dest, i):
        return table[lax.rem(me + ndev - dest, ndev), 0, i]

    def item(entry):
        time = lax.div(entry, nmom * NDISP)
        m = lax.rem(lax.div(entry, NDISP), nmom)
        d = lax.rem(entry, NDISP)
        ar = ar_ref[pl.ds(m * NDISP + d, 1), :]
        ai = ai_ref[pl.ds(m * NDISP + d, 1), :]
        x = fields[time * NDISP + d]
        first = lax.dot_general(plus[time * nmom + m], x, NT, preferred_element_type=f32)
        second = lax.dot_general(x, minus[time * nmom + m], NT, preferred_element_type=f32)
        g1r = first[:nvec, :nvec] + first[nvec:, nvec:]
        g1i = first[:nvec, nvec:] - first[nvec:, :nvec]
        g2r = second[:nvec, :nvec] + second[nvec:, nvec:]
        g2i = second[:nvec, nvec:] - second[nvec:, :nvec]
        return (
            (g1r - (ar * g2r - ai * g2i)) * factor,
            (g1i - (ar * g2i + ai * g2r)) * factor,
        )

    levels = outer.bit_length() - 1

    def flip(l):
        size = 1 << l
        return zpos + size * (1 - 2 * lax.rem(zpos // size, 2))

    def away(r):
        row = zpos
        for l in range(levels):
            row = row + lax.rem(r // (1 << l), 2) * (flip(l) - zpos)
        return row

    def copy1(n, i):
        return pltpu.make_async_remote_copy(
            src_ref=part1.at[n, i], dst_ref=recv1.at[n, i], send_sem=s1.at[n, i], recv_sem=r1.at[n, i],
            device_id=(cfg, space, 1 - core), device_id_type=MESH,
        )

    def copy2(n, j, i):
        return pltpu.make_async_remote_copy(
            src_ref=part2.at[n, i], dst_ref=recv2.at[j, i], send_sem=s2.at[j, i], recv_sem=r2.at[j, i],
            device_id=(cfg, zpos * inner + (1 - ypos), core), device_id_type=MESH,
        )

    def copy3(r, i):
        row = flip((r & -r).bit_length() - 1)
        return pltpu.make_async_remote_copy(
            src_ref=part3.at[r, i], dst_ref=recv3.at[r, i], send_sem=s3.at[r, i], recv_sem=r3.at[r, i],
            device_id=(cfg, row * inner + ypos, core), device_id_type=MESH,
        )

    def unit(n):
        last = n == nspace - 1
        across = jnp.logical_or(n == 0, jnp.logical_and(lax.rem(n, 2) == 1, n < nspace - 1))
        j = jnp.where(across, (n + 1) // 2, jnp.where(last, outer - 1, n // 2 - 1))
        row = away(outer - 1 - j)
        return across, j, (row * inner + jnp.where(across, 1 - ypos, ypos)) * ndiag

    ahead = nspace - 3

    def stored(n):
        return jnp.logical_and(core > 0, n >= ahead)

    def found(n, dest, side, i):
        entry = entry_of(dest, i)
        m = lax.rem(lax.div(entry, NDISP), nmom)
        final = jnp.logical_and(
            lax.div(entry, nmom * NDISP) == slices - 1, lax.rem(entry, NDISP) == NDISP - 1
        )
        return jnp.where(final, 6 * local + m, ((n - ahead) * 2 + side) * local + i)

    def prepare(n):
        _, _, chip = unit(n)
        for side in range(2):
            for i in range(local):
                place = ((n - ahead) * 2 + side) * local + i
                dest = chip + (1 - core if side == 0 else core)
                early[place, 0], early[place, 1] = item(entry_of(dest, i))

    def complete(m):
        early[6 * local + m, 0], early[6 * local + m, 1] = item(
            ((slices - 1) * nmom + m) * NDISP + NDISP - 1
        )

    def give(n):
        _, _, chip = unit(n)

        @pl.when(stored(n))
        def _():
            for i in range(local):
                part1[n, i] = early[found(n, chip + (1 - core), 0, i)].astype(bf16)
                copy1(n, i).start()

        @pl.when(jnp.logical_not(stored(n)))
        def _():
            for i in range(local):
                real, imag = item(entry_of(chip + (1 - core), i))
                part1[n, i, 0] = real.astype(bf16)
                part1[n, i, 1] = imag.astype(bf16)
                copy1(n, i).start()

    def keep(n):
        _, _, chip = unit(n)

        @pl.when(stored(n))
        def _():
            for i in range(local):
                own[n, i] = early[found(n, chip + core, 1, i)]

        @pl.when(jnp.logical_not(stored(n)))
        def _():
            for i in range(local):
                own[n, i, 0], own[n, i, 1] = item(entry_of(chip + core, i))

    def join(n):
        across, j, _ = unit(n)
        for i in range(local):
            copy1(n, i).wait_recv()
            total = own[n, i] + recv1[n, i].astype(f32)
            own[n, i] = total
            part2[n, i] = total.astype(bf16)

            @pl.when(across)
            def _():
                copy2(n, j, i).start()

    def collect_row(r, i):
        j = outer - 1 - r
        n = nspace - 1 if r == 0 else 2 * j + 2
        sources = [r + (1 << l) for l in range(levels) if r % (2 << l) == 0]
        copy2(0, j, i).wait()
        for source in sources:
            copy3(source, i).wait()
        total = own[n, i] + recv2[j, i].astype(f32)
        for source in sources:
            total = total + recv3[source, i].astype(f32)
        if r == 0:
            out_ref[i] = total.astype(bf16)
        else:
            part3[r, i] = total.astype(bf16)
            copy3(r, i).start()

    def collect(q):
        for r in range(outer - 1, -1, -1):
            @pl.when(outer - 1 - q // local == r)
            def _():
                collect_row(r, lax.rem(q, local))

    def halo(t):
        for h in range(2):
            v_copy(t, h).wait_recv()
            displace(t, 2, above, h * half, half)

    @pl.loop(0, slices - 1)
    def _(t):
        halo(t)

    @pl.when(core > 0)
    def _():
        @pl.loop(ahead, nspace)
        def _(n):
            prepare(n)

    halo(slices - 1)

    @pl.loop(0, 3 * nspace)
    def _(k):
        first_core = core == 0
        kind = jnp.where(
            first_core, jnp.where(k < nspace, 0, 1 + lax.rem(k - nspace + 2 * nspace, 2)), jnp.where(k < 3, lax.rem(k + 1, 3), lax.rem(k, 3))
        )
        n = jnp.where(first_core, jnp.where(k < nspace, k, (k - nspace + 2 * nspace) // 2 - nspace), k // 3)

        @pl.when(jnp.logical_and(kind == 0, jnp.logical_and(core > 0, n == ahead)))
        def _():
            @pl.loop(0, nmom // 2)
            def _(m):
                complete(2 * m)
                complete(2 * m + 1)

        @pl.when(kind == 0)
        def _():
            give(n)

        @pl.when(kind == 1)
        def _():
            keep(n)

        @pl.when(kind == 2)
        def _():
            join(n)

            waits = jnp.logical_not(first_core)
            first = jnp.where(jnp.logical_and(waits, n == 5), 2, n - 2)
            stop = jnp.where(
                jnp.logical_or(n < 2, jnp.logical_and(waits, n == 4)), first, n - 1
            )

            @pl.loop(first, stop)
            def _(q):
                collect(q)

            @pl.when(n == jnp.where(first_core, 1, nspace - 1))
            def _():
                t_copy.wait()
                mix(0)

            @pl.when(n == jnp.where(first_core, 3, nspace - 1))
            def _():
                mix(1)

    @pl.loop(nspace - 2, (outer - 1) * local)
    def _(q):
        collect(q)

    for i in range(local):
        collect_row(0, i)

    @pl.loop(0, nspace)
    def _(n):
        for i in range(local):
            copy1(n, i).wait_send()

    for t in range(slices):
        for h in range(2):
            v_copy(t, h).wait_send()
    for i in range(local):
        m_copy(i).wait()


def diagram_kernel(elem_ref, mix_ref, out_hbm, out_ref, store_sem):
    local, spins = mix_ref.shape[:2]
    group = 1

    def store(i, h):
        some = pl.ds(h * group, group)
        return pltpu.make_async_copy(out_ref.at[i, some], out_hbm.at[i, some], store_sem.at[i, h])

    pieces = [(i, h) for i in range(local) for h in range(spins // group)]
    for i, h in pieces:
        if h == 0:
            er, ei = elem_ref[i, 0], elem_ref[i, 1]
            square = jnp.concatenate(
                [jnp.concatenate([er, -ei], 1), jnp.concatenate([ei, er], 1)], 0
            )
        for r in range(h * group, (h + 1) * group):
            out_ref[i, r] = jnp.dot(
                square, mix_ref[i, r], preferred_element_type=f32
            ).astype(bf16)
        store(i, h).start()
    for i, h in pieces:
        store(i, h).wait()


def body(eigvecs, gauge_links, momenta, spin_mix, perambulators, contraction_list):
    slices, _, colors, nvec, depth, plane = eigvecs.shape
    assert depth == 1 and colors == 3
    nspace, ndiag = lax.axis_size("space"), lax.axis_size("diag")
    inner = 2
    outer = nspace // inner
    assert ndiag == 2 and inner * outer == nspace
    assert momenta.shape[0] % 2 == 0 and outer >= 4 and outer & (outer - 1) == 0 and contraction_list.shape[0] == 2
    ndev = nspace * ndiag
    scale = 1.0 / math.sqrt(3 * plane * ndev)
    nmom = momenta.shape[0]
    local = contraction_list.shape[0]
    count, spins = perambulators.shape[:2]
    width = perambulators.shape[4]
    vmem = pl.BlockSpec(memory_space=pltpu.VMEM)
    hbm = pl.BlockSpec(memory_space=pltpu.HBM)
    tile = (local, 2, nvec, nvec)
    field = (2 * nvec, 3 * plane)
    dma = pltpu.SemaphoreType.DMA
    elem, mixed = pl.pallas_call(
        functools.partial(
            elemental_kernel,
            (nspace, ndiag, inner, local, slices, nvec, plane, 0.5 * scale),
        ),
        out_shape=(
            jax.ShapeDtypeStruct(tile, bf16),
            jax.ShapeDtypeStruct((local, spins, 2 * nvec, width), bf16),
        ),
        in_specs=[hbm] * 6,
        out_specs=(vmem, pl.BlockSpec(memory_space=pl.ANY)),
        scratch_shapes=[
            pltpu.SMEM(contraction_list.shape, jnp.int32),
            pltpu.SMEM(momenta.shape, jnp.int32),
            pltpu.SMEM((spins, spins, spin_mix.shape[0]), f32),
            pltpu.VMEM(gauge_links.shape, f32),
            pltpu.VMEM((slices, 2, 3, nvec, plane), bf16),
            pltpu.VMEM((nmom, 3 * plane), f32),
            pltpu.VMEM((nmom, 3 * plane), f32),
            pltpu.VMEM((nmom * NDISP, nvec), f32),
            pltpu.VMEM((nmom * NDISP, nvec), f32),
            pltpu.VMEM((slices, 2, 3, nvec, plane), bf16),
            pltpu.VMEM((slices * NDISP,) + field, bf16),
            pltpu.VMEM((slices * nmom,) + field, bf16),
            pltpu.VMEM((slices * nmom,) + field, bf16),
            pltpu.VMEM((count, spins, 2 * nvec, width), bf16),
            pltpu.VMEM((local, spins, 2 * nvec, width), bf16),
            pltpu.VMEM((ndev, 1, 128), jnp.int32),
            pltpu.SMEM((ndev, 1, 128), jnp.int32),
            pltpu.VMEM((nspace,) + tile, bf16),
            pltpu.VMEM((nspace,) + tile, bf16),
            pltpu.VMEM((nspace,) + tile, f32),
            pltpu.VMEM((6 * local + nmom,) + tile[1:], f32),
            pltpu.VMEM((nspace,) + tile, bf16),
            pltpu.VMEM((outer,) + tile, bf16),
            pltpu.VMEM((outer,) + tile, bf16),
            pltpu.VMEM((outer,) + tile, bf16),
            dma((3,)), dma, dma((slices,)), dma, dma((local,)), dma((slices, 2)), dma((slices, 2)),
            dma((ndev,)), dma((ndev,)), dma,
            dma((nspace, local)), dma((nspace, local)),
            dma((outer, local)), dma((outer, local)),
            dma((outer, local)), dma((outer, local)),
        ],
        compiler_params=pltpu.CompilerParams(
            collective_id=0, has_side_effects=True, vmem_limit_bytes=44 * 1024 * 1024
        ),
    )(*(
        pltpu.with_memory_space_constraint(x, pltpu.HBM) for x in (
            contraction_list, momenta, spin_mix.transpose(1, 2, 0), gauge_links,
            eigvecs.reshape(slices, 2, 3, nvec, plane),
            perambulators.reshape(count, spins, 2 * nvec, width),
        )
    ))
    out = pl.pallas_call(
        diagram_kernel,
        in_specs=[vmem, vmem],
        out_specs=hbm,
        out_shape=jax.ShapeDtypeStruct((local, spins, 2 * nvec, width), bf16),
        scratch_shapes=[
            pltpu.VMEM((local, spins, 2 * nvec, width), bf16), dma((local, spins)),
        ],
        compiler_params=pltpu.CompilerParams(vmem_limit_bytes=24 * 1024 * 1024),
    )(elem, mixed)
    return out.reshape(local, spins, 2, nvec, width)


def solution(mesh):
    placed = (
        P("cfg", None, None, None, ("space", "diag"), None),
        P("cfg", None, None, None, None, ("space", "diag"), None),
        P(),
        P(),
        P(("cfg", "space", "diag"), None, None, None, None),
        P(("space", "diag"), None),
    )
    return jax.shard_map(
        body,
        mesh=mesh,
        in_specs=placed,
        out_specs=P(("cfg", "space", "diag"), None, None, None, None),
        check_vma=False,
    )
```
